32 devices in a mesh: dp: 8 (over z, y), seq: 4 (over x, core).
Axes of the slice: x: 2, y: 2, z: 4, core: 2. Of those that a mesh axis runs over, the one named last changes fastest.
Arguments:
- tokens: bfloat16 [2, 16, 1024, 1024], P(None, 'dp', 'seq'), may hold values from -6 to 6
- cotangent: bfloat16 [2, 16, 1024, 1024], P(None, 'dp', 'seq'), may hold values from -6 to 6
- lengths: int32 [2, 16], P(None, 'dp'), may hold values from 256 to 1024, as said below
- buckets: int32 [2047], replicated, may hold values from 0 to 31
- norm1_gain: float32 [1024], P(('dp', 'seq')), may hold values from 0.5 to 1.5
- w_query: float32 [1024, 1024], P(('dp', 'seq')), may hold values from -0.09375 to 0.09375
- w_key: float32 [1024, 1024], P(('dp', 'seq')), may hold values from -0.09375 to 0.09375
- w_value: float32 [1024, 1024], P(('dp', 'seq')), may hold values from -0.1875 to 0.1875
- w_out: float32 [1024, 1024], P(('dp', 'seq')), may hold values from -0.75 to 0.75
- rel_table: float32 [512], P(('dp', 'seq')), may hold values from -4 to 4
- norm2_gain: float32 [1024], P(('dp', 'seq')), may hold values from 0.5 to 1.5
- w_in: float32 [1024, 4096], P(('dp', 'seq')), may hold values from -0.1875 to 0.1875
- w_back: float32 [4096, 1024], P(('dp', 'seq')), may hold values from -0.125 to 0.125
Outputs:
- layer_out: bfloat16 [2, 16, 1024, 1024], P(None, 'dp', 'seq')
- input_grad: bfloat16 [2, 16, 1024, 1024], P(None, 'dp', 'seq')
- grad_norm1_gain: float32 [1024], P(('dp', 'seq'))
- grad_w_query: float32 [1024, 1024], P(('dp', 'seq'))
- grad_w_key: float32 [1024, 1024], P(('dp', 'seq'))
- grad_w_value: float32 [1024, 1024], P(('dp', 'seq'))
- grad_w_out: float32 [1024, 1024], P(('dp', 'seq'))
- grad_rel_table: float32 [512], P(('dp', 'seq'))
- grad_norm2_gain: float32 [1024], P(('dp', 'seq'))
- grad_w_in: float32 [1024, 4096], P(('dp', 'seq'))
- grad_w_back: float32 [4096, 1024], P(('dp', 'seq'))
The draws below stay inside these ranges and needn't reach their ends.
Inputs may be any that keep to these rules, and one draw needn't show every extreme that they name: `lengths`: in each micro-batch one sequence has exactly 1024 used slots and another exactly 256; used slots come first in a sequence.
All inputs are finite; a program needn't handle non-finite values.
Results may differ from the reference program's by a relative error of at most 0.03.
Values may be sent and summed in bfloat16 or wider, within the bound.
No kernel may reach another device: no remote copies, remote signals or barrier semaphores. Data moves between devices by JAX's collectives and lax.ppermute only.
A program may use at most 384 MiB of HBM per device.

```python
import jax
import jax.numpy as jnp
from jax import lax

D = 1024
HEADS = 16
DH = 64
FF = 4096
BUCKETS = 32
LEN = 1024
LEN_MIN = 256
MB = 2
SEQS = 16


def draw_lengths(key, part):
    first_key = jax.random.fold_in(key, 11)
    second_key = jax.random.fold_in(key, 23)
    length_draw = jax.random.randint(first_key, (MB, SEQS), LEN_MIN, LEN + 1)
    chosen = jax.random.randint(second_key, (MB, 1), 0, SEQS)
    column = jnp.arange(SEQS)[None, :]
    length_draw = jnp.where(column == chosen, LEN, length_draw)
    length_draw = jnp.where(column == (chosen + 1) % SEQS, LEN_MIN, length_draw)
    return length_draw.astype(jnp.int32)


def touch_ends(values, key, least, top_value):
    longest = values.shape.index(max(values.shape))
    spots = []
    for shift in (0, 1):
        where = [jax.random.randint(jax.random.fold_in(key, axis), (), 0, length) for axis, length in enumerate(values.shape)]
        where[longest] = (where[longest] + shift) % values.shape[longest]
        spots.append(tuple(where))
    return values.at[spots[0]].set(least).at[spots[1]].set(top_value)


def block_scale(stream_key, extent, split, smallest, top_value):
    level, own = 1.0, jax.random.fold_in(stream_key, 6)
    for axis_at, parts in split:
        heights = jnp.exp(jax.random.uniform(jax.random.fold_in(own, axis_at), (parts,), jnp.float32, smallest / len(split), top_value / len(split)))
        level = level * jnp.repeat(heights, extent[axis_at] // parts).reshape([-1 if axis == axis_at else 1 for axis in range(len(extent))])
    return level


def noise(rng, extent, spread, reach, split=(), kind=jnp.bfloat16):
    drawn = spread * jax.random.normal(rng, extent, jnp.float32)
    if split:
        drawn = drawn * block_scale(rng, extent, split, -0.22, 0.18)
    return jnp.clip(drawn, -reach, reach).astype(kind)


def setup_inputs(seed: int = 0) -> dict:
    seeds = jax.random.split(jax.random.key(seed), 14)
    return {
        "tokens": noise(seeds[0], (MB, SEQS, LEN, D), 1.0, 6.0, ((1, 8), (2, 4))),
        "cotangent": noise(seeds[1], (MB, SEQS, LEN, D), 1.0, 6.0, ((1, 8), (2, 4))),
        "lengths": draw_lengths(jax.random.fold_in(seeds[13], 71), 0),
        "buckets": touch_ends(jax.random.randint(seeds[3], (2 * LEN - 1,), 0, BUCKETS), jax.random.fold_in(seeds[3], 1), 0, BUCKETS - 1).astype(jnp.int32),
        "norm1_gain": jnp.clip(1.0 + 0.1 * jax.random.normal(seeds[4], (D,), jnp.float32), 0.5, 1.5),
        "w_query": noise(seeds[5], (D, D), (4 * D) ** -0.5, 0.09375, ((0, 32),), jnp.float32),
        "w_key": noise(seeds[6], (D, D), (4 * D) ** -0.5, 0.09375, ((0, 32),), jnp.float32),
        "w_value": noise(seeds[7], (D, D), D ** -0.5, 0.1875, ((0, 32),), jnp.float32),
        "w_out": noise(seeds[8], (D, D), (D // 16) ** -0.5, 0.75, ((0, 32),), jnp.float32),
        "rel_table": noise(seeds[9], (BUCKETS * HEADS,), 1.0, 4.0, ((0, 32),), jnp.float32),
        "norm2_gain": jnp.clip(1.0 + 0.1 * jax.random.normal(seeds[10], (D,), jnp.float32), 0.5, 1.5),
        "w_in": noise(seeds[11], (D, FF), D ** -0.5, 0.1875, ((0, 32),), jnp.float32),
        "w_back": noise(seeds[12], (FF, D), (FF // 2) ** -0.5, 0.125, ((0, 32),), jnp.float32),
    }


@jax.custom_vjp
def low(v):
    return lax.optimization_barrier(v.astype(jnp.bfloat16)).astype(jnp.float32)

@jax.custom_vjp
def low_back(v):
    return v

def low_keep(v):
    return (low(v), None)

def low_pass(kept, grad):
    return (grad,)

def back_keep(v):
    return (v, None)

def back_low(kept, grad):
    return (low(grad),)
low.defvjp(low_keep, low_pass)
low_back.defvjp(back_keep, back_low)
epsilon = 1e-06
floor_score = -1e+30
highest = lax.Precision.HIGHEST
root_coef = 0.7978845608
cubic_coef = 0.044715

def gelu_tanh(values):
    return 0.5 * values * (1.0 + jnp.tanh(root_coef * (values + cubic_coef * values * values * values)))

def matmul(left, right):
    return jnp.dot(left, right, precision=highest)

def rms_scaled(values, gain):
    inverse = lax.rsqrt(lax.optimization_barrier(jnp.mean(values * values, axis=-1, keepdims=True)) + epsilon)
    return values * inverse * gain

def reference(tokens, cotangent, lengths, buckets, norm1_gain, w_query, w_key, w_value, w_out, rel_table, norm2_gain, w_in, w_back):
    seq_total = MB * SEQS
    inputs = tokens.astype(jnp.float32).reshape(seq_total, LEN, D)
    seq_lengths = lengths.reshape(seq_total).astype(jnp.int32)
    positions = jnp.arange(LEN, dtype=jnp.int32)
    onehot = (buckets[:, None] == jnp.arange(BUCKETS, dtype=jnp.int32)[None, :]).astype(jnp.float32)
    offsets = positions[None, :] - positions[:, None] + (LEN - 1)
    params = tuple((p.astype(jnp.float32) for p in (norm1_gain, w_query, w_key, w_value, w_out, rel_table, norm2_gain, w_in, w_back)))

    def forward(params, inputs):
        gain_one, query_w, key_w, value_w, out_w, bias_table, gain_two, in_w, return_projection_weight = [low(p) for p in params]
        per_offset = matmul(onehot, bias_table.reshape(BUCKETS, HEADS))
        rel_bias = jnp.transpose(per_offset[offsets], (2, 0, 1))

        def one_sequence(values, length):
            hidden_one = low(rms_scaled(values, gain_one))
            per_head_queries = low_back(low(matmul(hidden_one, query_w))).reshape(LEN, HEADS, DH)
            per_head_keys = low_back(low(matmul(hidden_one, key_w))).reshape(LEN, HEADS, DH)
            per_head_values = low_back(low(matmul(hidden_one, value_w))).reshape(LEN, HEADS, DH)
            scores = low_back(jnp.einsum('qhd,khd->hqk', per_head_queries, per_head_keys, precision=highest) + rel_bias)
            scores = jnp.where((positions < length)[None, None, :], scores, floor_score)
            row_max = lax.optimization_barrier(jnp.max(scores, axis=-1, keepdims=True))
            exp_scores = jnp.exp(scores - row_max)
            attn_probs = exp_scores / lax.optimization_barrier(jnp.sum(exp_scores, axis=-1, keepdims=True))
            attended = jnp.einsum('hqk,khd->qhd', low(attn_probs), per_head_values, precision=highest).reshape(LEN, D)
            attended = low_back(low(attended))
            residual_mid = values + low_back(matmul(attended, out_w))
            hidden_two = low(rms_scaled(residual_mid, gain_two))
            pre_act = low_back(matmul(hidden_two, in_w))
            active = low(gelu_tanh(pre_act))
            return residual_mid + matmul(active, return_projection_weight)
        checked = jax.checkpoint(one_sequence)

        def scan_step(scan_carry, scan_item):
            return (scan_carry, checked(scan_item[0], scan_item[1]))
        unused, outputs = lax.scan(scan_step, None, (inputs, seq_lengths))
        return outputs
    outputs, pullback = jax.vjp(forward, params, inputs)
    row_mask = (positions[None, :] < seq_lengths[:, None]).astype(jnp.float32)[:, :, None]
    param_grads, input_grad = pullback(cotangent.astype(jnp.float32).reshape(seq_total, LEN, D) * row_mask)
    out_shape = tokens.shape
    return (outputs.astype(jnp.bfloat16).reshape(out_shape), input_grad.astype(jnp.bfloat16).reshape(out_shape), param_grads[0], param_grads[1], param_grads[2], param_grads[3], param_grads[4], param_grads[5], param_grads[6], param_grads[7], param_grads[8])
```

```python
import functools

import jax
import jax.numpy as jnp
from jax import lax
from jax.experimental import pallas as pl
from jax.experimental.pallas import tpu as pltpu
from jax.sharding import PartitionSpec as P

HEADS = 16
DH = 64
BUCKETS = 32


epsilon = 1e-06
floor_score = -1e30
highest = lax.Precision.HIGHEST
root_coef = 0.7978845608
cubic_coef = 0.044715


def gelu_tanh(values):
    return (
        0.5
        * values
        * (1.0 + jnp.tanh(root_coef * (values + cubic_coef * values * values * values)))
    )


def gelu_slope(values):
    inner = jnp.tanh(root_coef * (values + cubic_coef * values * values * values))
    return 0.5 * (1.0 + inner) + 0.5 * values * (1.0 - inner * inner) * root_coef * (
        1.0 + 3.0 * cubic_coef * values * values
    )


def project(acts, weight):
    return jnp.einsum("srd,de->sre", acts, weight, preferred_element_type=jnp.float32)


def project_back(grads_in, weight):
    return jnp.einsum("sre,de->srd", grads_in, weight, preferred_element_type=jnp.float32)


def contract(acts, grads_in):
    return jnp.einsum("srd,sre->de", acts, grads_in, preferred_element_type=jnp.float32)


def rms_forward(values, gain):
    inverse = lax.rsqrt(jnp.mean(values * values, axis=-1, keepdims=True) + epsilon)
    normed = values * inverse
    return (normed, inverse, (normed * gain.astype(jnp.float32)).astype(jnp.bfloat16))


def rms_backward(grad_hidden, normed, inverse, gain):
    scaled = grad_hidden * gain.astype(jnp.float32)
    grad_values = inverse * (scaled - normed * jnp.mean(scaled * normed, axis=-1, keepdims=True))
    return (grad_values, jnp.sum(grad_hidden * normed, axis=(0, 1)))


def score_block(per_head_queries, per_head_keys, rel_bias, key_valid):
    scores = (
        jnp.einsum(
            "ofck,owck->ocfw", per_head_queries, per_head_keys, preferred_element_type=jnp.float32
        )
        + rel_bias[None]
    )
    return jnp.where(key_valid, scores, floor_score)


def offset_sums(grid, first_row, seq_len):
    head_count, row_count, key_count = grid.shape
    flipped = grid[:, ::-1, :]
    padded = jnp.pad(flipped, ((0, 0), (0, 0), (0, row_count)))
    wide_len = key_count + row_count
    skewed = padded.reshape(head_count, row_count * wide_len)[:, : row_count * (wide_len - 1)]
    skewed = skewed.reshape(head_count, row_count, wide_len - 1)
    column_sums = jnp.sum(skewed, axis=1)
    placed = jnp.zeros((head_count, 2 * seq_len - 1), jnp.float32)
    begin = seq_len - row_count - first_row
    return lax.dynamic_update_slice(placed, column_sums, (jnp.int32(0), begin))


def run_micro(inputs, incoming, seq_lens, attn_set, mlp_set, context):
    onehot, offsets, row_pos, key_pos, first_row, seq_len = context
    gain_one, query_w, key_w, value_w, out_w, bias_table = attn_set
    gain_two, in_w, return_projection_weight = mlp_set
    seq_count, row_count, model_width = inputs.shape
    values = inputs.astype(jnp.float32)
    normed_one, inverse_one, hidden_one = rms_forward(values, gain_one)
    queries = project(hidden_one, query_w).astype(jnp.bfloat16)
    keys_own = project(hidden_one, key_w).astype(jnp.bfloat16)
    values_own = project(hidden_one, value_w).astype(jnp.bfloat16)
    keys_all, values_all = (
        lax.all_gather(keys_own, "seq", axis=1, tiled=True),
        lax.all_gather(values_own, "seq", axis=1, tiled=True),
    )
    per_offset = jnp.dot(
        onehot, bias_table.reshape(BUCKETS, HEADS), preferred_element_type=jnp.float32
    )
    rel_bias = jnp.transpose(per_offset[offsets], (2, 0, 1))
    key_valid = (key_pos[None, :] < seq_lens[:, None])[:, None, None, :]
    per_head_queries = queries.reshape(seq_count, row_count, HEADS, DH)
    per_head_keys = keys_all.reshape(seq_count, seq_len, HEADS, DH)
    per_head_values = values_all.reshape(seq_count, seq_len, HEADS, DH)
    scores = score_block(per_head_queries, per_head_keys, rel_bias, key_valid)
    row_max = jnp.max(scores, axis=-1, keepdims=True)
    exp_scores = jnp.exp(scores - row_max)
    row_total = jnp.sum(exp_scores, axis=-1, keepdims=True)
    attn_probs = exp_scores / row_total
    log_total = row_max + jnp.log(row_total)
    reduced_precision_probs = attn_probs.astype(jnp.bfloat16)
    attended = jnp.einsum(
        "jfpe,jefn->jpfn",
        reduced_precision_probs,
        per_head_values,
        preferred_element_type=jnp.float32,
    )
    attended = attended.reshape(seq_count, row_count, model_width).astype(jnp.bfloat16)
    residual_mid = values + project(attended, out_w)
    normed_two, inverse_two, hidden_two = rms_forward(residual_mid, gain_two)
    pre_act = project(hidden_two, in_w)
    active = gelu_tanh(pre_act).astype(jnp.bfloat16)
    result = (residual_mid + project(active, return_projection_weight)).astype(jnp.bfloat16)
    row_valid = (row_pos[None, :] < seq_lens[:, None]).astype(jnp.float32)[:, :, None]
    grad_out = incoming.astype(jnp.float32) * row_valid
    grad_low = grad_out.astype(jnp.bfloat16)
    grad_back = contract(active, grad_low)
    gradient_active_rows = project_back(grad_low, return_projection_weight)
    grad_pre = (gradient_active_rows * gelu_slope(pre_act)).astype(jnp.bfloat16)
    grad_in = contract(hidden_two, grad_pre)
    grad_hidden_two = project_back(grad_pre, in_w)
    grad_mixed, grad_gain_two = rms_backward(grad_hidden_two, normed_two, inverse_two, gain_two)
    grad_mixed = grad_mixed + grad_out
    grad_branch = grad_mixed.astype(jnp.bfloat16)
    grad_outw = contract(attended, grad_branch)
    gradient_attended_values = project_back(grad_branch, out_w).astype(jnp.bfloat16)
    gradient_attended_values = gradient_attended_values.reshape(seq_count, row_count, HEADS, DH)
    scores = score_block(per_head_queries, per_head_keys, rel_bias, key_valid)
    attn_probs = jnp.exp(scores - log_total)
    reduced_precision_probs = attn_probs.astype(jnp.bfloat16)
    grad_probs = jnp.einsum(
        "ofck,owck->ocfw",
        gradient_attended_values,
        per_head_values,
        preferred_element_type=jnp.float32,
    )
    inner_sum = jnp.sum(attn_probs * grad_probs, axis=-1, keepdims=True)
    gradient_score_matrix = (attn_probs * (grad_probs - inner_sum)).astype(jnp.bfloat16)
    grad_query = jnp.einsum(
        "jfpe,jefn->jpfn", gradient_score_matrix, per_head_keys, preferred_element_type=jnp.float32
    )
    grad_query = grad_query.astype(jnp.bfloat16).reshape(seq_count, row_count, model_width)
    key_part = jnp.einsum(
        "eciv,eicq->evcq",
        gradient_score_matrix,
        per_head_queries,
        preferred_element_type=jnp.float32,
    )
    value_part = jnp.einsum(
        "eciv,eicq->evcq",
        reduced_precision_probs,
        gradient_attended_values,
        preferred_element_type=jnp.float32,
    )
    key_part = key_part.reshape(seq_count, seq_len, model_width)
    value_part = value_part.reshape(seq_count, seq_len, model_width)
    grad_key, grad_value = (
        lax.psum_scatter(
            key_part.astype(jnp.bfloat16), "seq", scatter_dimension=1, tiled=True
        ).astype(jnp.float32),
        lax.psum_scatter(
            value_part.astype(jnp.bfloat16), "seq", scatter_dimension=1, tiled=True
        ).astype(jnp.float32),
    )
    grad_key = grad_key.astype(jnp.bfloat16)
    grad_value = grad_value.astype(jnp.bfloat16)
    offset_grad = offset_sums(
        jnp.sum(gradient_score_matrix.astype(jnp.float32), axis=0), first_row, seq_len
    )
    grad_table = jnp.dot(onehot.astype(jnp.float32).T, offset_grad.T, precision=highest).reshape(-1)
    grad_qw = contract(hidden_one, grad_query)
    grad_kw = contract(hidden_one, grad_key)
    grad_vw = contract(hidden_one, grad_value)
    grad_hidden_one = (
        project_back(grad_query, query_w)
        + project_back(grad_key, key_w)
        + project_back(grad_value, value_w)
    )
    grad_values, grad_gain_one = rms_backward(grad_hidden_one, normed_one, inverse_one, gain_one)
    grad_values = grad_values + grad_mixed
    gradients = (
        grad_gain_one,
        grad_qw,
        grad_kw,
        grad_vw,
        grad_outw,
        grad_table,
        grad_gain_two,
        grad_in,
        grad_back,
    )
    return (result, grad_values.astype(jnp.bfloat16), gradients)


def local(
    tokens,
    cotangent,
    lengths,
    buckets,
    norm1_gain,
    w_query,
    w_key,
    w_value,
    w_out,
    rel_table,
    norm2_gain,
    w_in,
    w_back,
):
    micro_count, seq_count, row_count, model_width = tokens.shape
    seq_parts = lax.axis_size("seq")
    seq_len = row_count * seq_parts
    first_row = lax.axis_index("seq") * row_count
    row_pos = first_row + jnp.arange(row_count, dtype=jnp.int32)
    key_pos = jnp.arange(seq_len, dtype=jnp.int32)
    onehot = (buckets[:, None] == jnp.arange(BUCKETS, dtype=jnp.int32)[None, :]).astype(
        jnp.bfloat16
    )
    offsets = key_pos[None, :] - row_pos[:, None] + (seq_len - 1)
    context = (onehot, offsets, row_pos, key_pos, first_row, seq_len)
    outputs = []
    input_grads = []
    pending = None
    shard_sums = None
    for micro_step in range(micro_count):
        attn_set = (
            lax.all_gather(norm1_gain.astype(jnp.bfloat16), ("dp", "seq"), axis=0, tiled=True),
            lax.all_gather(w_query.astype(jnp.bfloat16), ("dp", "seq"), axis=0, tiled=True),
            lax.all_gather(w_key.astype(jnp.bfloat16), ("dp", "seq"), axis=0, tiled=True),
            lax.all_gather(w_value.astype(jnp.bfloat16), ("dp", "seq"), axis=0, tiled=True),
            lax.all_gather(w_out.astype(jnp.bfloat16), ("dp", "seq"), axis=0, tiled=True),
            lax.all_gather(rel_table.astype(jnp.bfloat16), ("dp", "seq"), axis=0, tiled=True),
        )
        mlp_set = (
            lax.all_gather(norm2_gain.astype(jnp.bfloat16), ("dp", "seq"), axis=0, tiled=True),
            lax.all_gather(w_in.astype(jnp.bfloat16), ("dp", "seq"), axis=0, tiled=True),
            lax.all_gather(w_back.astype(jnp.bfloat16), ("dp", "seq"), axis=0, tiled=True),
        )
        layer_part, grad_part, gradients = run_micro(
            tokens[micro_step],
            cotangent[micro_step],
            lengths[micro_step],
            attn_set,
            mlp_set,
            context,
        )
        outputs.append(layer_part)
        input_grads.append(grad_part)
        pending = gradients if pending is None else jax.tree.map(jnp.add, pending, gradients)
    shard_sums = (
        lax.psum_scatter(pending[0], ("dp", "seq"), scatter_dimension=0, tiled=True),
        lax.psum_scatter(pending[1], ("dp", "seq"), scatter_dimension=0, tiled=True),
        lax.psum_scatter(pending[2], ("dp", "seq"), scatter_dimension=0, tiled=True),
        lax.psum_scatter(pending[3], ("dp", "seq"), scatter_dimension=0, tiled=True),
        lax.psum_scatter(pending[4], ("dp", "seq"), scatter_dimension=0, tiled=True),
        lax.psum_scatter(pending[5], ("dp", "seq"), scatter_dimension=0, tiled=True),
        lax.psum_scatter(pending[6], ("dp", "seq"), scatter_dimension=0, tiled=True),
        lax.psum_scatter(pending[7], ("dp", "seq"), scatter_dimension=0, tiled=True),
        lax.psum_scatter(pending[8], ("dp", "seq"), scatter_dimension=0, tiled=True),
    )
    return (
        jnp.stack(outputs),
        jnp.stack(input_grads),
        shard_sums[0],
        shard_sums[1],
        shard_sums[2],
        shard_sums[3],
        shard_sums[4],
        shard_sums[5],
        shard_sums[6],
        shard_sums[7],
        shard_sums[8],
    )


NT = (((1,), (1,)), ((), ()))
TN = (((0,), (0,)), ((), ()))
STRIP = 128

def _dot(a, b, dims=(((1,), (0,)), ((), ()))):
    return lax.dot_general(a, b, dims, preferred_element_type=jnp.float32)

def head_lanes(x, which, width=64):
    lane = lax.broadcasted_iota(jnp.int32, (1, x.shape[1]), 1)
    keep = (lane < width) if which == 0 else (lane >= width)
    return jnp.where(keep, x, jnp.zeros_like(x))

def skew(row, wide):
    rows = jnp.broadcast_to(row, (STRIP, wide))
    return pltpu.roll(rows, wide - (STRIP - 1), 1, stride=1, stride_axis=0)

def fwd_kernel(len_ref, q_ref, k_ref, v_ref, t_ref, o_ref, lse_ref, strip, *, rows, seq_len):
    wide = t_ref.shape[-1]
    length = len_ref[0]
    blocks = seq_len // rows
    per = rows // STRIP
    col_ok = lax.broadcasted_iota(jnp.int32, (1, seq_len), 1) < length
    lane = lax.broadcasted_iota(jnp.int32, (1, 128), 1)
    k2 = k_ref[...]
    v2 = v_ref[...]
    for a in range(2):
        strip[a] = skew(t_ref[0, a:a + 1, :], wide)

    def step(b, carry):
        base = pl.multiple_of(b * rows, rows)
        q2 = q_ref[pl.ds(base, rows), :]
        outs, stats = [], []
        for a in range(2):
            scores = _dot(head_lanes(q2, a), k2, NT)
            parts = []
            for i in range(per):
                off = pl.multiple_of((seq_len - STRIP) - (b * per + i) * STRIP, STRIP)
                parts.append(strip[a, :, pl.ds(off, seq_len)])
            bias = jnp.concatenate(parts, 0) if per > 1 else parts[0]
            scores = jnp.where(col_ok, scores + bias, floor_score)
            top = jnp.max(scores, axis=1, keepdims=True)
            probs = jnp.exp(scores - top)
            total = jnp.sum(probs, axis=1, keepdims=True)
            out = _dot(probs.astype(jnp.bfloat16), v2)
            outs.append(out * (1.0 / total))
            stats.append(top + jnp.log(total))
        o_ref[pl.ds(base, rows), :] = jnp.where(lane < 64, outs[0], outs[1]).astype(jnp.bfloat16)
        lse_ref[0, pl.ds(base, rows), :] = jnp.where(lane < 64, stats[0], stats[1])
        return carry

    lax.fori_loop(0, blocks, step, 0, unroll=2)

def attn_fwd(length, q, k, v, t, rows=256):
    seq_len, width = q.shape
    pairs = width // 128
    wide = t.shape[-1]
    blk = pl.BlockSpec((seq_len, 128), lambda p, n: (0, p))
    return pl.pallas_call(
        functools.partial(fwd_kernel, rows=rows, seq_len=seq_len),
        out_shape=(jax.ShapeDtypeStruct((seq_len, width), jnp.bfloat16),
                   jax.ShapeDtypeStruct((pairs, seq_len, 128), jnp.float32)),
        grid_spec=pltpu.PrefetchScalarGridSpec(
            num_scalar_prefetch=1, grid=(pairs,),
            in_specs=[blk, blk, blk, pl.BlockSpec((1, 2, wide), lambda p, n: (p, 0, 0))],
            out_specs=[blk, pl.BlockSpec((1, seq_len, 128), lambda p, n: (p, 0, 0))],
            scratch_shapes=[pltpu.VMEM((2, STRIP, wide), jnp.float32)]),
        compiler_params=pltpu.CompilerParams(vmem_limit_bytes=56 << 20),
        cost_estimate=pl.CostEstimate(flops=4 * seq_len * seq_len * width * 4, bytes_accessed=seq_len * width * 12, transcendentals=seq_len * seq_len * 16),
        name="attn_fwd",
    )(length, q, k, v, t)

def bwd_kernel(len_ref, q_ref, k_ref, v_ref, do_ref, o_ref, lse_ref, t_ref,
               dq_ref, dk_ref, dv_ref, g_ref, strip, acc, dq_acc, *, rows, seq_len):
    wide = t_ref.shape[-1]
    length = len_ref[0]
    blocks = seq_len // rows
    per = rows // STRIP
    lane = lax.broadcasted_iota(jnp.int32, (1, 128), 1)
    q2 = q_ref[...]
    do2 = do_ref[...]
    prod = (do2.astype(jnp.float32) * o_ref[...].astype(jnp.float32)).T
    stat = lse_ref[0].T
    lse_rows = [stat[0:1, :], stat[64:65, :]]
    delta_rows = [jnp.sum(prod[0:64], axis=0, keepdims=True), jnp.sum(prod[64:128], axis=0, keepdims=True)]
    for a in range(2):
        strip[a] = skew(t_ref[0, a:a + 1, :], wide)
    acc[...] = jnp.zeros_like(acc)
    dq_acc[...] = jnp.zeros_like(dq_acc)

    def step(b, carry):
        base = pl.multiple_of(b * rows, rows)
        k2 = k_ref[pl.ds(base, rows), :]
        v2 = v_ref[pl.ds(base, rows), :]
        row_ok = (base + lax.broadcasted_iota(jnp.int32, (rows, 1), 0)) < length
        dks, dvs = [], []
        for a in range(2):
            scores = _dot(head_lanes(k2, a), q2, NT)
            offs = [pl.multiple_of((seq_len - STRIP) - (b * per + i) * STRIP, STRIP) for i in range(per)]
            bias = [strip[a, :, pl.ds(off, seq_len)] for off in offs]
            bias = jnp.concatenate(bias, 0) if per > 1 else bias[0]
            probs = jnp.where(row_ok, jnp.exp(scores + bias - lse_rows[a]), 0.0)
            grad_probs = _dot(head_lanes(v2, a), do2, NT)
            grad_scores = probs * (grad_probs - delta_rows[a])
            for i, off in enumerate(offs):
                acc[a, :, pl.ds(off, seq_len)] += grad_scores[i * STRIP:(i + 1) * STRIP]
            probs_b = probs.astype(jnp.bfloat16)
            gs_b = grad_scores.astype(jnp.bfloat16)
            dvs.append(_dot(probs_b, do2))
            dks.append(_dot(gs_b, q2))
            dq_acc[a] += _dot(gs_b, k2, TN)
        dk_ref[pl.ds(base, rows), :] = jnp.where(lane < 64, dks[0], dks[1]).astype(jnp.bfloat16)
        dv_ref[pl.ds(base, rows), :] = jnp.where(lane < 64, dvs[0], dvs[1]).astype(jnp.bfloat16)
        return carry

    lax.fori_loop(0, blocks, step, 0)
    dq_ref[...] = jnp.where(lane < 64, dq_acc[0], dq_acc[1]).astype(jnp.bfloat16)
    for a in range(2):
        sums = acc[a]
        half = STRIP
        while half > 8:
            half //= 2
            sums = sums[:half] + pltpu.roll(sums[half:], wide - half, 1)
        while half > 1:
            half //= 2
            sums = sums + pltpu.roll(pltpu.roll(sums, 8 - half, 0), wide - half, 1)
        g_ref[0, a:a + 1, :] = pltpu.roll(sums, STRIP - 1, 1)[0:1]

def attn_bwd(length, q, k, v, do, o, lse, trev, rows=256):
    seq_len, width = q.shape
    pairs = width // 128
    wide = trev.shape[-1]
    blk = pl.BlockSpec((seq_len, 128), lambda p, n: (0, p))
    tb = pl.BlockSpec((1, 2, wide), lambda p, n: (p, 0, 0))
    mat = jax.ShapeDtypeStruct((seq_len, width), jnp.bfloat16)
    return pl.pallas_call(
        functools.partial(bwd_kernel, rows=rows, seq_len=seq_len),
        out_shape=(mat, mat, mat, jax.ShapeDtypeStruct((pairs, 2, wide), jnp.float32)),
        grid_spec=pltpu.PrefetchScalarGridSpec(
            num_scalar_prefetch=1, grid=(pairs,),
            in_specs=[blk, blk, blk, blk, blk, pl.BlockSpec((1, seq_len, 128), lambda p, n: (p, 0, 0)), tb],
            out_specs=[blk, blk, blk, tb],
            scratch_shapes=[pltpu.VMEM((2, STRIP, wide), jnp.float32), pltpu.VMEM((2, STRIP, wide), jnp.float32),
                            pltpu.VMEM((2, seq_len, 128), jnp.float32)]),
        compiler_params=pltpu.CompilerParams(vmem_limit_bytes=56 << 20),
        cost_estimate=pl.CostEstimate(flops=10 * seq_len * seq_len * width * 4, bytes_accessed=seq_len * width * 20, transcendentals=seq_len * seq_len * 16),
        name="attn_bwd",
    )(length, q, k, v, do, o, lse, trev)

LIMIT = 58 << 20

def qkv_kernel(x_ref, gain_ref, w_ref, h_ref, q_ref, k_ref, v_ref):
    x = x_ref[...].astype(jnp.float32)
    inverse = lax.rsqrt(jnp.mean(x * x, axis=1, keepdims=True) + epsilon)
    hidden = (x * inverse * gain_ref[...]).astype(jnp.bfloat16)
    h_ref[...] = hidden
    width = x.shape[1]
    for i, ref in enumerate((q_ref, k_ref, v_ref)):
        ref[...] = _dot(hidden, w_ref[:, i * width:(i + 1) * width]).astype(jnp.bfloat16)

def qkv_fwd(x, gain, w, rows=512):
    total, width = x.shape
    blk = pl.BlockSpec((rows, width), lambda i: (i, 0))
    mat = jax.ShapeDtypeStruct((total, width), jnp.bfloat16)
    return pl.pallas_call(
        qkv_kernel, out_shape=(mat,) * 4, grid=(total // rows,),
        in_specs=[blk, pl.BlockSpec((1, width), lambda i: (0, 0)),
                  pl.BlockSpec((width, 3 * width), lambda i: (0, 0), pipeline_mode=pl.Buffered(1))],
        out_specs=[blk] * 4,
        compiler_params=pltpu.CompilerParams(vmem_limit_bytes=LIMIT),
        cost_estimate=pl.CostEstimate(flops=6 * total * width * width, bytes_accessed=total * width * 10 + width * width * 6, transcendentals=0),
        name="qkv_fwd",
    )(x, gain, w)

def gelu_both(v):
    t = jnp.tanh(root_coef * (v + cubic_coef * v * v * v))
    half = 0.5 * (1.0 + t)
    slope = half + 0.5 * v * (1.0 - t * t) * (root_coef * (1.0 + 3.0 * cubic_coef * v * v))
    return v * half, slope

def mid_kernel(len_ref, x_ref, o_ref, g_ref, gain_ref, wo_ref, win_ref, wback_ref,
               out_ref, gb_ref, do_ref, gwo_ref, gwin_ref, gwback_ref,
               mixed, h2, h2t, acc, gh2, gm):
    step = pl.program_id(0)
    rows = x_ref.shape[0]

    part = 256

    @pl.when(step == 0)
    def _():
        def load(i, carry):
            at = pl.ds(pl.multiple_of(i * part, part), part)
            row_ok = i * part + lax.broadcasted_iota(jnp.int32, (part, 1), 0) < len_ref[0]
            gm[at, :] = jnp.where(row_ok, g_ref[at, :], jnp.zeros((part, g_ref.shape[1]), jnp.bfloat16))
            value = x_ref[at, :].astype(jnp.float32) + _dot(o_ref[at, :], wo_ref[...])
            mixed[at, :] = value
            acc[at, :] = value
            inverse = lax.rsqrt(jnp.mean(value * value, axis=1, keepdims=True) + epsilon)
            hidden = (value * inverse * gain_ref[...]).astype(jnp.bfloat16)
            h2[at, :] = hidden
            h2t[:, at] = hidden.T
            gh2[at, :] = jnp.zeros_like(value)
            return carry
        lax.fori_loop(0, rows // part, load, 0)

    pre = _dot(h2[...], win_ref[...])
    grad_active = _dot(gm[...], wback_ref[...], NT)
    act, slope = gelu_both(pre)
    active = act.astype(jnp.bfloat16)
    gpre = (grad_active * slope).astype(jnp.bfloat16)
    acc[...] += _dot(active, wback_ref[...])
    gwback_ref[...] = _dot(active, gm[...], TN).astype(jnp.bfloat16)
    gwin_ref[...] = _dot(h2t[...], gpre).astype(jnp.bfloat16)
    gh2[...] += _dot(gpre, win_ref[...], NT)

    @pl.when(step == pl.num_programs(0) - 1)
    def _():
        def finish(i, carry):
            at = pl.ds(pl.multiple_of(i * part, part), part)
            out_ref[at, :] = acc[at, :].astype(jnp.bfloat16)
            value = mixed[at, :]
            inverse = lax.rsqrt(jnp.mean(value * value, axis=1, keepdims=True) + epsilon)
            normed = value * inverse
            scaled = gh2[at, :] * gain_ref[...]
            grad = inverse * (scaled - normed * jnp.mean(scaled * normed, axis=1, keepdims=True)) + gm[at, :].astype(jnp.float32)
            gb = grad.astype(jnp.bfloat16)
            gb_ref[at, :] = gb
            do_ref[at, :] = _dot(gb, wo_ref[...], NT).astype(jnp.bfloat16)
            return carry
        lax.fori_loop(0, rows // part, finish, 0)
        gwo_ref[...] = _dot(o_ref[...], gb_ref[...], TN).astype(jnp.bfloat16)

def mid(length, x, o, g, gain, wo, win, wback, cols=512):
    rows, width = x.shape
    ff = win.shape[1]
    one = lambda shape: pl.BlockSpec(shape, lambda i, n: (0, 0), pipeline_mode=pl.Buffered(1))
    res = one
    mat = jax.ShapeDtypeStruct((rows, width), jnp.bfloat16)
    return pl.pallas_call(
        mid_kernel,
        out_shape=(mat, mat, mat, jax.ShapeDtypeStruct((width, width), jnp.bfloat16),
                   jax.ShapeDtypeStruct((width, ff), jnp.bfloat16), jax.ShapeDtypeStruct((ff, width), jnp.bfloat16)),
        grid_spec=pltpu.PrefetchScalarGridSpec(
            num_scalar_prefetch=1, grid=(ff // cols,),
            in_specs=[one((rows, width)), one((rows, width)), one((rows, width)), one((1, width)), one((width, width)),
                      pl.BlockSpec((width, cols), lambda i, n: (0, i)), pl.BlockSpec((cols, width), lambda i, n: (i, 0))],
            out_specs=[res((rows, width)), res((rows, width)), res((rows, width)), res((width, width)),
                       pl.BlockSpec((width, cols), lambda i, n: (0, i)), pl.BlockSpec((cols, width), lambda i, n: (i, 0))],
            scratch_shapes=[pltpu.VMEM((rows, width), jnp.float32), pltpu.VMEM((rows, width), jnp.bfloat16),
                            pltpu.VMEM((width, rows), jnp.bfloat16), pltpu.VMEM((rows, width), jnp.float32),
                            pltpu.VMEM((rows, width), jnp.float32), pltpu.VMEM((rows, width), jnp.bfloat16)]),
        compiler_params=pltpu.CompilerParams(vmem_limit_bytes=LIMIT),
        cost_estimate=pl.CostEstimate(flops=12 * rows * width * ff + 6 * rows * width * width, bytes_accessed=rows * width * 12 + width * width * 4 + width * ff * 8, transcendentals=rows * ff),
        name="mid",
    )(length, x, o, g, gain, wo, win, wback)

def gw_kernel(h_ref, dq_ref, dk_ref, dv_ref, out_ref):
    for i, ref in enumerate((dq_ref, dk_ref, dv_ref)):
        w = ref.shape[1]
        out_ref[:, i * w:(i + 1) * w] = _dot(h_ref[...], ref[...], TN).astype(jnp.bfloat16)

def qkv_gw(h, dq, dk, dv):
    rows, width = h.shape
    return pl.pallas_call(
        gw_kernel, out_shape=jax.ShapeDtypeStruct((width, 3 * width), jnp.bfloat16),
        compiler_params=pltpu.CompilerParams(vmem_limit_bytes=LIMIT),
        cost_estimate=pl.CostEstimate(flops=6 * rows * width * width, bytes_accessed=rows * width * 8 + width * width * 6, transcendentals=0),
        name="qkv_gw",
    )(h, dq, dk, dv)

def gx_kernel(x_ref, gb_ref, dq_ref, dk_ref, dv_ref, gain_ref, w_ref, out_ref):
    width = x_ref.shape[1]
    grad = _dot(dq_ref[...], w_ref[:, :width], NT)
    grad += _dot(dk_ref[...], w_ref[:, width:2 * width], NT)
    grad += _dot(dv_ref[...], w_ref[:, 2 * width:3 * width], NT)
    x = x_ref[...].astype(jnp.float32)
    inverse = lax.rsqrt(jnp.mean(x * x, axis=1, keepdims=True) + epsilon)
    normed = x * inverse
    scaled = grad * gain_ref[...]
    out = inverse * (scaled - normed * jnp.mean(scaled * normed, axis=1, keepdims=True)) + gb_ref[...].astype(jnp.float32)
    out_ref[...] = out.astype(jnp.bfloat16)

def qkv_gx(x, gb, dq, dk, dv, gain, w, rows=512):
    total, width = x.shape
    blk = pl.BlockSpec((rows, width), lambda i: (i, 0))
    return pl.pallas_call(
        gx_kernel, out_shape=jax.ShapeDtypeStruct((total, width), jnp.bfloat16), grid=(total // rows,),
        in_specs=[blk] * 5 + [pl.BlockSpec((1, width), lambda i: (0, 0)),
                              pl.BlockSpec((width, 3 * width), lambda i: (0, 0), pipeline_mode=pl.Buffered(1))],
        out_specs=blk,
        compiler_params=pltpu.CompilerParams(vmem_limit_bytes=LIMIT),
        cost_estimate=pl.CostEstimate(flops=6 * total * width * width, bytes_accessed=total * width * 12 + width * width * 6, transcendentals=0),
        name="qkv_gx",
    )(x, gb, dq, dk, dv, gain, w)
def exchange(blocks):
    parts = blocks.shape[0]
    me = lax.axis_index("seq")
    pick = lambda at: lax.dynamic_index_in_dim(blocks, at, 0, keepdims=True)
    out = lax.dynamic_update_slice_in_dim(jnp.zeros_like(blocks), pick(me), me, 0)
    for mask in range(1, parts):
        came = lax.ppermute(pick(me ^ mask), "seq", [(i, i ^ mask) for i in range(parts)])
        out = lax.dynamic_update_slice_in_dim(out, came, me ^ mask, 0)
    return out


def local_whole(tokens, cotangent, lengths, buckets, norm1_gain, w_query, w_key, w_value, w_out, rel_table, norm2_gain, w_in, w_back):
    micro_count, seq_count, row_count, width = tokens.shape
    parts = micro_count * seq_count
    seq_len = parts * row_count
    both = ("dp", "seq")
    me = lax.axis_index("seq")
    low = lambda v: v.astype(jnp.bfloat16)
    own = norm1_gain.shape[0]
    few = rel_table.shape[0]
    small = jnp.stack([norm1_gain, norm2_gain, jnp.pad(rel_table, (0, own - few))], 1)
    small = jnp.pad(low(small), ((0, 0), (0, 125)))
    shard1 = jnp.concatenate([low(w_query), low(w_key), low(w_value), small], 1)
    shard2 = jnp.concatenate([low(w_out), low(w_in)], 1)
    full1 = lax.all_gather(shard1, both, axis=0, tiled=True)
    x = exchange(tokens.reshape(parts, row_count, width)).reshape(seq_len, width)
    full2 = lax.all_gather(shard2, both, axis=0, tiled=True)
    full3 = lax.all_gather(low(w_back), both, axis=0, tiled=True)
    g = exchange(cotangent.reshape(parts, row_count, width)).reshape(seq_len, width)
    length = lax.dynamic_index_in_dim(lengths.reshape(parts), me, 0)

    extra = full1[:, 3 * width:]
    gain1 = extra[:, 0].astype(jnp.float32).reshape(1, width)
    gain2 = extra[:, 1].astype(jnp.float32).reshape(1, width)
    table = extra[:, 2].reshape(-1, own)[:, :few].reshape(BUCKETS, HEADS)
    ids = jnp.arange(BUCKETS, dtype=jnp.int32)[:, None]
    hot = low(jnp.pad(buckets, (0, 1), constant_values=-1)[None, :] == ids)
    hot_back = low(jnp.pad(buckets[::-1], (0, 1), constant_values=-1)[None, :] == ids)
    spread = lambda h: jnp.einsum("bh,bo->ho", table, h, preferred_element_type=jnp.float32).reshape(HEADS // 2, 2, -1)

    hidden, q, k, v = qkv_fwd(x, gain1, full1)
    attended, lse = attn_fwd(length, q, k, v, spread(hot))
    out, gb, grad_attended, gwo, gwin, gwback = mid(length, x, attended, g, gain2, full2[:, :width], full2[:, width:], full3)
    dq, dk, dv, g_off = attn_bwd(length, q, k, v, grad_attended, attended, lse, spread(hot_back))
    g_table = jnp.dot(hot_back.astype(jnp.float32), g_off.reshape(HEADS, -1).T, precision=highest)
    gw = qkv_gw(hidden, dq, dk, dv)
    gx = qkv_gx(x, gb, dq, dk, dv, gain1, full1)
    scatter = lambda v: lax.psum_scatter(v, both, scatter_dimension=0, tiled=True)
    column = jnp.pad(g_table.reshape(-1, few), ((0, 0), (0, own - few))).reshape(-1, 1)
    r2 = scatter(jnp.concatenate([gwo, gwin], 1)).astype(jnp.float32)
    r3 = scatter(gwback).astype(jnp.float32)
    r1 = scatter(jnp.concatenate([gw, jnp.pad(low(column), ((0, 0), (0, 127)))], 1)).astype(jnp.float32)
    layer_out = exchange(out.reshape(parts, row_count, width)).reshape(tokens.shape)
    input_grad = exchange(gx.reshape(parts, row_count, width)).reshape(tokens.shape)
    up = lambda v: v.astype(jnp.float32)
    g_gain1 = jnp.sum(up(shard1[:, :3 * width]) * r1[:, :3 * width], axis=1) / up(low(norm1_gain))
    g_gain2 = jnp.sum(up(shard2[:, width:]) * r2[:, width:], axis=1) / up(low(norm2_gain))
    return (layer_out, input_grad, g_gain1, r1[:, :width], r1[:, width:2 * width], r1[:, 2 * width:3 * width],
            r2[:, :width], r1[:few, 3 * width], g_gain2, r2[:, width:], r3)


def local_any(shape, tokens, *rest):
    whole = tokens.shape[0] * tokens.shape[1] == shape[1] and tokens.shape[3] % 128 == 0
    return (local_whole if whole else local)(tokens, *rest)


def solution(mesh):
    return jax.shard_map(
        functools.partial(local_any, mesh.devices.shape),
        mesh=mesh,
        in_specs=(
            P(None, "dp", "seq", None),
            P(None, "dp", "seq", None),
            P(None, "dp"),
            P(),
            P(("dp", "seq")),
            P(("dp", "seq"), None),
            P(("dp", "seq"), None),
            P(("dp", "seq"), None),
            P(("dp", "seq"), None),
            P(("dp", "seq")),
            P(("dp", "seq")),
            P(("dp", "seq"), None),
            P(("dp", "seq"), None),
        ),
        out_specs=(
            P(None, "dp", "seq", None),
            P(None, "dp", "seq", None),
            P(("dp", "seq")),
            P(("dp", "seq"), None),
            P(("dp", "seq"), None),
            P(("dp", "seq"), None),
            P(("dp", "seq"), None),
            P(("dp", "seq")),
            P(("dp", "seq")),
            P(("dp", "seq"), None),
            P(("dp", "seq"), None),
        ),
        check_vma=False,
    )
```

```python
import functools

import jax
import jax.numpy as jnp
from jax import lax
from jax.experimental import pallas as pl
from jax.experimental.pallas import tpu as pltpu
from jax.sharding import PartitionSpec as P

HEADS = 16
DH = 64
BUCKETS = 32


epsilon = 1e-06
floor_score = -1e30
highest = lax.Precision.HIGHEST
root_coef = 0.7978845608
cubic_coef = 0.044715


def gelu_tanh(values):
    return (
        0.5
        * values
        * (1.0 + jnp.tanh(root_coef * (values + cubic_coef * values * values * values)))
    )


def gelu_slope(values):
    inner = jnp.tanh(root_coef * (values + cubic_coef * values * values * values))
    return 0.5 * (1.0 + inner) + 0.5 * values * (1.0 - inner * inner) * root_coef * (
        1.0 + 3.0 * cubic_coef * values * values
    )


def project(acts, weight):
    return jnp.einsum("srd,de->sre", acts, weight, preferred_element_type=jnp.float32)


def project_back(grads_in, weight):
    return jnp.einsum("sre,de->srd", grads_in, weight, preferred_element_type=jnp.float32)


def contract(acts, grads_in):
    return jnp.einsum("srd,sre->de", acts, grads_in, preferred_element_type=jnp.float32)


def rms_forward(values, gain):
    inverse = lax.rsqrt(jnp.mean(values * values, axis=-1, keepdims=True) + epsilon)
    normed = values * inverse
    return (normed, inverse, (normed * gain.astype(jnp.float32)).astype(jnp.bfloat16))


def rms_backward(grad_hidden, normed, inverse, gain):
    scaled = grad_hidden * gain.astype(jnp.float32)
    grad_values = inverse * (scaled - normed * jnp.mean(scaled * normed, axis=-1, keepdims=True))
    return (grad_values, jnp.sum(grad_hidden * normed, axis=(0, 1)))


def score_block(per_head_queries, per_head_keys, rel_bias, key_valid):
    scores = (
        jnp.einsum(
            "ofck,owck->ocfw", per_head_queries, per_head_keys, preferred_element_type=jnp.float32
        )
        + rel_bias[None]
    )
    return jnp.where(key_valid, scores, floor_score)


def offset_sums(grid, first_row, seq_len):
    head_count, row_count, key_count = grid.shape
    flipped = grid[:, ::-1, :]
    padded = jnp.pad(flipped, ((0, 0), (0, 0), (0, row_count)))
    wide_len = key_count + row_count
    skewed = padded.reshape(head_count, row_count * wide_len)[:, : row_count * (wide_len - 1)]
    skewed = skewed.reshape(head_count, row_count, wide_len - 1)
    column_sums = jnp.sum(skewed, axis=1)
    placed = jnp.zeros((head_count, 2 * seq_len - 1), jnp.float32)
    begin = seq_len - row_count - first_row
    return lax.dynamic_update_slice(placed, column_sums, (jnp.int32(0), begin))


def run_micro(inputs, incoming, seq_lens, attn_set, mlp_set, context):
    onehot, offsets, row_pos, key_pos, first_row, seq_len = context
    gain_one, query_w, key_w, value_w, out_w, bias_table = attn_set
    gain_two, in_w, return_projection_weight = mlp_set
    seq_count, row_count, model_width = inputs.shape
    values = inputs.astype(jnp.float32)
    normed_one, inverse_one, hidden_one = rms_forward(values, gain_one)
    queries = project(hidden_one, query_w).astype(jnp.bfloat16)
    keys_own = project(hidden_one, key_w).astype(jnp.bfloat16)
    values_own = project(hidden_one, value_w).astype(jnp.bfloat16)
    keys_all, values_all = (
        lax.all_gather(keys_own, "seq", axis=1, tiled=True),
        lax.all_gather(values_own, "seq", axis=1, tiled=True),
    )
    per_offset = jnp.dot(
        onehot, bias_table.reshape(BUCKETS, HEADS), preferred_element_type=jnp.float32
    )
    rel_bias = jnp.transpose(per_offset[offsets], (2, 0, 1))
    key_valid = (key_pos[None, :] < seq_lens[:, None])[:, None, None, :]
    per_head_queries = queries.reshape(seq_count, row_count, HEADS, DH)
    per_head_keys = keys_all.reshape(seq_count, seq_len, HEADS, DH)
    per_head_values = values_all.reshape(seq_count, seq_len, HEADS, DH)
    scores = score_block(per_head_queries, per_head_keys, rel_bias, key_valid)
    row_max = jnp.max(scores, axis=-1, keepdims=True)
    exp_scores = jnp.exp(scores - row_max)
    row_total = jnp.sum(exp_scores, axis=-1, keepdims=True)
    attn_probs = exp_scores / row_total
    log_total = row_max + jnp.log(row_total)
    reduced_precision_probs = attn_probs.astype(jnp.bfloat16)
    attended = jnp.einsum(
        "jfpe,jefn->jpfn",
        reduced_precision_probs,
        per_head_values,
        preferred_element_type=jnp.float32,
    )
    attended = attended.reshape(seq_count, row_count, model_width).astype(jnp.bfloat16)
    residual_mid = values + project(attended, out_w)
    normed_two, inverse_two, hidden_two = rms_forward(residual_mid, gain_two)
    pre_act = project(hidden_two, in_w)
    active = gelu_tanh(pre_act).astype(jnp.bfloat16)
    result = (residual_mid + project(active, return_projection_weight)).astype(jnp.bfloat16)
    row_valid = (row_pos[None, :] < seq_lens[:, None]).astype(jnp.float32)[:, :, None]
    grad_out = incoming.astype(jnp.float32) * row_valid
    grad_low = grad_out.astype(jnp.bfloat16)
    grad_back = contract(active, grad_low)
    gradient_active_rows = project_back(grad_low, return_projection_weight)
    grad_pre = (gradient_active_rows * gelu_slope(pre_act)).astype(jnp.bfloat16)
    grad_in = contract(hidden_two, grad_pre)
    grad_hidden_two = project_back(grad_pre, in_w)
    grad_mixed, grad_gain_two = rms_backward(grad_hidden_two, normed_two, inverse_two, gain_two)
    grad_mixed = grad_mixed + grad_out
    grad_branch = grad_mixed.astype(jnp.bfloat16)
    grad_outw = contract(attended, grad_branch)
    gradient_attended_values = project_back(grad_branch, out_w).astype(jnp.bfloat16)
    gradient_attended_values = gradient_attended_values.reshape(seq_count, row_count, HEADS, DH)
    scores = score_block(per_head_queries, per_head_keys, rel_bias, key_valid)
    attn_probs = jnp.exp(scores - log_total)
    reduced_precision_probs = attn_probs.astype(jnp.bfloat16)
    grad_probs = jnp.einsum(
        "ofck,owck->ocfw",
        gradient_attended_values,
        per_head_values,
        preferred_element_type=jnp.float32,
    )
    inner_sum = jnp.sum(attn_probs * grad_probs, axis=-1, keepdims=True)
    gradient_score_matrix = (attn_probs * (grad_probs - inner_sum)).astype(jnp.bfloat16)
    grad_query = jnp.einsum(
        "jfpe,jefn->jpfn", gradient_score_matrix, per_head_keys, preferred_element_type=jnp.float32
    )
    grad_query = grad_query.astype(jnp.bfloat16).reshape(seq_count, row_count, model_width)
    key_part = jnp.einsum(
        "eciv,eicq->evcq",
        gradient_score_matrix,
        per_head_queries,
        preferred_element_type=jnp.float32,
    )
    value_part = jnp.einsum(
        "eciv,eicq->evcq",
        reduced_precision_probs,
        gradient_attended_values,
        preferred_element_type=jnp.float32,
    )
    key_part = key_part.reshape(seq_count, seq_len, model_width)
    value_part = value_part.reshape(seq_count, seq_len, model_width)
    grad_key, grad_value = (
        lax.psum_scatter(
            key_part.astype(jnp.bfloat16), "seq", scatter_dimension=1, tiled=True
        ).astype(jnp.float32),
        lax.psum_scatter(
            value_part.astype(jnp.bfloat16), "seq", scatter_dimension=1, tiled=True
        ).astype(jnp.float32),
    )
    grad_key = grad_key.astype(jnp.bfloat16)
    grad_value = grad_value.astype(jnp.bfloat16)
    offset_grad = offset_sums(
        jnp.sum(gradient_score_matrix.astype(jnp.float32), axis=0), first_row, seq_len
    )
    grad_table = jnp.dot(onehot.astype(jnp.float32).T, offset_grad.T, precision=highest).reshape(-1)
    grad_qw = contract(hidden_one, grad_query)
    grad_kw = contract(hidden_one, grad_key)
    grad_vw = contract(hidden_one, grad_value)
    grad_hidden_one = (
        project_back(grad_query, query_w)
        + project_back(grad_key, key_w)
        + project_back(grad_value, value_w)
    )
    grad_values, grad_gain_one = rms_backward(grad_hidden_one, normed_one, inverse_one, gain_one)
    grad_values = grad_values + grad_mixed
    gradients = (
        grad_gain_one,
        grad_qw,
        grad_kw,
        grad_vw,
        grad_outw,
        grad_table,
        grad_gain_two,
        grad_in,
        grad_back,
    )
    return (result, grad_values.astype(jnp.bfloat16), gradients)


def local(
    tokens,
    cotangent,
    lengths,
    buckets,
    norm1_gain,
    w_query,
    w_key,
    w_value,
    w_out,
    rel_table,
    norm2_gain,
    w_in,
    w_back,
):
    micro_count, seq_count, row_count, model_width = tokens.shape
    seq_parts = lax.axis_size("seq")
    seq_len = row_count * seq_parts
    first_row = lax.axis_index("seq") * row_count
    row_pos = first_row + jnp.arange(row_count, dtype=jnp.int32)
    key_pos = jnp.arange(seq_len, dtype=jnp.int32)
    onehot = (buckets[:, None] == jnp.arange(BUCKETS, dtype=jnp.int32)[None, :]).astype(
        jnp.bfloat16
    )
    offsets = key_pos[None, :] - row_pos[:, None] + (seq_len - 1)
    context = (onehot, offsets, row_pos, key_pos, first_row, seq_len)
    outputs = []
    input_grads = []
    pending = None
    shard_sums = None
    for micro_step in range(micro_count):
        attn_set = (
            lax.all_gather(norm1_gain.astype(jnp.bfloat16), ("dp", "seq"), axis=0, tiled=True),
            lax.all_gather(w_query.astype(jnp.bfloat16), ("dp", "seq"), axis=0, tiled=True),
            lax.all_gather(w_key.astype(jnp.bfloat16), ("dp", "seq"), axis=0, tiled=True),
            lax.all_gather(w_value.astype(jnp.bfloat16), ("dp", "seq"), axis=0, tiled=True),
            lax.all_gather(w_out.astype(jnp.bfloat16), ("dp", "seq"), axis=0, tiled=True),
            lax.all_gather(rel_table.astype(jnp.bfloat16), ("dp", "seq"), axis=0, tiled=True),
        )
        mlp_set = (
            lax.all_gather(norm2_gain.astype(jnp.bfloat16), ("dp", "seq"), axis=0, tiled=True),
            lax.all_gather(w_in.astype(jnp.bfloat16), ("dp", "seq"), axis=0, tiled=True),
            lax.all_gather(w_back.astype(jnp.bfloat16), ("dp", "seq"), axis=0, tiled=True),
        )
        layer_part, grad_part, gradients = run_micro(
            tokens[micro_step],
            cotangent[micro_step],
            lengths[micro_step],
            attn_set,
            mlp_set,
            context,
        )
        outputs.append(layer_part)
        input_grads.append(grad_part)
        pending = gradients if pending is None else jax.tree.map(jnp.add, pending, gradients)
    shard_sums = (
        lax.psum_scatter(pending[0], ("dp", "seq"), scatter_dimension=0, tiled=True),
        lax.psum_scatter(pending[1], ("dp", "seq"), scatter_dimension=0, tiled=True),
        lax.psum_scatter(pending[2], ("dp", "seq"), scatter_dimension=0, tiled=True),
        lax.psum_scatter(pending[3], ("dp", "seq"), scatter_dimension=0, tiled=True),
        lax.psum_scatter(pending[4], ("dp", "seq"), scatter_dimension=0, tiled=True),
        lax.psum_scatter(pending[5], ("dp", "seq"), scatter_dimension=0, tiled=True),
        lax.psum_scatter(pending[6], ("dp", "seq"), scatter_dimension=0, tiled=True),
        lax.psum_scatter(pending[7], ("dp", "seq"), scatter_dimension=0, tiled=True),
        lax.psum_scatter(pending[8], ("dp", "seq"), scatter_dimension=0, tiled=True),
    )
    return (
        jnp.stack(outputs),
        jnp.stack(input_grads),
        shard_sums[0],
        shard_sums[1],
        shard_sums[2],
        shard_sums[3],
        shard_sums[4],
        shard_sums[5],
        shard_sums[6],
        shard_sums[7],
        shard_sums[8],
    )


NT = (((1,), (1,)), ((), ()))
TN = (((0,), (0,)), ((), ()))
STRIP = 128
LIMIT = 58 << 20

def _dot(a, b, dims=(((1,), (0,)), ((), ()))):
    return lax.dot_general(a, b, dims, preferred_element_type=jnp.float32)

def head_lanes(x, which, width=64):
    lane = lax.broadcasted_iota(jnp.int32, (1, x.shape[1]), 1)
    keep = (lane < width) if which == 0 else (lane >= width)
    return jnp.where(keep, x, jnp.zeros_like(x))

def skew(row, wide):
    rows = jnp.broadcast_to(row, (STRIP, wide))
    return pltpu.roll(rows, wide - (STRIP - 1), 1, stride=1, stride_axis=0)

def fwd_kernel(len_ref, q_ref, k_ref, v_ref, t_ref, o_ref, lse_ref, strip, *, rows, seq_len):
    wide = t_ref.shape[-1]
    length = len_ref[0]
    pair = pl.program_id(0)
    blocks = seq_len // rows
    per = rows // STRIP
    col_ok = lax.broadcasted_iota(jnp.int32, (1, seq_len), 1) < length
    lane = lax.broadcasted_iota(jnp.int32, (1, 128), 1)
    k2 = k_ref[...]
    v2 = v_ref[...]
    for a in range(2):
        strip[a] = skew(t_ref[pl.ds(2 * pair + a, 1), :], wide)

    def step(b, carry):
        base = pl.multiple_of(b * rows, rows)
        q2 = q_ref[pl.ds(base, rows), :]
        outs, stats = [], []
        for a in range(2):
            scores = _dot(head_lanes(q2, a), k2, NT)
            parts = []
            for i in range(per):
                off = pl.multiple_of((seq_len - STRIP) - (b * per + i) * STRIP, STRIP)
                parts.append(strip[a, :, pl.ds(off, seq_len)])
            bias = jnp.concatenate(parts, 0) if per > 1 else parts[0]
            scores = jnp.where(col_ok, scores + bias, floor_score)
            top = jnp.max(scores, axis=1, keepdims=True)
            probs = jnp.exp(scores - top)
            total = jnp.sum(probs, axis=1, keepdims=True)
            out = _dot(probs.astype(jnp.bfloat16), v2)
            outs.append(out * (1.0 / total))
            stats.append(top + jnp.log(total))
        o_ref[pl.ds(base, rows), :] = jnp.where(lane < 64, outs[0], outs[1]).astype(jnp.bfloat16)
        lse_ref[0, pl.ds(base, rows), :] = jnp.where(lane < 64, stats[0], stats[1])
        return carry

    lax.fori_loop(0, blocks, step, 0, unroll=2)

def attn_fwd(length, q, k, v, t, rows=256):
    seq_len, width = q.shape
    pairs = width // 128
    wide = t.shape[-1]
    blk = pl.BlockSpec((seq_len, 128), lambda p, n: (0, p))
    return pl.pallas_call(
        functools.partial(fwd_kernel, rows=rows, seq_len=seq_len),
        out_shape=(jax.ShapeDtypeStruct((seq_len, width), jnp.bfloat16),
                   jax.ShapeDtypeStruct((pairs, seq_len, 128), jnp.float32)),
        grid_spec=pltpu.PrefetchScalarGridSpec(
            num_scalar_prefetch=1, grid=(pairs,),
            in_specs=[blk, blk, blk, pl.BlockSpec(t.shape, lambda p, n: (0, 0))],
            out_specs=[blk, pl.BlockSpec((1, seq_len, 128), lambda p, n: (p, 0, 0))],
            scratch_shapes=[pltpu.VMEM((2, STRIP, wide), jnp.float32)]),
        compiler_params=pltpu.CompilerParams(vmem_limit_bytes=40 << 20),
        cost_estimate=pl.CostEstimate(flops=8 * seq_len * seq_len * width, bytes_accessed=seq_len * width * 12, transcendentals=seq_len * seq_len * pairs * 2),
        name="attn_fwd",
    )(length, q, k, v, t)

def bwd_kernel(len_ref, q_ref, k_ref, v_ref, do_ref, o_ref, lse_ref, t_ref, *refs, rows, seq_len, first):
    dq_ref, dk_ref, dv_ref, g_ref, strip, acc, dq_acc = refs[-7:]
    wide = t_ref.shape[-1]
    length = len_ref[0]
    local_pair = pl.program_id(0)
    pair = first + local_pair
    blocks = seq_len // rows
    per = rows // STRIP
    lane = lax.broadcasted_iota(jnp.int32, (1, 128), 1)
    q2 = q_ref[...]
    do2 = do_ref[...]
    prod = (do2.astype(jnp.float32) * o_ref[...].astype(jnp.float32)).T
    stat = lse_ref[0].T
    lse_rows = [stat[0:1, :], stat[64:65, :]]
    delta_rows = [jnp.sum(prod[0:64], axis=0, keepdims=True), jnp.sum(prod[64:128], axis=0, keepdims=True)]
    for a in range(2):
        strip[a] = skew(t_ref[pl.ds(2 * pair + a, 1), :], wide)
    acc[...] = jnp.zeros_like(acc)
    dq_acc[...] = jnp.zeros_like(dq_acc)

    def step(b, carry):
        base = pl.multiple_of(b * rows, rows)
        k2 = k_ref[pl.ds(base, rows), :]
        v2 = v_ref[pl.ds(base, rows), :]
        row_ok = (base + lax.broadcasted_iota(jnp.int32, (rows, 1), 0)) < length
        dks, dvs = [], []
        for a in range(2):
            scores = _dot(head_lanes(k2, a), q2, NT)
            offs = [pl.multiple_of((seq_len - STRIP) - (b * per + i) * STRIP, STRIP) for i in range(per)]
            bias = [strip[a, :, pl.ds(off, seq_len)] for off in offs]
            bias = jnp.concatenate(bias, 0) if per > 1 else bias[0]
            probs = jnp.where(row_ok, jnp.exp(scores + bias - lse_rows[a]), 0.0)
            grad_probs = _dot(head_lanes(v2, a), do2, NT)
            grad_scores = probs * (grad_probs - delta_rows[a])
            for i, off in enumerate(offs):
                acc[a, :, pl.ds(off, seq_len)] += grad_scores[i * STRIP:(i + 1) * STRIP]
            probs_b = probs.astype(jnp.bfloat16)
            gs_b = grad_scores.astype(jnp.bfloat16)
            dvs.append(_dot(probs_b, do2))
            dks.append(_dot(gs_b, q2))
            dq_acc[a] += _dot(gs_b, k2, TN)
        dk_ref[pl.ds(base, rows), :] = jnp.where(lane < 64, dks[0], dks[1]).astype(jnp.bfloat16)
        dv_ref[pl.ds(base, rows), :] = jnp.where(lane < 64, dvs[0], dvs[1]).astype(jnp.bfloat16)
        return carry

    lax.fori_loop(0, blocks, step, 0)
    dq_ref[...] = jnp.where(lane < 64, dq_acc[0], dq_acc[1]).astype(jnp.bfloat16)
    for a in range(2):
        sums = acc[a]
        half = STRIP
        while half > 8:
            half //= 2
            sums = sums[:half] + pltpu.roll(sums[half:], wide - half, 1)
        while half > 1:
            half //= 2
            sums = sums + pltpu.roll(pltpu.roll(sums, 8 - half, 0), wide - half, 1)
        g_ref[pl.ds(2 * local_pair + a, 1), :] = pltpu.roll(sums, STRIP - 1, 1)[0:1]

def attn_bwd(length, q, k, v, do, o, lse, trev, first, count, prev=None, rows=256):
    seq_len, width = q.shape
    wide = trev.shape[-1]
    blk = pl.BlockSpec((seq_len, 128), lambda p, n: (0, first + p))
    mat = jax.ShapeDtypeStruct((seq_len, width), jnp.bfloat16)
    prev = tuple(prev) if prev is not None else ()
    return pl.pallas_call(
        functools.partial(bwd_kernel, rows=rows, seq_len=seq_len, first=first),
        out_shape=(mat, mat, mat, jax.ShapeDtypeStruct((2 * count, wide), jnp.float32)),
        grid_spec=pltpu.PrefetchScalarGridSpec(
            num_scalar_prefetch=1, grid=(count,),
            in_specs=[blk, blk, blk, blk, blk, pl.BlockSpec((1, seq_len, 128), lambda p, n: (first + p, 0, 0)),
                      pl.BlockSpec(trev.shape, lambda p, n: (0, 0))] + [pl.BlockSpec(memory_space=pl.ANY)] * len(prev),
            out_specs=[blk, blk, blk, pl.BlockSpec((2 * count, wide), lambda p, n: (0, 0))],
            scratch_shapes=[pltpu.VMEM((2, STRIP, wide), jnp.float32), pltpu.VMEM((2, STRIP, wide), jnp.float32),
                            pltpu.VMEM((2, seq_len, 128), jnp.float32)]),
        input_output_aliases={8 + i: i for i in range(len(prev))},
        compiler_params=pltpu.CompilerParams(vmem_limit_bytes=40 << 20),
        cost_estimate=pl.CostEstimate(flops=20 * seq_len * seq_len * 128 * count, bytes_accessed=seq_len * 128 * count * 20, transcendentals=seq_len * seq_len * count * 2),
        name="attn_bwd",
    )(length, q, k, v, do, o, lse, trev, *prev)

ANY = pl.BlockSpec(memory_space=pl.ANY)
VM = pl.BlockSpec(memory_space=pltpu.VMEM)
SM = pl.BlockSpec(memory_space=pltpu.SMEM)

def rms_inverse(value):
    return lax.rsqrt(jnp.mean(value * value, axis=1, keepdims=True) + epsilon)

def pull_sequence(me, whole_ref, came, dst, sem):
    rows = whole_ref.shape[1]
    for mask, ref in enumerate((whole_ref,) + tuple(came)):
        src = ref.at[me] if mask == 0 else ref.at[0]
        at = pl.multiple_of((me ^ mask) * rows, rows)
        pltpu.make_async_copy(src, dst.at[pl.ds(at, rows), :], sem).start()

def qkv_kernel(ids_ref, x4_ref, c1_ref, c2_ref, c3_ref, *refs, masks):
    gathered = refs[:len(masks)]
    bucket_ref = refs[len(masks)]
    x_out, h_out, q_out, k_out, v_out, w_out, gain_ref, t_ref, trev_ref, xs, hs, ps, ws, es, sems = refs[len(masks) + 1:]
    me, flat = ids_ref[0], ids_ref[1]
    width = xs.shape[1]
    own = width // es.shape[0]
    pull_sequence(me, x4_ref, (c1_ref, c2_ref, c3_ref), xs, sems.at[0])
    for ref, ids in zip(gathered, masks):
        for j, mask in enumerate(ids):
            shard = flat ^ mask
            pltpu.make_async_copy(ref.at[j, 3 * own:3 * own + 16, :], es.at[shard], sems.at[1]).start()
    for ref, ids in zip(gathered, masks):
        for j, mask in enumerate(ids):
            at = pl.multiple_of((flat ^ mask) * own, own)
            for i in range(3):
                pltpu.make_async_copy(ref.at[j, i * own:(i + 1) * own, :], ws.at[pl.ds(at, own), i * width:(i + 1) * width], sems.at[2]).start()
    pltpu.make_async_copy(es, es, sems.at[1]).wait()
    extras = es[...].astype(jnp.float32)
    gains = jnp.sum(extras, axis=0)
    gain_ref[...] = gains[0:8]
    table = extras[:, 8, 0:128].astype(jnp.bfloat16)
    ids = lax.broadcasted_iota(jnp.int32, (es.shape[0], 1), 0)
    heads = t_ref.shape[0]
    for i, ref in enumerate((t_ref, trev_ref)):
        hot = jnp.where(bucket_ref[i:i + 1, :] == ids, 1.0, 0.0).astype(jnp.bfloat16)
        ref[...] = _dot(table, hot, TN)[0:heads]
    pltpu.make_async_copy(xs, xs, sems.at[0]).wait()
    part = 256
    def norm(i, carry):
        at = pl.ds(pl.multiple_of(i * part, part), part)
        x = xs[at, :].astype(jnp.float32)
        hs[at, :] = (x * rms_inverse(x) * gains[0:1]).astype(jnp.bfloat16)
        return carry
    lax.fori_loop(0, xs.shape[0] // part, norm, 0)
    copies = [pltpu.make_async_copy(xs, x_out, sems.at[0]), pltpu.make_async_copy(hs, h_out, sems.at[1])]
    for copy in copies:
        copy.start()
    pltpu.make_async_copy(ws, ws, sems.at[2]).wait()
    copies.append(pltpu.make_async_copy(ws, w_out, sems.at[2]))
    copies[-1].start()
    for i, ref in enumerate((q_out, k_out, v_out)):
        ps[i] = _dot(hs[...], ws[:, i * width:(i + 1) * width]).astype(jnp.bfloat16)
        copies.append(pltpu.make_async_copy(ps.at[i], ref, sems.at[3 + i]))
        copies[-1].start()
    for copy in copies:
        copy.wait()

def qkv_fwd(ids, x4, came, gathered, masks, bucket_rows, heads):
    parts, rows, width = x4.shape
    total = parts * rows
    shards = sum(len(m) for m in masks)
    mat = jax.ShapeDtypeStruct((total, width), jnp.bfloat16)
    wide = bucket_rows.shape[1]
    vm = lambda *s: pltpu.VMEM(s, jnp.bfloat16)
    return pl.pallas_call(
        functools.partial(qkv_kernel, masks=masks),
        out_shape=(mat,) * 5 + (jax.ShapeDtypeStruct((width, 3 * width), jnp.bfloat16), jax.ShapeDtypeStruct((8, width), jnp.float32),
                                jax.ShapeDtypeStruct((heads, wide), jnp.float32), jax.ShapeDtypeStruct((heads, wide), jnp.float32)),
        in_specs=[SM] + [ANY] * (4 + len(gathered)) + [VM],
        out_specs=[ANY] * 6 + [VM] * 3,
        scratch_shapes=[vm(total, width), vm(total, width), vm(3, total, width), vm(width, 3 * width), vm(shards, 16, width), pltpu.SemaphoreType.DMA((6,))],
        compiler_params=pltpu.CompilerParams(vmem_limit_bytes=LIMIT),
        cost_estimate=pl.CostEstimate(flops=6 * total * width * width, bytes_accessed=total * width * 12 + width * width * 12, transcendentals=0),
        name="qkv_fwd",
    )(ids, x4, *came, *gathered, bucket_rows)

def gelu_both(v):
    t = jnp.tanh(root_coef * (v + cubic_coef * v * v * v))
    half = 0.5 * (1.0 + t)
    slope = half + 0.5 * v * (1.0 - t * t) * (root_coef * (1.0 + 3.0 * cubic_coef * v * v))
    return v * half, slope

def mid_kernel(ids_ref, x_ref, o_ref, g4_ref, c1_ref, c2_ref, c3_ref, gain_ref, wback_ref, wo_ref, win_ref,
               out_ref, gb_ref, do_ref, gw_ref, gwback_ref,
               mixed, h2, h2t, acc, gh2, gm, sem, *, ff_steps):
    step = pl.program_id(0)
    rows, width = x_ref.shape
    part = 256
    flat = lambda ref: ref[...].reshape(-1, ref.shape[-1])

    @pl.when(step == 0)
    def _():
        pull_sequence(ids_ref[0], g4_ref, (c1_ref, c2_ref, c3_ref), gm, sem)
        wo = flat(wo_ref)
        def load(i, carry):
            at = pl.ds(pl.multiple_of(i * part, part), part)
            value = x_ref[at, :].astype(jnp.float32) + _dot(o_ref[at, :], wo)
            mixed[at, :] = value
            acc[at, :] = value
            hidden = (value * rms_inverse(value) * gain_ref[1:2, :]).astype(jnp.bfloat16)
            h2[at, :] = hidden
            h2t[:, at] = hidden.T
            gh2[at, :] = jnp.zeros_like(value)
            return carry
        lax.fori_loop(0, rows // part, load, 0)
        pltpu.make_async_copy(gm, gm, sem).wait()
        row_ok = lax.broadcasted_iota(jnp.int32, (rows, 1), 0) < ids_ref[2]
        gm[...] = jnp.where(row_ok, gm[...], jnp.zeros_like(gm[...]))

    @pl.when(step < ff_steps)
    def _():
        win = flat(win_ref)
        wback = flat(wback_ref)
        pre = _dot(h2[...], win)
        grad_active = _dot(gm[...], wback, NT)
        act, slope = gelu_both(pre)
        active = act.astype(jnp.bfloat16)
        gpre = (grad_active * slope).astype(jnp.bfloat16)
        acc[...] += _dot(active, wback)
        gwback_ref[...] = _dot(active, gm[...], TN).astype(jnp.bfloat16)
        gw_ref[...] = _dot(h2t[...], gpre).astype(jnp.bfloat16).reshape(gw_ref.shape)
        gh2[...] += _dot(gpre, win, NT)

    @pl.when(step == ff_steps)
    def _():
        wo = flat(wo_ref)
        def finish(i, carry):
            at = pl.ds(pl.multiple_of(i * part, part), part)
            out_ref[at, :] = acc[at, :].astype(jnp.bfloat16)
            value = mixed[at, :]
            inverse = rms_inverse(value)
            normed = value * inverse
            scaled = gh2[at, :] * gain_ref[1:2, :]
            grad = inverse * (scaled - normed * jnp.mean(scaled * normed, axis=1, keepdims=True)) + gm[at, :].astype(jnp.float32)
            gb = grad.astype(jnp.bfloat16)
            gb_ref[at, :] = gb
            do_ref[at, :] = _dot(gb, wo, NT).astype(jnp.bfloat16)
            return carry
        lax.fori_loop(0, rows // part, finish, 0)

    @pl.when(step >= ff_steps)
    def _():
        cols = gw_ref.shape[-1]
        at = pl.ds(pl.multiple_of((step - ff_steps) * cols, cols), cols)
        gw_ref[...] = _dot(o_ref[...], gb_ref[:, at], TN).astype(jnp.bfloat16).reshape(gw_ref.shape)

def mid(ids, x, o, g4, came, gains, full, cols=512):
    rows, width = x.shape
    shards, stack, _ = full.shape
    own = width // shards
    ff_own = (stack - own) // 2
    ff = ff_own * shards
    ff_steps = ff // cols
    wide = width // cols
    one = lambda shape: pl.BlockSpec(shape, lambda i, n: (0,) * len(shape), pipeline_mode=pl.Buffered(1))
    last = lambda i: jnp.minimum(i, ff_steps - 1)
    mat = jax.ShapeDtypeStruct((rows, width), jnp.bfloat16)
    first = ff_own // own + 1
    gw_map = lambda i, n: (0, jnp.where(i < ff_steps, 1 + i // wide, 0), jnp.where(i < ff_steps, i % wide, i - ff_steps))
    return pl.pallas_call(
        functools.partial(mid_kernel, ff_steps=ff_steps),
        out_shape=(mat, mat, mat, jax.ShapeDtypeStruct((shards, own + ff_own, width), jnp.bfloat16), jax.ShapeDtypeStruct((ff, width), jnp.bfloat16)),
        grid_spec=pltpu.PrefetchScalarGridSpec(
            num_scalar_prefetch=1, grid=(ff_steps + wide,),
            in_specs=[one((rows, width)), one((rows, width)), ANY, ANY, ANY, ANY, one(gains.shape),
                      pl.BlockSpec((cols // ff_own, ff_own, width), lambda i, n: (last(i), 0, 0)),
                      pl.BlockSpec((shards, own, width), lambda i, n: (0, first - 1, 0), pipeline_mode=pl.Buffered(1)),
                      pl.BlockSpec((shards, own, cols), lambda i, n: (0, first + last(i) // wide, last(i) % wide))],
            out_specs=[one((rows, width)), one((rows, width)), one((rows, width)),
                       pl.BlockSpec((shards, own, cols), gw_map), pl.BlockSpec((cols, width), lambda i, n: (last(i), 0))],
            scratch_shapes=[pltpu.VMEM((rows, width), jnp.float32), pltpu.VMEM((rows, width), jnp.bfloat16),
                            pltpu.VMEM((width, rows), jnp.bfloat16), pltpu.VMEM((rows, width), jnp.float32),
                            pltpu.VMEM((rows, width), jnp.float32), pltpu.VMEM((rows, width), jnp.bfloat16), pltpu.SemaphoreType.DMA]),
        compiler_params=pltpu.CompilerParams(vmem_limit_bytes=LIMIT),
        cost_estimate=pl.CostEstimate(flops=12 * rows * width * ff + 6 * rows * width * width, bytes_accessed=rows * width * 12 + width * width * 4 + width * ff * 8, transcendentals=rows * ff),
        name="mid",
    )(ids, x, o, g4, *came, gains, full, full, full)

def gw_kernel(h_ref, dq_ref, dk_ref, dv_ref, bucket_ref, *refs):
    out_ref = refs[-1]
    shards, _, width = out_ref.shape
    own = width // shards
    for i, ref in enumerate((dq_ref, dk_ref, dv_ref)):
        out_ref[:, i * own:(i + 1) * own, :] = _dot(h_ref[...], ref[...], TN).astype(jnp.bfloat16).reshape(shards, own, width)
    offs = jnp.concatenate([ref[...] for ref in refs[:-1]], 0)
    ids = lax.broadcasted_iota(jnp.int32, (shards, 1), 0)
    hot = jnp.where(bucket_ref[1:2, :] == ids, 1.0, 0.0)
    table = lax.dot_general(hot, offs, NT, precision=lax.Precision.HIGHEST, preferred_element_type=jnp.float32)
    out_ref[:, 3 * own:, :] = jnp.zeros((shards, 16, width), jnp.bfloat16)
    out_ref[:, 3 * own:3 * own + 1, 0:offs.shape[0]] = table.astype(jnp.bfloat16).reshape(shards, 1, offs.shape[0])

def qkv_gw(h, dq, dk, dv, bucket_rows, offs, shards):
    rows, width = h.shape
    return pl.pallas_call(
        gw_kernel, out_shape=jax.ShapeDtypeStruct((shards, 3 * width // shards + 16, width), jnp.bfloat16),
        in_specs=[VM] * (5 + len(offs)), out_specs=VM,
        compiler_params=pltpu.CompilerParams(vmem_limit_bytes=LIMIT),
        cost_estimate=pl.CostEstimate(flops=6 * rows * width * width, bytes_accessed=rows * width * 8 + width * width * 6, transcendentals=0),
        name="qkv_gw",
    )(h, dq, dk, dv, bucket_rows, *offs)

def gx_kernel(x_ref, gb_ref, dq_ref, dk_ref, dv_ref, gain_ref, w_ref, out_ref):
    width = x_ref.shape[1]
    grad = _dot(dq_ref[...], w_ref[:, :width], NT)
    grad += _dot(dk_ref[...], w_ref[:, width:2 * width], NT)
    grad += _dot(dv_ref[...], w_ref[:, 2 * width:3 * width], NT)
    x = x_ref[...].astype(jnp.float32)
    inverse = rms_inverse(x)
    normed = x * inverse
    scaled = grad * gain_ref[0:1, :]
    out = inverse * (scaled - normed * jnp.mean(scaled * normed, axis=1, keepdims=True)) + gb_ref[...].astype(jnp.float32)
    out_ref[...] = out.astype(jnp.bfloat16)

def qkv_gx(x, gb, dq, dk, dv, gains, w, rows=512):
    total, width = x.shape
    blk = pl.BlockSpec((rows, width), lambda i: (i, 0))
    return pl.pallas_call(
        gx_kernel, out_shape=jax.ShapeDtypeStruct((total, width), jnp.bfloat16), grid=(total // rows,),
        in_specs=[blk] * 5 + [pl.BlockSpec(gains.shape, lambda i: (0, 0)),
                              pl.BlockSpec((width, 3 * width), lambda i: (0, 0), pipeline_mode=pl.Buffered(1))],
        out_specs=blk,
        compiler_params=pltpu.CompilerParams(vmem_limit_bytes=LIMIT),
        cost_estimate=pl.CostEstimate(flops=6 * total * width * width, bytes_accessed=total * width * 12 + width * width * 6, transcendentals=0),
        name="qkv_gx",
    )(x, gb, dq, dk, dv, gains, w)

def place_kernel(ids_ref, own_ref, c1_ref, c2_ref, c3_ref, out_ref, sem):
    me = ids_ref[0]
    copies = []
    for mask, ref in enumerate((own_ref, c1_ref, c2_ref, c3_ref)):
        src = ref.at[me] if mask == 0 else ref.at[0]
        copies.append(pltpu.make_async_copy(src, out_ref.at[me ^ mask], sem.at[mask]))
        copies[-1].start()
    for copy in copies:
        copy.wait()

def place(ids, own, came):
    return pl.pallas_call(
        place_kernel, out_shape=jax.ShapeDtypeStruct(own.shape, own.dtype),
        in_specs=[SM] + [ANY] * 4, out_specs=ANY, scratch_shapes=[pltpu.SemaphoreType.DMA((4,))],
        cost_estimate=pl.CostEstimate(flops=0, bytes_accessed=own.size * 4, transcendentals=0),
        name="place",
    )(ids, own, *came)
def swap(value, axis, mask):
    return lax.ppermute(value, axis, [(i, i ^ mask) for i in range(lax.axis_size(axis))])


def send_blocks(blocks, me):
    return tuple(swap(lax.dynamic_index_in_dim(blocks, me ^ mask, 0), "seq", mask) for mask in range(1, blocks.shape[0]))


MASKS = ((0, 8, 16, 24), (2, 10, 18, 26), (4, 12, 20, 28), (6, 14), (22, 30))


def gather_staged(shard):
    shard = shard[None]
    column = jnp.concatenate([shard] + [swap(shard, "dp", 2 * z) for z in (1, 2, 3)], 0)
    from_x, from_y = swap(column, "seq", 2), swap(column, "dp", 1)
    corner_x, corner_y = swap(from_y[:2], "seq", 2), swap(from_x[2:], "dp", 1)
    pieces = (column, from_x, from_y, corner_x, corner_y)
    masks = MASKS + tuple(tuple(m | 1 for m in row) for row in MASKS)
    return pieces + tuple(swap(p, "seq", 1) for p in pieces), masks


class Scatter:
    def __init__(self, grads, pos):
        self.z, self.y, self.x, self.c = pos
        self.grads = grads.reshape((4, 2, 2, 2) + grads.shape[1:])
        self.other = swap(lax.dynamic_index_in_dim(self.grads, 1 - self.c, 3, keepdims=False), "seq", 1)

    def fold(self):
        pick = lambda v, at, axis: lax.dynamic_index_in_dim(v, at, axis, keepdims=False)
        mine = pick(self.grads, self.c, 3)
        def quarter(dy, dx):
            cut = lambda v: pick(pick(v, self.y ^ dy, 1), self.x ^ dx, 1).astype(jnp.float32)
            return (cut(mine) + cut(self.other)).astype(jnp.bfloat16)
        far = quarter(1, 1)
        self.to_x, self.to_y, self.own = quarter(0, 1), quarter(1, 0), quarter(0, 0)
        self.came_x, self.came_y = swap(far[:2], "seq", 2), swap(far[2:], "dp", 1)

    def turn(self):
        add = lambda a, b: (a.astype(jnp.float32) + b.astype(jnp.float32)).astype(jnp.bfloat16)
        to_x = lax.dynamic_update_slice_in_dim(self.to_x, add(self.to_x[2:], self.came_y), 2, 0)
        to_y = lax.dynamic_update_slice_in_dim(self.to_y, add(self.to_y[:2], self.came_x), 0, 0)
        self.came_x, self.came_y = swap(to_x, "seq", 2), swap(to_y, "dp", 1)

    def column(self):
        total = self.own.astype(jnp.float32) + self.came_x.astype(jnp.float32) + self.came_y.astype(jnp.float32)
        total = total.astype(jnp.bfloat16)
        block = lambda k: lax.dynamic_index_in_dim(total, self.z ^ k, 0, keepdims=False)
        self.mine = block(0)
        self.came = [swap(block(k), "dp", 2 * k) for k in (1, 2, 3)]

    def result(self):
        return sum((c.astype(jnp.float32) for c in self.came), self.mine.astype(jnp.float32))


def tie(first, *later):
    return lax.optimization_barrier((first,) + later)[1:]


def local_whole(tokens, cotangent, lengths, buckets, norm1_gain, w_query, w_key, w_value, w_out, rel_table, norm2_gain, w_in, w_back):
    micro_count, seq_count, rows, width = tokens.shape
    parts = micro_count * seq_count
    both = ("dp", "seq")
    me, dp = lax.axis_index("seq"), lax.axis_index("dp")
    shards = lax.axis_size("seq") * lax.axis_size("dp")
    flat = dp * parts + me
    pos = (dp // 2, dp % 2, me // 2, me % 2)
    low = lambda v: v.astype(jnp.bfloat16)
    up = lambda v: v.astype(jnp.float32)
    own, ff_own = w_query.shape[0], w_back.shape[0]
    ids = jnp.stack([me, flat, lax.dynamic_index_in_dim(lengths.reshape(parts), me, 0, keepdims=False)])
    length = ids[2:3]

    place_row = lambda v: lax.dynamic_update_slice(jnp.zeros((1, width), jnp.bfloat16), low(v)[None], (0, flat * own))
    small = jnp.concatenate([place_row(norm1_gain), place_row(norm2_gain), jnp.zeros((6, width), jnp.bfloat16),
                             jnp.pad(low(rel_table)[None], ((0, 7), (0, width - HEADS)))], 0)
    shard1 = jnp.concatenate([low(w_query), low(w_key), low(w_value), small], 0)
    shard2 = jnp.concatenate([low(w_back), low(w_out)] + [low(w_in[:, i * width:(i + 1) * width]) for i in range(ff_own // own)], 0)
    x4, g4 = tokens.reshape(parts, rows, width), cotangent.reshape(parts, rows, width)
    gathered, masks = gather_staged(shard1)
    x_came = send_blocks(x4, me)
    g_came = send_blocks(g4, me)
    full2 = lax.all_gather(shard2, both, axis=0, tiled=False)
    bucket_rows = jnp.stack([jnp.pad(buckets, (0, 1), constant_values=-1), jnp.pad(buckets[::-1], (0, 1), constant_values=-1)])

    x, hidden, q, k, v, w_qkv, gains, t, t_back = qkv_fwd(ids, x4, x_came, gathered, masks, bucket_rows, HEADS)
    attended, lse = attn_fwd(length, q, k, v, t)
    out, gb, g_att, gw2, gw_back = mid(ids, x, attended, g4, g_came, gains, full2)
    sc2 = Scatter(gw2, pos)
    r_back = lax.psum_scatter(gw_back, both, scatter_dimension=0, tiled=True)
    out4 = out.reshape(parts, rows, width)
    out_came = send_blocks(out4, me)
    pairs = HEADS // 2
    count = pairs // 4
    back = lambda first, g, prev: attn_bwd(length, q, k, v, g, attended, lse, t_back, first, count, prev)
    dq, dk, dv, off0 = back(0, g_att, None)
    sc2.fold()
    g_att, = tie(sc2.own, g_att)
    dq, dk, dv, off1 = back(count, g_att, (dq, dk, dv))
    sc2.turn()
    g_att, = tie(sc2.own, g_att)
    layer_out = place(ids, out4, out_came)
    dq, dk, dv, off2 = back(2 * count, g_att, (dq, dk, dv))
    dq, dk, dv, off3 = back(3 * count, g_att, (dq, dk, dv))
    sc2.column()
    gw1 = qkv_gw(hidden, dq, dk, dv, bucket_rows, (off0, off1, off2, off3), shards)
    sc1 = Scatter(gw1, pos)
    gx = qkv_gx(x, gb, dq, dk, dv, gains, w_qkv)
    gx4 = gx.reshape(parts, rows, width)
    gx_came = send_blocks(gx4, me)
    sc1.fold()
    sc1.turn()
    sc1.column()
    input_grad = place(ids, gx4, gx_came)
    r1, r2, r_back = sc1.result(), sc2.result(), up(r_back)
    g_in = jnp.concatenate([r2[own * (1 + i):own * (2 + i)] for i in range(ff_own // own)], 1)
    prod = up(shard1[:3 * own]) * r1[:3 * own]
    g_gain1 = jnp.sum(prod[:own] + prod[own:2 * own] + prod[2 * own:], axis=1) / up(low(norm1_gain))
    g_gain2 = jnp.sum(up(low(w_in)) * g_in, axis=1) / up(low(norm2_gain))
    return (layer_out.reshape(tokens.shape), input_grad.reshape(tokens.shape), g_gain1, r1[:own], r1[own:2 * own], r1[2 * own:3 * own],
            r2[:own], r1[3 * own, :HEADS], g_gain2, g_in, r_back)


def local_any(shape, tokens, *rest):
    fits = tuple(shape) == (8, 4) and tokens.shape[0] * tokens.shape[1] == 4 and tokens.shape[3] == HEADS * DH == 1024
    return (local_whole if fits else local)(tokens, *rest)


def solution(mesh):
    return jax.shard_map(
        functools.partial(local_any, mesh.devices.shape),
        mesh=mesh,
        in_specs=(
            P(None, "dp", "seq", None),
            P(None, "dp", "seq", None),
            P(None, "dp"),
            P(),
            P(("dp", "seq")),
            P(("dp", "seq"), None),
            P(("dp", "seq"), None),
            P(("dp", "seq"), None),
            P(("dp", "seq"), None),
            P(("dp", "seq")),
            P(("dp", "seq")),
            P(("dp", "seq"), None),
            P(("dp", "seq"), None),
        ),
        out_specs=(
            P(None, "dp", "seq", None),
            P(None, "dp", "seq", None),
            P(("dp", "seq")),
            P(("dp", "seq"), None),
            P(("dp", "seq"), None),
            P(("dp", "seq"), None),
            P(("dp", "seq"), None),
            P(("dp", "seq")),
            P(("dp", "seq")),
            P(("dp", "seq"), None),
            P(("dp", "seq"), None),
        ),
        check_vma=False,
    )
```

```python
import functools

import jax
import jax.numpy as jnp
from jax import lax
from jax.experimental import pallas as pl
from jax.experimental.pallas import tpu as pltpu
from jax.sharding import PartitionSpec as P

HEADS = 16
DH = 64
BUCKETS = 32


epsilon = 1e-06
floor_score = -1e30
highest = lax.Precision.HIGHEST
root_coef = 0.7978845608
cubic_coef = 0.044715


def gelu_tanh(values):
    return (
        0.5
        * values
        * (1.0 + jnp.tanh(root_coef * (values + cubic_coef * values * values * values)))
    )


def gelu_slope(values):
    inner = jnp.tanh(root_coef * (values + cubic_coef * values * values * values))
    return 0.5 * (1.0 + inner) + 0.5 * values * (1.0 - inner * inner) * root_coef * (
        1.0 + 3.0 * cubic_coef * values * values
    )


def project(acts, weight):
    return jnp.einsum("srd,de->sre", acts, weight, preferred_element_type=jnp.float32)


def project_back(grads_in, weight):
    return jnp.einsum("sre,de->srd", grads_in, weight, preferred_element_type=jnp.float32)


def contract(acts, grads_in):
    return jnp.einsum("srd,sre->de", acts, grads_in, preferred_element_type=jnp.float32)


def rms_forward(values, gain):
    inverse = lax.rsqrt(jnp.mean(values * values, axis=-1, keepdims=True) + epsilon)
    normed = values * inverse
    return (normed, inverse, (normed * gain.astype(jnp.float32)).astype(jnp.bfloat16))


def rms_backward(grad_hidden, normed, inverse, gain):
    scaled = grad_hidden * gain.astype(jnp.float32)
    grad_values = inverse * (scaled - normed * jnp.mean(scaled * normed, axis=-1, keepdims=True))
    return (grad_values, jnp.sum(grad_hidden * normed, axis=(0, 1)))


def score_block(per_head_queries, per_head_keys, rel_bias, key_valid):
    scores = (
        jnp.einsum(
            "ofck,owck->ocfw", per_head_queries, per_head_keys, preferred_element_type=jnp.float32
        )
        + rel_bias[None]
    )
    return jnp.where(key_valid, scores, floor_score)


def offset_sums(grid, first_row, seq_len):
    head_count, row_count, key_count = grid.shape
    flipped = grid[:, ::-1, :]
    padded = jnp.pad(flipped, ((0, 0), (0, 0), (0, row_count)))
    wide_len = key_count + row_count
    skewed = padded.reshape(head_count, row_count * wide_len)[:, : row_count * (wide_len - 1)]
    skewed = skewed.reshape(head_count, row_count, wide_len - 1)
    column_sums = jnp.sum(skewed, axis=1)
    placed = jnp.zeros((head_count, 2 * seq_len - 1), jnp.float32)
    begin = seq_len - row_count - first_row
    return lax.dynamic_update_slice(placed, column_sums, (jnp.int32(0), begin))


def run_micro(inputs, incoming, seq_lens, attn_set, mlp_set, context):
    onehot, offsets, row_pos, key_pos, first_row, seq_len = context
    gain_one, query_w, key_w, value_w, out_w, bias_table = attn_set
    gain_two, in_w, return_projection_weight = mlp_set
    seq_count, row_count, model_width = inputs.shape
    values = inputs.astype(jnp.float32)
    normed_one, inverse_one, hidden_one = rms_forward(values, gain_one)
    queries = project(hidden_one, query_w).astype(jnp.bfloat16)
    keys_own = project(hidden_one, key_w).astype(jnp.bfloat16)
    values_own = project(hidden_one, value_w).astype(jnp.bfloat16)
    keys_all, values_all = (
        lax.all_gather(keys_own, "seq", axis=1, tiled=True),
        lax.all_gather(values_own, "seq", axis=1, tiled=True),
    )
    per_offset = jnp.dot(
        onehot, bias_table.reshape(BUCKETS, HEADS), preferred_element_type=jnp.float32
    )
    rel_bias = jnp.transpose(per_offset[offsets], (2, 0, 1))
    key_valid = (key_pos[None, :] < seq_lens[:, None])[:, None, None, :]
    per_head_queries = queries.reshape(seq_count, row_count, HEADS, DH)
    per_head_keys = keys_all.reshape(seq_count, seq_len, HEADS, DH)
    per_head_values = values_all.reshape(seq_count, seq_len, HEADS, DH)
    scores = score_block(per_head_queries, per_head_keys, rel_bias, key_valid)
    row_max = jnp.max(scores, axis=-1, keepdims=True)
    exp_scores = jnp.exp(scores - row_max)
    row_total = jnp.sum(exp_scores, axis=-1, keepdims=True)
    attn_probs = exp_scores / row_total
    log_total = row_max + jnp.log(row_total)
    reduced_precision_probs = attn_probs.astype(jnp.bfloat16)
    attended = jnp.einsum(
        "jfpe,jefn->jpfn",
        reduced_precision_probs,
        per_head_values,
        preferred_element_type=jnp.float32,
    )
    attended = attended.reshape(seq_count, row_count, model_width).astype(jnp.bfloat16)
    residual_mid = values + project(attended, out_w)
    normed_two, inverse_two, hidden_two = rms_forward(residual_mid, gain_two)
    pre_act = project(hidden_two, in_w)
    active = gelu_tanh(pre_act).astype(jnp.bfloat16)
    result = (residual_mid + project(active, return_projection_weight)).astype(jnp.bfloat16)
    row_valid = (row_pos[None, :] < seq_lens[:, None]).astype(jnp.float32)[:, :, None]
    grad_out = incoming.astype(jnp.float32) * row_valid
    grad_low = grad_out.astype(jnp.bfloat16)
    grad_back = contract(active, grad_low)
    gradient_active_rows = project_back(grad_low, return_projection_weight)
    grad_pre = (gradient_active_rows * gelu_slope(pre_act)).astype(jnp.bfloat16)
    grad_in = contract(hidden_two, grad_pre)
    grad_hidden_two = project_back(grad_pre, in_w)
    grad_mixed, grad_gain_two = rms_backward(grad_hidden_two, normed_two, inverse_two, gain_two)
    grad_mixed = grad_mixed + grad_out
    grad_branch = grad_mixed.astype(jnp.bfloat16)
    grad_outw = contract(attended, grad_branch)
    gradient_attended_values = project_back(grad_branch, out_w).astype(jnp.bfloat16)
    gradient_attended_values = gradient_attended_values.reshape(seq_count, row_count, HEADS, DH)
    scores = score_block(per_head_queries, per_head_keys, rel_bias, key_valid)
    attn_probs = jnp.exp(scores - log_total)
    reduced_precision_probs = attn_probs.astype(jnp.bfloat16)
    grad_probs = jnp.einsum(
        "ofck,owck->ocfw",
        gradient_attended_values,
        per_head_values,
        preferred_element_type=jnp.float32,
    )
    inner_sum = jnp.sum(attn_probs * grad_probs, axis=-1, keepdims=True)
    gradient_score_matrix = (attn_probs * (grad_probs - inner_sum)).astype(jnp.bfloat16)
    grad_query = jnp.einsum(
        "jfpe,jefn->jpfn", gradient_score_matrix, per_head_keys, preferred_element_type=jnp.float32
    )
    grad_query = grad_query.astype(jnp.bfloat16).reshape(seq_count, row_count, model_width)
    key_part = jnp.einsum(
        "eciv,eicq->evcq",
        gradient_score_matrix,
        per_head_queries,
        preferred_element_type=jnp.float32,
    )
    value_part = jnp.einsum(
        "eciv,eicq->evcq",
        reduced_precision_probs,
        gradient_attended_values,
        preferred_element_type=jnp.float32,
    )
    key_part = key_part.reshape(seq_count, seq_len, model_width)
    value_part = value_part.reshape(seq_count, seq_len, model_width)
    grad_key, grad_value = (
        lax.psum_scatter(
            key_part.astype(jnp.bfloat16), "seq", scatter_dimension=1, tiled=True
        ).astype(jnp.float32),
        lax.psum_scatter(
            value_part.astype(jnp.bfloat16), "seq", scatter_dimension=1, tiled=True
        ).astype(jnp.float32),
    )
    grad_key = grad_key.astype(jnp.bfloat16)
    grad_value = grad_value.astype(jnp.bfloat16)
    offset_grad = offset_sums(
        jnp.sum(gradient_score_matrix.astype(jnp.float32), axis=0), first_row, seq_len
    )
    grad_table = jnp.dot(onehot.astype(jnp.float32).T, offset_grad.T, precision=highest).reshape(-1)
    grad_qw = contract(hidden_one, grad_query)
    grad_kw = contract(hidden_one, grad_key)
    grad_vw = contract(hidden_one, grad_value)
    grad_hidden_one = (
        project_back(grad_query, query_w)
        + project_back(grad_key, key_w)
        + project_back(grad_value, value_w)
    )
    grad_values, grad_gain_one = rms_backward(grad_hidden_one, normed_one, inverse_one, gain_one)
    grad_values = grad_values + grad_mixed
    gradients = (
        grad_gain_one,
        grad_qw,
        grad_kw,
        grad_vw,
        grad_outw,
        grad_table,
        grad_gain_two,
        grad_in,
        grad_back,
    )
    return (result, grad_values.astype(jnp.bfloat16), gradients)


def local(
    tokens,
    cotangent,
    lengths,
    buckets,
    norm1_gain,
    w_query,
    w_key,
    w_value,
    w_out,
    rel_table,
    norm2_gain,
    w_in,
    w_back,
):
    micro_count, seq_count, row_count, model_width = tokens.shape
    seq_parts = lax.axis_size("seq")
    seq_len = row_count * seq_parts
    first_row = lax.axis_index("seq") * row_count
    row_pos = first_row + jnp.arange(row_count, dtype=jnp.int32)
    key_pos = jnp.arange(seq_len, dtype=jnp.int32)
    onehot = (buckets[:, None] == jnp.arange(BUCKETS, dtype=jnp.int32)[None, :]).astype(
        jnp.bfloat16
    )
    offsets = key_pos[None, :] - row_pos[:, None] + (seq_len - 1)
    context = (onehot, offsets, row_pos, key_pos, first_row, seq_len)
    outputs = []
    input_grads = []
    pending = None
    shard_sums = None
    for micro_step in range(micro_count):
        attn_set = (
            lax.all_gather(norm1_gain.astype(jnp.bfloat16), ("dp", "seq"), axis=0, tiled=True),
            lax.all_gather(w_query.astype(jnp.bfloat16), ("dp", "seq"), axis=0, tiled=True),
            lax.all_gather(w_key.astype(jnp.bfloat16), ("dp", "seq"), axis=0, tiled=True),
            lax.all_gather(w_value.astype(jnp.bfloat16), ("dp", "seq"), axis=0, tiled=True),
            lax.all_gather(w_out.astype(jnp.bfloat16), ("dp", "seq"), axis=0, tiled=True),
            lax.all_gather(rel_table.astype(jnp.bfloat16), ("dp", "seq"), axis=0, tiled=True),
        )
        mlp_set = (
            lax.all_gather(norm2_gain.astype(jnp.bfloat16), ("dp", "seq"), axis=0, tiled=True),
            lax.all_gather(w_in.astype(jnp.bfloat16), ("dp", "seq"), axis=0, tiled=True),
            lax.all_gather(w_back.astype(jnp.bfloat16), ("dp", "seq"), axis=0, tiled=True),
        )
        layer_part, grad_part, gradients = run_micro(
            tokens[micro_step],
            cotangent[micro_step],
            lengths[micro_step],
            attn_set,
            mlp_set,
            context,
        )
        outputs.append(layer_part)
        input_grads.append(grad_part)
        pending = gradients if pending is None else jax.tree.map(jnp.add, pending, gradients)
    shard_sums = (
        lax.psum_scatter(pending[0], ("dp", "seq"), scatter_dimension=0, tiled=True),
        lax.psum_scatter(pending[1], ("dp", "seq"), scatter_dimension=0, tiled=True),
        lax.psum_scatter(pending[2], ("dp", "seq"), scatter_dimension=0, tiled=True),
        lax.psum_scatter(pending[3], ("dp", "seq"), scatter_dimension=0, tiled=True),
        lax.psum_scatter(pending[4], ("dp", "seq"), scatter_dimension=0, tiled=True),
        lax.psum_scatter(pending[5], ("dp", "seq"), scatter_dimension=0, tiled=True),
        lax.psum_scatter(pending[6], ("dp", "seq"), scatter_dimension=0, tiled=True),
        lax.psum_scatter(pending[7], ("dp", "seq"), scatter_dimension=0, tiled=True),
        lax.psum_scatter(pending[8], ("dp", "seq"), scatter_dimension=0, tiled=True),
    )
    return (
        jnp.stack(outputs),
        jnp.stack(input_grads),
        shard_sums[0],
        shard_sums[1],
        shard_sums[2],
        shard_sums[3],
        shard_sums[4],
        shard_sums[5],
        shard_sums[6],
        shard_sums[7],
        shard_sums[8],
    )


NT = (((1,), (1,)), ((), ()))
TN = (((0,), (0,)), ((), ()))
STRIP = 128
LIMIT = 58 << 20
LIGHT = pl.CostEstimate(flops=1 << 20, bytes_accessed=1 << 16, transcendentals=0)

def _dot(a, b, dims=(((1,), (0,)), ((), ()))):
    return lax.dot_general(a, b, dims, preferred_element_type=jnp.float32)

def head_lanes(x, which, width=64):
    lane = lax.broadcasted_iota(jnp.int32, (1, x.shape[1]), 1)
    keep = (lane < width) if which == 0 else (lane >= width)
    return jnp.where(keep, x, jnp.zeros_like(x))

def skew(row, wide):
    rows = jnp.broadcast_to(row, (STRIP, wide))
    return pltpu.roll(rows, wide - (STRIP - 1), 1, stride=1, stride_axis=0)

def fwd_kernel(len_ref, q_ref, k_ref, v_ref, t_ref, o_ref, lse_ref, strip, *, rows, seq_len):
    wide = t_ref.shape[-1]
    length = len_ref[0]
    pair = pl.program_id(0)
    blocks = seq_len // rows
    per = rows // STRIP
    col_ok = lax.broadcasted_iota(jnp.int32, (1, seq_len), 1) < length
    lane = lax.broadcasted_iota(jnp.int32, (1, 128), 1)
    k2 = k_ref[...]
    v2 = v_ref[...]
    for a in range(2):
        strip[a] = skew(t_ref[pl.ds(2 * pair + a, 1), :], wide)

    def step(b, carry):
        base = pl.multiple_of(b * rows, rows)
        q2 = q_ref[pl.ds(base, rows), :]
        outs, stats = [], []
        for a in range(2):
            scores = _dot(head_lanes(q2, a), k2, NT)
            parts = []
            for i in range(per):
                off = pl.multiple_of((seq_len - STRIP) - (b * per + i) * STRIP, STRIP)
                parts.append(strip[a, :, pl.ds(off, seq_len)])
            bias = jnp.concatenate(parts, 0) if per > 1 else parts[0]
            scores = jnp.where(col_ok, scores + bias, floor_score)
            top = jnp.max(scores, axis=1, keepdims=True)
            probs = jnp.exp(scores - top)
            total = jnp.sum(probs, axis=1, keepdims=True)
            out = _dot(probs.astype(jnp.bfloat16), v2)
            outs.append(out * (1.0 / total))
            stats.append(top + jnp.log(total))
        o_ref[pl.ds(base, rows), :] = jnp.where(lane < 64, outs[0], outs[1]).astype(jnp.bfloat16)
        lse_ref[0, pl.ds(base, rows), :] = jnp.where(lane < 64, stats[0], stats[1])
        return carry

    lax.fori_loop(0, blocks, step, 0, unroll=2)

def attn_fwd(length, q, k, v, t, rows=256):
    seq_len, width = q.shape
    pairs = width // 128
    wide = t.shape[-1]
    blk = pl.BlockSpec((seq_len, 128), lambda p, n: (0, p))
    return pl.pallas_call(
        functools.partial(fwd_kernel, rows=rows, seq_len=seq_len),
        out_shape=(jax.ShapeDtypeStruct((seq_len, width), jnp.bfloat16),
                   jax.ShapeDtypeStruct((pairs, seq_len, 128), jnp.float32)),
        grid_spec=pltpu.PrefetchScalarGridSpec(
            num_scalar_prefetch=1, grid=(pairs,),
            in_specs=[blk, blk, blk, pl.BlockSpec(t.shape, lambda p, n: (0, 0))],
            out_specs=[blk, pl.BlockSpec((1, seq_len, 128), lambda p, n: (p, 0, 0))],
            scratch_shapes=[pltpu.VMEM((2, STRIP, wide), jnp.float32)]),
        compiler_params=pltpu.CompilerParams(vmem_limit_bytes=40 << 20),
        cost_estimate=LIGHT,
        name="attn_fwd",
    )(length, q, k, v, t)

def bwd_kernel(len_ref, q_ref, k_ref, v_ref, do_ref, o_ref, lse_ref, t_ref, *refs, rows, seq_len, first):
    dq_ref, dk_ref, dv_ref, g_ref, strip, acc, dq_acc = refs[-7:]
    wide = t_ref.shape[-1]
    length = len_ref[0]
    local_pair = pl.program_id(0)
    pair = first + local_pair
    blocks = seq_len // rows
    per = rows // STRIP
    lane = lax.broadcasted_iota(jnp.int32, (1, 128), 1)
    q2 = q_ref[...]
    do2 = do_ref[...]
    prod = (do2.astype(jnp.float32) * o_ref[...].astype(jnp.float32)).T
    stat = lse_ref[0].T
    lse_rows = [stat[0:1, :], stat[64:65, :]]
    delta_rows = [jnp.sum(prod[0:64], axis=0, keepdims=True), jnp.sum(prod[64:128], axis=0, keepdims=True)]
    for a in range(2):
        strip[a] = skew(t_ref[pl.ds(2 * pair + a, 1), :], wide)
    acc[...] = jnp.zeros_like(acc)
    dq_acc[...] = jnp.zeros_like(dq_acc)

    def step(b, carry):
        base = pl.multiple_of(b * rows, rows)
        k2 = k_ref[pl.ds(base, rows), :]
        v2 = v_ref[pl.ds(base, rows), :]
        row_ok = (base + lax.broadcasted_iota(jnp.int32, (rows, 1), 0)) < length
        dks, dvs = [], []
        for a in range(2):
            scores = _dot(head_lanes(k2, a), q2, NT)
            offs = [pl.multiple_of((seq_len - STRIP) - (b * per + i) * STRIP, STRIP) for i in range(per)]
            bias = [strip[a, :, pl.ds(off, seq_len)] for off in offs]
            bias = jnp.concatenate(bias, 0) if per > 1 else bias[0]
            probs = jnp.where(row_ok, jnp.exp(scores + bias - lse_rows[a]), 0.0)
            grad_probs = _dot(head_lanes(v2, a), do2, NT)
            grad_scores = probs * (grad_probs - delta_rows[a])
            for i, off in enumerate(offs):
                acc[a, :, pl.ds(off, seq_len)] += grad_scores[i * STRIP:(i + 1) * STRIP]
            probs_b = probs.astype(jnp.bfloat16)
            gs_b = grad_scores.astype(jnp.bfloat16)
            dvs.append(_dot(probs_b, do2))
            dks.append(_dot(gs_b, q2))
            dq_acc[a] += _dot(gs_b, k2, TN)
        dk_ref[pl.ds(base, rows), :] = jnp.where(lane < 64, dks[0], dks[1]).astype(jnp.bfloat16)
        dv_ref[pl.ds(base, rows), :] = jnp.where(lane < 64, dvs[0], dvs[1]).astype(jnp.bfloat16)
        return carry

    lax.fori_loop(0, blocks, step, 0)
    dq_ref[...] = jnp.where(lane < 64, dq_acc[0], dq_acc[1]).astype(jnp.bfloat16)
    for a in range(2):
        sums = acc[a]
        half = STRIP
        while half > 8:
            half //= 2
            sums = sums[:half] + pltpu.roll(sums[half:], wide - half, 1)
        while half > 1:
            half //= 2
            sums = sums + pltpu.roll(pltpu.roll(sums, 8 - half, 0), wide - half, 1)
        g_ref[pl.ds(2 * local_pair + a, 1), :] = pltpu.roll(sums, STRIP - 1, 1)[0:1]

def attn_bwd(length, q, k, v, do, o, lse, trev, first, count, prev=None, rows=256):
    seq_len, width = q.shape
    wide = trev.shape[-1]
    blk = pl.BlockSpec((seq_len, 128), lambda p, n: (0, first + p))
    mat = jax.ShapeDtypeStruct((seq_len, width), jnp.bfloat16)
    prev = tuple(prev) if prev is not None else ()
    return pl.pallas_call(
        functools.partial(bwd_kernel, rows=rows, seq_len=seq_len, first=first),
        out_shape=(mat, mat, mat, jax.ShapeDtypeStruct((2 * count, wide), jnp.float32)),
        grid_spec=pltpu.PrefetchScalarGridSpec(
            num_scalar_prefetch=1, grid=(count,),
            in_specs=[blk, blk, blk, blk, blk, pl.BlockSpec((1, seq_len, 128), lambda p, n: (first + p, 0, 0)),
                      pl.BlockSpec(trev.shape, lambda p, n: (0, 0))] + [pl.BlockSpec(memory_space=pl.ANY)] * len(prev),
            out_specs=[blk, blk, blk, pl.BlockSpec((2 * count, wide), lambda p, n: (0, 0))],
            scratch_shapes=[pltpu.VMEM((2, STRIP, wide), jnp.float32), pltpu.VMEM((2, STRIP, wide), jnp.float32),
                            pltpu.VMEM((2, seq_len, 128), jnp.float32)]),
        input_output_aliases={8 + i: i for i in range(len(prev))},
        compiler_params=pltpu.CompilerParams(vmem_limit_bytes=40 << 20),
        cost_estimate=LIGHT,
        name="attn_bwd",
    )(length, q, k, v, do, o, lse, trev, *prev)

ANY = pl.BlockSpec(memory_space=pl.ANY)
VM = pl.BlockSpec(memory_space=pltpu.VMEM)
SM = pl.BlockSpec(memory_space=pltpu.SMEM)

def rms_inverse(value):
    return lax.rsqrt(jnp.mean(value * value, axis=1, keepdims=True) + epsilon)

def pull_sequence(me, whole_ref, came, dst, sem):
    rows = whole_ref.shape[1]
    for mask, ref in enumerate((whole_ref,) + tuple(came)):
        src = ref.at[me] if mask == 0 else ref.at[0]
        at = pl.multiple_of((me ^ mask) * rows, rows)
        pltpu.make_async_copy(src, dst.at[pl.ds(at, rows), :], sem).start()

def qkv_kernel(ids_ref, x4_ref, c1_ref, c2_ref, c3_ref, *refs, masks):
    gathered = refs[:len(masks)]
    bucket_ref = refs[len(masks)]
    x_out, h_out, q_out, k_out, v_out, w_out, gain_ref, t_ref, trev_ref, xs, hs, ps, ws, es, sems = refs[len(masks) + 1:]
    me, flat = ids_ref[0], ids_ref[1]
    width = xs.shape[1]
    own = width // es.shape[0]
    pull_sequence(me, x4_ref, (c1_ref, c2_ref, c3_ref), xs, sems.at[0])
    for ref, ids in zip(gathered, masks):
        for j, mask in enumerate(ids):
            shard = flat ^ mask
            pltpu.make_async_copy(ref.at[j, 3 * own:3 * own + 16, :], es.at[shard], sems.at[1]).start()
    for ref, ids in zip(gathered, masks):
        for j, mask in enumerate(ids):
            at = pl.multiple_of((flat ^ mask) * own, own)
            for i in range(3):
                pltpu.make_async_copy(ref.at[j, i * own:(i + 1) * own, :], ws.at[pl.ds(at, own), i * width:(i + 1) * width], sems.at[2]).start()
    pltpu.make_async_copy(es, es, sems.at[1]).wait()
    extras = es[...].astype(jnp.float32)
    gains = jnp.sum(extras, axis=0)
    gain_ref[...] = gains[0:8]
    table = extras[:, 8, 0:128].astype(jnp.bfloat16)
    ids = lax.broadcasted_iota(jnp.int32, (es.shape[0], 1), 0)
    heads = t_ref.shape[0]
    for i, ref in enumerate((t_ref, trev_ref)):
        hot = jnp.where(bucket_ref[i:i + 1, :] == ids, 1.0, 0.0).astype(jnp.bfloat16)
        ref[...] = _dot(table, hot, TN)[0:heads]
    pltpu.make_async_copy(xs, xs, sems.at[0]).wait()
    part = 256
    def norm(i, carry):
        at = pl.ds(pl.multiple_of(i * part, part), part)
        x = xs[at, :].astype(jnp.float32)
        hs[at, :] = (x * rms_inverse(x) * gains[0:1]).astype(jnp.bfloat16)
        return carry
    lax.fori_loop(0, xs.shape[0] // part, norm, 0)
    copies = [pltpu.make_async_copy(xs, x_out, sems.at[0]), pltpu.make_async_copy(hs, h_out, sems.at[1])]
    for copy in copies:
        copy.start()
    pltpu.make_async_copy(ws, ws, sems.at[2]).wait()
    copies.append(pltpu.make_async_copy(ws, w_out, sems.at[2]))
    copies[-1].start()
    for i, ref in enumerate((q_out, k_out, v_out)):
        ps[i] = _dot(hs[...], ws[:, i * width:(i + 1) * width]).astype(jnp.bfloat16)
        copies.append(pltpu.make_async_copy(ps.at[i], ref, sems.at[3 + i]))
        copies[-1].start()
    for copy in copies:
        copy.wait()

def qkv_fwd(ids, x4, came, gathered, masks, bucket_rows, heads):
    parts, rows, width = x4.shape
    total = parts * rows
    shards = sum(len(m) for m in masks)
    mat = jax.ShapeDtypeStruct((total, width), jnp.bfloat16)
    wide = bucket_rows.shape[1]
    vm = lambda *s: pltpu.VMEM(s, jnp.bfloat16)
    return pl.pallas_call(
        functools.partial(qkv_kernel, masks=masks),
        out_shape=(mat,) * 5 + (jax.ShapeDtypeStruct((width, 3 * width), jnp.bfloat16), jax.ShapeDtypeStruct((8, width), jnp.float32),
                                jax.ShapeDtypeStruct((heads, wide), jnp.float32), jax.ShapeDtypeStruct((heads, wide), jnp.float32)),
        in_specs=[SM] + [ANY] * (4 + len(gathered)) + [VM],
        out_specs=[ANY] * 6 + [VM] * 3,
        scratch_shapes=[vm(total, width), vm(total, width), vm(3, total, width), vm(width, 3 * width), vm(shards, 16, width), pltpu.SemaphoreType.DMA((6,))],
        compiler_params=pltpu.CompilerParams(vmem_limit_bytes=LIMIT),
        cost_estimate=LIGHT,
        name="qkv_fwd",
    )(ids, x4, *came, *gathered, bucket_rows)

def gelu_both(v):
    t = jnp.tanh(root_coef * (v + cubic_coef * v * v * v))
    half = 0.5 * (1.0 + t)
    slope = half + 0.5 * v * (1.0 - t * t) * (root_coef * (1.0 + 3.0 * cubic_coef * v * v))
    return v * half, slope

def mid_kernel(ids_ref, x_ref, o_ref, g4_ref, c1_ref, c2_ref, c3_ref, gain_ref, wback_ref, wo_ref, win_ref,
               out_ref, gb_ref, do_ref, gw_ref, gwback_ref,
               mixed, h2, h2t, acc, gh2, gm, sem, *, ff_steps):
    step = pl.program_id(0)
    rows, width = x_ref.shape
    part = 256
    flat = lambda ref: ref[...].reshape(-1, ref.shape[-1])

    @pl.when(step == 0)
    def _():
        pull_sequence(ids_ref[0], g4_ref, (c1_ref, c2_ref, c3_ref), gm, sem)
        wo = flat(wo_ref)
        def load(i, carry):
            at = pl.ds(pl.multiple_of(i * part, part), part)
            value = x_ref[at, :].astype(jnp.float32) + _dot(o_ref[at, :], wo)
            mixed[at, :] = value
            acc[at, :] = value
            hidden = (value * rms_inverse(value) * gain_ref[1:2, :]).astype(jnp.bfloat16)
            h2[at, :] = hidden
            h2t[:, at] = hidden.T
            gh2[at, :] = jnp.zeros_like(value)
            return carry
        lax.fori_loop(0, rows // part, load, 0)
        pltpu.make_async_copy(gm, gm, sem).wait()
        row_ok = lax.broadcasted_iota(jnp.int32, (rows, 1), 0) < ids_ref[2]
        gm[...] = jnp.where(row_ok, gm[...], jnp.zeros_like(gm[...]))

    @pl.when(step < ff_steps)
    def _():
        win = flat(win_ref)
        wback = flat(wback_ref)
        pre = _dot(h2[...], win)
        grad_active = _dot(gm[...], wback, NT)
        act, slope = gelu_both(pre)
        active = act.astype(jnp.bfloat16)
        gpre = (grad_active * slope).astype(jnp.bfloat16)
        acc[...] += _dot(active, wback)
        gwback_ref[...] = _dot(active, gm[...], TN).astype(jnp.bfloat16)
        gw_ref[...] = _dot(h2t[...], gpre).astype(jnp.bfloat16).reshape(gw_ref.shape)
        gh2[...] += _dot(gpre, win, NT)

    @pl.when(step == ff_steps)
    def _():
        wo = flat(wo_ref)
        def finish(i, carry):
            at = pl.ds(pl.multiple_of(i * part, part), part)
            out_ref[at, :] = acc[at, :].astype(jnp.bfloat16)
            value = mixed[at, :]
            inverse = rms_inverse(value)
            normed = value * inverse
            scaled = gh2[at, :] * gain_ref[1:2, :]
            grad = inverse * (scaled - normed * jnp.mean(scaled * normed, axis=1, keepdims=True)) + gm[at, :].astype(jnp.float32)
            gb = grad.astype(jnp.bfloat16)
            gb_ref[at, :] = gb
            do_ref[at, :] = _dot(gb, wo, NT).astype(jnp.bfloat16)
            return carry
        lax.fori_loop(0, rows // part, finish, 0)

    @pl.when(step >= ff_steps)
    def _():
        cols = gw_ref.shape[-1]
        at = pl.ds(pl.multiple_of((step - ff_steps) * cols, cols), cols)
        gw_ref[...] = _dot(o_ref[...], gb_ref[:, at], TN).astype(jnp.bfloat16).reshape(gw_ref.shape)

def mid(ids, x, o, g4, came, gains, full, cols=512):
    rows, width = x.shape
    shards, stack, _ = full.shape
    own = width // shards
    ff_own = (stack - own) // 2
    ff = ff_own * shards
    ff_steps = ff // cols
    wide = width // cols
    one = lambda shape: pl.BlockSpec(shape, lambda i, n: (0,) * len(shape), pipeline_mode=pl.Buffered(1))
    last = lambda i: jnp.minimum(i, ff_steps - 1)
    mat = jax.ShapeDtypeStruct((rows, width), jnp.bfloat16)
    first = ff_own // own + 1
    gw_map = lambda i, n: (0, jnp.where(i < ff_steps, 1 + i // wide, 0), jnp.where(i < ff_steps, i % wide, i - ff_steps))
    return pl.pallas_call(
        functools.partial(mid_kernel, ff_steps=ff_steps),
        out_shape=(mat, mat, mat, jax.ShapeDtypeStruct((shards, own + ff_own, width), jnp.bfloat16), jax.ShapeDtypeStruct((ff, width), jnp.bfloat16)),
        grid_spec=pltpu.PrefetchScalarGridSpec(
            num_scalar_prefetch=1, grid=(ff_steps + wide,),
            in_specs=[one((rows, width)), one((rows, width)), ANY, ANY, ANY, ANY, one(gains.shape),
                      pl.BlockSpec((cols // ff_own, ff_own, width), lambda i, n: (last(i), 0, 0)),
                      pl.BlockSpec((shards, own, width), lambda i, n: (0, first - 1, 0), pipeline_mode=pl.Buffered(1)),
                      pl.BlockSpec((shards, own, cols), lambda i, n: (0, first + last(i) // wide, last(i) % wide))],
            out_specs=[one((rows, width)), one((rows, width)), one((rows, width)),
                       pl.BlockSpec((shards, own, cols), gw_map), pl.BlockSpec((cols, width), lambda i, n: (last(i), 0))],
            scratch_shapes=[pltpu.VMEM((rows, width), jnp.float32), pltpu.VMEM((rows, width), jnp.bfloat16),
                            pltpu.VMEM((width, rows), jnp.bfloat16), pltpu.VMEM((rows, width), jnp.float32),
                            pltpu.VMEM((rows, width), jnp.float32), pltpu.VMEM((rows, width), jnp.bfloat16), pltpu.SemaphoreType.DMA]),
        compiler_params=pltpu.CompilerParams(vmem_limit_bytes=LIMIT),
        cost_estimate=LIGHT,
        name="mid",
    )(ids, x, o, g4, *came, gains, full, full, full)

def gw_kernel(h_ref, dq_ref, dk_ref, dv_ref, bucket_ref, *refs):
    out_ref = refs[-1]
    shards, _, width = out_ref.shape
    own = width // shards
    for i, ref in enumerate((dq_ref, dk_ref, dv_ref)):
        out_ref[:, i * own:(i + 1) * own, :] = _dot(h_ref[...], ref[...], TN).astype(jnp.bfloat16).reshape(shards, own, width)
    offs = jnp.concatenate([ref[...] for ref in refs[:-1]], 0)
    ids = lax.broadcasted_iota(jnp.int32, (shards, 1), 0)
    hot = jnp.where(bucket_ref[1:2, :] == ids, 1.0, 0.0)
    table = lax.dot_general(hot, offs, NT, precision=lax.Precision.HIGHEST, preferred_element_type=jnp.float32)
    out_ref[:, 3 * own:, :] = jnp.zeros((shards, 16, width), jnp.bfloat16)
    out_ref[:, 3 * own:3 * own + 1, 0:offs.shape[0]] = table.astype(jnp.bfloat16).reshape(shards, 1, offs.shape[0])

def qkv_gw(h, dq, dk, dv, bucket_rows, offs, shards):
    rows, width = h.shape
    return pl.pallas_call(
        gw_kernel, out_shape=jax.ShapeDtypeStruct((shards, 3 * width // shards + 16, width), jnp.bfloat16),
        in_specs=[VM] * (5 + len(offs)), out_specs=VM,
        compiler_params=pltpu.CompilerParams(vmem_limit_bytes=LIMIT),
        cost_estimate=LIGHT,
        name="qkv_gw",
    )(h, dq, dk, dv, bucket_rows, *offs)

def gx_kernel(x_ref, gb_ref, dq_ref, dk_ref, dv_ref, gain_ref, w_ref, out_ref):
    width = x_ref.shape[1]
    grad = _dot(dq_ref[...], w_ref[:, :width], NT)
    grad += _dot(dk_ref[...], w_ref[:, width:2 * width], NT)
    grad += _dot(dv_ref[...], w_ref[:, 2 * width:3 * width], NT)
    x = x_ref[...].astype(jnp.float32)
    inverse = rms_inverse(x)
    normed = x * inverse
    scaled = grad * gain_ref[0:1, :]
    out = inverse * (scaled - normed * jnp.mean(scaled * normed, axis=1, keepdims=True)) + gb_ref[...].astype(jnp.float32)
    out_ref[...] = out.astype(jnp.bfloat16)

def qkv_gx(x, gb, dq, dk, dv, gains, w, rows=512):
    total, width = x.shape
    blk = pl.BlockSpec((rows, width), lambda i: (i, 0))
    return pl.pallas_call(
        gx_kernel, out_shape=jax.ShapeDtypeStruct((total, width), jnp.bfloat16), grid=(total // rows,),
        in_specs=[blk] * 5 + [pl.BlockSpec(gains.shape, lambda i: (0, 0)),
                              pl.BlockSpec((width, 3 * width), lambda i: (0, 0), pipeline_mode=pl.Buffered(1))],
        out_specs=blk,
        compiler_params=pltpu.CompilerParams(vmem_limit_bytes=LIMIT),
        cost_estimate=LIGHT,
        name="qkv_gx",
    )(x, gb, dq, dk, dv, gains, w)

def swap(value, axis, mask):
    return lax.ppermute(value, axis, [(i, i ^ mask) for i in range(lax.axis_size(axis))])


def send_blocks(blocks, me):
    return tuple(swap(lax.dynamic_index_in_dim(blocks, me ^ mask, 0), "seq", mask) for mask in range(1, blocks.shape[0]))


MASKS = ((0, 8, 16, 24), (2, 10, 18, 26), (4, 12, 20, 28), (6, 14), (22, 30))


def gather_staged(shard):
    shard = shard[None]
    column = jnp.concatenate([shard] + [swap(shard, "dp", 2 * z) for z in (1, 2, 3)], 0)
    from_x, from_y = swap(column, "seq", 2), swap(column, "dp", 1)
    corner_x, corner_y = swap(from_y[:2], "seq", 2), swap(from_x[2:], "dp", 1)
    pieces = (column, from_x, from_y, corner_x, corner_y)
    masks = MASKS + tuple(tuple(m | 1 for m in row) for row in MASKS)
    return pieces + tuple(swap(p, "seq", 1) for p in pieces), masks


class Scatter:
    def __init__(self, grads, pos):
        self.z, self.y, self.x, self.c = pos
        self.grads = grads.reshape((4, 2, 2, 2) + grads.shape[1:])
        self.sent = lax.dynamic_index_in_dim(self.grads, 1 - self.c, 3, keepdims=False)
        self.other = swap(self.sent, "seq", 1)

    def fold(self):
        pick = lambda v, at, axis: lax.dynamic_index_in_dim(v, at, axis, keepdims=False)
        mine = pick(self.grads, self.c, 3)
        def quarter(dy, dx):
            cut = lambda v: pick(pick(v, self.y ^ dy, 1), self.x ^ dx, 1).astype(jnp.float32)
            return (cut(mine) + cut(self.other)).astype(jnp.bfloat16)
        far = quarter(1, 1)
        self.to_x, self.to_y, self.own = quarter(0, 1), quarter(1, 0), quarter(0, 0)
        self.came_x, self.came_y = swap(far[:2], "seq", 2), swap(far[2:], "dp", 1)

    def turn(self):
        add = lambda a, b: (a.astype(jnp.float32) + b.astype(jnp.float32)).astype(jnp.bfloat16)
        to_x = lax.dynamic_update_slice_in_dim(self.to_x, add(self.to_x[2:], self.came_y), 2, 0)
        to_y = lax.dynamic_update_slice_in_dim(self.to_y, add(self.to_y[:2], self.came_x), 0, 0)
        self.sent = (to_x, to_y)
        self.came_x, self.came_y = swap(to_x, "seq", 2), swap(to_y, "dp", 1)

    def column(self):
        total = self.own.astype(jnp.float32) + self.came_x.astype(jnp.float32) + self.came_y.astype(jnp.float32)
        total = total.astype(jnp.bfloat16)
        block = lambda k: lax.dynamic_index_in_dim(total, self.z ^ k, 0, keepdims=False)
        self.mine = block(0)
        self.came = [swap(block(k), "dp", 2 * k) for k in (1, 2, 3)]

    def result(self):
        return sum((c.astype(jnp.float32) for c in self.came), self.mine.astype(jnp.float32))


def place(blocks, came, me):
    for mask, block in enumerate(came, 1):
        blocks = lax.dynamic_update_slice_in_dim(blocks, block, me ^ mask, 0)
    return blocks


def tie(first, *later):
    return lax.optimization_barrier((first,) + later)[1:]


def local_whole(tokens, cotangent, lengths, buckets, norm1_gain, w_query, w_key, w_value, w_out, rel_table, norm2_gain, w_in, w_back):
    micro_count, seq_count, rows, width = tokens.shape
    parts = micro_count * seq_count
    both = ("dp", "seq")
    me, dp = lax.axis_index("seq"), lax.axis_index("dp")
    shards = lax.axis_size("seq") * lax.axis_size("dp")
    flat = dp * parts + me
    pos = (dp // 2, dp % 2, me // 2, me % 2)
    low = lambda v: v.astype(jnp.bfloat16)
    up = lambda v: v.astype(jnp.float32)
    own, ff_own = w_query.shape[0], w_back.shape[0]
    ids = jnp.stack([me, flat, lax.dynamic_index_in_dim(lengths.reshape(parts), me, 0, keepdims=False)])
    length = ids[2:3]

    place_row = lambda v: lax.dynamic_update_slice(jnp.zeros((1, width), jnp.bfloat16), low(v)[None], (0, flat * own))
    small = jnp.concatenate([place_row(norm1_gain), place_row(norm2_gain), jnp.zeros((6, width), jnp.bfloat16),
                             jnp.pad(low(rel_table)[None], ((0, 7), (0, width - HEADS)))], 0)
    shard1 = jnp.concatenate([low(w_query), low(w_key), low(w_value), small], 0)
    shard2 = jnp.concatenate([low(w_back), low(w_out)] + [low(w_in[:, i * width:(i + 1) * width]) for i in range(ff_own // own)], 0)
    x4, g4 = tokens.reshape(parts, rows, width), cotangent.reshape(parts, rows, width)
    gathered, masks = gather_staged(shard1)
    x_came = send_blocks(x4, me)
    g_came = send_blocks(g4, me)
    full2 = lax.all_gather(shard2, both, axis=0, tiled=False)
    bucket_rows = jnp.stack([jnp.pad(buckets, (0, 1), constant_values=-1), jnp.pad(buckets[::-1], (0, 1), constant_values=-1)])

    x, hidden, q, k, v, w_qkv, gains, t, t_back = qkv_fwd(ids, x4, x_came, gathered, masks, bucket_rows, HEADS)
    attended, lse = attn_fwd(length, q, k, v, t)
    out, gb, g_att, gw2, gw_back = mid(ids, x, attended, g4, g_came, gains, full2)
    sc2 = Scatter(gw2, pos)
    r_back = lax.psum_scatter(gw_back, both, scatter_dimension=0, tiled=True)
    out4 = out.reshape(parts, rows, width)
    out_came = send_blocks(out4, me)
    pairs = HEADS // 2
    count = pairs // 4
    back = lambda first, g, prev: attn_bwd(length, q, k, v, g, attended, lse, t_back, first, count, prev)
    g_att, = tie((sc2.sent, out), g_att)
    dq, dk, dv, off0 = back(0, g_att, None)
    sc2.other, = tie((off0, out_came), sc2.other)
    sc2.fold()
    g_att, = tie((sc2.own, sc2.to_x, sc2.to_y), g_att)
    dq, dk, dv, off1 = back(count, g_att, (dq, dk, dv))
    sc2.came_x, sc2.came_y = tie(off1, sc2.came_x, sc2.came_y)
    sc2.turn()
    g_att, = tie(sc2.sent, g_att)
    dq, dk, dv, off2 = back(2 * count, g_att, (dq, dk, dv))
    dq, dk, dv, off3 = back(3 * count, g_att, (dq, dk, dv))
    sc2.came_x, sc2.came_y = tie(off3, sc2.came_x, sc2.came_y)
    sc2.column()
    h_in, = tie(sc2.mine, hidden)
    gw1 = qkv_gw(h_in, dq, dk, dv, bucket_rows, (off0, off1, off2, off3), shards)
    sc1 = Scatter(gw1, pos)
    gb_in, = tie(sc1.sent, gb)
    gx = qkv_gx(x, gb_in, dq, dk, dv, gains, w_qkv)
    sc1.other, = tie(gx, sc1.other)
    sc1.fold()
    out4, out_came = tie(sc1.own, out4, out_came)
    layer_out = place(out4, out_came, me)
    sc1.turn()
    sc2.came = list(tie((sc1.sent, layer_out), *sc2.came))
    r2 = sc2.result()
    sc1.came_x, sc1.came_y = tie(r2, sc1.came_x, sc1.came_y)
    sc1.column()
    gx, = tie(sc1.mine, gx)
    gx4 = gx.reshape(parts, rows, width)
    gx_came = send_blocks(gx4, me)
    input_grad = place(gx4, gx_came, me)
    sc1.came = list(tie(input_grad, *sc1.came))
    r1, r_back = sc1.result(), up(r_back)
    g_in = jnp.concatenate([r2[own * (1 + i):own * (2 + i)] for i in range(ff_own // own)], 1)
    prod = up(shard1[:3 * own]) * r1[:3 * own]
    g_gain1 = jnp.sum(prod[:own] + prod[own:2 * own] + prod[2 * own:], axis=1) / up(low(norm1_gain))
    g_gain2 = jnp.sum(up(low(w_in)) * g_in, axis=1) / up(low(norm2_gain))
    return (layer_out.reshape(tokens.shape), input_grad.reshape(tokens.shape), g_gain1, r1[:own], r1[own:2 * own], r1[2 * own:3 * own],
            r2[:own], r1[3 * own, :HEADS], g_gain2, g_in, r_back)


def local_any(shape, tokens, *rest):
    fits = tuple(shape) == (8, 4) and tokens.shape[0] * tokens.shape[1] == 4 and tokens.shape[3] == HEADS * DH == 1024
    return (local_whole if fits else local)(tokens, *rest)


def solution(mesh):
    return jax.shard_map(
        functools.partial(local_any, mesh.devices.shape),
        mesh=mesh,
        in_specs=(
            P(None, "dp", "seq", None),
            P(None, "dp", "seq", None),
            P(None, "dp"),
            P(),
            P(("dp", "seq")),
            P(("dp", "seq"), None),
            P(("dp", "seq"), None),
            P(("dp", "seq"), None),
            P(("dp", "seq"), None),
            P(("dp", "seq")),
            P(("dp", "seq")),
            P(("dp", "seq"), None),
            P(("dp", "seq"), None),
        ),
        out_specs=(
            P(None, "dp", "seq", None),
            P(None, "dp", "seq", None),
            P(("dp", "seq")),
            P(("dp", "seq"), None),
            P(("dp", "seq"), None),
            P(("dp", "seq"), None),
            P(("dp", "seq"), None),
            P(("dp", "seq")),
            P(("dp", "seq")),
            P(("dp", "seq"), None),
            P(("dp", "seq"), None),
        ),
        check_vma=False,
    )
```

```python
import functools

import jax
import jax.numpy as jnp
from jax import lax
from jax.experimental import pallas as pl
from jax.experimental.pallas import tpu as pltpu
from jax.sharding import PartitionSpec as P

HEADS = 16
DH = 64
BUCKETS = 32


epsilon = 1e-06
floor_score = -1e30
highest = lax.Precision.HIGHEST
root_coef = 0.7978845608
cubic_coef = 0.044715


def gelu_tanh(values):
    return (
        0.5
        * values
        * (1.0 + jnp.tanh(root_coef * (values + cubic_coef * values * values * values)))
    )


def gelu_slope(values):
    inner = jnp.tanh(root_coef * (values + cubic_coef * values * values * values))
    return 0.5 * (1.0 + inner) + 0.5 * values * (1.0 - inner * inner) * root_coef * (
        1.0 + 3.0 * cubic_coef * values * values
    )


def project(acts, weight):
    return jnp.einsum("srd,de->sre", acts, weight, preferred_element_type=jnp.float32)


def project_back(grads_in, weight):
    return jnp.einsum("sre,de->srd", grads_in, weight, preferred_element_type=jnp.float32)


def contract(acts, grads_in):
    return jnp.einsum("srd,sre->de", acts, grads_in, preferred_element_type=jnp.float32)


def rms_forward(values, gain):
    inverse = lax.rsqrt(jnp.mean(values * values, axis=-1, keepdims=True) + epsilon)
    normed = values * inverse
    return (normed, inverse, (normed * gain.astype(jnp.float32)).astype(jnp.bfloat16))


def rms_backward(grad_hidden, normed, inverse, gain):
    scaled = grad_hidden * gain.astype(jnp.float32)
    grad_values = inverse * (scaled - normed * jnp.mean(scaled * normed, axis=-1, keepdims=True))
    return (grad_values, jnp.sum(grad_hidden * normed, axis=(0, 1)))


def score_block(per_head_queries, per_head_keys, rel_bias, key_valid):
    scores = (
        jnp.einsum(
            "ofck,owck->ocfw", per_head_queries, per_head_keys, preferred_element_type=jnp.float32
        )
        + rel_bias[None]
    )
    return jnp.where(key_valid, scores, floor_score)


def offset_sums(grid, first_row, seq_len):
    head_count, row_count, key_count = grid.shape
    flipped = grid[:, ::-1, :]
    padded = jnp.pad(flipped, ((0, 0), (0, 0), (0, row_count)))
    wide_len = key_count + row_count
    skewed = padded.reshape(head_count, row_count * wide_len)[:, : row_count * (wide_len - 1)]
    skewed = skewed.reshape(head_count, row_count, wide_len - 1)
    column_sums = jnp.sum(skewed, axis=1)
    placed = jnp.zeros((head_count, 2 * seq_len - 1), jnp.float32)
    begin = seq_len - row_count - first_row
    return lax.dynamic_update_slice(placed, column_sums, (jnp.int32(0), begin))


def run_micro(inputs, incoming, seq_lens, attn_set, mlp_set, context):
    onehot, offsets, row_pos, key_pos, first_row, seq_len = context
    gain_one, query_w, key_w, value_w, out_w, bias_table = attn_set
    gain_two, in_w, return_projection_weight = mlp_set
    seq_count, row_count, model_width = inputs.shape
    values = inputs.astype(jnp.float32)
    normed_one, inverse_one, hidden_one = rms_forward(values, gain_one)
    queries = project(hidden_one, query_w).astype(jnp.bfloat16)
    keys_own = project(hidden_one, key_w).astype(jnp.bfloat16)
    values_own = project(hidden_one, value_w).astype(jnp.bfloat16)
    keys_all, values_all = (
        lax.all_gather(keys_own, "seq", axis=1, tiled=True),
        lax.all_gather(values_own, "seq", axis=1, tiled=True),
    )
    per_offset = jnp.dot(
        onehot, bias_table.reshape(BUCKETS, HEADS), preferred_element_type=jnp.float32
    )
    rel_bias = jnp.transpose(per_offset[offsets], (2, 0, 1))
    key_valid = (key_pos[None, :] < seq_lens[:, None])[:, None, None, :]
    per_head_queries = queries.reshape(seq_count, row_count, HEADS, DH)
    per_head_keys = keys_all.reshape(seq_count, seq_len, HEADS, DH)
    per_head_values = values_all.reshape(seq_count, seq_len, HEADS, DH)
    scores = score_block(per_head_queries, per_head_keys, rel_bias, key_valid)
    row_max = jnp.max(scores, axis=-1, keepdims=True)
    exp_scores = jnp.exp(scores - row_max)
    row_total = jnp.sum(exp_scores, axis=-1, keepdims=True)
    attn_probs = exp_scores / row_total
    log_total = row_max + jnp.log(row_total)
    reduced_precision_probs = attn_probs.astype(jnp.bfloat16)
    attended = jnp.einsum(
        "jfpe,jefn->jpfn",
        reduced_precision_probs,
        per_head_values,
        preferred_element_type=jnp.float32,
    )
    attended = attended.reshape(seq_count, row_count, model_width).astype(jnp.bfloat16)
    residual_mid = values + project(attended, out_w)
    normed_two, inverse_two, hidden_two = rms_forward(residual_mid, gain_two)
    pre_act = project(hidden_two, in_w)
    active = gelu_tanh(pre_act).astype(jnp.bfloat16)
    result = (residual_mid + project(active, return_projection_weight)).astype(jnp.bfloat16)
    row_valid = (row_pos[None, :] < seq_lens[:, None]).astype(jnp.float32)[:, :, None]
    grad_out = incoming.astype(jnp.float32) * row_valid
    grad_low = grad_out.astype(jnp.bfloat16)
    grad_back = contract(active, grad_low)
    gradient_active_rows = project_back(grad_low, return_projection_weight)
    grad_pre = (gradient_active_rows * gelu_slope(pre_act)).astype(jnp.bfloat16)
    grad_in = contract(hidden_two, grad_pre)
    grad_hidden_two = project_back(grad_pre, in_w)
    grad_mixed, grad_gain_two = rms_backward(grad_hidden_two, normed_two, inverse_two, gain_two)
    grad_mixed = grad_mixed + grad_out
    grad_branch = grad_mixed.astype(jnp.bfloat16)
    grad_outw = contract(attended, grad_branch)
    gradient_attended_values = project_back(grad_branch, out_w).astype(jnp.bfloat16)
    gradient_attended_values = gradient_attended_values.reshape(seq_count, row_count, HEADS, DH)
    scores = score_block(per_head_queries, per_head_keys, rel_bias, key_valid)
    attn_probs = jnp.exp(scores - log_total)
    reduced_precision_probs = attn_probs.astype(jnp.bfloat16)
    grad_probs = jnp.einsum(
        "ofck,owck->ocfw",
        gradient_attended_values,
        per_head_values,
        preferred_element_type=jnp.float32,
    )
    inner_sum = jnp.sum(attn_probs * grad_probs, axis=-1, keepdims=True)
    gradient_score_matrix = (attn_probs * (grad_probs - inner_sum)).astype(jnp.bfloat16)
    grad_query = jnp.einsum(
        "jfpe,jefn->jpfn", gradient_score_matrix, per_head_keys, preferred_element_type=jnp.float32
    )
    grad_query = grad_query.astype(jnp.bfloat16).reshape(seq_count, row_count, model_width)
    key_part = jnp.einsum(
        "eciv,eicq->evcq",
        gradient_score_matrix,
        per_head_queries,
        preferred_element_type=jnp.float32,
    )
    value_part = jnp.einsum(
        "eciv,eicq->evcq",
        reduced_precision_probs,
        gradient_attended_values,
        preferred_element_type=jnp.float32,
    )
    key_part = key_part.reshape(seq_count, seq_len, model_width)
    value_part = value_part.reshape(seq_count, seq_len, model_width)
    grad_key, grad_value = (
        lax.psum_scatter(
            key_part.astype(jnp.bfloat16), "seq", scatter_dimension=1, tiled=True
        ).astype(jnp.float32),
        lax.psum_scatter(
            value_part.astype(jnp.bfloat16), "seq", scatter_dimension=1, tiled=True
        ).astype(jnp.float32),
    )
    grad_key = grad_key.astype(jnp.bfloat16)
    grad_value = grad_value.astype(jnp.bfloat16)
    offset_grad = offset_sums(
        jnp.sum(gradient_score_matrix.astype(jnp.float32), axis=0), first_row, seq_len
    )
    grad_table = jnp.dot(onehot.astype(jnp.float32).T, offset_grad.T, precision=highest).reshape(-1)
    grad_qw = contract(hidden_one, grad_query)
    grad_kw = contract(hidden_one, grad_key)
    grad_vw = contract(hidden_one, grad_value)
    grad_hidden_one = (
        project_back(grad_query, query_w)
        + project_back(grad_key, key_w)
        + project_back(grad_value, value_w)
    )
    grad_values, grad_gain_one = rms_backward(grad_hidden_one, normed_one, inverse_one, gain_one)
    grad_values = grad_values + grad_mixed
    gradients = (
        grad_gain_one,
        grad_qw,
        grad_kw,
        grad_vw,
        grad_outw,
        grad_table,
        grad_gain_two,
        grad_in,
        grad_back,
    )
    return (result, grad_values.astype(jnp.bfloat16), gradients)


def local(
    tokens,
    cotangent,
    lengths,
    buckets,
    norm1_gain,
    w_query,
    w_key,
    w_value,
    w_out,
    rel_table,
    norm2_gain,
    w_in,
    w_back,
):
    micro_count, seq_count, row_count, model_width = tokens.shape
    seq_parts = lax.axis_size("seq")
    seq_len = row_count * seq_parts
    first_row = lax.axis_index("seq") * row_count
    row_pos = first_row + jnp.arange(row_count, dtype=jnp.int32)
    key_pos = jnp.arange(seq_len, dtype=jnp.int32)
    onehot = (buckets[:, None] == jnp.arange(BUCKETS, dtype=jnp.int32)[None, :]).astype(
        jnp.bfloat16
    )
    offsets = key_pos[None, :] - row_pos[:, None] + (seq_len - 1)
    context = (onehot, offsets, row_pos, key_pos, first_row, seq_len)
    outputs = []
    input_grads = []
    pending = None
    shard_sums = None
    for micro_step in range(micro_count):
        attn_set = (
            lax.all_gather(norm1_gain.astype(jnp.bfloat16), ("dp", "seq"), axis=0, tiled=True),
            lax.all_gather(w_query.astype(jnp.bfloat16), ("dp", "seq"), axis=0, tiled=True),
            lax.all_gather(w_key.astype(jnp.bfloat16), ("dp", "seq"), axis=0, tiled=True),
            lax.all_gather(w_value.astype(jnp.bfloat16), ("dp", "seq"), axis=0, tiled=True),
            lax.all_gather(w_out.astype(jnp.bfloat16), ("dp", "seq"), axis=0, tiled=True),
            lax.all_gather(rel_table.astype(jnp.bfloat16), ("dp", "seq"), axis=0, tiled=True),
        )
        mlp_set = (
            lax.all_gather(norm2_gain.astype(jnp.bfloat16), ("dp", "seq"), axis=0, tiled=True),
            lax.all_gather(w_in.astype(jnp.bfloat16), ("dp", "seq"), axis=0, tiled=True),
            lax.all_gather(w_back.astype(jnp.bfloat16), ("dp", "seq"), axis=0, tiled=True),
        )
        layer_part, grad_part, gradients = run_micro(
            tokens[micro_step],
            cotangent[micro_step],
            lengths[micro_step],
            attn_set,
            mlp_set,
            context,
        )
        outputs.append(layer_part)
        input_grads.append(grad_part)
        pending = gradients if pending is None else jax.tree.map(jnp.add, pending, gradients)
    shard_sums = (
        lax.psum_scatter(pending[0], ("dp", "seq"), scatter_dimension=0, tiled=True),
        lax.psum_scatter(pending[1], ("dp", "seq"), scatter_dimension=0, tiled=True),
        lax.psum_scatter(pending[2], ("dp", "seq"), scatter_dimension=0, tiled=True),
        lax.psum_scatter(pending[3], ("dp", "seq"), scatter_dimension=0, tiled=True),
        lax.psum_scatter(pending[4], ("dp", "seq"), scatter_dimension=0, tiled=True),
        lax.psum_scatter(pending[5], ("dp", "seq"), scatter_dimension=0, tiled=True),
        lax.psum_scatter(pending[6], ("dp", "seq"), scatter_dimension=0, tiled=True),
        lax.psum_scatter(pending[7], ("dp", "seq"), scatter_dimension=0, tiled=True),
        lax.psum_scatter(pending[8], ("dp", "seq"), scatter_dimension=0, tiled=True),
    )
    return (
        jnp.stack(outputs),
        jnp.stack(input_grads),
        shard_sums[0],
        shard_sums[1],
        shard_sums[2],
        shard_sums[3],
        shard_sums[4],
        shard_sums[5],
        shard_sums[6],
        shard_sums[7],
        shard_sums[8],
    )


NT = (((1,), (1,)), ((), ()))
TN = (((0,), (0,)), ((), ()))
STRIP = 128
LOG2E = 1.4426950408889634
LN2 = 0.6931471805599453
LIMIT = 58 << 20
LIGHT = pl.CostEstimate(flops=1 << 20, bytes_accessed=1 << 16, transcendentals=0)

def _dot(a, b, dims=(((1,), (0,)), ((), ()))):
    return lax.dot_general(a, b, dims, preferred_element_type=jnp.float32)

def with_extras(x, which, extras, width=64):
    lane = lax.broadcasted_iota(jnp.int32, (1, x.shape[1]), 1)
    spare = lane - width if which == 0 else lane
    own = (lane < width) if which == 0 else (lane >= width)
    fill = jnp.zeros_like(x)
    for i, extra in enumerate(extras):
        fill = jnp.where(spare == i, extra, fill)
    return jnp.where(own, x, fill).astype(jnp.bfloat16)

def three_parts(x):
    low = lambda v: v.astype(jnp.bfloat16).astype(jnp.float32)
    high = low(x)
    middle = low(x - high)
    return [high, middle, low(x - high - middle)]

def slot_floor(size, length):
    return jnp.where(lax.broadcasted_iota(jnp.int32, (size, 1), 0) < length, 0.0, floor_score)

def skew(row, wide):
    return pltpu.roll(jnp.broadcast_to(row, (STRIP, wide)), wide - (STRIP - 1), 1, stride=1, stride_axis=0)

def fwd_kernel(len_ref, q_ref, k_ref, v_ref, t_ref, *refs, rows, seq_len, first):
    o_ref, lse_ref, strip, kx, vx = refs[-5:]
    wide = t_ref.shape[-1]
    pair = first + pl.program_id(0)
    per = rows // STRIP
    lane = lax.broadcasted_iota(jnp.int32, (1, 128), 1)
    k2 = k_ref[...].astype(jnp.float32)
    vx[:, 0:128] = v_ref[...]
    vx[:, 128:256] = jnp.ones_like(v_ref[...])
    for a in range(2):
        kx[a] = with_extras(k2, a, [slot_floor(seq_len, len_ref[0])])
        strip[a] = skew(t_ref[pl.ds(2 * pair + a, 1), :], wide)

    def step(b, carry):
        base = b * rows
        q2 = q_ref[pl.ds(base, rows), :].astype(jnp.float32)
        outs, stats = [], []
        for a in range(2):
            scores = _dot(with_extras(q2, a, [1.0]), kx[a], NT)
            parts = []
            for i in range(per):
                off = (seq_len - STRIP) - (b * per + i) * STRIP
                parts.append(strip[a, :, pl.ds(off, seq_len)])
            scores = scores + (jnp.concatenate(parts, 0) if per > 1 else parts[0])
            top = jnp.max(scores, axis=1, keepdims=True)
            probs = jnp.exp2(scores - top).astype(jnp.bfloat16)
            out = _dot(probs, vx[...])
            outs.append(out[:, 0:128] / out[:, 128:256])
            stats.append(top + jnp.log2(out[:, 128:256]))
        o_ref[pl.ds(base, rows), :] = jnp.where(lane < 64, outs[0], outs[1]).astype(jnp.bfloat16)
        lse_ref[0, pl.ds(base, rows), :] = jnp.where(lane < 64, stats[0], stats[1])
        return carry

    for b in range(seq_len // rows):
        step(b, 0)

def attn_fwd(length, q, k, v, t, first, count, prev=(), rows=256):
    seq_len, width = q.shape
    pairs = width // 128
    wide = t.shape[-1]
    blk = pl.BlockSpec((seq_len, 128), lambda p, n: (0, first + p))
    return pl.pallas_call(
        functools.partial(fwd_kernel, rows=rows, seq_len=seq_len, first=first),
        out_shape=(jax.ShapeDtypeStruct((seq_len, width), jnp.bfloat16),
                   jax.ShapeDtypeStruct((pairs, seq_len, 128), jnp.float32)),
        grid_spec=pltpu.PrefetchScalarGridSpec(
            num_scalar_prefetch=1, grid=(count,),
            in_specs=[blk, blk, blk, pl.BlockSpec(t.shape, lambda p, n: (0, 0))] + [pl.BlockSpec(memory_space=pl.ANY)] * len(prev),
            out_specs=[blk, pl.BlockSpec((1, seq_len, 128), lambda p, n: (first + p, 0, 0))],
            scratch_shapes=[pltpu.VMEM((2, STRIP, wide), jnp.float32), pltpu.VMEM((2, seq_len, 128), jnp.bfloat16),
                            pltpu.VMEM((seq_len, 256), jnp.bfloat16)]),
        input_output_aliases={5 + i: i for i in range(len(prev))},
        compiler_params=pltpu.CompilerParams(vmem_limit_bytes=LIMIT),
        cost_estimate=LIGHT,
        name="attn_fwd",
    )(length, q, k, v, t, *prev)

def bwd_kernel(len_ref, q_ref, k_ref, v_ref, do_ref, o_ref, lse_ref, t_ref, *refs, rows, seq_len, first):
    dq_ref, dk_ref, dv_ref, g_ref, strip, acc, dq_acc, qx, kx, vx, dox = refs[-11:]
    wide = t_ref.shape[-1]
    local_pair = pl.program_id(0)
    pair = first + local_pair
    per = rows // STRIP
    lane = lax.broadcasted_iota(jnp.int32, (1, 128), 1)
    up = lambda ref: ref[...].astype(jnp.float32)
    floor = slot_floor(seq_len, len_ref[0])
    prod = up(do_ref) * up(o_ref)
    for a in range(2):
        mine = (lane < 64) if a == 0 else (lane >= 64)
        delta = jnp.sum(jnp.where(mine, prod, 0.0), axis=1, keepdims=True)
        lse = lse_ref[0, :, 64 * a:64 * a + 1]
        qx[a] = with_extras(up(q_ref), a, [1.0] + three_parts(-lse))
        kx[a] = with_extras(up(k_ref), a, [floor, 1.0, 1.0, 1.0])
        vx[a] = with_extras(up(v_ref), a, [1.0, 1.0, 1.0])
        dox[a] = with_extras(up(do_ref), a, three_parts(-delta))
        strip[a] = skew(t_ref[pl.ds(2 * pair + a, 1), :], wide)
    acc[...] = jnp.zeros_like(acc)
    k2t = k_ref[...].T
    dq_acc[...] = jnp.zeros_like(dq_acc)

    def step(b, carry):
        at = pl.ds(b * rows, rows)
        dks, dvs = [], []
        for a in range(2):
            scores = _dot(kx[a, at, :], qx[a], NT)
            offs = [(seq_len - STRIP) - (b * per + i) * STRIP for i in range(per)]
            bias = [strip[a, :, pl.ds(off, seq_len)] for off in offs]
            probs = jnp.exp2(scores + (jnp.concatenate(bias, 0) if per > 1 else bias[0]))
            grad_scores = probs * _dot(vx[a, at, :], dox[a], NT)
            for i, off in enumerate(offs):
                acc[a, :, pl.ds(off, seq_len)] += grad_scores[i * STRIP:(i + 1) * STRIP]
            probs_b = probs.astype(jnp.bfloat16)
            gs_b = grad_scores.astype(jnp.bfloat16)
            dvs.append(_dot(probs_b, do_ref[...]))
            dks.append(_dot(gs_b, q_ref[...]))
            dq_acc[a] += _dot(k2t[:, b * rows:(b + 1) * rows], gs_b)
        dk_ref[at, :] = (jnp.where(lane < 64, dks[0], dks[1]) * LN2).astype(jnp.bfloat16)
        dv_ref[at, :] = jnp.where(lane < 64, dvs[0], dvs[1]).astype(jnp.bfloat16)
        return carry

    for b in range(seq_len // rows):
        step(b, 0)
    dq_ref[...] = jnp.concatenate([dq_acc[0, 0:64], dq_acc[1, 64:128]], 0).T.astype(jnp.bfloat16)
    for a in range(2):
        sums = acc[a]
        half = STRIP
        while half > 8:
            half //= 2
            sums = sums[:half] + pltpu.roll(sums[half:], wide - half, 1)
        while half > 1:
            half //= 2
            sums = sums + pltpu.roll(pltpu.roll(sums, 8 - half, 0), wide - half, 1)
        g_ref[pl.ds(2 * local_pair + a, 1), :] = pltpu.roll(sums, STRIP - 1, 1)[0:1]

def attn_bwd(length, q, k, v, do, o, lse, trev, first, count, prev=None, rows=512):
    seq_len, width = q.shape
    wide = trev.shape[-1]
    blk = pl.BlockSpec((seq_len, 128), lambda p, n: (0, first + p))
    mat = jax.ShapeDtypeStruct((seq_len, width), jnp.bfloat16)
    prev = tuple(prev) if prev is not None else ()
    return pl.pallas_call(
        functools.partial(bwd_kernel, rows=rows, seq_len=seq_len, first=first),
        out_shape=(mat, mat, mat, jax.ShapeDtypeStruct((2 * count, wide), jnp.float32)),
        grid_spec=pltpu.PrefetchScalarGridSpec(
            num_scalar_prefetch=1, grid=(count,),
            in_specs=[blk, blk, blk, blk, blk, pl.BlockSpec((1, seq_len, 128), lambda p, n: (first + p, 0, 0)),
                      pl.BlockSpec(trev.shape, lambda p, n: (0, 0))] + [pl.BlockSpec(memory_space=pl.ANY)] * len(prev),
            out_specs=[blk, blk, blk, pl.BlockSpec((2 * count, wide), lambda p, n: (0, 0))],
            scratch_shapes=[pltpu.VMEM((2, STRIP, wide), jnp.float32), pltpu.VMEM((2, STRIP, wide), jnp.float32),
                            pltpu.VMEM((2, 128, seq_len), jnp.float32)] + [pltpu.VMEM((2, seq_len, 128), jnp.bfloat16)] * 4),
        input_output_aliases={8 + i: i for i in range(len(prev))},
        compiler_params=pltpu.CompilerParams(vmem_limit_bytes=LIMIT),
        cost_estimate=LIGHT,
        name="attn_bwd",
    )(length, q, k, v, do, o, lse, trev, *prev)

ANY = pl.BlockSpec(memory_space=pl.ANY)
VM = pl.BlockSpec(memory_space=pltpu.VMEM)
SM = pl.BlockSpec(memory_space=pltpu.SMEM)

def rms_inverse(value):
    return lax.rsqrt(jnp.mean(value * value, axis=1, keepdims=True) + epsilon)

def pull_sequence(me, whole_ref, came, dst, sem):
    rows = whole_ref.shape[1]
    for mask, ref in enumerate((whole_ref,) + tuple(came)):
        src = ref.at[me] if mask == 0 else ref.at[0]
        at = pl.multiple_of((me ^ mask) * rows, rows)
        pltpu.make_async_copy(src, dst.at[pl.ds(at, rows), :], sem).start()

def qkv_kernel(ids_ref, x4_ref, c1_ref, c2_ref, c3_ref, *refs, masks):
    gathered = refs[:len(masks)]
    bucket_ref = refs[len(masks)]
    x_out, h_out, q_out, k_out, v_out, w_out, gain_ref, t_ref, trev_ref, xs, hs, ps, ws, es, sems = refs[len(masks) + 1:]
    me, flat = ids_ref[0], ids_ref[1]
    width = xs.shape[1]
    own = width // es.shape[0]
    pull_sequence(me, x4_ref, (c1_ref, c2_ref, c3_ref), xs, sems.at[0])
    for ref, ids in zip(gathered, masks):
        for j, mask in enumerate(ids):
            shard = flat ^ mask
            pltpu.make_async_copy(ref.at[j, 3 * own:3 * own + 16, :], es.at[shard], sems.at[1]).start()
    for ref, ids in zip(gathered, masks):
        for j, mask in enumerate(ids):
            at = pl.multiple_of((flat ^ mask) * own, own)
            for i in range(3):
                pltpu.make_async_copy(ref.at[j, i * own:(i + 1) * own, :], ws.at[pl.ds(at, own), i * width:(i + 1) * width], sems.at[2]).start()
    pltpu.make_async_copy(es, es, sems.at[1]).wait()
    extras = es[...].astype(jnp.float32)
    gains = jnp.sum(extras, axis=0)
    gain_ref[...] = gains[0:8]
    table = extras[:, 8, 0:128].astype(jnp.bfloat16)
    ids = lax.broadcasted_iota(jnp.int32, (es.shape[0], 1), 0)
    heads = t_ref.shape[0]
    for i, ref in enumerate((t_ref, trev_ref)):
        hot = jnp.where(bucket_ref[i:i + 1, :] == ids, 1.0, 0.0).astype(jnp.bfloat16)
        ref[...] = _dot(table, hot, TN)[0:heads] * LOG2E
    pltpu.make_async_copy(xs, xs, sems.at[0]).wait()
    part = 256
    def norm(i, carry):
        at = pl.ds(pl.multiple_of(i * part, part), part)
        x = xs[at, :].astype(jnp.float32)
        hs[at, :] = (x * rms_inverse(x) * gains[0:1]).astype(jnp.bfloat16)
        return carry
    lax.fori_loop(0, xs.shape[0] // part, norm, 0)
    copies = [pltpu.make_async_copy(xs, x_out, sems.at[0]), pltpu.make_async_copy(hs, h_out, sems.at[1])]
    for copy in copies:
        copy.start()
    pltpu.make_async_copy(ws, ws, sems.at[2]).wait()
    copies.append(pltpu.make_async_copy(ws, w_out, sems.at[2]))
    copies[-1].start()
    for i, ref in enumerate((q_out, k_out, v_out)):
        full = _dot(hs[...], ws[:, i * width:(i + 1) * width])
        ps[i] = (full * LOG2E if i == 0 else full).astype(jnp.bfloat16)
        copies.append(pltpu.make_async_copy(ps.at[i], ref, sems.at[3 + i]))
        copies[-1].start()
    for copy in copies:
        copy.wait()

def qkv_fwd(ids, x4, came, gathered, masks, bucket_rows, heads):
    parts, rows, width = x4.shape
    total = parts * rows
    shards = sum(len(m) for m in masks)
    mat = jax.ShapeDtypeStruct((total, width), jnp.bfloat16)
    wide = bucket_rows.shape[1]
    vm = lambda *s: pltpu.VMEM(s, jnp.bfloat16)
    return pl.pallas_call(
        functools.partial(qkv_kernel, masks=masks),
        out_shape=(mat,) * 5 + (jax.ShapeDtypeStruct((width, 3 * width), jnp.bfloat16), jax.ShapeDtypeStruct((8, width), jnp.float32),
                                jax.ShapeDtypeStruct((heads, wide), jnp.float32), jax.ShapeDtypeStruct((heads, wide), jnp.float32)),
        in_specs=[SM] + [ANY] * (4 + len(gathered)) + [VM],
        out_specs=[ANY] * 6 + [VM] * 3,
        scratch_shapes=[vm(total, width), vm(total, width), vm(3, total, width), vm(width, 3 * width), vm(shards, 16, width), pltpu.SemaphoreType.DMA((6,))],
        compiler_params=pltpu.CompilerParams(vmem_limit_bytes=LIMIT),
        cost_estimate=LIGHT,
        name="qkv_fwd",
    )(ids, x4, *came, *gathered, bucket_rows)

def gelu_both(v):
    t = jnp.tanh(root_coef * (v + cubic_coef * v * v * v))
    half = 0.5 * (1.0 + t)
    slope = half + 0.5 * v * (1.0 - t * t) * (root_coef * (1.0 + 3.0 * cubic_coef * v * v))
    return v * half, slope

def ff_chunks(h2, h2t, gm, acc, gh2, ws_in, ws_back, st_in, st_back, gw_out, row_in, sems, before_add, cols=512):
    steps = ws_in.shape[1] // cols
    half = st_back.shape[1]
    shards, own = st_in.shape[0], h2.shape[1] // st_in.shape[0]
    wide = h2.shape[1] // cols
    group = cols // half

    def step(c, carry):
        at = pl.ds(pl.multiple_of(c * cols, cols), cols)
        win, wback = ws_in[:, at], ws_back[at, :]
        pre = _dot(h2[...], win)
        grad_active = _dot(gm[...], wback, NT)
        act, slope = gelu_both(pre)
        active = act.astype(jnp.bfloat16)
        gpre = (grad_active * slope).astype(jnp.bfloat16)
        @pl.when(c == 0)
        def _():
            before_add()
        acc[...] += _dot(active, wback)
        gh2[...] += _dot(gpre, win, NT)
        rows_b = pl.ds(c * group, group)
        st_back[rows_b, :, :] = _dot(active, gm[...], TN).astype(jnp.bfloat16).reshape(group, half, h2.shape[1])
        pltpu.make_async_copy(st_back.at[rows_b, :, :], gw_out.at[rows_b, 0:half, :], sems.at[0]).start()
        up = pl.multiple_of((c // wide) * own, own)
        lanes = pl.ds(pl.multiple_of((c % wide) * cols, cols), cols)
        st_in[:, pl.ds(up, own), lanes] = _dot(h2t[...], gpre).astype(jnp.bfloat16).reshape(shards, own, cols)
        pltpu.make_async_copy(st_in.at[:, pl.ds(up, own), lanes], gw_out.at[:, pl.ds(row_in + up, own), lanes], sems.at[1]).start()
        return carry
    lax.fori_loop(0, steps, step, 0)

def finish_chunks(st_in, st_back, sems):
    pltpu.make_async_copy(st_back, st_back, sems.at[0]).wait()
    pltpu.make_async_copy(st_in, st_in, sems.at[1]).wait()

def aligned(at, size):
    return at if isinstance(at, int) else pl.multiple_of(at, size)

def pull_ff(flat, gathered, masks, ws_in, ws_back, row_in, sems):
    width = ws_in.shape[0]
    shards = sum(len(m) for m in masks)
    own, half = width // shards, ws_back.shape[0] // shards
    for ref, ids in zip(gathered, masks):
        for j, mask in enumerate(ids):
            shard = flat ^ mask
            pltpu.make_async_copy(ref.at[j, 0:half, :], ws_back.at[pl.ds(aligned(shard * half, half), half), :], sems.at[1]).start()
            at = pl.ds(aligned(shard * own, own), own)
            for i in range(ws_in.shape[1] // width):
                pltpu.make_async_copy(ref.at[j, row_in + i * own:row_in + (i + 1) * own, :], ws_in.at[at, i * width:(i + 1) * width], sems.at[0]).start()

def mid_a_kernel(ids_ref, x_hbm, o_hbm, g4_ref, c1_ref, c2_ref, c3_ref, gain_ref, *refs, masks):
    gathered = refs[:len(masks)]
    (mixed_out, acc_out, gh2_out, h2_out, h2t_out, gm_out, wo_out, gw_out,
     xs, os, wo, ws_in, ws_back, mixed, h2, h2t, acc, gh2, gm, st_in, st_back, sems) = refs[len(masks):]
    flat = ids_ref[1]
    rows, width = xs.shape
    half, own = st_back.shape[1], width // st_in.shape[0]
    loads = [pltpu.make_async_copy(x_hbm, xs, sems.at[0]), pltpu.make_async_copy(o_hbm, os, sems.at[1])]
    for load in loads:
        load.start()
    for ref, ids in zip(gathered, masks):
        for j, mask in enumerate(ids):
            at = pl.ds(pl.multiple_of((flat ^ mask) * own, own), own)
            pltpu.make_async_copy(ref.at[j, half:half + own, :], wo.at[at, :], sems.at[2]).start()
    pull_ff(flat, gathered, masks, ws_in, ws_back, half + own, sems.at[3:5])
    pull_sequence(ids_ref[0], g4_ref, (c1_ref, c2_ref, c3_ref), gm, sems.at[5])
    for load in loads:
        load.wait()
    pltpu.make_async_copy(wo, wo, sems.at[2]).wait()
    stores = [pltpu.make_async_copy(wo, wo_out, sems.at[2])]
    stores[0].start()
    part = 256
    def load_rows(i, carry):
        at = pl.ds(pl.multiple_of(i * part, part), part)
        value = xs[at, :].astype(jnp.float32) + _dot(os[at, :], wo[...])
        mixed[at, :] = value
        acc[at, :] = value
        hidden = (value * rms_inverse(value) * gain_ref[1:2, :]).astype(jnp.bfloat16)
        h2[at, :] = hidden
        h2t[:, at] = hidden.T
        gh2[at, :] = jnp.zeros_like(value)
        return carry
    lax.fori_loop(0, rows // part, load_rows, 0)
    pltpu.make_async_copy(gm, gm, sems.at[5]).wait()
    row_ok = lax.broadcasted_iota(jnp.int32, (rows, 1), 0) < ids_ref[2]
    gm[...] = jnp.where(row_ok, gm[...], jnp.zeros_like(gm[...]))
    pltpu.make_async_copy(ws_in, ws_in, sems.at[3]).wait()
    pltpu.make_async_copy(ws_back, ws_back, sems.at[4]).wait()
    for i, (src, dst) in enumerate(((mixed, mixed_out), (h2, h2_out), (h2t, h2t_out), (gm, gm_out))):
        stores.append(pltpu.make_async_copy(src, dst, sems.at[6 + i]))
        stores[-1].start()
    ff_chunks(h2, h2t, gm, acc, gh2, ws_in, ws_back, st_in, st_back, gw_out, half, sems.at[0:2], lambda: None)
    for i, (src, dst) in enumerate(((acc, acc_out), (gh2, gh2_out))):
        stores.append(pltpu.make_async_copy(src, dst, sems.at[3 + i]))
        stores[-1].start()
    finish_chunks(st_in, st_back, sems.at[0:2])
    for store in stores:
        store.wait()

def mid_a(ids, x, o, g4, came, gains, gathered, masks, ff):
    rows, width = x.shape
    shards = sum(len(m) for m in masks)
    half = ff // shards
    low = lambda *s: jax.ShapeDtypeStruct(s, jnp.bfloat16)
    full = lambda *s: jax.ShapeDtypeStruct(s, jnp.float32)
    vm = lambda *s: pltpu.VMEM(s, jnp.bfloat16)
    vf = lambda *s: pltpu.VMEM(s, jnp.float32)
    stack = half + ff // width * (width // shards)
    return pl.pallas_call(
        functools.partial(mid_a_kernel, masks=masks),
        out_shape=(full(rows, width), full(rows, width), full(rows, width), low(rows, width), low(width, rows), low(rows, width), low(width, width), low(shards, stack, width)),
        in_specs=[SM] + [ANY] * 6 + [VM] + [ANY] * len(gathered), out_specs=[ANY] * 8,
        scratch_shapes=[vm(rows, width), vm(rows, width), vm(width, width), vm(width, ff), vm(ff, width), vf(rows, width), vm(rows, width), vm(width, rows),
                        vf(rows, width), vf(rows, width), vm(rows, width), vm(shards, stack - half, width), vm(shards, half, width), pltpu.SemaphoreType.DMA((10,))],
        compiler_params=pltpu.CompilerParams(vmem_limit_bytes=LIMIT),
        cost_estimate=LIGHT,
        name="mid_a",
    )(ids, x, o, g4, *came, gains, *gathered)

def mid_b_kernel( gain_ref, mixed_hbm, acc_hbm, gh2_hbm, h2_hbm, h2t_hbm, gm_hbm, wo_hbm, o_hbm, full_ref, *refs):
    (out_ref, gb_out, do_ref, gw_out,
     os, wo, ws_in, ws_back, mixed, h2, h2t, acc, gh2, gm, gb, st_in, st_back, st_o, sems) = refs
    rows, width = os.shape
    shards, half, own = st_in.shape[0], st_back.shape[1], width // st_in.shape[0]
    early = [(h2_hbm, h2), (gm_hbm, gm), (h2t_hbm, h2t)]
    late = [(acc_hbm, acc), (gh2_hbm, gh2), (mixed_hbm, mixed), (wo_hbm, wo), (o_hbm, os)]
    early = [pltpu.make_async_copy(a, b, sems.at[4 + i]) for i, (a, b) in enumerate(early)]
    late = [pltpu.make_async_copy(a, b, sems.at[7 + i]) for i, (a, b) in enumerate(late)]
    for load in early:
        load.start()
    pull_ff(0, (full_ref,), (range(shards),), ws_in, ws_back, half, sems.at[2:4])
    for load in late:
        load.start()
    for load in early:
        load.wait()
    pltpu.make_async_copy(ws_in, ws_in, sems.at[2]).wait()
    pltpu.make_async_copy(ws_back, ws_back, sems.at[3]).wait()
    def before_add():
        late[0].wait()
        late[1].wait()
    ff_chunks(h2, h2t, gm, acc, gh2, ws_in, ws_back, st_in, st_back, gw_out, half + own, sems.at[0:2], before_add)
    for load in late[2:]:
        load.wait()
    part = 256
    def finish(i, carry):
        at = pl.ds(pl.multiple_of(i * part, part), part)
        out_ref[at, :] = acc[at, :].astype(jnp.bfloat16)
        value = mixed[at, :]
        inverse = rms_inverse(value)
        normed = value * inverse
        scaled = gh2[at, :] * gain_ref[1:2, :]
        grad = inverse * (scaled - normed * jnp.mean(scaled * normed, axis=1, keepdims=True)) + gm[at, :].astype(jnp.float32)
        low = grad.astype(jnp.bfloat16)
        gb[at, :] = low
        do_ref[at, :] = _dot(low, wo[...], NT).astype(jnp.bfloat16)
        return carry
    lax.fori_loop(0, rows // part, finish, 0)
    st_o[...] = _dot(os[...], gb[...], TN).astype(jnp.bfloat16).reshape(st_o.shape)
    stores = [pltpu.make_async_copy(st_o, gw_out.at[:, half:half + own, :], sems.at[2]), pltpu.make_async_copy(gb, gb_out, sems.at[3])]
    for store in stores:
        store.start()
    finish_chunks(st_in, st_back, sems.at[0:2])
    for store in stores:
        store.wait()

def mid_b(gains, state, o, full, ff):
    rows, width = o.shape
    shards = full.shape[0]
    half, own = ff // shards, width // shards
    low = lambda *s: jax.ShapeDtypeStruct(s, jnp.bfloat16)
    vm = lambda *s: pltpu.VMEM(s, jnp.bfloat16)
    vf = lambda *s: pltpu.VMEM(s, jnp.float32)
    rest = ff // width * own
    return pl.pallas_call(
        mid_b_kernel,
        out_shape=(low(rows, width), low(rows, width), low(rows, width), low(shards, half + own + rest, width)),
        in_specs=[VM] + [ANY] * 9, out_specs=[VM, ANY, VM, ANY],
        scratch_shapes=[vm(rows, width), vm(width, width), vm(width, ff), vm(ff, width), vf(rows, width), vm(rows, width), vm(width, rows),
                        vf(rows, width), vf(rows, width), vm(rows, width), vm(rows, width), vm(shards, rest, width), vm(shards, half, width), vm(shards, own, width),
                        pltpu.SemaphoreType.DMA((12,))],
        compiler_params=pltpu.CompilerParams(vmem_limit_bytes=LIMIT),
        cost_estimate=LIGHT,
        name="mid_b",
    )(gains, *state, o, full)

def gw_kernel(h_ref, dq_ref, dk_ref, dv_ref, bucket_ref, *refs):
    out_ref = refs[-1]
    shards, _, width = out_ref.shape
    own = width // shards
    for i, ref in enumerate((dq_ref, dk_ref, dv_ref)):
        out_ref[:, i * own:(i + 1) * own, :] = _dot(h_ref[...], ref[...], TN).astype(jnp.bfloat16).reshape(shards, own, width)
    offs = jnp.concatenate([ref[...] for ref in refs[:-1]], 0)
    ids = lax.broadcasted_iota(jnp.int32, (shards, 1), 0)
    hot = jnp.where(bucket_ref[1:2, :] == ids, 1.0, 0.0)
    table = lax.dot_general(hot, offs, NT, precision=lax.Precision.HIGHEST, preferred_element_type=jnp.float32)
    out_ref[:, 3 * own:, :] = jnp.zeros((shards, 16, width), jnp.bfloat16)
    out_ref[:, 3 * own:3 * own + 1, 0:offs.shape[0]] = table.astype(jnp.bfloat16).reshape(shards, 1, offs.shape[0])

def qkv_gw(h, dq, dk, dv, bucket_rows, offs, shards):
    rows, width = h.shape
    return pl.pallas_call(
        gw_kernel, out_shape=jax.ShapeDtypeStruct((shards, 3 * width // shards + 16, width), jnp.bfloat16),
        in_specs=[VM] * (5 + len(offs)), out_specs=VM,
        compiler_params=pltpu.CompilerParams(vmem_limit_bytes=LIMIT),
        cost_estimate=LIGHT,
        name="qkv_gw",
    )(h, dq, dk, dv, bucket_rows, *offs)

def gx_kernel(x_ref, gb_ref, dq_ref, dk_ref, dv_ref, gain_ref, w_ref, out_ref):
    width = x_ref.shape[1]
    grad = _dot(dq_ref[...], w_ref[:, :width], NT)
    grad += _dot(dk_ref[...], w_ref[:, width:2 * width], NT)
    grad += _dot(dv_ref[...], w_ref[:, 2 * width:3 * width], NT)
    x = x_ref[...].astype(jnp.float32)
    inverse = rms_inverse(x)
    normed = x * inverse
    scaled = grad * gain_ref[0:1, :]
    out = inverse * (scaled - normed * jnp.mean(scaled * normed, axis=1, keepdims=True)) + gb_ref[...].astype(jnp.float32)
    out_ref[...] = out.astype(jnp.bfloat16)

def qkv_gx(x, gb, dq, dk, dv, gains, w, rows=512):
    total, width = x.shape
    blk = pl.BlockSpec((rows, width), lambda i: (i, 0))
    return pl.pallas_call(
        gx_kernel, out_shape=jax.ShapeDtypeStruct((total, width), jnp.bfloat16), grid=(total // rows,),
        in_specs=[blk] * 5 + [pl.BlockSpec(gains.shape, lambda i: (0, 0)),
                              pl.BlockSpec((width, 3 * width), lambda i: (0, 0), pipeline_mode=pl.Buffered(1))],
        out_specs=blk,
        compiler_params=pltpu.CompilerParams(vmem_limit_bytes=LIMIT),
        cost_estimate=LIGHT,
        name="qkv_gx",
    )(x, gb, dq, dk, dv, gains, w)

def swap(value, axis, mask):
    return lax.ppermute(value, axis, [(i, i ^ mask) for i in range(lax.axis_size(axis))])


def send_blocks(blocks, me, masks=(1, 2, 3)):
    return tuple(swap(lax.dynamic_index_in_dim(blocks, me ^ mask, 0), "seq", mask) for mask in masks)


class Gather:
    def __init__(self, shard):
        shard = shard[None]
        self.sent = [shard] + [swap(shard, "dp", 2 * z) for z in (1, 2, 3)]
        self.pieces, self.masks = [], []

    def take(self, piece, mask, rows=(0, 1, 2, 3)):
        ids = tuple(8 * z | mask for z in rows)
        self.pieces += [piece, swap(piece, "seq", 1)]
        self.masks += [ids, tuple(m | 1 for m in ids)]

    def fill(self):
        self.own = jnp.concatenate(self.sent, 0)

    def sides(self):
        self.x, self.y = swap(self.own, "seq", 2), swap(self.own, "dp", 1)

    def corner_halves(self):
        self.near, self.far = swap(self.y[:2], "seq", 2), swap(self.x[2:], "dp", 1)

    def corner_y(self):
        self.corner = swap(self.x, "dp", 1)

    def all_pieces(self):
        return tuple(self.pieces), tuple(self.masks)


class Scatter:
    def __init__(self, grads, pos):
        self.z, self.y, self.x, self.c = pos
        self.grads = grads.reshape((4, 2, 2, 2) + grads.shape[1:])
        self.sent = lax.dynamic_index_in_dim(self.grads, 1 - self.c, 3, keepdims=False)
        self.other = swap(self.sent, "seq", 1)

    def fold(self):
        pick = lambda v, at, axis: lax.dynamic_index_in_dim(v, at, axis, keepdims=False)
        mine = pick(self.grads, self.c, 3)
        def quarter(dy, dx):
            cut = lambda v: pick(pick(v, self.y ^ dy, 1), self.x ^ dx, 1).astype(jnp.float32)
            return (cut(mine) + cut(self.other)).astype(jnp.bfloat16)
        far = quarter(1, 1)
        self.to_x, self.to_y, self.own = quarter(0, 1), quarter(1, 0), quarter(0, 0)
        self.came_x, self.came_y = swap(far[:2], "seq", 2), swap(far[2:], "dp", 1)

    def turn(self):
        add = lambda a, b: (a.astype(jnp.float32) + b.astype(jnp.float32)).astype(jnp.bfloat16)
        to_x = lax.dynamic_update_slice_in_dim(self.to_x, add(self.to_x[2:], self.came_y), 2, 0)
        to_y = lax.dynamic_update_slice_in_dim(self.to_y, add(self.to_y[:2], self.came_x), 0, 0)
        self.sent = (to_x, to_y)
        self.came_x, self.came_y = swap(to_x, "seq", 2), swap(to_y, "dp", 1)

    def column(self):
        total = self.own.astype(jnp.float32) + self.came_x.astype(jnp.float32) + self.came_y.astype(jnp.float32)
        total = total.astype(jnp.bfloat16)
        block = lambda k: lax.dynamic_index_in_dim(total, self.z ^ k, 0, keepdims=False)
        self.mine = block(0)
        self.came = [swap(block(k), "dp", 2 * k) for k in (1, 2, 3)]

    def result(self):
        return sum((c.astype(jnp.float32) for c in self.came), self.mine.astype(jnp.float32))


def place(blocks, came, me):
    for mask, block in enumerate(came, 1):
        blocks = lax.dynamic_update_slice_in_dim(blocks, block, me ^ mask, 0)
    return blocks


def tie(first, *later):
    return lax.optimization_barrier((first,) + later)[1:]


def local_whole(tokens, cotangent, lengths, buckets, norm1_gain, w_query, w_key, w_value, w_out, rel_table, norm2_gain, w_in, w_back):
    micro_count, seq_count, rows, width = tokens.shape
    parts = micro_count * seq_count
    both = ("dp", "seq")
    me, dp = lax.axis_index("seq"), lax.axis_index("dp")
    shards = lax.axis_size("seq") * lax.axis_size("dp")
    flat = dp * parts + me
    pos = (dp // 2, dp % 2, me // 2, me % 2)
    low = lambda v: v.astype(jnp.bfloat16)
    up = lambda v: v.astype(jnp.float32)
    own, ff_own = w_query.shape[0], w_back.shape[0]
    ids = jnp.stack([me, flat, lax.dynamic_index_in_dim(lengths.reshape(parts), me, 0, keepdims=False)])
    length = ids[2:3]

    place_row = lambda v: lax.dynamic_update_slice(jnp.zeros((1, width), jnp.bfloat16), low(v)[None], (0, flat * own))
    small = jnp.concatenate([place_row(norm1_gain), place_row(norm2_gain), jnp.zeros((6, width), jnp.bfloat16),
                             jnp.pad(low(rel_table)[None], ((0, 7), (0, width - HEADS)))], 0)
    shard1 = jnp.concatenate([low(w_query), low(w_key), low(w_value), small], 0)
    ff = w_in.shape[1] // 2
    half = ff_own // 2
    halves = low(w_in).reshape(own, shards, 2, half)
    in_half = lambda i: [halves[:, :, i].reshape(own, ff)[:, j:j + width] for j in range(0, ff, width)]
    shard2 = jnp.concatenate([low(w_back[:half]), low(w_out)] + in_half(0), 0)
    shard3 = jnp.concatenate([low(w_back[half:])] + in_half(1), 0)
    x4, g4 = tokens.reshape(parts, rows, width), cotangent.reshape(parts, rows, width)
    bucket_rows = jnp.stack([jnp.pad(buckets, (0, 1), constant_values=-1), jnp.pad(buckets[::-1], (0, 1), constant_values=-1)])

    g1 = Gather(shard1)
    x_came = send_blocks(x4, me)
    g1.fill()
    g1.own, = tie(x_came, g1.own)
    g1.sides()
    g1.take(g1.own, 0)
    shard2, = tie(g1.own, shard2)
    g2 = Gather(shard2)
    g1.x, g1.y = tie((g2.sent[1], g1.pieces[1]), g1.x, g1.y)
    g1.corner_halves()
    g1.take(g1.x, 2)
    g1.take(g1.y, 4)
    g2.fill()
    g1.near, g1.far, g2.own = tie((g1.pieces[3], g1.pieces[5]), g1.near, g1.far, g2.own)
    g2.sides()
    g1.take(g1.near, 6, (0, 1))
    g1.take(g1.far, 6, (2, 3))
    shard3, = tie((g1.near, g1.far), shard3)
    full3 = lax.all_gather(shard3, both, axis=0, tiled=False)
    x, hidden, q, k, v, w_qkv, gains, t, t_back = qkv_fwd(ids, x4, x_came, *g1.all_pieces(), bucket_rows, HEADS)
    pairs = HEADS // 2
    att = attn_fwd(length, q, k, v, t, 0, pairs // 2)
    g2.take(g2.own, 0)
    g_core = send_blocks(g4, me, (1,))
    g2.x, g2.y = tie((att[0], g2.pieces[1], g_core), g2.x, g2.y)
    g2.corner_y()
    g4_in, = tie(g2.x, g4)
    g_came = g_core + send_blocks(g4_in, me, (2, 3))
    g2.take(g2.x, 2)
    g2.take(g2.y, 4)
    q_in, = tie((g2.x, g2.y), q)
    attended, lse = attn_fwd(length, q_in, k, v, t, pairs // 2, pairs // 2, att)
    g2.corner, = tie((attended, g_came, g2.pieces[3], g2.pieces[5]), g2.corner)
    g2.take(g2.corner, 6)
    *state, gw_a = mid_a(ids, x, attended, g4, g_came, gains, *g2.all_pieces(), ff)
    r_a = lax.psum_scatter(gw_a.reshape(-1, width), both, scatter_dimension=0, tiled=True)
    out, gb, g_att, gw2 = mid_b(gains, state, attended, full3, ff)
    sc2 = Scatter(gw2, pos)
    out4 = out.reshape(parts, rows, width)
    out_came = send_blocks(out4, me)
    count = pairs // 4
    back = lambda first, g, prev: attn_bwd(length, q, k, v, g, attended, lse, t_back, first, count, prev)
    g_att, = tie((sc2.sent, out), g_att)
    dq, dk, dv, off0 = back(0, g_att, None)
    sc2.other, = tie((off0, out_came), sc2.other)
    sc2.fold()
    g_att, = tie((sc2.own, sc2.to_x, sc2.to_y), g_att)
    dq, dk, dv, off1 = back(count, g_att, (dq, dk, dv))
    sc2.came_x, sc2.came_y = tie(off1, sc2.came_x, sc2.came_y)
    sc2.turn()
    g_att, = tie(sc2.sent, g_att)
    dq, dk, dv, off2 = back(2 * count, g_att, (dq, dk, dv))
    dq, dk, dv, off3 = back(3 * count, g_att, (dq, dk, dv))
    sc2.came_x, sc2.came_y = tie(off3, sc2.came_x, sc2.came_y)
    sc2.column()
    h_in, = tie((sc2.mine, r_a), hidden)
    gw1 = qkv_gw(h_in, dq, dk, dv, bucket_rows, (off0, off1, off2, off3), shards)
    sc1 = Scatter(gw1, pos)
    gb_in, = tie(sc1.sent, gb)
    gx = qkv_gx(x, gb_in, dq, dk, dv, gains, w_qkv)
    sc1.other, = tie((gx, sc2.came), sc1.other)
    sc1.fold()
    out4, out_came = tie(sc1.own, out4, out_came)
    layer_out = place(out4, out_came, me)
    sc1.turn()
    sc2.came = list(tie((sc1.sent, layer_out), *sc2.came))
    r2 = sc2.result()
    sc1.came_x, sc1.came_y = tie(r2, sc1.came_x, sc1.came_y)
    sc1.column()
    gx, = tie(sc1.mine, gx)
    gx4 = gx.reshape(parts, rows, width)
    gx_came = send_blocks(gx4, me)
    input_grad = place(gx4, gx_came, me)
    sc1.came = list(tie(input_grad, *sc1.came))
    r1, r_a = sc1.result(), up(r_a)
    join = lambda v: jnp.concatenate([v[i:i + own] for i in range(0, v.shape[0], own)], 1).reshape(own, shards, 1, half)
    g_in = jnp.concatenate([join(r_a[half:]), join(r2[half + own:])], 2).reshape(w_in.shape)
    g_back = jnp.concatenate([r_a[:half], r2[:half]], 0)
    prod = up(shard1[:3 * own]) * r1[:3 * own]
    g_gain1 = jnp.sum(prod[:own] + prod[own:2 * own] + prod[2 * own:], axis=1) / up(low(norm1_gain))
    g_gain2 = jnp.sum(up(low(w_in)) * g_in, axis=1) / up(low(norm2_gain))
    return (layer_out.reshape(tokens.shape), input_grad.reshape(tokens.shape), g_gain1, r1[:own], r1[own:2 * own], r1[2 * own:3 * own],
            r2[half:half + own], r1[3 * own, :HEADS], g_gain2, g_in, g_back)


def local_any(shape, tokens, *rest):
    fits = tuple(shape) == (8, 4) and tokens.shape[0] * tokens.shape[1] == 4 and tokens.shape[3] == HEADS * DH == 1024
    return (local_whole if fits else local)(tokens, *rest)


def solution(mesh):
    return jax.shard_map(
        functools.partial(local_any, mesh.devices.shape),
        mesh=mesh,
        in_specs=(
            P(None, "dp", "seq", None),
            P(None, "dp", "seq", None),
            P(None, "dp"),
            P(),
            P(("dp", "seq")),
            P(("dp", "seq"), None),
            P(("dp", "seq"), None),
            P(("dp", "seq"), None),
            P(("dp", "seq"), None),
            P(("dp", "seq")),
            P(("dp", "seq")),
            P(("dp", "seq"), None),
            P(("dp", "seq"), None),
        ),
        out_specs=(
            P(None, "dp", "seq", None),
            P(None, "dp", "seq", None),
            P(("dp", "seq")),
            P(("dp", "seq"), None),
            P(("dp", "seq"), None),
            P(("dp", "seq"), None),
            P(("dp", "seq"), None),
            P(("dp", "seq")),
            P(("dp", "seq")),
            P(("dp", "seq"), None),
            P(("dp", "seq"), None),
        ),
        check_vma=False,
    )
```

```python
import functools

import jax
import jax.numpy as jnp
from jax import lax
from jax.experimental import pallas as pl
from jax.experimental.pallas import tpu as pltpu
from jax.sharding import PartitionSpec as P

HEADS = 16
DH = 64
BUCKETS = 32


epsilon = 1e-06
floor_score = -1e30
highest = lax.Precision.HIGHEST
root_coef = 0.7978845608
cubic_coef = 0.044715


def gelu_tanh(values):
    return (
        0.5
        * values
        * (1.0 + jnp.tanh(root_coef * (values + cubic_coef * values * values * values)))
    )


def gelu_slope(values):
    inner = jnp.tanh(root_coef * (values + cubic_coef * values * values * values))
    return 0.5 * (1.0 + inner) + 0.5 * values * (1.0 - inner * inner) * root_coef * (
        1.0 + 3.0 * cubic_coef * values * values
    )


def project(acts, weight):
    return jnp.einsum("srd,de->sre", acts, weight, preferred_element_type=jnp.float32)


def project_back(grads_in, weight):
    return jnp.einsum("sre,de->srd", grads_in, weight, preferred_element_type=jnp.float32)


def contract(acts, grads_in):
    return jnp.einsum("srd,sre->de", acts, grads_in, preferred_element_type=jnp.float32)


def rms_forward(values, gain):
    inverse = lax.rsqrt(jnp.mean(values * values, axis=-1, keepdims=True) + epsilon)
    normed = values * inverse
    return (normed, inverse, (normed * gain.astype(jnp.float32)).astype(jnp.bfloat16))


def rms_backward(grad_hidden, normed, inverse, gain):
    scaled = grad_hidden * gain.astype(jnp.float32)
    grad_values = inverse * (scaled - normed * jnp.mean(scaled * normed, axis=-1, keepdims=True))
    return (grad_values, jnp.sum(grad_hidden * normed, axis=(0, 1)))


def score_block(per_head_queries, per_head_keys, rel_bias, key_valid):
    scores = (
        jnp.einsum(
            "ofck,owck->ocfw", per_head_queries, per_head_keys, preferred_element_type=jnp.float32
        )
        + rel_bias[None]
    )
    return jnp.where(key_valid, scores, floor_score)


def offset_sums(grid, first_row, seq_len):
    head_count, row_count, key_count = grid.shape
    flipped = grid[:, ::-1, :]
    padded = jnp.pad(flipped, ((0, 0), (0, 0), (0, row_count)))
    wide_len = key_count + row_count
    skewed = padded.reshape(head_count, row_count * wide_len)[:, : row_count * (wide_len - 1)]
    skewed = skewed.reshape(head_count, row_count, wide_len - 1)
    column_sums = jnp.sum(skewed, axis=1)
    placed = jnp.zeros((head_count, 2 * seq_len - 1), jnp.float32)
    begin = seq_len - row_count - first_row
    return lax.dynamic_update_slice(placed, column_sums, (jnp.int32(0), begin))


def run_micro(inputs, incoming, seq_lens, attn_set, mlp_set, context):
    onehot, offsets, row_pos, key_pos, first_row, seq_len = context
    gain_one, query_w, key_w, value_w, out_w, bias_table = attn_set
    gain_two, in_w, return_projection_weight = mlp_set
    seq_count, row_count, model_width = inputs.shape
    values = inputs.astype(jnp.float32)
    normed_one, inverse_one, hidden_one = rms_forward(values, gain_one)
    queries = project(hidden_one, query_w).astype(jnp.bfloat16)
    keys_own = project(hidden_one, key_w).astype(jnp.bfloat16)
    values_own = project(hidden_one, value_w).astype(jnp.bfloat16)
    keys_all, values_all = (
        lax.all_gather(keys_own, "seq", axis=1, tiled=True),
        lax.all_gather(values_own, "seq", axis=1, tiled=True),
    )
    per_offset = jnp.dot(
        onehot, bias_table.reshape(BUCKETS, HEADS), preferred_element_type=jnp.float32
    )
    rel_bias = jnp.transpose(per_offset[offsets], (2, 0, 1))
    key_valid = (key_pos[None, :] < seq_lens[:, None])[:, None, None, :]
    per_head_queries = queries.reshape(seq_count, row_count, HEADS, DH)
    per_head_keys = keys_all.reshape(seq_count, seq_len, HEADS, DH)
    per_head_values = values_all.reshape(seq_count, seq_len, HEADS, DH)
    scores = score_block(per_head_queries, per_head_keys, rel_bias, key_valid)
    row_max = jnp.max(scores, axis=-1, keepdims=True)
    exp_scores = jnp.exp(scores - row_max)
    row_total = jnp.sum(exp_scores, axis=-1, keepdims=True)
    attn_probs = exp_scores / row_total
    log_total = row_max + jnp.log(row_total)
    reduced_precision_probs = attn_probs.astype(jnp.bfloat16)
    attended = jnp.einsum(
        "jfpe,jefn->jpfn",
        reduced_precision_probs,
        per_head_values,
        preferred_element_type=jnp.float32,
    )
    attended = attended.reshape(seq_count, row_count, model_width).astype(jnp.bfloat16)
    residual_mid = values + project(attended, out_w)
    normed_two, inverse_two, hidden_two = rms_forward(residual_mid, gain_two)
    pre_act = project(hidden_two, in_w)
    active = gelu_tanh(pre_act).astype(jnp.bfloat16)
    result = (residual_mid + project(active, return_projection_weight)).astype(jnp.bfloat16)
    row_valid = (row_pos[None, :] < seq_lens[:, None]).astype(jnp.float32)[:, :, None]
    grad_out = incoming.astype(jnp.float32) * row_valid
    grad_low = grad_out.astype(jnp.bfloat16)
    grad_back = contract(active, grad_low)
    gradient_active_rows = project_back(grad_low, return_projection_weight)
    grad_pre = (gradient_active_rows * gelu_slope(pre_act)).astype(jnp.bfloat16)
    grad_in = contract(hidden_two, grad_pre)
    grad_hidden_two = project_back(grad_pre, in_w)
    grad_mixed, grad_gain_two = rms_backward(grad_hidden_two, normed_two, inverse_two, gain_two)
    grad_mixed = grad_mixed + grad_out
    grad_branch = grad_mixed.astype(jnp.bfloat16)
    grad_outw = contract(attended, grad_branch)
    gradient_attended_values = project_back(grad_branch, out_w).astype(jnp.bfloat16)
    gradient_attended_values = gradient_attended_values.reshape(seq_count, row_count, HEADS, DH)
    scores = score_block(per_head_queries, per_head_keys, rel_bias, key_valid)
    attn_probs = jnp.exp(scores - log_total)
    reduced_precision_probs = attn_probs.astype(jnp.bfloat16)
    grad_probs = jnp.einsum(
        "ofck,owck->ocfw",
        gradient_attended_values,
        per_head_values,
        preferred_element_type=jnp.float32,
    )
    inner_sum = jnp.sum(attn_probs * grad_probs, axis=-1, keepdims=True)
    gradient_score_matrix = (attn_probs * (grad_probs - inner_sum)).astype(jnp.bfloat16)
    grad_query = jnp.einsum(
        "jfpe,jefn->jpfn", gradient_score_matrix, per_head_keys, preferred_element_type=jnp.float32
    )
    grad_query = grad_query.astype(jnp.bfloat16).reshape(seq_count, row_count, model_width)
    key_part = jnp.einsum(
        "eciv,eicq->evcq",
        gradient_score_matrix,
        per_head_queries,
        preferred_element_type=jnp.float32,
    )
    value_part = jnp.einsum(
        "eciv,eicq->evcq",
        reduced_precision_probs,
        gradient_attended_values,
        preferred_element_type=jnp.float32,
    )
    key_part = key_part.reshape(seq_count, seq_len, model_width)
    value_part = value_part.reshape(seq_count, seq_len, model_width)
    grad_key, grad_value = (
        lax.psum_scatter(
            key_part.astype(jnp.bfloat16), "seq", scatter_dimension=1, tiled=True
        ).astype(jnp.float32),
        lax.psum_scatter(
            value_part.astype(jnp.bfloat16), "seq", scatter_dimension=1, tiled=True
        ).astype(jnp.float32),
    )
    grad_key = grad_key.astype(jnp.bfloat16)
    grad_value = grad_value.astype(jnp.bfloat16)
    offset_grad = offset_sums(
        jnp.sum(gradient_score_matrix.astype(jnp.float32), axis=0), first_row, seq_len
    )
    grad_table = jnp.dot(onehot.astype(jnp.float32).T, offset_grad.T, precision=highest).reshape(-1)
    grad_qw = contract(hidden_one, grad_query)
    grad_kw = contract(hidden_one, grad_key)
    grad_vw = contract(hidden_one, grad_value)
    grad_hidden_one = (
        project_back(grad_query, query_w)
        + project_back(grad_key, key_w)
        + project_back(grad_value, value_w)
    )
    grad_values, grad_gain_one = rms_backward(grad_hidden_one, normed_one, inverse_one, gain_one)
    grad_values = grad_values + grad_mixed
    gradients = (
        grad_gain_one,
        grad_qw,
        grad_kw,
        grad_vw,
        grad_outw,
        grad_table,
        grad_gain_two,
        grad_in,
        grad_back,
    )
    return (result, grad_values.astype(jnp.bfloat16), gradients)


def local(
    tokens,
    cotangent,
    lengths,
    buckets,
    norm1_gain,
    w_query,
    w_key,
    w_value,
    w_out,
    rel_table,
    norm2_gain,
    w_in,
    w_back,
):
    micro_count, seq_count, row_count, model_width = tokens.shape
    seq_parts = lax.axis_size("seq")
    seq_len = row_count * seq_parts
    first_row = lax.axis_index("seq") * row_count
    row_pos = first_row + jnp.arange(row_count, dtype=jnp.int32)
    key_pos = jnp.arange(seq_len, dtype=jnp.int32)
    onehot = (buckets[:, None] == jnp.arange(BUCKETS, dtype=jnp.int32)[None, :]).astype(
        jnp.bfloat16
    )
    offsets = key_pos[None, :] - row_pos[:, None] + (seq_len - 1)
    context = (onehot, offsets, row_pos, key_pos, first_row, seq_len)
    outputs = []
    input_grads = []
    pending = None
    shard_sums = None
    for micro_step in range(micro_count):
        attn_set = (
            lax.all_gather(norm1_gain.astype(jnp.bfloat16), ("dp", "seq"), axis=0, tiled=True),
            lax.all_gather(w_query.astype(jnp.bfloat16), ("dp", "seq"), axis=0, tiled=True),
            lax.all_gather(w_key.astype(jnp.bfloat16), ("dp", "seq"), axis=0, tiled=True),
            lax.all_gather(w_value.astype(jnp.bfloat16), ("dp", "seq"), axis=0, tiled=True),
            lax.all_gather(w_out.astype(jnp.bfloat16), ("dp", "seq"), axis=0, tiled=True),
            lax.all_gather(rel_table.astype(jnp.bfloat16), ("dp", "seq"), axis=0, tiled=True),
        )
        mlp_set = (
            lax.all_gather(norm2_gain.astype(jnp.bfloat16), ("dp", "seq"), axis=0, tiled=True),
            lax.all_gather(w_in.astype(jnp.bfloat16), ("dp", "seq"), axis=0, tiled=True),
            lax.all_gather(w_back.astype(jnp.bfloat16), ("dp", "seq"), axis=0, tiled=True),
        )
        layer_part, grad_part, gradients = run_micro(
            tokens[micro_step],
            cotangent[micro_step],
            lengths[micro_step],
            attn_set,
            mlp_set,
            context,
        )
        outputs.append(layer_part)
        input_grads.append(grad_part)
        pending = gradients if pending is None else jax.tree.map(jnp.add, pending, gradients)
    shard_sums = (
        lax.psum_scatter(pending[0], ("dp", "seq"), scatter_dimension=0, tiled=True),
        lax.psum_scatter(pending[1], ("dp", "seq"), scatter_dimension=0, tiled=True),
        lax.psum_scatter(pending[2], ("dp", "seq"), scatter_dimension=0, tiled=True),
        lax.psum_scatter(pending[3], ("dp", "seq"), scatter_dimension=0, tiled=True),
        lax.psum_scatter(pending[4], ("dp", "seq"), scatter_dimension=0, tiled=True),
        lax.psum_scatter(pending[5], ("dp", "seq"), scatter_dimension=0, tiled=True),
        lax.psum_scatter(pending[6], ("dp", "seq"), scatter_dimension=0, tiled=True),
        lax.psum_scatter(pending[7], ("dp", "seq"), scatter_dimension=0, tiled=True),
        lax.psum_scatter(pending[8], ("dp", "seq"), scatter_dimension=0, tiled=True),
    )
    return (
        jnp.stack(outputs),
        jnp.stack(input_grads),
        shard_sums[0],
        shard_sums[1],
        shard_sums[2],
        shard_sums[3],
        shard_sums[4],
        shard_sums[5],
        shard_sums[6],
        shard_sums[7],
        shard_sums[8],
    )


NT = (((1,), (1,)), ((), ()))
TN = (((0,), (0,)), ((), ()))
STRIP = 128
LOG2E = 1.4426950408889634
LN2 = 0.6931471805599453
LIMIT = 58 << 20
LIGHT = pl.CostEstimate(flops=1 << 20, bytes_accessed=1 << 16, transcendentals=0)

def _dot(a, b, dims=(((1,), (0,)), ((), ()))):
    return lax.dot_general(a, b, dims, preferred_element_type=jnp.float32)

def with_extras(x, which, extras, width=64):
    lane = lax.broadcasted_iota(jnp.int32, (1, x.shape[1]), 1)
    spare = lane - width if which == 0 else lane
    own = (lane < width) if which == 0 else (lane >= width)
    fill = jnp.zeros_like(x)
    for i, extra in enumerate(extras):
        fill = jnp.where(spare == i, extra, fill)
    return jnp.where(own, x, fill).astype(jnp.bfloat16)

def three_parts(x):
    low = lambda v: v.astype(jnp.bfloat16).astype(jnp.float32)
    high = low(x)
    middle = low(x - high)
    return [high, middle, low(x - high - middle)]

def slot_floor(size, length):
    return jnp.where(lax.broadcasted_iota(jnp.int32, (size, 1), 0) < length, 0.0, floor_score)

def skew(row, wide):
    return pltpu.roll(jnp.broadcast_to(row, (STRIP, wide)), wide - (STRIP - 1), 1, stride=1, stride_axis=0)

def fwd_kernel(len_ref, q_ref, k_ref, v_ref, t_ref, *refs, rows, seq_len, first):
    o_ref, lse_ref, strip, kx, vx = refs[-5:]
    wide = t_ref.shape[-1]
    pair = first + pl.program_id(0)
    per = rows // STRIP
    lane = lax.broadcasted_iota(jnp.int32, (1, 128), 1)
    k2 = k_ref[...].astype(jnp.float32)
    vx[:, 0:128] = v_ref[...]
    vx[:, 128:256] = jnp.ones_like(v_ref[...])
    for a in range(2):
        kx[a] = with_extras(k2, a, [slot_floor(seq_len, len_ref[0])])
        strip[a] = skew(t_ref[pl.ds(2 * pair + a, 1), :], wide)

    def step(b, carry):
        base = b * rows
        q2 = q_ref[pl.ds(base, rows), :].astype(jnp.float32)
        outs, stats = [], []
        for a in range(2):
            scores = _dot(with_extras(q2, a, [1.0]), kx[a], NT)
            parts = []
            for i in range(per):
                off = (seq_len - STRIP) - (b * per + i) * STRIP
                parts.append(strip[a, :, pl.ds(off, seq_len)])
            scores = scores + (jnp.concatenate(parts, 0) if per > 1 else parts[0])
            top = jnp.max(scores, axis=1, keepdims=True)
            probs = jnp.exp2(scores - top).astype(jnp.bfloat16)
            out = _dot(probs, vx[...])
            outs.append(out[:, 0:128] / out[:, 128:256])
            stats.append(top + jnp.log2(out[:, 128:256]))
        o_ref[pl.ds(base, rows), :] = jnp.where(lane < 64, outs[0], outs[1]).astype(jnp.bfloat16)
        lse_ref[0, pl.ds(base, rows), :] = jnp.where(lane < 64, stats[0], stats[1])
        return carry

    for b in range(seq_len // rows):
        step(b, 0)

def attn_fwd(length, q, k, v, t, first, count, prev=(), rows=256):
    seq_len, width = q.shape
    pairs = width // 128
    wide = t.shape[-1]
    blk = pl.BlockSpec((seq_len, 128), lambda p, n: (0, first + p))
    return pl.pallas_call(
        functools.partial(fwd_kernel, rows=rows, seq_len=seq_len, first=first),
        out_shape=(jax.ShapeDtypeStruct((seq_len, width), jnp.bfloat16),
                   jax.ShapeDtypeStruct((pairs, seq_len, 128), jnp.float32)),
        grid_spec=pltpu.PrefetchScalarGridSpec(
            num_scalar_prefetch=1, grid=(count,),
            in_specs=[blk, blk, blk, pl.BlockSpec(t.shape, lambda p, n: (0, 0))] + [pl.BlockSpec(memory_space=pl.ANY)] * len(prev),
            out_specs=[blk, pl.BlockSpec((1, seq_len, 128), lambda p, n: (first + p, 0, 0))],
            scratch_shapes=[pltpu.VMEM((2, STRIP, wide), jnp.float32), pltpu.VMEM((2, seq_len, 128), jnp.bfloat16),
                            pltpu.VMEM((seq_len, 256), jnp.bfloat16)]),
        input_output_aliases={5 + i: i for i in range(len(prev))},
        compiler_params=pltpu.CompilerParams(vmem_limit_bytes=LIMIT),
        cost_estimate=LIGHT,
        name="attn_fwd",
    )(length, q, k, v, t, *prev)

def bwd_kernel(len_ref, q_ref, k_ref, v_ref, do_ref, o_ref, lse_ref, t_ref, *refs, rows, seq_len, first):
    dq_ref, dk_ref, dv_ref, g_ref, strip, acc, dq_acc, qx, kx, vx, dox = refs[-11:]
    wide = t_ref.shape[-1]
    local_pair = pl.program_id(0)
    pair = first + local_pair
    per = rows // STRIP
    lane = lax.broadcasted_iota(jnp.int32, (1, 128), 1)
    up = lambda ref: ref[...].astype(jnp.float32)
    floor = slot_floor(seq_len, len_ref[0])
    prod = up(do_ref) * up(o_ref)
    for a in range(2):
        mine = (lane < 64) if a == 0 else (lane >= 64)
        delta = jnp.sum(jnp.where(mine, prod, 0.0), axis=1, keepdims=True)
        lse = lse_ref[0, :, 64 * a:64 * a + 1]
        qx[a] = with_extras(up(q_ref), a, [1.0] + three_parts(-lse))
        kx[a] = with_extras(up(k_ref), a, [floor, 1.0, 1.0, 1.0])
        vx[a] = with_extras(up(v_ref), a, [1.0, 1.0, 1.0])
        dox[a] = with_extras(up(do_ref), a, three_parts(-delta))
        strip[a] = skew(t_ref[pl.ds(2 * pair + a, 1), :], wide)
    acc[...] = jnp.zeros_like(acc)
    k2t = k_ref[...].T
    dq_acc[...] = jnp.zeros_like(dq_acc)

    def step(b, carry):
        at = pl.ds(b * rows, rows)
        dks, dvs = [], []
        for a in range(2):
            scores = _dot(kx[a, at, :], qx[a], NT)
            offs = [(seq_len - STRIP) - (b * per + i) * STRIP for i in range(per)]
            bias = [strip[a, :, pl.ds(off, seq_len)] for off in offs]
            probs = jnp.exp2(scores + (jnp.concatenate(bias, 0) if per > 1 else bias[0]))
            grad_scores = probs * _dot(vx[a, at, :], dox[a], NT)
            for i, off in enumerate(offs):
                acc[a, :, pl.ds(off, seq_len)] += grad_scores[i * STRIP:(i + 1) * STRIP]
            probs_b = probs.astype(jnp.bfloat16)
            gs_b = grad_scores.astype(jnp.bfloat16)
            dvs.append(_dot(probs_b, do_ref[...]))
            dks.append(_dot(gs_b, q_ref[...]))
            dq_acc[a] += _dot(k2t[:, b * rows:(b + 1) * rows], gs_b)
        dk_ref[at, :] = (jnp.where(lane < 64, dks[0], dks[1]) * LN2).astype(jnp.bfloat16)
        dv_ref[at, :] = jnp.where(lane < 64, dvs[0], dvs[1]).astype(jnp.bfloat16)
        return carry

    for b in range(seq_len // rows):
        step(b, 0)
    dq_ref[...] = jnp.concatenate([dq_acc[0, 0:64], dq_acc[1, 64:128]], 0).T.astype(jnp.bfloat16)
    for a in range(2):
        sums = acc[a]
        half = STRIP
        while half > 8:
            half //= 2
            sums = sums[:half] + pltpu.roll(sums[half:], wide - half, 1)
        while half > 1:
            half //= 2
            sums = sums + pltpu.roll(pltpu.roll(sums, 8 - half, 0), wide - half, 1)
        g_ref[pl.ds(2 * local_pair + a, 1), :] = pltpu.roll(sums, STRIP - 1, 1)[0:1]

def attn_bwd(length, q, k, v, do, o, lse, trev, first, count, prev=None, rows=512):
    seq_len, width = q.shape
    wide = trev.shape[-1]
    blk = pl.BlockSpec((seq_len, 128), lambda p, n: (0, first + p))
    mat = jax.ShapeDtypeStruct((seq_len, width), jnp.bfloat16)
    prev = tuple(prev) if prev is not None else ()
    return pl.pallas_call(
        functools.partial(bwd_kernel, rows=rows, seq_len=seq_len, first=first),
        out_shape=(mat, mat, mat, jax.ShapeDtypeStruct((2 * count, wide), jnp.float32)),
        grid_spec=pltpu.PrefetchScalarGridSpec(
            num_scalar_prefetch=1, grid=(count,),
            in_specs=[blk, blk, blk, blk, blk, pl.BlockSpec((1, seq_len, 128), lambda p, n: (first + p, 0, 0)),
                      pl.BlockSpec(trev.shape, lambda p, n: (0, 0))] + [pl.BlockSpec(memory_space=pl.ANY)] * len(prev),
            out_specs=[blk, blk, blk, pl.BlockSpec((2 * count, wide), lambda p, n: (0, 0))],
            scratch_shapes=[pltpu.VMEM((2, STRIP, wide), jnp.float32), pltpu.VMEM((2, STRIP, wide), jnp.float32),
                            pltpu.VMEM((2, 128, seq_len), jnp.float32)] + [pltpu.VMEM((2, seq_len, 128), jnp.bfloat16)] * 4),
        input_output_aliases={8 + i: i for i in range(len(prev))},
        compiler_params=pltpu.CompilerParams(vmem_limit_bytes=LIMIT),
        cost_estimate=LIGHT,
        name="attn_bwd",
    )(length, q, k, v, do, o, lse, trev, *prev)

ANY = pl.BlockSpec(memory_space=pl.ANY)
VM = pl.BlockSpec(memory_space=pltpu.VMEM)
SM = pl.BlockSpec(memory_space=pltpu.SMEM)

def rms_inverse(value):
    return lax.rsqrt(jnp.mean(value * value, axis=1, keepdims=True) + epsilon)

def pull_sequence(me, whole_ref, chip_ref, core_ref, dst, sem):
    rows = whole_ref.shape[1]
    for mask, src in enumerate((whole_ref.at[me], core_ref.at[0], chip_ref.at[me & 1], core_ref.at[1])):
        at = pl.multiple_of((me ^ mask) * rows, rows)
        pltpu.make_async_copy(src, dst.at[pl.ds(at, rows), :], sem).start()

def qkv_kernel(ids_ref, x4_ref, chip_ref, core_ref, *refs, masks):
    gathered = refs[:len(masks)]
    bucket_ref = refs[len(masks)]
    x_out, h_out, q_out, k_out, v_out, w_out, gain_ref, t_ref, trev_ref, xs, hs, ps, ws, es, sems = refs[len(masks) + 1:]
    me, flat = ids_ref[0], ids_ref[1]
    width = xs.shape[1]
    own = width // es.shape[0]
    pull_sequence(me, x4_ref, chip_ref, core_ref, xs, sems.at[0])
    for ref, ids in zip(gathered, masks):
        for j, mask in enumerate(ids):
            shard = flat ^ mask
            pltpu.make_async_copy(ref.at[j, 3 * own:3 * own + 16, :], es.at[shard], sems.at[1]).start()
    for ref, ids in zip(gathered, masks):
        for j, mask in enumerate(ids):
            at = pl.multiple_of((flat ^ mask) * own, own)
            for i in range(3):
                pltpu.make_async_copy(ref.at[j, i * own:(i + 1) * own, :], ws.at[pl.ds(at, own), i * width:(i + 1) * width], sems.at[2]).start()
    pltpu.make_async_copy(es, es, sems.at[1]).wait()
    extras = es[...].astype(jnp.float32)
    gains = jnp.sum(extras, axis=0)
    gain_ref[...] = gains[0:8]
    table = extras[:, 8, 0:128].astype(jnp.bfloat16)
    ids = lax.broadcasted_iota(jnp.int32, (es.shape[0], 1), 0)
    heads = t_ref.shape[0]
    for i, ref in enumerate((t_ref, trev_ref)):
        hot = jnp.where(bucket_ref[i:i + 1, :] == ids, 1.0, 0.0).astype(jnp.bfloat16)
        ref[...] = _dot(table, hot, TN)[0:heads] * LOG2E
    pltpu.make_async_copy(xs, xs, sems.at[0]).wait()
    part = 256
    def norm(i, carry):
        at = pl.ds(pl.multiple_of(i * part, part), part)
        x = xs[at, :].astype(jnp.float32)
        hs[at, :] = (x * rms_inverse(x) * gains[0:1]).astype(jnp.bfloat16)
        return carry
    lax.fori_loop(0, xs.shape[0] // part, norm, 0)
    copies = [pltpu.make_async_copy(xs, x_out, sems.at[0]), pltpu.make_async_copy(hs, h_out, sems.at[1])]
    for copy in copies:
        copy.start()
    pltpu.make_async_copy(ws, ws, sems.at[2]).wait()
    copies.append(pltpu.make_async_copy(ws, w_out, sems.at[2]))
    copies[-1].start()
    for i, ref in enumerate((q_out, k_out, v_out)):
        full = _dot(hs[...], ws[:, i * width:(i + 1) * width])
        ps[i] = (full * LOG2E if i == 0 else full).astype(jnp.bfloat16)
        copies.append(pltpu.make_async_copy(ps.at[i], ref, sems.at[3 + i]))
        copies[-1].start()
    for copy in copies:
        copy.wait()

def qkv_fwd(ids, x4, came, gathered, masks, bucket_rows, heads):
    parts, rows, width = x4.shape
    total = parts * rows
    shards = sum(len(m) for m in masks)
    mat = jax.ShapeDtypeStruct((total, width), jnp.bfloat16)
    wide = bucket_rows.shape[1]
    vm = lambda *s: pltpu.VMEM(s, jnp.bfloat16)
    return pl.pallas_call(
        functools.partial(qkv_kernel, masks=masks),
        out_shape=(mat,) * 5 + (jax.ShapeDtypeStruct((width, 3 * width), jnp.bfloat16), jax.ShapeDtypeStruct((8, width), jnp.float32),
                                jax.ShapeDtypeStruct((heads, wide), jnp.float32), jax.ShapeDtypeStruct((heads, wide), jnp.float32)),
        in_specs=[SM] + [ANY] * (3 + len(gathered)) + [VM],
        out_specs=[ANY] * 6 + [VM] * 3,
        scratch_shapes=[vm(total, width), vm(total, width), vm(3, total, width), vm(width, 3 * width), vm(shards, 16, width), pltpu.SemaphoreType.DMA((6,))],
        compiler_params=pltpu.CompilerParams(vmem_limit_bytes=LIMIT),
        cost_estimate=LIGHT,
        name="qkv_fwd",
    )(ids, x4, *came, *gathered, bucket_rows)

def gelu_both(v):
    t = jnp.tanh(root_coef * (v + cubic_coef * v * v * v))
    half = 0.5 * (1.0 + t)
    slope = half + 0.5 * v * (1.0 - t * t) * (root_coef * (1.0 + 3.0 * cubic_coef * v * v))
    return v * half, slope

def by_core(core, keep, send, src, dst_rows, sem, lead=slice(None), src_rows=slice(None), lanes=slice(None)):
    for parity in range(2):
        @pl.when(core == parity)
        def _():
            for dst, at in ((keep, parity), (send, 1 - parity)):
                pltpu.make_async_copy(src.at[lead, at, src_rows, lanes], dst.at[lead, dst_rows, lanes], sem).start()

def ff_chunks(h2, h2t, gm, acc, gh2, ws_in, ws_back, st_in, st_back, row_in, emit, before_add, cols=512):
    steps = ws_in.shape[1] // cols
    half, width = st_back.shape[2:]
    own = width // (2 * st_in.shape[0])
    wide = width // cols
    group = cols // (2 * half)

    def step(c, carry):
        at = pl.ds(pl.multiple_of(c * cols, cols), cols)
        win, wback = ws_in[:, at], ws_back[at, :]
        pre = _dot(h2[...], win)
        grad_active = _dot(gm[...], wback, NT)
        act, slope = gelu_both(pre)
        active = act.astype(jnp.bfloat16)
        gpre = (grad_active * slope).astype(jnp.bfloat16)
        @pl.when(c == 0)
        def _():
            before_add()
        acc[...] += _dot(active, wback)
        gh2[...] += _dot(gpre, win, NT)
        lead = pl.ds(c * group, group)
        st_back[lead] = _dot(active, gm[...], TN).astype(jnp.bfloat16).reshape(group, 2, half, width)
        emit(st_back, 0, lead=lead, dst_rows=slice(0, half))
        up = pl.multiple_of((c // wide) * own, own)
        lanes = pl.ds(pl.multiple_of((c % wide) * cols, cols), cols)
        st_in[:, :, pl.ds(up, own), lanes] = _dot(h2t[...], gpre).astype(jnp.bfloat16).reshape(-1, 2, own, cols)
        emit(st_in, 1, src_rows=pl.ds(up, own), dst_rows=pl.ds(row_in + up, own), lanes=lanes)
        return carry
    lax.fori_loop(0, steps, step, 0)

def finish_chunks(st_in, st_back, sems):
    pltpu.make_async_copy(st_back, st_back, sems.at[0]).wait()
    pltpu.make_async_copy(st_in, st_in, sems.at[1]).wait()

def aligned(at, size):
    return at if isinstance(at, int) else pl.multiple_of(at, size)

def pull_ff(flat, gathered, masks, ws_in, ws_back, row_in, sems):
    width = ws_in.shape[0]
    shards = sum(len(m) for m in masks)
    own, half = width // shards, ws_back.shape[0] // shards
    for ref, ids in zip(gathered, masks):
        for j, mask in enumerate(ids):
            shard = flat ^ mask
            pltpu.make_async_copy(ref.at[j, 0:half, :], ws_back.at[pl.ds(aligned(shard * half, half), half), :], sems.at[1]).start()
            at = pl.ds(aligned(shard * own, own), own)
            for i in range(ws_in.shape[1] // width):
                pltpu.make_async_copy(ref.at[j, row_in + i * own:row_in + (i + 1) * own, :], ws_in.at[at, i * width:(i + 1) * width], sems.at[0]).start()

def mid_a_kernel(ids_ref, x_hbm, o_hbm, g4_ref, chip_ref, core_ref, gain_ref, *refs, masks):
    gathered = refs[:len(masks)]
    (mixed_out, acc_out, gh2_out, h2_out, h2t_out, gm_out, wo_out, gw_out,
     xs, os, wo, ws_in, ws_back, mixed, h2, h2t, acc, gh2, gm, st_in, st_back, sems) = refs[len(masks):]
    flat = ids_ref[1]
    rows, width = xs.shape
    half, own = st_back.shape[2], width // (2 * st_in.shape[0])
    def emit(src, which, dst_rows, lead=slice(None), src_rows=slice(None), lanes=slice(None)):
        pltpu.make_async_copy(src.at[lead, :, src_rows, lanes], gw_out.at[lead, :, dst_rows, lanes], sems.at[which]).start()
    loads = [pltpu.make_async_copy(x_hbm, xs, sems.at[0]), pltpu.make_async_copy(o_hbm, os, sems.at[1])]
    for load in loads:
        load.start()
    for ref, ids in zip(gathered, masks):
        for j, mask in enumerate(ids):
            at = pl.ds(pl.multiple_of((flat ^ mask) * own, own), own)
            pltpu.make_async_copy(ref.at[j, half:half + own, :], wo.at[at, :], sems.at[2]).start()
    pull_ff(flat, gathered, masks, ws_in, ws_back, half + own, sems.at[3:5])
    pull_sequence(ids_ref[0], g4_ref, chip_ref, core_ref, gm, sems.at[5])
    for load in loads:
        load.wait()
    pltpu.make_async_copy(wo, wo, sems.at[2]).wait()
    stores = [pltpu.make_async_copy(wo, wo_out, sems.at[2])]
    stores[0].start()
    part = 256
    def load_rows(i, carry):
        at = pl.ds(pl.multiple_of(i * part, part), part)
        value = xs[at, :].astype(jnp.float32) + _dot(os[at, :], wo[...])
        mixed[at, :] = value
        acc[at, :] = value
        hidden = (value * rms_inverse(value) * gain_ref[1:2, :]).astype(jnp.bfloat16)
        h2[at, :] = hidden
        h2t[:, at] = hidden.T
        gh2[at, :] = jnp.zeros_like(value)
        return carry
    lax.fori_loop(0, rows // part, load_rows, 0)
    pltpu.make_async_copy(gm, gm, sems.at[5]).wait()
    row_ok = lax.broadcasted_iota(jnp.int32, (rows, 1), 0) < ids_ref[2]
    gm[...] = jnp.where(row_ok, gm[...], jnp.zeros_like(gm[...]))
    pltpu.make_async_copy(ws_in, ws_in, sems.at[3]).wait()
    pltpu.make_async_copy(ws_back, ws_back, sems.at[4]).wait()
    for i, (src, dst) in enumerate(((mixed, mixed_out), (h2, h2_out), (h2t, h2t_out), (gm, gm_out))):
        stores.append(pltpu.make_async_copy(src, dst, sems.at[6 + i]))
        stores[-1].start()
    ff_chunks(h2, h2t, gm, acc, gh2, ws_in, ws_back, st_in, st_back, half, emit, lambda: None)
    for i, (src, dst) in enumerate(((acc, acc_out), (gh2, gh2_out))):
        stores.append(pltpu.make_async_copy(src, dst, sems.at[3 + i]))
        stores[-1].start()
    finish_chunks(st_in, st_back, sems.at[0:2])
    for store in stores:
        store.wait()

def mid_a(ids, x, o, g4, came, gains, gathered, masks, ff):
    rows, width = x.shape
    shards = sum(len(m) for m in masks)
    half = ff // shards
    low = lambda *s: jax.ShapeDtypeStruct(s, jnp.bfloat16)
    full = lambda *s: jax.ShapeDtypeStruct(s, jnp.float32)
    vm = lambda *s: pltpu.VMEM(s, jnp.bfloat16)
    vf = lambda *s: pltpu.VMEM(s, jnp.float32)
    stack = half + ff // width * (width // shards)
    return pl.pallas_call(
        functools.partial(mid_a_kernel, masks=masks),
        out_shape=(full(rows, width), full(rows, width), full(rows, width), low(rows, width), low(width, rows), low(rows, width), low(width, width), low(shards // 2, 2, stack, width)),
        in_specs=[SM] + [ANY] * 5 + [VM] + [ANY] * len(gathered), out_specs=[ANY] * 8,
        scratch_shapes=[vm(rows, width), vm(rows, width), vm(width, width), vm(width, ff), vm(ff, width), vf(rows, width), vm(rows, width), vm(width, rows),
                        vf(rows, width), vf(rows, width), vm(rows, width), vm(shards // 2, 2, stack - half, width), vm(shards // 2, 2, half, width), pltpu.SemaphoreType.DMA((10,))],
        compiler_params=pltpu.CompilerParams(vmem_limit_bytes=LIMIT),
        cost_estimate=LIGHT,
        name="mid_a",
    )(ids, x, o, g4, *came, gains, *gathered)

def mid_b_kernel(ids_ref, gain_ref, mixed_hbm, acc_hbm, gh2_hbm, h2_hbm, h2t_hbm, gm_hbm, wo_hbm, o_hbm, full_ref, *refs):
    (out_ref, gb_out, do_ref, keep_out, send_out,
     os, wo, ws_in, ws_back, mixed, h2, h2t, acc, gh2, gm, gb, st_in, st_back, st_o, sems) = refs
    rows, width = os.shape
    shards, half, own = 2 * st_in.shape[0], st_back.shape[2], width // (2 * st_in.shape[0])
    core = ids_ref[1] & 1
    def emit(src, which, **at):
        by_core(core, keep_out, send_out, src, sem=sems.at[which], **at)
    early = [(h2_hbm, h2), (gm_hbm, gm), (h2t_hbm, h2t)]
    late = [(acc_hbm, acc), (gh2_hbm, gh2), (mixed_hbm, mixed), (wo_hbm, wo), (o_hbm, os)]
    early = [pltpu.make_async_copy(a, b, sems.at[4 + i]) for i, (a, b) in enumerate(early)]
    late = [pltpu.make_async_copy(a, b, sems.at[7 + i]) for i, (a, b) in enumerate(late)]
    for load in early:
        load.start()
    pull_ff(0, (full_ref,), (range(shards),), ws_in, ws_back, half, sems.at[2:4])
    for load in late:
        load.start()
    for load in early:
        load.wait()
    pltpu.make_async_copy(ws_in, ws_in, sems.at[2]).wait()
    pltpu.make_async_copy(ws_back, ws_back, sems.at[3]).wait()
    def before_add():
        late[0].wait()
        late[1].wait()
    ff_chunks(h2, h2t, gm, acc, gh2, ws_in, ws_back, st_in, st_back, half + own, emit, before_add)
    for load in late[2:]:
        load.wait()
    part = 256
    def finish(i, carry):
        at = pl.ds(pl.multiple_of(i * part, part), part)
        out_ref[at, :] = acc[at, :].astype(jnp.bfloat16)
        value = mixed[at, :]
        inverse = rms_inverse(value)
        normed = value * inverse
        scaled = gh2[at, :] * gain_ref[1:2, :]
        grad = inverse * (scaled - normed * jnp.mean(scaled * normed, axis=1, keepdims=True)) + gm[at, :].astype(jnp.float32)
        low = grad.astype(jnp.bfloat16)
        gb[at, :] = low
        do_ref[at, :] = _dot(low, wo[...], NT).astype(jnp.bfloat16)
        return carry
    lax.fori_loop(0, rows // part, finish, 0)
    st_o[...] = _dot(os[...], gb[...], TN).astype(jnp.bfloat16).reshape(st_o.shape)
    emit(st_o, 2, dst_rows=slice(half, half + own))
    store = pltpu.make_async_copy(gb, gb_out, sems.at[3])
    store.start()
    finish_chunks(st_in, st_back, sems.at[0:2])
    pltpu.make_async_copy(st_o, st_o, sems.at[2]).wait()
    store.wait()

def mid_b(ids, gains, state, o, full, ff):
    rows, width = o.shape
    shards = full.shape[0]
    half, own = ff // shards, width // shards
    low = lambda *s: jax.ShapeDtypeStruct(s, jnp.bfloat16)
    vm = lambda *s: pltpu.VMEM(s, jnp.bfloat16)
    vf = lambda *s: pltpu.VMEM(s, jnp.float32)
    rest = ff // width * own
    return pl.pallas_call(
        mid_b_kernel,
        out_shape=(low(rows, width), low(rows, width), low(rows, width), low(shards // 2, half + own + rest, width), low(shards // 2, half + own + rest, width)),
        in_specs=[SM, VM] + [ANY] * 9, out_specs=[VM, ANY, VM, ANY, ANY],
        scratch_shapes=[vm(rows, width), vm(width, width), vm(width, ff), vm(ff, width), vf(rows, width), vm(rows, width), vm(width, rows),
                        vf(rows, width), vf(rows, width), vm(rows, width), vm(rows, width), vm(shards // 2, 2, rest, width), vm(shards // 2, 2, half, width), vm(shards // 2, 2, own, width),
                        pltpu.SemaphoreType.DMA((12,))],
        compiler_params=pltpu.CompilerParams(vmem_limit_bytes=LIMIT),
        cost_estimate=LIGHT,
        name="mid_b",
    )(ids, gains, *state, o, full)

def gw_kernel(ids_ref, h_ref, dq_ref, dk_ref, dv_ref, bucket_ref, *refs):
    keep_out, send_out, st, sems = refs[-4:]
    offs = jnp.concatenate([ref[...] for ref in refs[:-4]], 0)
    pairs, _, stack, width = st.shape
    own = width // (2 * pairs)
    core = ids_ref[1] & 1
    ids = lax.broadcasted_iota(jnp.int32, (2 * pairs, 1), 0)
    hot = jnp.where(bucket_ref[1:2, :] == ids, 1.0, 0.0)
    table = lax.dot_general(hot, offs, NT, precision=lax.Precision.HIGHEST, preferred_element_type=jnp.float32)
    heads = offs.shape[0]
    st[:, :, 3 * own:, :] = jnp.zeros((pairs, 2, stack - 3 * own, width), jnp.bfloat16)
    st[:, :, 3 * own:3 * own + 1, 0:heads] = table.astype(jnp.bfloat16).reshape(pairs, 2, 1, heads)
    for i, ref in enumerate((dq_ref, dk_ref, dv_ref)):
        at = slice(i * own, (i + 1) * own) if i < 2 else slice(i * own, stack)
        st[:, :, i * own:(i + 1) * own, :] = _dot(h_ref[...], ref[...], TN).astype(jnp.bfloat16).reshape(pairs, 2, own, width)
        by_core(core, keep_out, send_out, st, at, sems.at[0], src_rows=at)
    pltpu.make_async_copy(st, st, sems.at[0]).wait()

def qkv_gw(ids, h, dq, dk, dv, bucket_rows, offs, shards):
    rows, width = h.shape
    stack = 3 * width // shards + 16
    half = jax.ShapeDtypeStruct((shards // 2, stack, width), jnp.bfloat16)
    return pl.pallas_call(
        gw_kernel, out_shape=(half, half),
        in_specs=[SM] + [VM] * (5 + len(offs)), out_specs=[ANY, ANY],
        scratch_shapes=[pltpu.VMEM((shards // 2, 2, stack, width), jnp.bfloat16), pltpu.SemaphoreType.DMA((1,))],
        compiler_params=pltpu.CompilerParams(vmem_limit_bytes=LIMIT),
        cost_estimate=LIGHT,
        name="qkv_gw",
    )(ids, h, dq, dk, dv, bucket_rows, *offs)

def gx_kernel(x_ref, gb_ref, dq_ref, dk_ref, dv_ref, gain_ref, w_ref, out_ref):
    width = x_ref.shape[1]
    grad = _dot(dq_ref[...], w_ref[:, :width], NT)
    grad += _dot(dk_ref[...], w_ref[:, width:2 * width], NT)
    grad += _dot(dv_ref[...], w_ref[:, 2 * width:3 * width], NT)
    x = x_ref[...].astype(jnp.float32)
    inverse = rms_inverse(x)
    normed = x * inverse
    scaled = grad * gain_ref[0:1, :]
    out = inverse * (scaled - normed * jnp.mean(scaled * normed, axis=1, keepdims=True)) + gb_ref[...].astype(jnp.float32)
    out_ref[...] = out.astype(jnp.bfloat16)

def qkv_gx(x, gb, dq, dk, dv, gains, w, rows=512):
    total, width = x.shape
    blk = pl.BlockSpec((rows, width), lambda i: (i, 0))
    return pl.pallas_call(
        gx_kernel, out_shape=jax.ShapeDtypeStruct((total, width), jnp.bfloat16), grid=(total // rows,),
        in_specs=[blk] * 5 + [pl.BlockSpec(gains.shape, lambda i: (0, 0)),
                              pl.BlockSpec((width, 3 * width), lambda i: (0, 0), pipeline_mode=pl.Buffered(1))],
        out_specs=blk,
        compiler_params=pltpu.CompilerParams(vmem_limit_bytes=LIMIT),
        cost_estimate=LIGHT,
        name="qkv_gx",
    )(x, gb, dq, dk, dv, gains, w)

def swap(value, axis, mask):
    return lax.ppermute(value, axis, [(i, i ^ mask) for i in range(lax.axis_size(axis))])


def send_chip(blocks, me):
    return swap(lax.dynamic_slice_in_dim(blocks, 2 * (1 - me // 2), 2, 0), "seq", 2)


def send_core(blocks, from_chip, me):
    own = lax.dynamic_index_in_dim(blocks, me ^ 1, 0)
    passed = lax.dynamic_index_in_dim(from_chip, 1 - me % 2, 0)
    return swap(jnp.concatenate([own, passed], 0), "seq", 1)


class Gather:
    def __init__(self, shard):
        shard = shard[None]
        self.sent = [shard] + [swap(shard, "dp", 2 * z) for z in (1, 2, 3)]
        self.pieces, self.masks = [], []

    def take(self, piece, mask, rows=(0, 1, 2, 3)):
        ids = tuple(8 * z | mask for z in rows)
        self.pieces += [piece, swap(piece, "seq", 1)]
        self.masks += [ids, tuple(m | 1 for m in ids)]

    def fill(self):
        self.own = jnp.concatenate(self.sent, 0)

    def sides(self):
        self.x, self.y = swap(self.own, "seq", 2), swap(self.own, "dp", 1)

    def corner_halves(self):
        self.near, self.far = swap(self.y[:2], "seq", 2), swap(self.x[2:], "dp", 1)

    def corner_y(self):
        self.corner = swap(self.x, "dp", 1)

    def all_pieces(self):
        return tuple(self.pieces), tuple(self.masks)


class Scatter:
    def __init__(self, keep, send, pos, corner_y):
        self.z, self.y, self.x = pos
        cube = (4, 2, 2) + keep.shape[1:]
        self.mine, self.sent, self.corner_y = keep.reshape(cube), send.reshape(cube), corner_y
        self.other = swap(self.sent, "seq", 1)

    def fold(self):
        pick = lambda v, at, axis: lax.dynamic_index_in_dim(v, at, axis, keepdims=False)
        def quarter(dy, dx):
            cut = lambda v: pick(pick(v, self.y ^ dy, 1), self.x ^ dx, 1).astype(jnp.float32)
            return (cut(self.mine) + cut(self.other)).astype(jnp.bfloat16)
        far = quarter(1, 1)
        self.to_x, self.to_y, self.own = quarter(0, 1), quarter(1, 0), quarter(0, 0)
        if self.corner_y:
            self.came_x, self.came_y = None, swap(far, "dp", 1)
        else:
            self.came_x, self.came_y = swap(far[:2], "seq", 2), swap(far[2:], "dp", 1)

    def turn(self):
        add = lambda a, b: (a.astype(jnp.float32) + b.astype(jnp.float32)).astype(jnp.bfloat16)
        if self.corner_y:
            to_x, to_y = add(self.to_x, self.came_y), self.to_y
        else:
            to_x = lax.dynamic_update_slice_in_dim(self.to_x, add(self.to_x[2:], self.came_y), 2, 0)
            to_y = lax.dynamic_update_slice_in_dim(self.to_y, add(self.to_y[:2], self.came_x), 0, 0)
        self.sent = (to_x, to_y)
        self.came_x, self.came_y = swap(to_x, "seq", 2), swap(to_y, "dp", 1)

    def column(self):
        total = self.own.astype(jnp.float32) + self.came_x.astype(jnp.float32) + self.came_y.astype(jnp.float32)
        total = total.astype(jnp.bfloat16)
        block = lambda k: lax.dynamic_index_in_dim(total, self.z ^ k, 0, keepdims=False)
        self.mine = block(0)
        self.came = [swap(block(k), "dp", 2 * k) for k in (1, 2, 3)]

    def result(self):
        return sum((c.astype(jnp.float32) for c in self.came), self.mine.astype(jnp.float32))


def place(blocks, from_chip, from_core, me):
    for mask, block in ((1, from_core[0:1]), (2, lax.dynamic_index_in_dim(from_chip, me % 2, 0)), (3, from_core[1:2])):
        blocks = lax.dynamic_update_slice_in_dim(blocks, block, me ^ mask, 0)
    return blocks


def tie(first, *later):
    return lax.optimization_barrier((first,) + later)[1:]


def local_whole(tokens, cotangent, lengths, buckets, norm1_gain, w_query, w_key, w_value, w_out, rel_table, norm2_gain, w_in, w_back):
    micro_count, seq_count, rows, width = tokens.shape
    parts = micro_count * seq_count
    both = ("dp", "seq")
    me, dp = lax.axis_index("seq"), lax.axis_index("dp")
    shards = lax.axis_size("seq") * lax.axis_size("dp")
    flat = dp * parts + me
    pos = (dp // 2, dp % 2, me // 2)
    low = lambda v: v.astype(jnp.bfloat16)
    up = lambda v: v.astype(jnp.float32)
    own, ff_own = w_query.shape[0], w_back.shape[0]
    ids = jnp.stack([me, flat, lax.dynamic_index_in_dim(lengths.reshape(parts), me, 0, keepdims=False)])
    length = ids[2:3]

    place_row = lambda v: lax.dynamic_update_slice(jnp.zeros((1, width), jnp.bfloat16), low(v)[None], (0, flat * own))
    small = jnp.concatenate([place_row(norm1_gain), place_row(norm2_gain), jnp.zeros((6, width), jnp.bfloat16),
                             jnp.pad(low(rel_table)[None], ((0, 7), (0, width - HEADS)))], 0)
    shard1 = jnp.concatenate([low(w_query), low(w_key), low(w_value), small], 0)
    ff = w_in.shape[1] // 2
    half = ff_own // 2
    halves = low(w_in).reshape(own, shards, 2, half)
    in_half = lambda i: [halves[:, :, i].reshape(own, ff)[:, j:j + width] for j in range(0, ff, width)]
    shard2 = jnp.concatenate([low(w_back[:half]), low(w_out)] + in_half(0), 0)
    shard3 = jnp.concatenate([low(w_back[half:])] + in_half(1), 0)
    x4, g4 = tokens.reshape(parts, rows, width), cotangent.reshape(parts, rows, width)
    bucket_rows = jnp.stack([jnp.pad(buckets, (0, 1), constant_values=-1), jnp.pad(buckets[::-1], (0, 1), constant_values=-1)])

    g1 = Gather(shard1)
    x_chip = send_chip(x4, me)
    g2 = Gather(shard2)
    g1.fill()
    g1.own, = tie((x_chip, g2.sent[1], shard3), g1.own)
    g1.sides()
    g1.x, g1.y = tie(g2.sent[2], g1.x, g1.y)
    g1.corner_halves()
    g2.fill()
    g1.take(g1.own, 0)
    g1.near, g1.far, g2.own = tie(g1.pieces[1], g1.near, g1.far, g2.own)
    g2.sides()
    g1.x, g1.y, x4_in = tie((g1.near, g1.far), g1.x, g1.y, x4)
    g1.take(g1.x, 2)
    g1.take(g1.y, 4)
    g1.take(g1.near, 6, (0, 1))
    g1.take(g1.far, 6, (2, 3))
    x_core = send_core(x4_in, x_chip, me)
    shard3, = tie((g1.near, g1.far), shard3)
    full3 = lax.all_gather(shard3, both, axis=0, tiled=False)
    x, hidden, q, k, v, w_qkv, gains, t, t_back = qkv_fwd(ids, x4, (x_chip, x_core), *g1.all_pieces(), bucket_rows, HEADS)
    pairs = HEADS // 2
    att = attn_fwd(length, q, k, v, t, 0, pairs // 2)
    g2.take(g2.own, 0)
    g2.x, g2.y = tie((att[0], g2.pieces[1]), g2.x, g2.y)
    g2.corner_y()
    g4_in, = tie(g2.x, g4)
    g_chip = send_chip(g4_in, me)
    g2.take(g2.x, 2)
    g2.take(g2.y, 4)
    q_in, = tie((g2.x, g2.y), q)
    attended, lse = attn_fwd(length, q_in, k, v, t, pairs // 2, pairs // 2, att)
    g2.corner, g_chip = tie((attended, g2.pieces[3], g2.pieces[5]), g2.corner, g_chip)
    g2.take(g2.corner, 6)
    g_core = send_core(g4, g_chip, me)
    *state, gw_a = mid_a(ids, x, attended, g4, (g_chip, g_core), gains, *g2.all_pieces(), ff)
    r_a = lax.psum_scatter(gw_a.reshape(-1, width), both, scatter_dimension=0, tiled=True)
    out, gb, g_att, keep2, send2 = mid_b(ids, gains, state, attended, full3, ff)
    sc2 = Scatter(keep2, send2, pos, True)
    out4 = out.reshape(parts, rows, width)
    out_chip = send_chip(out4, me)
    count = pairs // 4
    back = lambda first, g, prev: attn_bwd(length, q, k, v, g, attended, lse, t_back, first, count, prev)
    dq, dk, dv, off0 = back(0, g_att, None)
    sc2.other, = tie(off0, sc2.other)
    sc2.fold()
    g_att, = tie((sc2.own, sc2.to_x, sc2.to_y), g_att)
    dq, dk, dv, off1 = back(count, g_att, (dq, dk, dv))
    sc2.came_y, sc2.to_x = tie((off1, out_chip), sc2.came_y, sc2.to_x)
    sc2.turn()
    out4_in, out_chip = tie(sc2.sent, out4, out_chip)
    out_core = send_core(out4_in, out_chip, me)
    g_att, = tie(sc2.sent, g_att)
    dq, dk, dv, off2 = back(2 * count, g_att, (dq, dk, dv))
    dq, dk, dv, off3 = back(3 * count, g_att, (dq, dk, dv))
    sc2.came_x, sc2.came_y = tie((off3, out_core), sc2.came_x, sc2.came_y)
    sc2.column()
    h_in, = tie((sc2.mine, r_a), hidden)
    keep1, send1 = qkv_gw(ids, h_in, dq, dk, dv, bucket_rows, (off0, off1, off2, off3), shards)
    sc1 = Scatter(keep1, send1, pos, False)
    gb_in, = tie(send1, gb)
    gx = qkv_gx(x, gb_in, dq, dk, dv, gains, w_qkv)
    sc1.other, = tie(gx, sc1.other)
    sc1.fold()
    out4, out_chip, out_core = tie(sc1.own, out4, out_chip, out_core)
    layer_out = place(out4, out_chip, out_core, me)
    sc1.came_x, sc1.came_y = tie((layer_out, sc2.came), sc1.came_x, sc1.came_y)
    sc1.turn()
    sc2.came = list(tie(sc1.sent, *sc2.came))
    r2 = sc2.result()
    sc1.came_x, sc1.came_y = tie(r2, sc1.came_x, sc1.came_y)
    sc1.column()
    gx, = tie(sc1.mine, gx)
    gx4 = gx.reshape(parts, rows, width)
    gx_chip = send_chip(gx4, me)
    gx_chip, = tie(sc1.came, gx_chip)
    gx_core = send_core(gx4, gx_chip, me)
    input_grad = place(gx4, gx_chip, gx_core, me)
    sc1.came = list(tie(input_grad, *sc1.came))
    r1, r_a = sc1.result(), up(r_a)
    join = lambda v: jnp.concatenate([v[i:i + own] for i in range(0, v.shape[0], own)], 1).reshape(own, shards, 1, half)
    g_in = jnp.concatenate([join(r_a[half:]), join(r2[half + own:])], 2).reshape(w_in.shape)
    g_back = jnp.concatenate([r_a[:half], r2[:half]], 0)
    prod = up(shard1[:3 * own]) * r1[:3 * own]
    g_gain1 = jnp.sum(prod[:own] + prod[own:2 * own] + prod[2 * own:], axis=1) / up(low(norm1_gain))
    g_gain2 = jnp.sum(up(low(w_in)) * g_in, axis=1) / up(low(norm2_gain))
    return (layer_out.reshape(tokens.shape), input_grad.reshape(tokens.shape), g_gain1, r1[:own], r1[own:2 * own], r1[2 * own:3 * own],
            r2[half:half + own], r1[3 * own, :HEADS], g_gain2, g_in, g_back)


def local_any(shape, tokens, *rest):
    fits = tuple(shape) == (8, 4) and tokens.shape[0] * tokens.shape[1] == 4 and tokens.shape[3] == HEADS * DH == 1024
    return (local_whole if fits else local)(tokens, *rest)


def solution(mesh):
    return jax.shard_map(
        functools.partial(local_any, mesh.devices.shape),
        mesh=mesh,
        in_specs=(
            P(None, "dp", "seq", None),
            P(None, "dp", "seq", None),
            P(None, "dp"),
            P(),
            P(("dp", "seq")),
            P(("dp", "seq"), None),
            P(("dp", "seq"), None),
            P(("dp", "seq"), None),
            P(("dp", "seq"), None),
            P(("dp", "seq")),
            P(("dp", "seq")),
            P(("dp", "seq"), None),
            P(("dp", "seq"), None),
        ),
        out_specs=(
            P(None, "dp", "seq", None),
            P(None, "dp", "seq", None),
            P(("dp", "seq")),
            P(("dp", "seq"), None),
            P(("dp", "seq"), None),
            P(("dp", "seq"), None),
            P(("dp", "seq"), None),
            P(("dp", "seq")),
            P(("dp", "seq")),
            P(("dp", "seq"), None),
            P(("dp", "seq"), None),
        ),
        check_vma=False,
    )
```

```python
import functools

import jax
import jax.numpy as jnp
from jax import lax
from jax.experimental import pallas as pl
from jax.experimental.pallas import tpu as pltpu
from jax.sharding import PartitionSpec as P

HEADS = 16
DH = 64
BUCKETS = 32


epsilon = 1e-06
floor_score = -1e30
highest = lax.Precision.HIGHEST
root_coef = 0.7978845608
cubic_coef = 0.044715


def gelu_tanh(values):
    return (
        0.5
        * values
        * (1.0 + jnp.tanh(root_coef * (values + cubic_coef * values * values * values)))
    )


def gelu_slope(values):
    inner = jnp.tanh(root_coef * (values + cubic_coef * values * values * values))
    return 0.5 * (1.0 + inner) + 0.5 * values * (1.0 - inner * inner) * root_coef * (
        1.0 + 3.0 * cubic_coef * values * values
    )


def project(acts, weight):
    return jnp.einsum("srd,de->sre", acts, weight, preferred_element_type=jnp.float32)


def project_back(grads_in, weight):
    return jnp.einsum("sre,de->srd", grads_in, weight, preferred_element_type=jnp.float32)


def contract(acts, grads_in):
    return jnp.einsum("srd,sre->de", acts, grads_in, preferred_element_type=jnp.float32)


def rms_forward(values, gain):
    inverse = lax.rsqrt(jnp.mean(values * values, axis=-1, keepdims=True) + epsilon)
    normed = values * inverse
    return (normed, inverse, (normed * gain.astype(jnp.float32)).astype(jnp.bfloat16))


def rms_backward(grad_hidden, normed, inverse, gain):
    scaled = grad_hidden * gain.astype(jnp.float32)
    grad_values = inverse * (scaled - normed * jnp.mean(scaled * normed, axis=-1, keepdims=True))
    return (grad_values, jnp.sum(grad_hidden * normed, axis=(0, 1)))


def score_block(per_head_queries, per_head_keys, rel_bias, key_valid):
    scores = (
        jnp.einsum(
            "ofck,owck->ocfw", per_head_queries, per_head_keys, preferred_element_type=jnp.float32
        )
        + rel_bias[None]
    )
    return jnp.where(key_valid, scores, floor_score)


def offset_sums(grid, first_row, seq_len):
    head_count, row_count, key_count = grid.shape
    flipped = grid[:, ::-1, :]
    padded = jnp.pad(flipped, ((0, 0), (0, 0), (0, row_count)))
    wide_len = key_count + row_count
    skewed = padded.reshape(head_count, row_count * wide_len)[:, : row_count * (wide_len - 1)]
    skewed = skewed.reshape(head_count, row_count, wide_len - 1)
    column_sums = jnp.sum(skewed, axis=1)
    placed = jnp.zeros((head_count, 2 * seq_len - 1), jnp.float32)
    begin = seq_len - row_count - first_row
    return lax.dynamic_update_slice(placed, column_sums, (jnp.int32(0), begin))


def run_micro(inputs, incoming, seq_lens, attn_set, mlp_set, context):
    onehot, offsets, row_pos, key_pos, first_row, seq_len = context
    gain_one, query_w, key_w, value_w, out_w, bias_table = attn_set
    gain_two, in_w, return_projection_weight = mlp_set
    seq_count, row_count, model_width = inputs.shape
    values = inputs.astype(jnp.float32)
    normed_one, inverse_one, hidden_one = rms_forward(values, gain_one)
    queries = project(hidden_one, query_w).astype(jnp.bfloat16)
    keys_own = project(hidden_one, key_w).astype(jnp.bfloat16)
    values_own = project(hidden_one, value_w).astype(jnp.bfloat16)
    keys_all, values_all = (
        lax.all_gather(keys_own, "seq", axis=1, tiled=True),
        lax.all_gather(values_own, "seq", axis=1, tiled=True),
    )
    per_offset = jnp.dot(
        onehot, bias_table.reshape(BUCKETS, HEADS), preferred_element_type=jnp.float32
    )
    rel_bias = jnp.transpose(per_offset[offsets], (2, 0, 1))
    key_valid = (key_pos[None, :] < seq_lens[:, None])[:, None, None, :]
    per_head_queries = queries.reshape(seq_count, row_count, HEADS, DH)
    per_head_keys = keys_all.reshape(seq_count, seq_len, HEADS, DH)
    per_head_values = values_all.reshape(seq_count, seq_len, HEADS, DH)
    scores = score_block(per_head_queries, per_head_keys, rel_bias, key_valid)
    row_max = jnp.max(scores, axis=-1, keepdims=True)
    exp_scores = jnp.exp(scores - row_max)
    row_total = jnp.sum(exp_scores, axis=-1, keepdims=True)
    attn_probs = exp_scores / row_total
    log_total = row_max + jnp.log(row_total)
    reduced_precision_probs = attn_probs.astype(jnp.bfloat16)
    attended = jnp.einsum(
        "jfpe,jefn->jpfn",
        reduced_precision_probs,
        per_head_values,
        preferred_element_type=jnp.float32,
    )
    attended = attended.reshape(seq_count, row_count, model_width).astype(jnp.bfloat16)
    residual_mid = values + project(attended, out_w)
    normed_two, inverse_two, hidden_two = rms_forward(residual_mid, gain_two)
    pre_act = project(hidden_two, in_w)
    active = gelu_tanh(pre_act).astype(jnp.bfloat16)
    result = (residual_mid + project(active, return_projection_weight)).astype(jnp.bfloat16)
    row_valid = (row_pos[None, :] < seq_lens[:, None]).astype(jnp.float32)[:, :, None]
    grad_out = incoming.astype(jnp.float32) * row_valid
    grad_low = grad_out.astype(jnp.bfloat16)
    grad_back = contract(active, grad_low)
    gradient_active_rows = project_back(grad_low, return_projection_weight)
    grad_pre = (gradient_active_rows * gelu_slope(pre_act)).astype(jnp.bfloat16)
    grad_in = contract(hidden_two, grad_pre)
    grad_hidden_two = project_back(grad_pre, in_w)
    grad_mixed, grad_gain_two = rms_backward(grad_hidden_two, normed_two, inverse_two, gain_two)
    grad_mixed = grad_mixed + grad_out
    grad_branch = grad_mixed.astype(jnp.bfloat16)
    grad_outw = contract(attended, grad_branch)
    gradient_attended_values = project_back(grad_branch, out_w).astype(jnp.bfloat16)
    gradient_attended_values = gradient_attended_values.reshape(seq_count, row_count, HEADS, DH)
    scores = score_block(per_head_queries, per_head_keys, rel_bias, key_valid)
    attn_probs = jnp.exp(scores - log_total)
    reduced_precision_probs = attn_probs.astype(jnp.bfloat16)
    grad_probs = jnp.einsum(
        "ofck,owck->ocfw",
        gradient_attended_values,
        per_head_values,
        preferred_element_type=jnp.float32,
    )
    inner_sum = jnp.sum(attn_probs * grad_probs, axis=-1, keepdims=True)
    gradient_score_matrix = (attn_probs * (grad_probs - inner_sum)).astype(jnp.bfloat16)
    grad_query = jnp.einsum(
        "jfpe,jefn->jpfn", gradient_score_matrix, per_head_keys, preferred_element_type=jnp.float32
    )
    grad_query = grad_query.astype(jnp.bfloat16).reshape(seq_count, row_count, model_width)
    key_part = jnp.einsum(
        "eciv,eicq->evcq",
        gradient_score_matrix,
        per_head_queries,
        preferred_element_type=jnp.float32,
    )
    value_part = jnp.einsum(
        "eciv,eicq->evcq",
        reduced_precision_probs,
        gradient_attended_values,
        preferred_element_type=jnp.float32,
    )
    key_part = key_part.reshape(seq_count, seq_len, model_width)
    value_part = value_part.reshape(seq_count, seq_len, model_width)
    grad_key, grad_value = (
        lax.psum_scatter(
            key_part.astype(jnp.bfloat16), "seq", scatter_dimension=1, tiled=True
        ).astype(jnp.float32),
        lax.psum_scatter(
            value_part.astype(jnp.bfloat16), "seq", scatter_dimension=1, tiled=True
        ).astype(jnp.float32),
    )
    grad_key = grad_key.astype(jnp.bfloat16)
    grad_value = grad_value.astype(jnp.bfloat16)
    offset_grad = offset_sums(
        jnp.sum(gradient_score_matrix.astype(jnp.float32), axis=0), first_row, seq_len
    )
    grad_table = jnp.dot(onehot.astype(jnp.float32).T, offset_grad.T, precision=highest).reshape(-1)
    grad_qw = contract(hidden_one, grad_query)
    grad_kw = contract(hidden_one, grad_key)
    grad_vw = contract(hidden_one, grad_value)
    grad_hidden_one = (
        project_back(grad_query, query_w)
        + project_back(grad_key, key_w)
        + project_back(grad_value, value_w)
    )
    grad_values, grad_gain_one = rms_backward(grad_hidden_one, normed_one, inverse_one, gain_one)
    grad_values = grad_values + grad_mixed
    gradients = (
        grad_gain_one,
        grad_qw,
        grad_kw,
        grad_vw,
        grad_outw,
        grad_table,
        grad_gain_two,
        grad_in,
        grad_back,
    )
    return (result, grad_values.astype(jnp.bfloat16), gradients)


def local(
    tokens,
    cotangent,
    lengths,
    buckets,
    norm1_gain,
    w_query,
    w_key,
    w_value,
    w_out,
    rel_table,
    norm2_gain,
    w_in,
    w_back,
):
    micro_count, seq_count, row_count, model_width = tokens.shape
    seq_parts = lax.axis_size("seq")
    seq_len = row_count * seq_parts
    first_row = lax.axis_index("seq") * row_count
    row_pos = first_row + jnp.arange(row_count, dtype=jnp.int32)
    key_pos = jnp.arange(seq_len, dtype=jnp.int32)
    onehot = (buckets[:, None] == jnp.arange(BUCKETS, dtype=jnp.int32)[None, :]).astype(
        jnp.bfloat16
    )
    offsets = key_pos[None, :] - row_pos[:, None] + (seq_len - 1)
    context = (onehot, offsets, row_pos, key_pos, first_row, seq_len)
    outputs = []
    input_grads = []
    pending = None
    shard_sums = None
    for micro_step in range(micro_count):
        attn_set = (
            lax.all_gather(norm1_gain.astype(jnp.bfloat16), ("dp", "seq"), axis=0, tiled=True),
            lax.all_gather(w_query.astype(jnp.bfloat16), ("dp", "seq"), axis=0, tiled=True),
            lax.all_gather(w_key.astype(jnp.bfloat16), ("dp", "seq"), axis=0, tiled=True),
            lax.all_gather(w_value.astype(jnp.bfloat16), ("dp", "seq"), axis=0, tiled=True),
            lax.all_gather(w_out.astype(jnp.bfloat16), ("dp", "seq"), axis=0, tiled=True),
            lax.all_gather(rel_table.astype(jnp.bfloat16), ("dp", "seq"), axis=0, tiled=True),
        )
        mlp_set = (
            lax.all_gather(norm2_gain.astype(jnp.bfloat16), ("dp", "seq"), axis=0, tiled=True),
            lax.all_gather(w_in.astype(jnp.bfloat16), ("dp", "seq"), axis=0, tiled=True),
            lax.all_gather(w_back.astype(jnp.bfloat16), ("dp", "seq"), axis=0, tiled=True),
        )
        layer_part, grad_part, gradients = run_micro(
            tokens[micro_step],
            cotangent[micro_step],
            lengths[micro_step],
            attn_set,
            mlp_set,
            context,
        )
        outputs.append(layer_part)
        input_grads.append(grad_part)
        pending = gradients if pending is None else jax.tree.map(jnp.add, pending, gradients)
    shard_sums = (
        lax.psum_scatter(pending[0], ("dp", "seq"), scatter_dimension=0, tiled=True),
        lax.psum_scatter(pending[1], ("dp", "seq"), scatter_dimension=0, tiled=True),
        lax.psum_scatter(pending[2], ("dp", "seq"), scatter_dimension=0, tiled=True),
        lax.psum_scatter(pending[3], ("dp", "seq"), scatter_dimension=0, tiled=True),
        lax.psum_scatter(pending[4], ("dp", "seq"), scatter_dimension=0, tiled=True),
        lax.psum_scatter(pending[5], ("dp", "seq"), scatter_dimension=0, tiled=True),
        lax.psum_scatter(pending[6], ("dp", "seq"), scatter_dimension=0, tiled=True),
        lax.psum_scatter(pending[7], ("dp", "seq"), scatter_dimension=0, tiled=True),
        lax.psum_scatter(pending[8], ("dp", "seq"), scatter_dimension=0, tiled=True),
    )
    return (
        jnp.stack(outputs),
        jnp.stack(input_grads),
        shard_sums[0],
        shard_sums[1],
        shard_sums[2],
        shard_sums[3],
        shard_sums[4],
        shard_sums[5],
        shard_sums[6],
        shard_sums[7],
        shard_sums[8],
    )


NT = (((1,), (1,)), ((), ()))
TN = (((0,), (0,)), ((), ()))
STRIP = 128
LOG2E = 1.4426950408889634
LN2 = 0.6931471805599453
LIMIT = 58 << 20
LIGHT = pl.CostEstimate(flops=1 << 20, bytes_accessed=1 << 16, transcendentals=0)

def _dot(a, b, dims=(((1,), (0,)), ((), ()))):
    return lax.dot_general(a, b, dims, preferred_element_type=jnp.float32)

def with_extras(x, which, extras, width=64):
    lane = lax.broadcasted_iota(jnp.int32, (1, x.shape[1]), 1)
    spare = lane - width if which == 0 else lane
    own = (lane < width) if which == 0 else (lane >= width)
    fill = jnp.zeros_like(x)
    for i, extra in enumerate(extras):
        fill = jnp.where(spare == i, extra, fill)
    return jnp.where(own, x, fill).astype(jnp.bfloat16)

def three_parts(x):
    low = lambda v: v.astype(jnp.bfloat16).astype(jnp.float32)
    high = low(x)
    middle = low(x - high)
    return [high, middle, low(x - high - middle)]

def slot_floor(size, length):
    return jnp.where(lax.broadcasted_iota(jnp.int32, (size, 1), 0) < length, 0.0, floor_score)

def skew(row, wide):
    return pltpu.roll(jnp.broadcast_to(row, (STRIP, wide)), wide - (STRIP - 1), 1, stride=1, stride_axis=0)

def fwd_kernel(len_ref, q_ref, k_ref, v_ref, t_ref, *refs, rows, seq_len, first):
    o_ref, lse_ref, strip, kx, vx = refs[-5:]
    wide = t_ref.shape[-1]
    pair = first + pl.program_id(0)
    per = rows // STRIP
    lane = lax.broadcasted_iota(jnp.int32, (1, 128), 1)
    k2 = k_ref[...].astype(jnp.float32)
    vx[:, 0:128] = v_ref[...]
    vx[:, 128:256] = jnp.ones_like(v_ref[...])
    for a in range(2):
        kx[a] = with_extras(k2, a, [slot_floor(seq_len, len_ref[0])])
        strip[a] = skew(t_ref[pl.ds(2 * pair + a, 1), :], wide)

    def step(b, carry):
        base = b * rows
        q2 = q_ref[pl.ds(base, rows), :].astype(jnp.float32)
        outs, stats = [], []
        for a in range(2):
            scores = _dot(with_extras(q2, a, [1.0]), kx[a], NT)
            parts = []
            for i in range(per):
                off = (seq_len - STRIP) - (b * per + i) * STRIP
                parts.append(strip[a, :, pl.ds(off, seq_len)])
            scores = scores + (jnp.concatenate(parts, 0) if per > 1 else parts[0])
            top = jnp.max(scores, axis=1, keepdims=True)
            probs = jnp.exp2(scores - top).astype(jnp.bfloat16)
            out = _dot(probs, vx[...])
            outs.append(out[:, 0:128] / out[:, 128:256])
            stats.append(top + jnp.log2(out[:, 128:256]))
        o_ref[pl.ds(base, rows), :] = jnp.where(lane < 64, outs[0], outs[1]).astype(jnp.bfloat16)
        lse_ref[0, pl.ds(base, rows), :] = jnp.where(lane < 64, stats[0], stats[1])
        return carry

    for b in range(seq_len // rows):
        step(b, 0)

def attn_fwd(length, q, k, v, t, first, count, prev=(), rows=256):
    seq_len, width = q.shape
    pairs = width // 128
    wide = t.shape[-1]
    blk = pl.BlockSpec((seq_len, 128), lambda p, n: (0, first + p))
    return pl.pallas_call(
        functools.partial(fwd_kernel, rows=rows, seq_len=seq_len, first=first),
        out_shape=(jax.ShapeDtypeStruct((seq_len, width), jnp.bfloat16),
                   jax.ShapeDtypeStruct((pairs, seq_len, 128), jnp.float32)),
        grid_spec=pltpu.PrefetchScalarGridSpec(
            num_scalar_prefetch=1, grid=(count,),
            in_specs=[blk, blk, blk, pl.BlockSpec(t.shape, lambda p, n: (0, 0))] + [pl.BlockSpec(memory_space=pl.ANY)] * len(prev),
            out_specs=[blk, pl.BlockSpec((1, seq_len, 128), lambda p, n: (first + p, 0, 0))],
            scratch_shapes=[pltpu.VMEM((2, STRIP, wide), jnp.float32), pltpu.VMEM((2, seq_len, 128), jnp.bfloat16),
                            pltpu.VMEM((seq_len, 256), jnp.bfloat16)]),
        input_output_aliases={5 + i: i for i in range(len(prev))},
        compiler_params=pltpu.CompilerParams(vmem_limit_bytes=LIMIT),
        cost_estimate=LIGHT,
        name="attn_fwd",
    )(length, q, k, v, t, *prev)

def bwd_kernel(len_ref, q_ref, k_ref, v_ref, do_ref, o_ref, lse_ref, t_ref, *refs, rows, seq_len, first):
    dq_ref, dk_ref, dv_ref, g_ref, strip, acc, dq_acc, qx, kx, vx, dox = refs[-11:]
    wide = t_ref.shape[-1]
    local_pair = pl.program_id(0)
    pair = first + local_pair
    per = rows // STRIP
    lane = lax.broadcasted_iota(jnp.int32, (1, 128), 1)
    up = lambda ref: ref[...].astype(jnp.float32)
    floor = slot_floor(seq_len, len_ref[0])
    prod = up(do_ref) * up(o_ref)
    for a in range(2):
        mine = (lane < 64) if a == 0 else (lane >= 64)
        delta = jnp.sum(jnp.where(mine, prod, 0.0), axis=1, keepdims=True)
        lse = lse_ref[0, :, 64 * a:64 * a + 1]
        qx[a] = with_extras(up(q_ref), a, [1.0] + three_parts(-lse))
        kx[a] = with_extras(up(k_ref), a, [floor, 1.0, 1.0, 1.0])
        vx[a] = with_extras(up(v_ref), a, [1.0, 1.0, 1.0])
        dox[a] = with_extras(up(do_ref), a, three_parts(-delta))
        strip[a] = skew(t_ref[pl.ds(2 * pair + a, 1), :], wide)
    acc[...] = jnp.zeros_like(acc)
    k2t = k_ref[...].T
    dq_acc[...] = jnp.zeros_like(dq_acc)

    def step(b, carry):
        at = pl.ds(b * rows, rows)
        dks, dvs = [], []
        for a in range(2):
            scores = _dot(kx[a, at, :], qx[a], NT)
            offs = [(seq_len - STRIP) - (b * per + i) * STRIP for i in range(per)]
            bias = [strip[a, :, pl.ds(off, seq_len)] for off in offs]
            probs = jnp.exp2(scores + (jnp.concatenate(bias, 0) if per > 1 else bias[0]))
            grad_scores = probs * _dot(vx[a, at, :], dox[a], NT)
            for i, off in enumerate(offs):
                acc[a, :, pl.ds(off, seq_len)] += grad_scores[i * STRIP:(i + 1) * STRIP]
            probs_b = probs.astype(jnp.bfloat16)
            gs_b = grad_scores.astype(jnp.bfloat16)
            dvs.append(_dot(probs_b, do_ref[...]))
            dks.append(_dot(gs_b, q_ref[...]))
            dq_acc[a] += _dot(k2t[:, b * rows:(b + 1) * rows], gs_b)
        dk_ref[at, :] = (jnp.where(lane < 64, dks[0], dks[1]) * LN2).astype(jnp.bfloat16)
        dv_ref[at, :] = jnp.where(lane < 64, dvs[0], dvs[1]).astype(jnp.bfloat16)
        return carry

    for b in range(seq_len // rows):
        step(b, 0)
    dq_ref[...] = jnp.concatenate([dq_acc[0, 0:64], dq_acc[1, 64:128]], 0).T.astype(jnp.bfloat16)
    for a in range(2):
        sums = acc[a]
        half = STRIP
        while half > 8:
            half //= 2
            sums = sums[:half] + pltpu.roll(sums[half:], wide - half, 1)
        while half > 1:
            half //= 2
            sums = sums + pltpu.roll(pltpu.roll(sums, 8 - half, 0), wide - half, 1)
        g_ref[pl.ds(2 * local_pair + a, 1), :] = pltpu.roll(sums, STRIP - 1, 1)[0:1]

def attn_bwd(length, q, k, v, do, o, lse, trev, first, count, prev=None, rows=512):
    seq_len, width = q.shape
    wide = trev.shape[-1]
    blk = pl.BlockSpec((seq_len, 128), lambda p, n: (0, first + p))
    mat = jax.ShapeDtypeStruct((seq_len, width), jnp.bfloat16)
    prev = tuple(prev) if prev is not None else ()
    return pl.pallas_call(
        functools.partial(bwd_kernel, rows=rows, seq_len=seq_len, first=first),
        out_shape=(mat, mat, mat, jax.ShapeDtypeStruct((2 * count, wide), jnp.float32)),
        grid_spec=pltpu.PrefetchScalarGridSpec(
            num_scalar_prefetch=1, grid=(count,),
            in_specs=[blk, blk, blk, blk, blk, pl.BlockSpec((1, seq_len, 128), lambda p, n: (first + p, 0, 0)),
                      pl.BlockSpec(trev.shape, lambda p, n: (0, 0))] + [pl.BlockSpec(memory_space=pl.ANY)] * len(prev),
            out_specs=[blk, blk, blk, pl.BlockSpec((2 * count, wide), lambda p, n: (0, 0))],
            scratch_shapes=[pltpu.VMEM((2, STRIP, wide), jnp.float32), pltpu.VMEM((2, STRIP, wide), jnp.float32),
                            pltpu.VMEM((2, 128, seq_len), jnp.float32)] + [pltpu.VMEM((2, seq_len, 128), jnp.bfloat16)] * 4),
        input_output_aliases={8 + i: i for i in range(len(prev))},
        compiler_params=pltpu.CompilerParams(vmem_limit_bytes=LIMIT),
        cost_estimate=LIGHT,
        name="attn_bwd",
    )(length, q, k, v, do, o, lse, trev, *prev)

ANY = pl.BlockSpec(memory_space=pl.ANY)
VM = pl.BlockSpec(memory_space=pltpu.VMEM)
SM = pl.BlockSpec(memory_space=pltpu.SMEM)

def rms_inverse(value):
    return lax.rsqrt(jnp.mean(value * value, axis=1, keepdims=True) + epsilon)

def pull_sequence(me, whole_ref, chip_ref, core_ref, dst, sem):
    rows = whole_ref.shape[1]
    for mask, src in enumerate((whole_ref.at[me], core_ref.at[0], chip_ref.at[me & 1], core_ref.at[1])):
        at = pl.multiple_of((me ^ mask) * rows, rows)
        pltpu.make_async_copy(src, dst.at[pl.ds(at, rows), :], sem).start()

def qkv_kernel(ids_ref, x4_ref, chip_ref, core_ref, *refs, masks):
    gathered = refs[:len(masks)]
    bucket_ref = refs[len(masks)]
    x_out, h_out, q_out, k_out, v_out, w_out, gain_ref, t_ref, trev_ref, xs, hs, ps, ws, es, sems = refs[len(masks) + 1:]
    me, flat = ids_ref[0], ids_ref[1]
    width = xs.shape[1]
    own = width // es.shape[0]
    pull_sequence(me, x4_ref, chip_ref, core_ref, xs, sems.at[0])
    for ref, ids in zip(gathered, masks):
        for j, mask in enumerate(ids):
            shard = flat ^ mask
            pltpu.make_async_copy(ref.at[j, 3 * own:3 * own + 16, :], es.at[shard], sems.at[1]).start()
    for ref, ids in zip(gathered, masks):
        for j, mask in enumerate(ids):
            at = pl.multiple_of((flat ^ mask) * own, own)
            for i in range(3):
                pltpu.make_async_copy(ref.at[j, i * own:(i + 1) * own, :], ws.at[pl.ds(at, own), i * width:(i + 1) * width], sems.at[2]).start()
    pltpu.make_async_copy(es, es, sems.at[1]).wait()
    extras = es[...].astype(jnp.float32)
    gains = jnp.sum(extras, axis=0)
    gain_ref[...] = gains[0:8]
    table = extras[:, 8, 0:128].astype(jnp.bfloat16)
    ids = lax.broadcasted_iota(jnp.int32, (es.shape[0], 1), 0)
    heads = t_ref.shape[0]
    for i, ref in enumerate((t_ref, trev_ref)):
        hot = jnp.where(bucket_ref[i:i + 1, :] == ids, 1.0, 0.0).astype(jnp.bfloat16)
        ref[...] = _dot(table, hot, TN)[0:heads] * LOG2E
    pltpu.make_async_copy(xs, xs, sems.at[0]).wait()
    part = 256
    def norm(i, carry):
        at = pl.ds(pl.multiple_of(i * part, part), part)
        x = xs[at, :].astype(jnp.float32)
        hs[at, :] = (x * rms_inverse(x) * gains[0:1]).astype(jnp.bfloat16)
        return carry
    lax.fori_loop(0, xs.shape[0] // part, norm, 0)
    copies = [pltpu.make_async_copy(xs, x_out, sems.at[0]), pltpu.make_async_copy(hs, h_out, sems.at[1])]
    for copy in copies:
        copy.start()
    pltpu.make_async_copy(ws, ws, sems.at[2]).wait()
    copies.append(pltpu.make_async_copy(ws, w_out, sems.at[2]))
    copies[-1].start()
    for i, ref in enumerate((q_out, k_out, v_out)):
        full = _dot(hs[...], ws[:, i * width:(i + 1) * width])
        ps[i] = (full * LOG2E if i == 0 else full).astype(jnp.bfloat16)
        copies.append(pltpu.make_async_copy(ps.at[i], ref, sems.at[3 + i]))
        copies[-1].start()
    for copy in copies:
        copy.wait()

def qkv_fwd(ids, x4, came, gathered, masks, bucket_rows, heads):
    parts, rows, width = x4.shape
    total = parts * rows
    shards = sum(len(m) for m in masks)
    mat = jax.ShapeDtypeStruct((total, width), jnp.bfloat16)
    wide = bucket_rows.shape[1]
    vm = lambda *s: pltpu.VMEM(s, jnp.bfloat16)
    return pl.pallas_call(
        functools.partial(qkv_kernel, masks=masks),
        out_shape=(mat,) * 5 + (jax.ShapeDtypeStruct((width, 3 * width), jnp.bfloat16), jax.ShapeDtypeStruct((8, width), jnp.float32),
                                jax.ShapeDtypeStruct((heads, wide), jnp.float32), jax.ShapeDtypeStruct((heads, wide), jnp.float32)),
        in_specs=[SM] + [ANY] * (3 + len(gathered)) + [VM],
        out_specs=[ANY] * 6 + [VM] * 3,
        scratch_shapes=[vm(total, width), vm(total, width), vm(3, total, width), vm(width, 3 * width), vm(shards, 16, width), pltpu.SemaphoreType.DMA((6,))],
        compiler_params=pltpu.CompilerParams(vmem_limit_bytes=LIMIT),
        cost_estimate=LIGHT,
        name="qkv_fwd",
    )(ids, x4, *came, *gathered, bucket_rows)

def gelu_both(v):
    t = jnp.tanh(root_coef * (v + cubic_coef * v * v * v))
    half = 0.5 * (1.0 + t)
    slope = half + 0.5 * v * (1.0 - t * t) * (root_coef * (1.0 + 3.0 * cubic_coef * v * v))
    return v * half, slope

def by_core(core, keep, send, src, dst_rows, sem, lead=slice(None), src_rows=slice(None), lanes=slice(None)):
    for parity in range(2):
        @pl.when(core == parity)
        def _():
            for dst, at in ((keep, parity), (send, 1 - parity)):
                pltpu.make_async_copy(src.at[lead, at, src_rows, lanes], dst.at[lead, dst_rows, lanes], sem).start()

def ff_chunks(h2, h2t, gm, acc, gh2, ws_in, ws_back, st_in, st_back, row_in, emit, before_add, cols=512):
    steps = ws_in.shape[1] // cols
    half, width = st_back.shape[2:]
    own = width // (2 * st_in.shape[0])
    wide = width // cols
    group = cols // (2 * half)

    def step(c, carry):
        at = pl.ds(pl.multiple_of(c * cols, cols), cols)
        win, wback = ws_in[:, at], ws_back[at, :]
        pre = _dot(h2[...], win)
        grad_active = _dot(gm[...], wback, NT)
        act, slope = gelu_both(pre)
        active = act.astype(jnp.bfloat16)
        gpre = (grad_active * slope).astype(jnp.bfloat16)
        @pl.when(c == 0)
        def _():
            before_add()
        acc[...] += _dot(active, wback)
        gh2[...] += _dot(gpre, win, NT)
        lead = pl.ds(c * group, group)
        st_back[lead] = _dot(active, gm[...], TN).astype(jnp.bfloat16).reshape(group, 2, half, width)
        emit(st_back, 0, lead=lead, dst_rows=slice(0, half))
        up = pl.multiple_of((c // wide) * own, own)
        lanes = pl.ds(pl.multiple_of((c % wide) * cols, cols), cols)
        st_in[:, :, pl.ds(up, own), lanes] = _dot(h2t[...], gpre).astype(jnp.bfloat16).reshape(-1, 2, own, cols)
        emit(st_in, 1, src_rows=pl.ds(up, own), dst_rows=pl.ds(row_in + up, own), lanes=lanes)
        return carry
    lax.fori_loop(0, steps, step, 0)

def finish_chunks(st_in, st_back, sems):
    pltpu.make_async_copy(st_back, st_back, sems.at[0]).wait()
    pltpu.make_async_copy(st_in, st_in, sems.at[1]).wait()

def aligned(at, size):
    return at if isinstance(at, int) else pl.multiple_of(at, size)

def pull_ff(flat, gathered, masks, ws_in, ws_back, row_in, sems):
    width = ws_in.shape[0]
    shards = sum(len(m) for m in masks)
    own, half = width // shards, ws_back.shape[0] // shards
    for ref, ids in zip(gathered, masks):
        for j, mask in enumerate(ids):
            shard = flat ^ mask
            pltpu.make_async_copy(ref.at[j, 0:half, :], ws_back.at[pl.ds(aligned(shard * half, half), half), :], sems.at[1]).start()
            at = pl.ds(aligned(shard * own, own), own)
            for i in range(ws_in.shape[1] // width):
                pltpu.make_async_copy(ref.at[j, row_in + i * own:row_in + (i + 1) * own, :], ws_in.at[at, i * width:(i + 1) * width], sems.at[0]).start()

def mid_a_kernel(ids_ref, x_hbm, o_hbm, g4_ref, chip_ref, core_ref, gain_ref, *refs, masks):
    gathered = refs[:len(masks)]
    (mixed_out, acc_out, gh2_out, h2_out, h2t_out, gm_out, wo_out, gw_out,
     xs, os, wo, ws_in, ws_back, mixed, h2, h2t, acc, gh2, gm, st_in, st_back, sems) = refs[len(masks):]
    flat = ids_ref[1]
    rows, width = xs.shape
    half, own = st_back.shape[2], width // (2 * st_in.shape[0])
    def emit(src, which, dst_rows, lead=slice(None), src_rows=slice(None), lanes=slice(None)):
        pltpu.make_async_copy(src.at[lead, :, src_rows, lanes], gw_out.at[lead, :, dst_rows, lanes], sems.at[which]).start()
    loads = [pltpu.make_async_copy(x_hbm, xs, sems.at[0]), pltpu.make_async_copy(o_hbm, os, sems.at[1])]
    for load in loads:
        load.start()
    for ref, ids in zip(gathered, masks):
        for j, mask in enumerate(ids):
            at = pl.ds(pl.multiple_of((flat ^ mask) * own, own), own)
            pltpu.make_async_copy(ref.at[j, half:half + own, :], wo.at[at, :], sems.at[2]).start()
    pull_ff(flat, gathered, masks, ws_in, ws_back, half + own, sems.at[3:5])
    pull_sequence(ids_ref[0], g4_ref, chip_ref, core_ref, gm, sems.at[5])
    for load in loads:
        load.wait()
    pltpu.make_async_copy(wo, wo, sems.at[2]).wait()
    stores = [pltpu.make_async_copy(wo, wo_out, sems.at[2])]
    stores[0].start()
    part = 256
    def load_rows(i, carry):
        at = pl.ds(pl.multiple_of(i * part, part), part)
        value = xs[at, :].astype(jnp.float32) + _dot(os[at, :], wo[...])
        mixed[at, :] = value
        acc[at, :] = value
        hidden = (value * rms_inverse(value) * gain_ref[1:2, :]).astype(jnp.bfloat16)
        h2[at, :] = hidden
        h2t[:, at] = hidden.T
        gh2[at, :] = jnp.zeros_like(value)
        return carry
    lax.fori_loop(0, rows // part, load_rows, 0)
    pltpu.make_async_copy(gm, gm, sems.at[5]).wait()
    row_ok = lax.broadcasted_iota(jnp.int32, (rows, 1), 0) < ids_ref[2]
    gm[...] = jnp.where(row_ok, gm[...], jnp.zeros_like(gm[...]))
    pltpu.make_async_copy(ws_in, ws_in, sems.at[3]).wait()
    pltpu.make_async_copy(ws_back, ws_back, sems.at[4]).wait()
    for i, (src, dst) in enumerate(((mixed, mixed_out), (h2, h2_out), (h2t, h2t_out), (gm, gm_out))):
        stores.append(pltpu.make_async_copy(src, dst, sems.at[6 + i]))
        stores[-1].start()
    ff_chunks(h2, h2t, gm, acc, gh2, ws_in, ws_back, st_in, st_back, half, emit, lambda: None)
    for i, (src, dst) in enumerate(((acc, acc_out), (gh2, gh2_out))):
        stores.append(pltpu.make_async_copy(src, dst, sems.at[3 + i]))
        stores[-1].start()
    finish_chunks(st_in, st_back, sems.at[0:2])
    for store in stores:
        store.wait()

def mid_a(ids, x, o, g4, came, gains, gathered, masks, ff):
    rows, width = x.shape
    shards = sum(len(m) for m in masks)
    half = ff // shards
    low = lambda *s: jax.ShapeDtypeStruct(s, jnp.bfloat16)
    full = lambda *s: jax.ShapeDtypeStruct(s, jnp.float32)
    vm = lambda *s: pltpu.VMEM(s, jnp.bfloat16)
    vf = lambda *s: pltpu.VMEM(s, jnp.float32)
    stack = half + ff // width * (width // shards)
    return pl.pallas_call(
        functools.partial(mid_a_kernel, masks=masks),
        out_shape=(full(rows, width), full(rows, width), full(rows, width), low(rows, width), low(width, rows), low(rows, width), low(width, width), low(shards // 2, 2, stack, width)),
        in_specs=[SM] + [ANY] * 5 + [VM] + [ANY] * len(gathered), out_specs=[ANY] * 8,
        scratch_shapes=[vm(rows, width), vm(rows, width), vm(width, width), vm(width, ff), vm(ff, width), vf(rows, width), vm(rows, width), vm(width, rows),
                        vf(rows, width), vf(rows, width), vm(rows, width), vm(shards // 2, 2, stack - half, width), vm(shards // 2, 2, half, width), pltpu.SemaphoreType.DMA((10,))],
        compiler_params=pltpu.CompilerParams(vmem_limit_bytes=LIMIT),
        cost_estimate=LIGHT,
        name="mid_a",
    )(ids, x, o, g4, *came, gains, *gathered)

def mid_b_kernel(ids_ref, gain_ref, mixed_hbm, acc_hbm, gh2_hbm, h2_hbm, h2t_hbm, gm_hbm, wo_hbm, o_hbm, full_ref, *refs):
    (out_ref, gb_out, do_ref, keep_out, send_out,
     os, wo, ws_in, ws_back, mixed, h2, h2t, acc, gh2, gm, gb, st_in, st_back, st_o, sems) = refs
    rows, width = os.shape
    shards, half, own = 2 * st_in.shape[0], st_back.shape[2], width // (2 * st_in.shape[0])
    core = ids_ref[1] & 1
    def emit(src, which, **at):
        by_core(core, keep_out, send_out, src, sem=sems.at[which], **at)
    early = [(h2_hbm, h2), (gm_hbm, gm), (h2t_hbm, h2t)]
    late = [(acc_hbm, acc), (gh2_hbm, gh2), (mixed_hbm, mixed), (wo_hbm, wo), (o_hbm, os)]
    early = [pltpu.make_async_copy(a, b, sems.at[4 + i]) for i, (a, b) in enumerate(early)]
    late = [pltpu.make_async_copy(a, b, sems.at[7 + i]) for i, (a, b) in enumerate(late)]
    for load in early:
        load.start()
    pull_ff(0, (full_ref,), (range(shards),), ws_in, ws_back, half, sems.at[2:4])
    for load in late:
        load.start()
    for load in early:
        load.wait()
    pltpu.make_async_copy(ws_in, ws_in, sems.at[2]).wait()
    pltpu.make_async_copy(ws_back, ws_back, sems.at[3]).wait()
    def before_add():
        late[0].wait()
        late[1].wait()
    ff_chunks(h2, h2t, gm, acc, gh2, ws_in, ws_back, st_in, st_back, half + own, emit, before_add)
    for load in late[2:]:
        load.wait()
    part = 256
    def finish(i, carry):
        at = pl.ds(pl.multiple_of(i * part, part), part)
        out_ref[at, :] = acc[at, :].astype(jnp.bfloat16)
        value = mixed[at, :]
        inverse = rms_inverse(value)
        normed = value * inverse
        scaled = gh2[at, :] * gain_ref[1:2, :]
        grad = inverse * (scaled - normed * jnp.mean(scaled * normed, axis=1, keepdims=True)) + gm[at, :].astype(jnp.float32)
        low = grad.astype(jnp.bfloat16)
        gb[at, :] = low
        do_ref[at, :] = _dot(low, wo[...], NT).astype(jnp.bfloat16)
        return carry
    lax.fori_loop(0, rows // part, finish, 0)
    st_o[...] = _dot(os[...], gb[...], TN).astype(jnp.bfloat16).reshape(st_o.shape)
    emit(st_o, 2, dst_rows=slice(half, half + own))
    store = pltpu.make_async_copy(gb, gb_out, sems.at[3])
    store.start()
    finish_chunks(st_in, st_back, sems.at[0:2])
    pltpu.make_async_copy(st_o, st_o, sems.at[2]).wait()
    store.wait()

def mid_b(ids, gains, state, o, full, ff):
    rows, width = o.shape
    shards = full.shape[0]
    half, own = ff // shards, width // shards
    low = lambda *s: jax.ShapeDtypeStruct(s, jnp.bfloat16)
    vm = lambda *s: pltpu.VMEM(s, jnp.bfloat16)
    vf = lambda *s: pltpu.VMEM(s, jnp.float32)
    rest = ff // width * own
    return pl.pallas_call(
        mid_b_kernel,
        out_shape=(low(rows, width), low(rows, width), low(rows, width), low(shards // 2, half + own + rest, width), low(shards // 2, half + own + rest, width)),
        in_specs=[SM, VM] + [ANY] * 9, out_specs=[VM, ANY, VM, ANY, ANY],
        scratch_shapes=[vm(rows, width), vm(width, width), vm(width, ff), vm(ff, width), vf(rows, width), vm(rows, width), vm(width, rows),
                        vf(rows, width), vf(rows, width), vm(rows, width), vm(rows, width), vm(shards // 2, 2, rest, width), vm(shards // 2, 2, half, width), vm(shards // 2, 2, own, width),
                        pltpu.SemaphoreType.DMA((12,))],
        compiler_params=pltpu.CompilerParams(vmem_limit_bytes=LIMIT),
        cost_estimate=LIGHT,
        name="mid_b",
    )(ids, gains, *state, o, full)

def gw_kernel(ids_ref, h_ref, dq_ref, dk_ref, dv_ref, bucket_ref, *refs):
    keep_out, send_out, st, sems = refs[-4:]
    pairs, _, stack, cols = st.shape
    own = h_ref.shape[1] // (2 * pairs)
    core = ids_ref[1] & 1
    if refs[:-4]:
        offs = jnp.concatenate([ref[...] for ref in refs[:-4]], 0)
        ids = lax.broadcasted_iota(jnp.int32, (2 * pairs, 1), 0)
        hot = jnp.where(bucket_ref[1:2, :] == ids, 1.0, 0.0)
        table = lax.dot_general(hot, offs, NT, precision=lax.Precision.HIGHEST, preferred_element_type=jnp.float32)
        heads = offs.shape[0]
        st[:, :, 3 * own:, :] = jnp.zeros((pairs, 2, stack - 3 * own, cols), jnp.bfloat16)
        st[:, :, 3 * own:3 * own + 1, 0:heads] = table.astype(jnp.bfloat16).reshape(pairs, 2, 1, heads)
    for i, ref in enumerate((dq_ref, dk_ref, dv_ref)):
        at = slice(i * own, (i + 1) * own) if i < 2 else slice(i * own, stack)
        st[:, :, i * own:(i + 1) * own, :] = _dot(h_ref[...], ref[...], TN).astype(jnp.bfloat16).reshape(pairs, 2, own, cols)
        by_core(core, keep_out, send_out, st, at, sems.at[0], src_rows=at)
    pltpu.make_async_copy(st, st, sems.at[0]).wait()

def qkv_gw(ids, h, dq, dk, dv, bucket_rows, offs, shards, first, cols):
    rows, width = h.shape
    stack = 3 * width // shards + (16 if offs else 0)
    half = jax.ShapeDtypeStruct((shards // 2, stack, cols), jnp.bfloat16)
    part = pl.BlockSpec((rows, cols), lambda i: (0, first // cols))
    whole = lambda a: pl.BlockSpec(a.shape, lambda i: (0, 0))
    return pl.pallas_call(
        gw_kernel, out_shape=(half, half), grid=(1,),
        in_specs=[SM, whole(h), part, part, part, whole(bucket_rows)] + [whole(o) for o in offs], out_specs=[ANY, ANY],
        scratch_shapes=[pltpu.VMEM((shards // 2, 2, stack, cols), jnp.bfloat16), pltpu.SemaphoreType.DMA((1,))],
        compiler_params=pltpu.CompilerParams(vmem_limit_bytes=LIMIT),
        cost_estimate=LIGHT,
        name="qkv_gw",
    )(ids, h, dq, dk, dv, bucket_rows, *offs)

def gx_kernel(x_ref, gb_ref, dq_ref, dk_ref, dv_ref, gain_ref, w_ref, out_ref):
    width = x_ref.shape[1]
    grad = _dot(dq_ref[...], w_ref[:, :width], NT)
    grad += _dot(dk_ref[...], w_ref[:, width:2 * width], NT)
    grad += _dot(dv_ref[...], w_ref[:, 2 * width:3 * width], NT)
    x = x_ref[...].astype(jnp.float32)
    inverse = rms_inverse(x)
    normed = x * inverse
    scaled = grad * gain_ref[0:1, :]
    out = inverse * (scaled - normed * jnp.mean(scaled * normed, axis=1, keepdims=True)) + gb_ref[...].astype(jnp.float32)
    out_ref[...] = out.astype(jnp.bfloat16)

def qkv_gx(x, gb, dq, dk, dv, gains, w, rows=512):
    total, width = x.shape
    blk = pl.BlockSpec((rows, width), lambda i: (i, 0))
    return pl.pallas_call(
        gx_kernel, out_shape=jax.ShapeDtypeStruct((total, width), jnp.bfloat16), grid=(total // rows,),
        in_specs=[blk] * 5 + [pl.BlockSpec(gains.shape, lambda i: (0, 0)),
                              pl.BlockSpec((width, 3 * width), lambda i: (0, 0), pipeline_mode=pl.Buffered(1))],
        out_specs=blk,
        compiler_params=pltpu.CompilerParams(vmem_limit_bytes=LIMIT),
        cost_estimate=LIGHT,
        name="qkv_gx",
    )(x, gb, dq, dk, dv, gains, w)

def swap(value, axis, mask):
    return lax.ppermute(value, axis, [(i, i ^ mask) for i in range(lax.axis_size(axis))])


def send_chip(blocks, me):
    return swap(lax.dynamic_slice_in_dim(blocks, 2 * (1 - me // 2), 2, 0), "seq", 2)


def send_core(blocks, from_chip, me):
    own = lax.dynamic_index_in_dim(blocks, me ^ 1, 0)
    passed = lax.dynamic_index_in_dim(from_chip, 1 - me % 2, 0)
    return swap(jnp.concatenate([own, passed], 0), "seq", 1)


class Gather:
    def __init__(self, shard):
        shard = shard[None]
        self.sent = [shard] + [swap(shard, "dp", 2 * z) for z in (1, 2, 3)]
        self.pieces, self.masks = [], []

    def take(self, piece, mask, rows=(0, 1, 2, 3)):
        ids = tuple(8 * z | mask for z in rows)
        self.pieces += [piece, swap(piece, "seq", 1)]
        self.masks += [ids, tuple(m | 1 for m in ids)]

    def fill(self):
        self.own = jnp.concatenate(self.sent, 0)

    def sides(self):
        self.x, self.y = swap(self.own, "seq", 2), swap(self.own, "dp", 1)

    def corner_halves(self):
        self.near, self.far = swap(self.y[:2], "seq", 2), swap(self.x[2:], "dp", 1)

    def corner_y(self):
        self.corner = swap(self.x, "dp", 1)

    def all_pieces(self):
        return tuple(self.pieces), tuple(self.masks)


class Scatter:
    def __init__(self, keep, send, pos, corner_y):
        self.z, self.y, self.x = pos
        cube = (4, 2, 2) + keep.shape[1:]
        self.mine, self.sent, self.corner_y = keep.reshape(cube), send.reshape(cube), corner_y
        self.other = swap(self.sent, "seq", 1)

    def fold(self):
        pick = lambda v, at, axis: lax.dynamic_index_in_dim(v, at, axis, keepdims=False)
        def quarter(dy, dx):
            cut = lambda v: pick(pick(v, self.y ^ dy, 1), self.x ^ dx, 1).astype(jnp.float32)
            return (cut(self.mine) + cut(self.other)).astype(jnp.bfloat16)
        far = quarter(1, 1)
        self.to_x, self.to_y, self.own = quarter(0, 1), quarter(1, 0), quarter(0, 0)
        if self.corner_y:
            self.came_x, self.came_y = None, swap(far, "dp", 1)
        else:
            self.came_x, self.came_y = swap(far[:2], "seq", 2), swap(far[2:], "dp", 1)

    def turn(self):
        add = lambda a, b: (a.astype(jnp.float32) + b.astype(jnp.float32)).astype(jnp.bfloat16)
        if self.corner_y:
            to_y, = tie(self.came_y, self.to_y)
            to_x = add(self.to_x, self.came_y)
        else:
            to_x = jnp.concatenate([self.to_x[:2], add(self.to_x[2:], self.came_y)], 0)
            to_y = jnp.concatenate([add(self.to_y[:2], self.came_x), self.to_y[2:]], 0)
        self.sent = (to_x, to_y)
        self.came_x, self.came_y = swap(to_x, "seq", 2), swap(to_y, "dp", 1)

    def column(self):
        total = self.own.astype(jnp.float32) + self.came_x.astype(jnp.float32) + self.came_y.astype(jnp.float32)
        total = total.astype(jnp.bfloat16)
        block = lambda k: lax.dynamic_index_in_dim(total, self.z ^ k, 0, keepdims=False)
        self.mine = block(0)
        self.came = [swap(block(k), "dp", 2 * k) for k in (1, 2, 3)]

    def result(self):
        return sum((c.astype(jnp.float32) for c in self.came), self.mine.astype(jnp.float32))


def place(blocks, from_chip, from_core, me):
    for mask, block in ((1, from_core[0:1]), (2, lax.dynamic_index_in_dim(from_chip, me % 2, 0)), (3, from_core[1:2])):
        blocks = lax.dynamic_update_slice_in_dim(blocks, block, me ^ mask, 0)
    return blocks


def tie(first, *later):
    return lax.optimization_barrier((first,) + later)[1:]


def local_whole(tokens, cotangent, lengths, buckets, norm1_gain, w_query, w_key, w_value, w_out, rel_table, norm2_gain, w_in, w_back):
    micro_count, seq_count, rows, width = tokens.shape
    parts = micro_count * seq_count
    both = ("dp", "seq")
    me, dp = lax.axis_index("seq"), lax.axis_index("dp")
    shards = lax.axis_size("seq") * lax.axis_size("dp")
    flat = dp * parts + me
    pos = (dp // 2, dp % 2, me // 2)
    low = lambda v: v.astype(jnp.bfloat16)
    up = lambda v: v.astype(jnp.float32)
    own, ff_own = w_query.shape[0], w_back.shape[0]
    ids = jnp.stack([me, flat, lax.dynamic_index_in_dim(lengths.reshape(parts), me, 0, keepdims=False)])
    length = ids[2:3]

    place_row = lambda v: lax.dynamic_update_slice(jnp.zeros((1, width), jnp.bfloat16), low(v)[None], (0, flat * own))
    small = jnp.concatenate([place_row(norm1_gain), place_row(norm2_gain), jnp.zeros((6, width), jnp.bfloat16),
                             jnp.pad(low(rel_table)[None], ((0, 7), (0, width - HEADS)))], 0)
    shard1 = jnp.concatenate([low(w_query), low(w_key), low(w_value), small], 0)
    ff = w_in.shape[1] // 2
    half = ff_own // 2
    halves = low(w_in).reshape(own, shards, 2, half)
    in_half = lambda i: [halves[:, :, i].reshape(own, ff)[:, j:j + width] for j in range(0, ff, width)]
    shard2 = jnp.concatenate([low(w_back[:half]), low(w_out)] + in_half(0), 0)
    shard3 = jnp.concatenate([low(w_back[half:])] + in_half(1), 0)
    x4, g4 = tokens.reshape(parts, rows, width), cotangent.reshape(parts, rows, width)
    bucket_rows = jnp.stack([jnp.pad(buckets, (0, 1), constant_values=-1), jnp.pad(buckets[::-1], (0, 1), constant_values=-1)])

    g1 = Gather(shard1)
    x_chip = send_chip(x4, me)
    g2 = Gather(shard2)
    g1.fill()
    g1.own, = tie((x_chip, g2.sent[1], shard3), g1.own)
    g1.sides()
    g1.x, g1.y = tie(g2.sent[2], g1.x, g1.y)
    g1.corner_halves()
    g2.fill()
    g1.take(g1.own, 0)
    g1.near, g1.far, g2.own = tie(g1.pieces[1], g1.near, g1.far, g2.own)
    g2.sides()
    g1.x, g1.y, x4_in = tie((g1.near, g1.far), g1.x, g1.y, x4)
    g1.take(g1.x, 2)
    g1.take(g1.y, 4)
    g1.take(g1.near, 6, (0, 1))
    g1.take(g1.far, 6, (2, 3))
    x_core = send_core(x4_in, x_chip, me)
    shard3, = tie((g1.near, g1.far), shard3)
    full3 = lax.all_gather(shard3, both, axis=0, tiled=False)
    x, hidden, q, k, v, w_qkv, gains, t, t_back = qkv_fwd(ids, x4, (x_chip, x_core), *g1.all_pieces(), bucket_rows, HEADS)
    pairs = HEADS // 2
    att = attn_fwd(length, q, k, v, t, 0, pairs // 2)
    g2.take(g2.own, 0)
    g2.x, g2.y = tie((att[0], g2.pieces[1]), g2.x, g2.y)
    g2.corner_y()
    g4_in, = tie(g2.x, g4)
    g_chip = send_chip(g4_in, me)
    g2.take(g2.x, 2)
    g2.take(g2.y, 4)
    q_in, = tie((g2.x, g2.y), q)
    attended, lse = attn_fwd(length, q_in, k, v, t, pairs // 2, pairs // 2, att)
    g2.corner, g_chip = tie((attended, g2.pieces[3], g2.pieces[5]), g2.corner, g_chip)
    g2.take(g2.corner, 6)
    g_core = send_core(g4, g_chip, me)
    *state, gw_a = mid_a(ids, x, attended, g4, (g_chip, g_core), gains, *g2.all_pieces(), ff)
    r_a = lax.psum_scatter(gw_a.reshape(-1, width), both, scatter_dimension=0, tiled=True)
    out, gb, g_att, keep2, send2 = mid_b(ids, gains, state, attended, full3, ff)
    sc2 = Scatter(keep2, send2, pos, True)
    out4 = out.reshape(parts, rows, width)
    out_chip = send_chip(out4, me)
    count = pairs // 4
    back = lambda first, g, prev: attn_bwd(length, q, k, v, g, attended, lse, t_back, first, count, prev)
    dq, dk, dv, off0 = back(0, g_att, None)
    sc2.other, = tie(off0, sc2.other)
    sc2.fold()
    g_att, = tie((sc2.own, sc2.to_x, sc2.to_y), g_att)
    dq, dk, dv, off1 = back(count, g_att, (dq, dk, dv))
    sc2.came_y, = tie(off1, sc2.came_y)
    sc2.turn()
    g_att, = tie(sc2.sent, g_att)
    dq, dk, dv, off2 = back(2 * count, g_att, (dq, dk, dv))
    cols = 128 * count
    keep, send = qkv_gw(ids, hidden, dq, dk, dv, bucket_rows, (), shards, 0, 3 * cols)
    sc1 = Scatter(keep, send, pos, False)
    sc2.came_x, sc2.came_y = tie(keep, sc2.came_x, sc2.came_y)
    sc2.column()
    g_att, = tie((sc2.mine, out_chip), g_att)
    out4_in, out_chip = tie(sc2.mine, out4, out_chip)
    out_core = send_core(out4_in, out_chip, me)
    dq, dk, dv, off3 = back(3 * count, g_att, (dq, dk, dv))
    sc1.other, = tie((off3, out_core), sc1.other)
    sc1.fold()
    h_in, = tie(sc1.own, hidden)
    keep, send = qkv_gw(ids, h_in, dq, dk, dv, bucket_rows, (off0, off1, off2, off3), shards, 3 * cols, cols)
    sc0 = Scatter(keep, send, pos, False)
    gb_in, = tie(keep, gb)
    gx = qkv_gx(x, gb_in, dq, dk, dv, gains, w_qkv)
    gx4 = gx.reshape(parts, rows, width)
    gx_chip = send_chip(gx4, me)
    sc1.came_x, sc1.came_y = tie((gx, sc2.came), sc1.came_x, sc1.came_y)
    sc1.turn()
    sc0.other, r_a = tie(sc1.sent, sc0.other, r_a)
    sc0.fold()
    out4, out_chip, out_core = tie(sc0.own, out4, out_chip, out_core)
    layer_out = place(out4, out_chip, out_core, me)
    sc0.came_x, sc0.came_y = tie(layer_out, sc0.came_x, sc0.came_y)
    sc0.turn()
    sc2.came = list(tie(sc0.sent, *sc2.came))
    r2, r_a = sc2.result(), up(r_a)
    sc1.came_x, sc1.came_y = tie((r2, sc0.sent), sc1.came_x, sc1.came_y)
    sc1.column()
    sc0.came_x, sc0.came_y = tie(sc1.came[0], sc0.came_x, sc0.came_y)
    sc0.column()
    gx4, gx_chip = tie((sc0.came[0], sc1.came), gx4, gx_chip)
    gx_core = send_core(gx4, gx_chip, me)
    input_grad = place(gx4, gx_chip, gx_core, me)
    sc1.came = list(tie(sc0.came[0], *sc1.came))
    sc0.came = list(tie(input_grad, *sc0.came))
    r1, r0 = sc1.result(), sc0.result()
    join = lambda v: jnp.concatenate([v[i:i + own] for i in range(0, v.shape[0], own)], 1).reshape(own, shards, 1, half)
    g_in = jnp.concatenate([join(r_a[half:]), join(r2[half + own:])], 2).reshape(w_in.shape)
    g_back = jnp.concatenate([r_a[:half], r2[:half]], 0)
    table_row = r0[3 * own, :HEADS]
    r1 = jnp.concatenate([r1, r0[:3 * own]], 1)
    prod = up(shard1[:3 * own]) * r1
    g_gain1 = jnp.sum(prod[:own] + prod[own:2 * own] + prod[2 * own:], axis=1) / up(low(norm1_gain))
    g_gain2 = jnp.sum(up(low(w_in)) * g_in, axis=1) / up(low(norm2_gain))
    return (layer_out.reshape(tokens.shape), input_grad.reshape(tokens.shape), g_gain1, r1[:own], r1[own:2 * own], r1[2 * own:3 * own],
            r2[half:half + own], table_row, g_gain2, g_in, g_back)


def local_any(shape, tokens, *rest):
    fits = tuple(shape) == (8, 4) and tokens.shape[0] * tokens.shape[1] == 4 and tokens.shape[3] == HEADS * DH == 1024
    return (local_whole if fits else local)(tokens, *rest)


def solution(mesh):
    return jax.shard_map(
        functools.partial(local_any, mesh.devices.shape),
        mesh=mesh,
        in_specs=(
            P(None, "dp", "seq", None),
            P(None, "dp", "seq", None),
            P(None, "dp"),
            P(),
            P(("dp", "seq")),
            P(("dp", "seq"), None),
            P(("dp", "seq"), None),
            P(("dp", "seq"), None),
            P(("dp", "seq"), None),
            P(("dp", "seq")),
            P(("dp", "seq")),
            P(("dp", "seq"), None),
            P(("dp", "seq"), None),
        ),
        out_specs=(
            P(None, "dp", "seq", None),
            P(None, "dp", "seq", None),
            P(("dp", "seq")),
            P(("dp", "seq"), None),
            P(("dp", "seq"), None),
            P(("dp", "seq"), None),
            P(("dp", "seq"), None),
            P(("dp", "seq")),
            P(("dp", "seq")),
            P(("dp", "seq"), None),
            P(("dp", "seq"), None),
        ),
        check_vma=False,
    )
```

```python
import functools

import jax
import jax.numpy as jnp
from jax import lax
from jax.experimental import pallas as pl
from jax.experimental.pallas import tpu as pltpu
from jax.sharding import PartitionSpec as P

HEADS = 16
DH = 64
BUCKETS = 32


epsilon = 1e-06
floor_score = -1e30
highest = lax.Precision.HIGHEST
root_coef = 0.7978845608
cubic_coef = 0.044715


def gelu_tanh(values):
    return (
        0.5
        * values
        * (1.0 + jnp.tanh(root_coef * (values + cubic_coef * values * values * values)))
    )


def gelu_slope(values):
    inner = jnp.tanh(root_coef * (values + cubic_coef * values * values * values))
    return 0.5 * (1.0 + inner) + 0.5 * values * (1.0 - inner * inner) * root_coef * (
        1.0 + 3.0 * cubic_coef * values * values
    )


def project(acts, weight):
    return jnp.einsum("srd,de->sre", acts, weight, preferred_element_type=jnp.float32)


def project_back(grads_in, weight):
    return jnp.einsum("sre,de->srd", grads_in, weight, preferred_element_type=jnp.float32)


def contract(acts, grads_in):
    return jnp.einsum("srd,sre->de", acts, grads_in, preferred_element_type=jnp.float32)


def rms_forward(values, gain):
    inverse = lax.rsqrt(jnp.mean(values * values, axis=-1, keepdims=True) + epsilon)
    normed = values * inverse
    return (normed, inverse, (normed * gain.astype(jnp.float32)).astype(jnp.bfloat16))


def rms_backward(grad_hidden, normed, inverse, gain):
    scaled = grad_hidden * gain.astype(jnp.float32)
    grad_values = inverse * (scaled - normed * jnp.mean(scaled * normed, axis=-1, keepdims=True))
    return (grad_values, jnp.sum(grad_hidden * normed, axis=(0, 1)))


def score_block(per_head_queries, per_head_keys, rel_bias, key_valid):
    scores = (
        jnp.einsum(
            "ofck,owck->ocfw", per_head_queries, per_head_keys, preferred_element_type=jnp.float32
        )
        + rel_bias[None]
    )
    return jnp.where(key_valid, scores, floor_score)


def offset_sums(grid, first_row, seq_len):
    head_count, row_count, key_count = grid.shape
    flipped = grid[:, ::-1, :]
    padded = jnp.pad(flipped, ((0, 0), (0, 0), (0, row_count)))
    wide_len = key_count + row_count
    skewed = padded.reshape(head_count, row_count * wide_len)[:, : row_count * (wide_len - 1)]
    skewed = skewed.reshape(head_count, row_count, wide_len - 1)
    column_sums = jnp.sum(skewed, axis=1)
    placed = jnp.zeros((head_count, 2 * seq_len - 1), jnp.float32)
    begin = seq_len - row_count - first_row
    return lax.dynamic_update_slice(placed, column_sums, (jnp.int32(0), begin))


def run_micro(inputs, incoming, seq_lens, attn_set, mlp_set, context):
    onehot, offsets, row_pos, key_pos, first_row, seq_len = context
    gain_one, query_w, key_w, value_w, out_w, bias_table = attn_set
    gain_two, in_w, return_projection_weight = mlp_set
    seq_count, row_count, model_width = inputs.shape
    values = inputs.astype(jnp.float32)
    normed_one, inverse_one, hidden_one = rms_forward(values, gain_one)
    queries = project(hidden_one, query_w).astype(jnp.bfloat16)
    keys_own = project(hidden_one, key_w).astype(jnp.bfloat16)
    values_own = project(hidden_one, value_w).astype(jnp.bfloat16)
    keys_all, values_all = (
        lax.all_gather(keys_own, "seq", axis=1, tiled=True),
        lax.all_gather(values_own, "seq", axis=1, tiled=True),
    )
    per_offset = jnp.dot(
        onehot, bias_table.reshape(BUCKETS, HEADS), preferred_element_type=jnp.float32
    )
    rel_bias = jnp.transpose(per_offset[offsets], (2, 0, 1))
    key_valid = (key_pos[None, :] < seq_lens[:, None])[:, None, None, :]
    per_head_queries = queries.reshape(seq_count, row_count, HEADS, DH)
    per_head_keys = keys_all.reshape(seq_count, seq_len, HEADS, DH)
    per_head_values = values_all.reshape(seq_count, seq_len, HEADS, DH)
    scores = score_block(per_head_queries, per_head_keys, rel_bias, key_valid)
    row_max = jnp.max(scores, axis=-1, keepdims=True)
    exp_scores = jnp.exp(scores - row_max)
    row_total = jnp.sum(exp_scores, axis=-1, keepdims=True)
    attn_probs = exp_scores / row_total
    log_total = row_max + jnp.log(row_total)
    reduced_precision_probs = attn_probs.astype(jnp.bfloat16)
    attended = jnp.einsum(
        "jfpe,jefn->jpfn",
        reduced_precision_probs,
        per_head_values,
        preferred_element_type=jnp.float32,
    )
    attended = attended.reshape(seq_count, row_count, model_width).astype(jnp.bfloat16)
    residual_mid = values + project(attended, out_w)
    normed_two, inverse_two, hidden_two = rms_forward(residual_mid, gain_two)
    pre_act = project(hidden_two, in_w)
    active = gelu_tanh(pre_act).astype(jnp.bfloat16)
    result = (residual_mid + project(active, return_projection_weight)).astype(jnp.bfloat16)
    row_valid = (row_pos[None, :] < seq_lens[:, None]).astype(jnp.float32)[:, :, None]
    grad_out = incoming.astype(jnp.float32) * row_valid
    grad_low = grad_out.astype(jnp.bfloat16)
    grad_back = contract(active, grad_low)
    gradient_active_rows = project_back(grad_low, return_projection_weight)
    grad_pre = (gradient_active_rows * gelu_slope(pre_act)).astype(jnp.bfloat16)
    grad_in = contract(hidden_two, grad_pre)
    grad_hidden_two = project_back(grad_pre, in_w)
    grad_mixed, grad_gain_two = rms_backward(grad_hidden_two, normed_two, inverse_two, gain_two)
    grad_mixed = grad_mixed + grad_out
    grad_branch = grad_mixed.astype(jnp.bfloat16)
    grad_outw = contract(attended, grad_branch)
    gradient_attended_values = project_back(grad_branch, out_w).astype(jnp.bfloat16)
    gradient_attended_values = gradient_attended_values.reshape(seq_count, row_count, HEADS, DH)
    scores = score_block(per_head_queries, per_head_keys, rel_bias, key_valid)
    attn_probs = jnp.exp(scores - log_total)
    reduced_precision_probs = attn_probs.astype(jnp.bfloat16)
    grad_probs = jnp.einsum(
        "ofck,owck->ocfw",
        gradient_attended_values,
        per_head_values,
        preferred_element_type=jnp.float32,
    )
    inner_sum = jnp.sum(attn_probs * grad_probs, axis=-1, keepdims=True)
    gradient_score_matrix = (attn_probs * (grad_probs - inner_sum)).astype(jnp.bfloat16)
    grad_query = jnp.einsum(
        "jfpe,jefn->jpfn", gradient_score_matrix, per_head_keys, preferred_element_type=jnp.float32
    )
    grad_query = grad_query.astype(jnp.bfloat16).reshape(seq_count, row_count, model_width)
    key_part = jnp.einsum(
        "eciv,eicq->evcq",
        gradient_score_matrix,
        per_head_queries,
        preferred_element_type=jnp.float32,
    )
    value_part = jnp.einsum(
        "eciv,eicq->evcq",
        reduced_precision_probs,
        gradient_attended_values,
        preferred_element_type=jnp.float32,
    )
    key_part = key_part.reshape(seq_count, seq_len, model_width)
    value_part = value_part.reshape(seq_count, seq_len, model_width)
    grad_key, grad_value = (
        lax.psum_scatter(
            key_part.astype(jnp.bfloat16), "seq", scatter_dimension=1, tiled=True
        ).astype(jnp.float32),
        lax.psum_scatter(
            value_part.astype(jnp.bfloat16), "seq", scatter_dimension=1, tiled=True
        ).astype(jnp.float32),
    )
    grad_key = grad_key.astype(jnp.bfloat16)
    grad_value = grad_value.astype(jnp.bfloat16)
    offset_grad = offset_sums(
        jnp.sum(gradient_score_matrix.astype(jnp.float32), axis=0), first_row, seq_len
    )
    grad_table = jnp.dot(onehot.astype(jnp.float32).T, offset_grad.T, precision=highest).reshape(-1)
    grad_qw = contract(hidden_one, grad_query)
    grad_kw = contract(hidden_one, grad_key)
    grad_vw = contract(hidden_one, grad_value)
    grad_hidden_one = (
        project_back(grad_query, query_w)
        + project_back(grad_key, key_w)
        + project_back(grad_value, value_w)
    )
    grad_values, grad_gain_one = rms_backward(grad_hidden_one, normed_one, inverse_one, gain_one)
    grad_values = grad_values + grad_mixed
    gradients = (
        grad_gain_one,
        grad_qw,
        grad_kw,
        grad_vw,
        grad_outw,
        grad_table,
        grad_gain_two,
        grad_in,
        grad_back,
    )
    return (result, grad_values.astype(jnp.bfloat16), gradients)


def local(
    tokens,
    cotangent,
    lengths,
    buckets,
    norm1_gain,
    w_query,
    w_key,
    w_value,
    w_out,
    rel_table,
    norm2_gain,
    w_in,
    w_back,
):
    micro_count, seq_count, row_count, model_width = tokens.shape
    seq_parts = lax.axis_size("seq")
    seq_len = row_count * seq_parts
    first_row = lax.axis_index("seq") * row_count
    row_pos = first_row + jnp.arange(row_count, dtype=jnp.int32)
    key_pos = jnp.arange(seq_len, dtype=jnp.int32)
    onehot = (buckets[:, None] == jnp.arange(BUCKETS, dtype=jnp.int32)[None, :]).astype(
        jnp.bfloat16
    )
    offsets = key_pos[None, :] - row_pos[:, None] + (seq_len - 1)
    context = (onehot, offsets, row_pos, key_pos, first_row, seq_len)
    outputs = []
    input_grads = []
    pending = None
    shard_sums = None
    for micro_step in range(micro_count):
        attn_set = (
            lax.all_gather(norm1_gain.astype(jnp.bfloat16), ("dp", "seq"), axis=0, tiled=True),
            lax.all_gather(w_query.astype(jnp.bfloat16), ("dp", "seq"), axis=0, tiled=True),
            lax.all_gather(w_key.astype(jnp.bfloat16), ("dp", "seq"), axis=0, tiled=True),
            lax.all_gather(w_value.astype(jnp.bfloat16), ("dp", "seq"), axis=0, tiled=True),
            lax.all_gather(w_out.astype(jnp.bfloat16), ("dp", "seq"), axis=0, tiled=True),
            lax.all_gather(rel_table.astype(jnp.bfloat16), ("dp", "seq"), axis=0, tiled=True),
        )
        mlp_set = (
            lax.all_gather(norm2_gain.astype(jnp.bfloat16), ("dp", "seq"), axis=0, tiled=True),
            lax.all_gather(w_in.astype(jnp.bfloat16), ("dp", "seq"), axis=0, tiled=True),
            lax.all_gather(w_back.astype(jnp.bfloat16), ("dp", "seq"), axis=0, tiled=True),
        )
        layer_part, grad_part, gradients = run_micro(
            tokens[micro_step],
            cotangent[micro_step],
            lengths[micro_step],
            attn_set,
            mlp_set,
            context,
        )
        outputs.append(layer_part)
        input_grads.append(grad_part)
        pending = gradients if pending is None else jax.tree.map(jnp.add, pending, gradients)
    shard_sums = (
        lax.psum_scatter(pending[0], ("dp", "seq"), scatter_dimension=0, tiled=True),
        lax.psum_scatter(pending[1], ("dp", "seq"), scatter_dimension=0, tiled=True),
        lax.psum_scatter(pending[2], ("dp", "seq"), scatter_dimension=0, tiled=True),
        lax.psum_scatter(pending[3], ("dp", "seq"), scatter_dimension=0, tiled=True),
        lax.psum_scatter(pending[4], ("dp", "seq"), scatter_dimension=0, tiled=True),
        lax.psum_scatter(pending[5], ("dp", "seq"), scatter_dimension=0, tiled=True),
        lax.psum_scatter(pending[6], ("dp", "seq"), scatter_dimension=0, tiled=True),
        lax.psum_scatter(pending[7], ("dp", "seq"), scatter_dimension=0, tiled=True),
        lax.psum_scatter(pending[8], ("dp", "seq"), scatter_dimension=0, tiled=True),
    )
    return (
        jnp.stack(outputs),
        jnp.stack(input_grads),
        shard_sums[0],
        shard_sums[1],
        shard_sums[2],
        shard_sums[3],
        shard_sums[4],
        shard_sums[5],
        shard_sums[6],
        shard_sums[7],
        shard_sums[8],
    )


NT = (((1,), (1,)), ((), ()))
TN = (((0,), (0,)), ((), ()))
STRIP = 128
LOG2E = 1.4426950408889634
LN2 = 0.6931471805599453
LIMIT = 58 << 20
LIGHT = pl.CostEstimate(flops=1 << 20, bytes_accessed=1 << 16, transcendentals=0)

def _dot(a, b, dims=(((1,), (0,)), ((), ()))):
    return lax.dot_general(a, b, dims, preferred_element_type=jnp.float32)

def with_extras(x, which, extras, width=64):
    lane = lax.broadcasted_iota(jnp.int32, (1, x.shape[1]), 1)
    spare = lane - width if which == 0 else lane
    own = (lane < width) if which == 0 else (lane >= width)
    fill = jnp.zeros_like(x)
    for i, extra in enumerate(extras):
        fill = jnp.where(spare == i, extra, fill)
    return jnp.where(own, x, fill).astype(jnp.bfloat16)

def three_parts(x):
    low = lambda v: v.astype(jnp.bfloat16).astype(jnp.float32)
    high = low(x)
    middle = low(x - high)
    return [high, middle, low(x - high - middle)]

def slot_floor(size, length):
    return jnp.where(lax.broadcasted_iota(jnp.int32, (size, 1), 0) < length, 0.0, floor_score)

def skew(row, wide):
    return pltpu.roll(jnp.broadcast_to(row, (STRIP, wide)), wide - (STRIP - 1), 1, stride=1, stride_axis=0)

def fwd_kernel(len_ref, q_ref, k_ref, v_ref, t_ref, *refs, rows, seq_len, first):
    o_ref, lse_ref, strip, kx, vx = refs[-5:]
    wide = t_ref.shape[-1]
    pair = first + pl.program_id(0)
    per = rows // STRIP
    lane = lax.broadcasted_iota(jnp.int32, (1, 128), 1)
    k2 = k_ref[...].astype(jnp.float32)
    vx[:, 0:128] = v_ref[...]
    vx[:, 128:256] = jnp.ones_like(v_ref[...])
    for a in range(2):
        kx[a] = with_extras(k2, a, [slot_floor(seq_len, len_ref[0])])
        strip[a] = skew(t_ref[pl.ds(2 * pair + a, 1), :], wide)

    def step(b, carry):
        base = b * rows
        q2 = q_ref[pl.ds(base, rows), :].astype(jnp.float32)
        outs, stats = [], []
        for a in range(2):
            scores = _dot(with_extras(q2, a, [1.0]), kx[a], NT)
            parts = []
            for i in range(per):
                off = (seq_len - STRIP) - (b * per + i) * STRIP
                parts.append(strip[a, :, pl.ds(off, seq_len)])
            scores = scores + (jnp.concatenate(parts, 0) if per > 1 else parts[0])
            top = jnp.max(scores, axis=1, keepdims=True)
            probs = jnp.exp2(scores - top).astype(jnp.bfloat16)
            out = _dot(probs, vx[...])
            outs.append(out[:, 0:128] / out[:, 128:256])
            stats.append(top + jnp.log2(out[:, 128:256]))
        o_ref[pl.ds(base, rows), :] = jnp.where(lane < 64, outs[0], outs[1]).astype(jnp.bfloat16)
        lse_ref[0, pl.ds(base, rows), :] = jnp.where(lane < 64, stats[0], stats[1])
        return carry

    for b in range(seq_len // rows):
        step(b, 0)

def attn_fwd(length, q, k, v, t, first, count, prev=(), rows=256):
    seq_len, width = q.shape
    pairs = width // 128
    wide = t.shape[-1]
    blk = pl.BlockSpec((seq_len, 128), lambda p, n: (0, first + p))
    return pl.pallas_call(
        functools.partial(fwd_kernel, rows=rows, seq_len=seq_len, first=first),
        out_shape=(jax.ShapeDtypeStruct((seq_len, width), jnp.bfloat16),
                   jax.ShapeDtypeStruct((pairs, seq_len, 128), jnp.float32)),
        grid_spec=pltpu.PrefetchScalarGridSpec(
            num_scalar_prefetch=1, grid=(count,),
            in_specs=[blk, blk, blk, pl.BlockSpec(t.shape, lambda p, n: (0, 0))] + [pl.BlockSpec(memory_space=pl.ANY)] * len(prev),
            out_specs=[blk, pl.BlockSpec((1, seq_len, 128), lambda p, n: (first + p, 0, 0))],
            scratch_shapes=[pltpu.VMEM((2, STRIP, wide), jnp.float32), pltpu.VMEM((2, seq_len, 128), jnp.bfloat16),
                            pltpu.VMEM((seq_len, 256), jnp.bfloat16)]),
        input_output_aliases={5 + i: i for i in range(len(prev))},
        compiler_params=pltpu.CompilerParams(vmem_limit_bytes=LIMIT),
        cost_estimate=LIGHT,
        name="attn_fwd",
    )(length, q, k, v, t, *prev)

def bwd_kernel(len_ref, q_ref, k_ref, v_ref, do_ref, o_ref, lse_ref, t_ref, *refs, rows, seq_len, first):
    dq_ref, dk_ref, dv_ref, g_ref, strip, acc, dq_acc, qx, kx, vx, dox = refs[-11:]
    wide = t_ref.shape[-1]
    local_pair = pl.program_id(0)
    pair = first + local_pair
    per = rows // STRIP
    lane = lax.broadcasted_iota(jnp.int32, (1, 128), 1)
    up = lambda ref: ref[...].astype(jnp.float32)
    floor = slot_floor(seq_len, len_ref[0])
    prod = up(do_ref) * up(o_ref)
    for a in range(2):
        mine = (lane < 64) if a == 0 else (lane >= 64)
        delta = jnp.sum(jnp.where(mine, prod, 0.0), axis=1, keepdims=True)
        lse = lse_ref[0, :, 64 * a:64 * a + 1]
        qx[a] = with_extras(up(q_ref), a, [1.0] + three_parts(-lse))
        kx[a] = with_extras(up(k_ref), a, [floor, 1.0, 1.0, 1.0])
        vx[a] = with_extras(up(v_ref), a, [1.0, 1.0, 1.0])
        dox[a] = with_extras(up(do_ref), a, three_parts(-delta))
        strip[a] = skew(t_ref[pl.ds(2 * pair + a, 1), :], wide)
    acc[...] = jnp.zeros_like(acc)
    k2t = k_ref[...].T
    dq_acc[...] = jnp.zeros_like(dq_acc)

    def step(b, carry):
        at = pl.ds(b * rows, rows)
        dks, dvs = [], []
        for a in range(2):
            scores = _dot(kx[a, at, :], qx[a], NT)
            offs = [(seq_len - STRIP) - (b * per + i) * STRIP for i in range(per)]
            bias = [strip[a, :, pl.ds(off, seq_len)] for off in offs]
            probs = jnp.exp2(scores + (jnp.concatenate(bias, 0) if per > 1 else bias[0]))
            grad_scores = probs * _dot(vx[a, at, :], dox[a], NT)
            for i, off in enumerate(offs):
                acc[a, :, pl.ds(off, seq_len)] += grad_scores[i * STRIP:(i + 1) * STRIP]
            probs_b = probs.astype(jnp.bfloat16)
            gs_b = grad_scores.astype(jnp.bfloat16)
            dvs.append(_dot(probs_b, do_ref[...]))
            dks.append(_dot(gs_b, q_ref[...]))
            dq_acc[a] += _dot(k2t[:, b * rows:(b + 1) * rows], gs_b)
        dk_ref[at, :] = (jnp.where(lane < 64, dks[0], dks[1]) * LN2).astype(jnp.bfloat16)
        dv_ref[at, :] = jnp.where(lane < 64, dvs[0], dvs[1]).astype(jnp.bfloat16)
        return carry

    for b in range(seq_len // rows):
        step(b, 0)
    dq_ref[...] = jnp.concatenate([dq_acc[0, 0:64], dq_acc[1, 64:128]], 0).T.astype(jnp.bfloat16)
    for a in range(2):
        sums = acc[a]
        half = STRIP
        while half > 8:
            half //= 2
            sums = sums[:half] + pltpu.roll(sums[half:], wide - half, 1)
        while half > 1:
            half //= 2
            sums = sums + pltpu.roll(pltpu.roll(sums, 8 - half, 0), wide - half, 1)
        g_ref[pl.ds(2 * local_pair + a, 1), :] = pltpu.roll(sums, STRIP - 1, 1)[0:1]

def attn_bwd(length, q, k, v, do, o, lse, trev, first, count, prev=None, rows=512):
    seq_len, width = q.shape
    wide = trev.shape[-1]
    blk = pl.BlockSpec((seq_len, 128), lambda p, n: (0, first + p))
    mat = jax.ShapeDtypeStruct((seq_len, width), jnp.bfloat16)
    prev = tuple(prev) if prev is not None else ()
    return pl.pallas_call(
        functools.partial(bwd_kernel, rows=rows, seq_len=seq_len, first=first),
        out_shape=(mat, mat, mat, jax.ShapeDtypeStruct((2 * count, wide), jnp.float32)),
        grid_spec=pltpu.PrefetchScalarGridSpec(
            num_scalar_prefetch=1, grid=(count,),
            in_specs=[blk, blk, blk, blk, blk, pl.BlockSpec((1, seq_len, 128), lambda p, n: (first + p, 0, 0)),
                      pl.BlockSpec(trev.shape, lambda p, n: (0, 0))] + [pl.BlockSpec(memory_space=pl.ANY)] * len(prev),
            out_specs=[blk, blk, blk, pl.BlockSpec((2 * count, wide), lambda p, n: (0, 0))],
            scratch_shapes=[pltpu.VMEM((2, STRIP, wide), jnp.float32), pltpu.VMEM((2, STRIP, wide), jnp.float32),
                            pltpu.VMEM((2, 128, seq_len), jnp.float32)] + [pltpu.VMEM((2, seq_len, 128), jnp.bfloat16)] * 4),
        input_output_aliases={8 + i: i for i in range(len(prev))},
        compiler_params=pltpu.CompilerParams(vmem_limit_bytes=LIMIT),
        cost_estimate=LIGHT,
        name="attn_bwd",
    )(length, q, k, v, do, o, lse, trev, *prev)

ANY = pl.BlockSpec(memory_space=pl.ANY)
VM = pl.BlockSpec(memory_space=pltpu.VMEM)
SM = pl.BlockSpec(memory_space=pltpu.SMEM)

def rms_inverse(value):
    return lax.rsqrt(jnp.mean(value * value, axis=1, keepdims=True) + epsilon)

def pull_sequence(me, whole_ref, chip_ref, core_ref, dst, sem):
    rows = whole_ref.shape[1]
    for mask, src in enumerate((whole_ref.at[me], core_ref.at[0], chip_ref.at[me & 1], core_ref.at[1])):
        at = pl.multiple_of((me ^ mask) * rows, rows)
        pltpu.make_async_copy(src, dst.at[pl.ds(at, rows), :], sem).start()

def qkv_kernel(ids_ref, x4_ref, chip_ref, core_ref, *refs, masks):
    gathered = refs[:len(masks)]
    bucket_ref = refs[len(masks)]
    x_out, h_out, q_out, k_out, v_out, w_out, gain_ref, t_ref, trev_ref, xs, hs, ps, ws, es, sems = refs[len(masks) + 1:]
    me, flat = ids_ref[0], ids_ref[1]
    width = xs.shape[1]
    own = width // es.shape[0]
    pull_sequence(me, x4_ref, chip_ref, core_ref, xs, sems.at[0])
    for ref, ids in zip(gathered, masks):
        for j, mask in enumerate(ids):
            shard = flat ^ mask
            pltpu.make_async_copy(ref.at[j, 3 * own:3 * own + 16, :], es.at[shard], sems.at[1]).start()
    for ref, ids in zip(gathered, masks):
        for j, mask in enumerate(ids):
            at = pl.multiple_of((flat ^ mask) * own, own)
            for i in range(3):
                pltpu.make_async_copy(ref.at[j, i * own:(i + 1) * own, :], ws.at[pl.ds(at, own), i * width:(i + 1) * width], sems.at[2]).start()
    pltpu.make_async_copy(es, es, sems.at[1]).wait()
    extras = es[...].astype(jnp.float32)
    gains = jnp.sum(extras, axis=0)
    gain_ref[...] = gains[0:8]
    table = extras[:, 8, 0:128].astype(jnp.bfloat16)
    ids = lax.broadcasted_iota(jnp.int32, (es.shape[0], 1), 0)
    heads = t_ref.shape[0]
    for i, ref in enumerate((t_ref, trev_ref)):
        hot = jnp.where(bucket_ref[i:i + 1, :] == ids, 1.0, 0.0).astype(jnp.bfloat16)
        ref[...] = _dot(table, hot, TN)[0:heads] * LOG2E
    pltpu.make_async_copy(xs, xs, sems.at[0]).wait()
    part = 256
    def norm(i, carry):
        at = pl.ds(pl.multiple_of(i * part, part), part)
        x = xs[at, :].astype(jnp.float32)
        hs[at, :] = (x * rms_inverse(x) * gains[0:1]).astype(jnp.bfloat16)
        return carry
    lax.fori_loop(0, xs.shape[0] // part, norm, 0)
    copies = [pltpu.make_async_copy(xs, x_out, sems.at[0]), pltpu.make_async_copy(hs, h_out, sems.at[1])]
    for copy in copies:
        copy.start()
    pltpu.make_async_copy(ws, ws, sems.at[2]).wait()
    copies.append(pltpu.make_async_copy(ws, w_out, sems.at[2]))
    copies[-1].start()
    for i, ref in enumerate((q_out, k_out, v_out)):
        full = _dot(hs[...], ws[:, i * width:(i + 1) * width])
        ps[i] = (full * LOG2E if i == 0 else full).astype(jnp.bfloat16)
        copies.append(pltpu.make_async_copy(ps.at[i], ref, sems.at[3 + i]))
        copies[-1].start()
    for copy in copies:
        copy.wait()

def qkv_fwd(ids, x4, came, gathered, masks, bucket_rows, heads):
    parts, rows, width = x4.shape
    total = parts * rows
    shards = sum(len(m) for m in masks)
    mat = jax.ShapeDtypeStruct((total, width), jnp.bfloat16)
    wide = bucket_rows.shape[1]
    vm = lambda *s: pltpu.VMEM(s, jnp.bfloat16)
    return pl.pallas_call(
        functools.partial(qkv_kernel, masks=masks),
        out_shape=(mat,) * 5 + (jax.ShapeDtypeStruct((width, 3 * width), jnp.bfloat16), jax.ShapeDtypeStruct((8, width), jnp.float32),
                                jax.ShapeDtypeStruct((heads, wide), jnp.float32), jax.ShapeDtypeStruct((heads, wide), jnp.float32)),
        in_specs=[SM] + [ANY] * (3 + len(gathered)) + [VM],
        out_specs=[ANY] * 6 + [VM] * 3,
        scratch_shapes=[vm(total, width), vm(total, width), vm(3, total, width), vm(width, 3 * width), vm(shards, 16, width), pltpu.SemaphoreType.DMA((6,))],
        compiler_params=pltpu.CompilerParams(vmem_limit_bytes=LIMIT),
        cost_estimate=LIGHT,
        name="qkv_fwd",
    )(ids, x4, *came, *gathered, bucket_rows)

def gelu_both(v):
    t = jnp.tanh(root_coef * (v + cubic_coef * v * v * v))
    half = 0.5 * (1.0 + t)
    slope = half + 0.5 * v * (1.0 - t * t) * (root_coef * (1.0 + 3.0 * cubic_coef * v * v))
    return v * half, slope

def by_core(core, keep, send, src, dst_rows, sem, lead=slice(None), src_rows=slice(None), lanes=slice(None)):
    for parity in range(2):
        @pl.when(core == parity)
        def _():
            for dst, at in ((keep, parity), (send, 1 - parity)):
                pltpu.make_async_copy(src.at[lead, at, src_rows, lanes], dst.at[lead, dst_rows, lanes], sem).start()

def ff_chunks(h2, h2t, gm, acc, gh2, ws_in, ws_back, st_in, st_back, row_in, emit, before_add, cols=512):
    steps = ws_in.shape[1] // cols
    half, width = st_back.shape[2:]
    own = width // (2 * st_in.shape[0])
    wide = width // cols
    group = cols // (2 * half)

    def step(c, carry):
        at = pl.ds(pl.multiple_of(c * cols, cols), cols)
        win, wback = ws_in[:, at], ws_back[at, :]
        pre = _dot(h2[...], win)
        grad_active = _dot(gm[...], wback, NT)
        act, slope = gelu_both(pre)
        active = act.astype(jnp.bfloat16)
        gpre = (grad_active * slope).astype(jnp.bfloat16)
        @pl.when(c == 0)
        def _():
            before_add()
        acc[...] += _dot(active, wback)
        gh2[...] += _dot(gpre, win, NT)
        lead = pl.ds(c * group, group)
        st_back[lead] = _dot(active, gm[...], TN).astype(jnp.bfloat16).reshape(group, 2, half, width)
        emit(st_back, 0, lead=lead, dst_rows=slice(0, half))
        up = pl.multiple_of((c // wide) * own, own)
        lanes = pl.ds(pl.multiple_of((c % wide) * cols, cols), cols)
        st_in[:, :, pl.ds(up, own), lanes] = _dot(h2t[...], gpre).astype(jnp.bfloat16).reshape(-1, 2, own, cols)
        emit(st_in, 1, src_rows=pl.ds(up, own), dst_rows=pl.ds(row_in + up, own), lanes=lanes)
        return carry
    lax.fori_loop(0, steps, step, 0)

def finish_chunks(st_in, st_back, sems):
    pltpu.make_async_copy(st_back, st_back, sems.at[0]).wait()
    pltpu.make_async_copy(st_in, st_in, sems.at[1]).wait()

def aligned(at, size):
    return at if isinstance(at, int) else pl.multiple_of(at, size)

def pull_ff(flat, gathered, masks, ws_in, ws_back, row_in, sems):
    width = ws_in.shape[0]
    shards = sum(len(m) for m in masks)
    own, half = width // shards, ws_back.shape[0] // shards
    for ref, ids in zip(gathered, masks):
        for j, mask in enumerate(ids):
            shard = flat ^ mask
            pltpu.make_async_copy(ref.at[j, 0:half, :], ws_back.at[pl.ds(aligned(shard * half, half), half), :], sems.at[1]).start()
            at = pl.ds(aligned(shard * own, own), own)
            for i in range(ws_in.shape[1] // width):
                pltpu.make_async_copy(ref.at[j, row_in + i * own:row_in + (i + 1) * own, :], ws_in.at[at, i * width:(i + 1) * width], sems.at[0]).start()

def mid_a_kernel(ids_ref, x_hbm, o_hbm, g4_ref, chip_ref, core_ref, gain_ref, *refs, masks):
    gathered = refs[:len(masks)]
    (mixed_out, acc_out, gh2_out, h2_out, h2t_out, gm_out, wo_out, keep_out, send_out,
     xs, os, wo, ws_in, ws_back, mixed, h2, h2t, acc, gh2, gm, st_in, st_back, sems) = refs[len(masks):]
    flat = ids_ref[1]
    rows, width = xs.shape
    half, own = st_back.shape[2], width // (2 * st_in.shape[0])
    core = flat & 1
    def emit(src, which, **at):
        by_core(core, keep_out, send_out, src, sem=sems.at[which], **at)
    loads = [pltpu.make_async_copy(x_hbm, xs, sems.at[0]), pltpu.make_async_copy(o_hbm, os, sems.at[1])]
    for load in loads:
        load.start()
    for ref, ids in zip(gathered, masks):
        for j, mask in enumerate(ids):
            at = pl.ds(pl.multiple_of((flat ^ mask) * own, own), own)
            pltpu.make_async_copy(ref.at[j, half:half + own, :], wo.at[at, :], sems.at[2]).start()
    pull_ff(flat, gathered, masks, ws_in, ws_back, half + own, sems.at[3:5])
    pull_sequence(ids_ref[0], g4_ref, chip_ref, core_ref, gm, sems.at[5])
    for load in loads:
        load.wait()
    pltpu.make_async_copy(wo, wo, sems.at[2]).wait()
    stores = [pltpu.make_async_copy(wo, wo_out, sems.at[2])]
    stores[0].start()
    part = 256
    def load_rows(i, carry):
        at = pl.ds(pl.multiple_of(i * part, part), part)
        value = xs[at, :].astype(jnp.float32) + _dot(os[at, :], wo[...])
        mixed[at, :] = value
        acc[at, :] = value
        hidden = (value * rms_inverse(value) * gain_ref[1:2, :]).astype(jnp.bfloat16)
        h2[at, :] = hidden
        h2t[:, at] = hidden.T
        gh2[at, :] = jnp.zeros_like(value)
        return carry
    lax.fori_loop(0, rows // part, load_rows, 0)
    pltpu.make_async_copy(gm, gm, sems.at[5]).wait()
    row_ok = lax.broadcasted_iota(jnp.int32, (rows, 1), 0) < ids_ref[2]
    gm[...] = jnp.where(row_ok, gm[...], jnp.zeros_like(gm[...]))
    pltpu.make_async_copy(ws_in, ws_in, sems.at[3]).wait()
    pltpu.make_async_copy(ws_back, ws_back, sems.at[4]).wait()
    for i, (src, dst) in enumerate(((mixed, mixed_out), (h2, h2_out), (h2t, h2t_out), (gm, gm_out))):
        stores.append(pltpu.make_async_copy(src, dst, sems.at[6 + i]))
        stores[-1].start()
    ff_chunks(h2, h2t, gm, acc, gh2, ws_in, ws_back, st_in, st_back, half, emit, lambda: None)
    for i, (src, dst) in enumerate(((acc, acc_out), (gh2, gh2_out))):
        stores.append(pltpu.make_async_copy(src, dst, sems.at[3 + i]))
        stores[-1].start()
    finish_chunks(st_in, st_back, sems.at[0:2])
    for store in stores:
        store.wait()

def mid_a(ids, x, o, g4, came, gains, gathered, masks, ff):
    rows, width = x.shape
    shards = sum(len(m) for m in masks)
    half = ff // shards
    low = lambda *s: jax.ShapeDtypeStruct(s, jnp.bfloat16)
    full = lambda *s: jax.ShapeDtypeStruct(s, jnp.float32)
    vm = lambda *s: pltpu.VMEM(s, jnp.bfloat16)
    vf = lambda *s: pltpu.VMEM(s, jnp.float32)
    stack = half + ff // width * (width // shards)
    return pl.pallas_call(
        functools.partial(mid_a_kernel, masks=masks),
        out_shape=(full(rows, width), full(rows, width), full(rows, width), low(rows, width), low(width, rows), low(rows, width), low(width, width), low(shards // 2, stack, width), low(shards // 2, stack, width)),
        in_specs=[SM] + [ANY] * 5 + [VM] + [ANY] * len(gathered), out_specs=[ANY] * 9,
        scratch_shapes=[vm(rows, width), vm(rows, width), vm(width, width), vm(width, ff), vm(ff, width), vf(rows, width), vm(rows, width), vm(width, rows),
                        vf(rows, width), vf(rows, width), vm(rows, width), vm(shards // 2, 2, stack - half, width), vm(shards // 2, 2, half, width), pltpu.SemaphoreType.DMA((10,))],
        compiler_params=pltpu.CompilerParams(vmem_limit_bytes=LIMIT),
        cost_estimate=LIGHT,
        name="mid_a",
    )(ids, x, o, g4, *came, gains, *gathered)

def mid_b_kernel(ids_ref, gain_ref, mixed_hbm, acc_hbm, gh2_hbm, h2_hbm, h2t_hbm, gm_hbm, wo_hbm, o_hbm, full_ref, *refs):
    (out_ref, gb_out, do_ref, keep_out, send_out,
     os, wo, ws_in, ws_back, mixed, h2, h2t, acc, gh2, gm, gb, st_in, st_back, st_o, sems) = refs
    rows, width = os.shape
    shards, half, own = 2 * st_in.shape[0], st_back.shape[2], width // (2 * st_in.shape[0])
    core = ids_ref[1] & 1
    def emit(src, which, **at):
        by_core(core, keep_out, send_out, src, sem=sems.at[which], **at)
    early = [(h2_hbm, h2), (gm_hbm, gm), (h2t_hbm, h2t)]
    late = [(acc_hbm, acc), (gh2_hbm, gh2), (mixed_hbm, mixed), (wo_hbm, wo), (o_hbm, os)]
    early = [pltpu.make_async_copy(a, b, sems.at[4 + i]) for i, (a, b) in enumerate(early)]
    late = [pltpu.make_async_copy(a, b, sems.at[7 + i]) for i, (a, b) in enumerate(late)]
    for load in early:
        load.start()
    pull_ff(0, (full_ref,), (range(shards),), ws_in, ws_back, half, sems.at[2:4])
    for load in late:
        load.start()
    for load in early:
        load.wait()
    pltpu.make_async_copy(ws_in, ws_in, sems.at[2]).wait()
    pltpu.make_async_copy(ws_back, ws_back, sems.at[3]).wait()
    def before_add():
        late[0].wait()
        late[1].wait()
    ff_chunks(h2, h2t, gm, acc, gh2, ws_in, ws_back, st_in, st_back, half + own, emit, before_add)
    for load in late[2:]:
        load.wait()
    part = 256
    def finish(i, carry):
        at = pl.ds(pl.multiple_of(i * part, part), part)
        out_ref[at, :] = acc[at, :].astype(jnp.bfloat16)
        value = mixed[at, :]
        inverse = rms_inverse(value)
        normed = value * inverse
        scaled = gh2[at, :] * gain_ref[1:2, :]
        grad = inverse * (scaled - normed * jnp.mean(scaled * normed, axis=1, keepdims=True)) + gm[at, :].astype(jnp.float32)
        low = grad.astype(jnp.bfloat16)
        gb[at, :] = low
        do_ref[at, :] = _dot(low, wo[...], NT).astype(jnp.bfloat16)
        return carry
    lax.fori_loop(0, rows // part, finish, 0)
    st_o[...] = _dot(os[...], gb[...], TN).astype(jnp.bfloat16).reshape(st_o.shape)
    emit(st_o, 2, dst_rows=slice(half, half + own))
    store = pltpu.make_async_copy(gb, gb_out, sems.at[3])
    store.start()
    finish_chunks(st_in, st_back, sems.at[0:2])
    pltpu.make_async_copy(st_o, st_o, sems.at[2]).wait()
    store.wait()

def mid_b(ids, gains, state, o, full, ff):
    rows, width = o.shape
    shards = full.shape[0]
    half, own = ff // shards, width // shards
    low = lambda *s: jax.ShapeDtypeStruct(s, jnp.bfloat16)
    vm = lambda *s: pltpu.VMEM(s, jnp.bfloat16)
    vf = lambda *s: pltpu.VMEM(s, jnp.float32)
    rest = ff // width * own
    return pl.pallas_call(
        mid_b_kernel,
        out_shape=(low(rows, width), low(rows, width), low(rows, width), low(shards // 2, half + own + rest, width), low(shards // 2, half + own + rest, width)),
        in_specs=[SM, VM] + [ANY] * 9, out_specs=[VM, ANY, VM, ANY, ANY],
        scratch_shapes=[vm(rows, width), vm(width, width), vm(width, ff), vm(ff, width), vf(rows, width), vm(rows, width), vm(width, rows),
                        vf(rows, width), vf(rows, width), vm(rows, width), vm(rows, width), vm(shards // 2, 2, rest, width), vm(shards // 2, 2, half, width), vm(shards // 2, 2, own, width),
                        pltpu.SemaphoreType.DMA((12,))],
        compiler_params=pltpu.CompilerParams(vmem_limit_bytes=LIMIT),
        cost_estimate=LIGHT,
        name="mid_b",
    )(ids, gains, *state, o, full)

def gw_kernel(ids_ref, h_ref, dq_ref, dk_ref, dv_ref, bucket_ref, *refs):
    keep_out, send_out, st, sems = refs[-4:]
    offs = jnp.concatenate([ref[...] for ref in refs[:-4]], 0)
    pairs, _, stack, width = st.shape
    own = width // (2 * pairs)
    core = ids_ref[1] & 1
    ids = lax.broadcasted_iota(jnp.int32, (2 * pairs, 1), 0)
    hot = jnp.where(bucket_ref[1:2, :] == ids, 1.0, 0.0)
    table = lax.dot_general(hot, offs, NT, precision=lax.Precision.HIGHEST, preferred_element_type=jnp.float32)
    heads = offs.shape[0]
    st[:, :, 3 * own:, :] = jnp.zeros((pairs, 2, stack - 3 * own, width), jnp.bfloat16)
    st[:, :, 3 * own:3 * own + 1, 0:heads] = table.astype(jnp.bfloat16).reshape(pairs, 2, 1, heads)
    for i, ref in enumerate((dq_ref, dk_ref, dv_ref)):
        at = slice(i * own, (i + 1) * own) if i < 2 else slice(i * own, stack)
        st[:, :, i * own:(i + 1) * own, :] = _dot(h_ref[...], ref[...], TN).astype(jnp.bfloat16).reshape(pairs, 2, own, width)
        by_core(core, keep_out, send_out, st, at, sems.at[0], src_rows=at)
    pltpu.make_async_copy(st, st, sems.at[0]).wait()

def qkv_gw(ids, h, dq, dk, dv, bucket_rows, offs, shards):
    rows, width = h.shape
    stack = 3 * width // shards + 16
    half = jax.ShapeDtypeStruct((shards // 2, stack, width), jnp.bfloat16)
    return pl.pallas_call(
        gw_kernel, out_shape=(half, half),
        in_specs=[SM] + [VM] * (5 + len(offs)), out_specs=[ANY, ANY],
        scratch_shapes=[pltpu.VMEM((shards // 2, 2, stack, width), jnp.bfloat16), pltpu.SemaphoreType.DMA((1,))],
        compiler_params=pltpu.CompilerParams(vmem_limit_bytes=LIMIT),
        cost_estimate=LIGHT,
        name="qkv_gw",
    )(ids, h, dq, dk, dv, bucket_rows, *offs)

def gx_kernel(x_ref, gb_ref, dq_ref, dk_ref, dv_ref, gain_ref, w_ref, out_ref):
    width = x_ref.shape[1]
    grad = _dot(dq_ref[...], w_ref[:, :width], NT)
    grad += _dot(dk_ref[...], w_ref[:, width:2 * width], NT)
    grad += _dot(dv_ref[...], w_ref[:, 2 * width:3 * width], NT)
    x = x_ref[...].astype(jnp.float32)
    inverse = rms_inverse(x)
    normed = x * inverse
    scaled = grad * gain_ref[0:1, :]
    out = inverse * (scaled - normed * jnp.mean(scaled * normed, axis=1, keepdims=True)) + gb_ref[...].astype(jnp.float32)
    out_ref[...] = out.astype(jnp.bfloat16)

def qkv_gx(x, gb, dq, dk, dv, gains, w, rows=512):
    total, width = x.shape
    blk = pl.BlockSpec((rows, width), lambda i: (i, 0))
    return pl.pallas_call(
        gx_kernel, out_shape=jax.ShapeDtypeStruct((total, width), jnp.bfloat16), grid=(total // rows,),
        in_specs=[blk] * 5 + [pl.BlockSpec(gains.shape, lambda i: (0, 0)),
                              pl.BlockSpec((width, 3 * width), lambda i: (0, 0), pipeline_mode=pl.Buffered(1))],
        out_specs=blk,
        compiler_params=pltpu.CompilerParams(vmem_limit_bytes=LIMIT),
        cost_estimate=LIGHT,
        name="qkv_gx",
    )(x, gb, dq, dk, dv, gains, w)

def swap(value, axis, mask):
    return lax.ppermute(value, axis, [(i, i ^ mask) for i in range(lax.axis_size(axis))])


def send_chip(blocks, me):
    return swap(lax.dynamic_slice_in_dim(blocks, 2 * (1 - me // 2), 2, 0), "seq", 2)


def send_core(blocks, from_chip, me):
    own = lax.dynamic_index_in_dim(blocks, me ^ 1, 0)
    passed = lax.dynamic_index_in_dim(from_chip, 1 - me % 2, 0)
    return swap(jnp.concatenate([own, passed], 0), "seq", 1)


class Gather:
    def __init__(self, shard):
        shard = shard[None]
        self.sent = [shard] + [swap(shard, "dp", 2 * z) for z in (1, 2, 3)]
        self.pieces, self.masks = [], []

    def take(self, piece, mask, rows=(0, 1, 2, 3)):
        ids = tuple(8 * z | mask for z in rows)
        self.pieces += [piece, swap(piece, "seq", 1)]
        self.masks += [ids, tuple(m | 1 for m in ids)]

    def fill(self):
        self.own = jnp.concatenate(self.sent, 0)

    def sides(self):
        self.x, self.y = swap(self.own, "seq", 2), swap(self.own, "dp", 1)

    def corner_halves(self):
        self.near, self.far = swap(self.y[:2], "seq", 2), swap(self.x[2:], "dp", 1)

    def corner_y(self):
        self.corner = swap(self.x, "dp", 1)

    def all_pieces(self):
        return tuple(self.pieces), tuple(self.masks)


class Scatter:
    def __init__(self, keep, send, pos, corner_y):
        self.z, self.y, self.x = pos
        cube = (4, 2, 2) + keep.shape[1:]
        self.mine, self.sent, self.corner_y = keep.reshape(cube), send.reshape(cube), corner_y
        self.other = swap(self.sent, "seq", 1)

    def fold(self):
        pick = lambda v, at, axis: lax.dynamic_index_in_dim(v, at, axis, keepdims=False)
        def quarter(dy, dx):
            cut = lambda v: pick(pick(v, self.y ^ dy, 1), self.x ^ dx, 1).astype(jnp.float32)
            return (cut(self.mine) + cut(self.other)).astype(jnp.bfloat16)
        far = quarter(1, 1)
        self.to_x, self.to_y, self.own = quarter(0, 1), quarter(1, 0), quarter(0, 0)
        if self.corner_y:
            self.came_x, self.came_y = None, swap(far, "dp", 1)
        else:
            self.came_x, self.came_y = swap(far[:2], "seq", 2), swap(far[2:], "dp", 1)

    def turn(self):
        add = lambda a, b: (a.astype(jnp.float32) + b.astype(jnp.float32)).astype(jnp.bfloat16)
        if self.corner_y:
            to_y, = tie(self.came_y, self.to_y)
            to_x = add(self.to_x, self.came_y)
        else:
            to_x = lax.dynamic_update_slice_in_dim(self.to_x, add(self.to_x[2:], self.came_y), 2, 0)
            to_y = lax.dynamic_update_slice_in_dim(self.to_y, add(self.to_y[:2], self.came_x), 0, 0)
        self.sent = (to_x, to_y)
        self.came_x, self.came_y = swap(to_x, "seq", 2), swap(to_y, "dp", 1)

    def column(self):
        total = self.own.astype(jnp.float32) + self.came_x.astype(jnp.float32) + self.came_y.astype(jnp.float32)
        total = total.astype(jnp.bfloat16)
        block = lambda k: lax.dynamic_index_in_dim(total, self.z ^ k, 0, keepdims=False)
        self.mine = block(0)
        self.came = [swap(block(k), "dp", 2 * k) for k in (1, 2, 3)]

    def result(self):
        return sum((c.astype(jnp.float32) for c in self.came), self.mine.astype(jnp.float32))


def place(blocks, from_chip, from_core, me):
    for mask, block in ((1, from_core[0:1]), (2, lax.dynamic_index_in_dim(from_chip, me % 2, 0)), (3, from_core[1:2])):
        blocks = lax.dynamic_update_slice_in_dim(blocks, block, me ^ mask, 0)
    return blocks


def tie(first, *later):
    return lax.optimization_barrier((first,) + later)[1:]


def local_whole(tokens, cotangent, lengths, buckets, norm1_gain, w_query, w_key, w_value, w_out, rel_table, norm2_gain, w_in, w_back):
    micro_count, seq_count, rows, width = tokens.shape
    parts = micro_count * seq_count
    both = ("dp", "seq")
    me, dp = lax.axis_index("seq"), lax.axis_index("dp")
    shards = lax.axis_size("seq") * lax.axis_size("dp")
    flat = dp * parts + me
    pos = (dp // 2, dp % 2, me // 2)
    low = lambda v: v.astype(jnp.bfloat16)
    up = lambda v: v.astype(jnp.float32)
    own, ff_own = w_query.shape[0], w_back.shape[0]
    ids = jnp.stack([me, flat, lax.dynamic_index_in_dim(lengths.reshape(parts), me, 0, keepdims=False)])
    length = ids[2:3]

    place_row = lambda v: lax.dynamic_update_slice(jnp.zeros((1, width), jnp.bfloat16), low(v)[None], (0, flat * own))
    small = jnp.concatenate([place_row(norm1_gain), place_row(norm2_gain), jnp.zeros((6, width), jnp.bfloat16),
                             jnp.pad(low(rel_table)[None], ((0, 7), (0, width - HEADS)))], 0)
    shard1 = jnp.concatenate([low(w_query), low(w_key), low(w_value), small], 0)
    ff = w_in.shape[1] // 2
    half = ff_own // 2
    halves = low(w_in).reshape(own, shards, 2, half)
    in_half = lambda i: [halves[:, :, i].reshape(own, ff)[:, j:j + width] for j in range(0, ff, width)]
    shard2 = jnp.concatenate([low(w_back[:half]), low(w_out)] + in_half(0), 0)
    shard3 = jnp.concatenate([low(w_back[half:])] + in_half(1), 0)
    x4, g4 = tokens.reshape(parts, rows, width), cotangent.reshape(parts, rows, width)
    bucket_rows = jnp.stack([jnp.pad(buckets, (0, 1), constant_values=-1), jnp.pad(buckets[::-1], (0, 1), constant_values=-1)])

    g1 = Gather(shard1)
    x_chip = send_chip(x4, me)
    g2 = Gather(shard2)
    g1.fill()
    g1.own, = tie((x_chip, g2.sent[1], shard3), g1.own)
    g1.sides()
    g1.x, g1.y = tie(g2.sent[2], g1.x, g1.y)
    g1.corner_halves()
    g2.fill()
    g1.take(g1.own, 0)
    g1.near, g1.far, g2.own = tie(g1.pieces[1], g1.near, g1.far, g2.own)
    g2.sides()
    g1.x, g1.y, x4_in = tie((g1.near, g1.far), g1.x, g1.y, x4)
    g1.take(g1.x, 2)
    g1.take(g1.y, 4)
    g1.take(g1.near, 6, (0, 1))
    g1.take(g1.far, 6, (2, 3))
    x_core = send_core(x4_in, x_chip, me)
    shard3, = tie((g1.near, g1.far), shard3)
    full3 = lax.all_gather(shard3, both, axis=0, tiled=False)
    x, hidden, q, k, v, w_qkv, gains, t, t_back = qkv_fwd(ids, x4, (x_chip, x_core), *g1.all_pieces(), bucket_rows, HEADS)
    pairs = HEADS // 2
    att = attn_fwd(length, q, k, v, t, 0, pairs // 2)
    g2.take(g2.own, 0)
    g2.x, g2.y = tie((att[0], g2.pieces[1]), g2.x, g2.y)
    g2.corner_y()
    g4_in, = tie(g2.x, g4)
    g_chip = send_chip(g4_in, me)
    g2.take(g2.x, 2)
    g2.take(g2.y, 4)
    q_in, = tie((g2.x, g2.y), q)
    attended, lse = attn_fwd(length, q_in, k, v, t, pairs // 2, pairs // 2, att)
    g2.corner, g_chip = tie((attended, g2.pieces[3], g2.pieces[5]), g2.corner, g_chip)
    g2.take(g2.corner, 6)
    g_core = send_core(g4, g_chip, me)
    *state, keep3, send3 = mid_a(ids, x, attended, g4, (g_chip, g_core), gains, *g2.all_pieces(), ff)
    sc3 = Scatter(keep3, send3, pos, True)
    out, gb, g_att, keep2, send2 = mid_b(ids, gains, state, attended, full3, ff)
    sc3.other, = tie(gb, sc3.other)
    sc3.fold()
    send2, = tie(sc3.own, send2)
    sc2 = Scatter(keep2, send2, pos, False)
    out4 = out.reshape(parts, rows, width)
    out4, = tie(sc3.own, out4)
    out_chip = send_chip(out4, me)
    count = pairs // 4
    back = lambda first, g, prev: attn_bwd(length, q, k, v, g, attended, lse, t_back, first, count, prev)
    g_att, = tie(sc3.own, g_att)
    dq, dk, dv, off0 = back(0, g_att, None)
    sc2.other, = tie(off0, sc2.other)
    sc2.fold()
    sc3.came_y, = tie(sc2.own, sc3.came_y)
    sc3.turn()
    g_att, = tie(sc3.sent, g_att)
    dq, dk, dv, off1 = back(count, g_att, (dq, dk, dv))
    sc2.came_x, sc2.came_y = tie((off1, out_chip), sc2.came_x, sc2.came_y)
    sc2.turn()
    out4_in, out_chip = tie(sc2.sent, out4, out_chip)
    out_core = send_core(out4_in, out_chip, me)
    g_att, = tie(sc2.sent, g_att)
    dq, dk, dv, off2 = back(2 * count, g_att, (dq, dk, dv))
    sc3.came_x, sc3.came_y = tie((off2, out_core), sc3.came_x, sc3.came_y)
    sc3.column()
    g_att, = tie(sc3.mine, g_att)
    dq, dk, dv, off3 = back(3 * count, g_att, (dq, dk, dv))
    sc2.came_x, sc2.came_y = tie(off3, sc2.came_x, sc2.came_y)
    sc2.column()
    h_in, = tie((sc2.mine, sc3.came), hidden)
    keep1, send1 = qkv_gw(ids, h_in, dq, dk, dv, bucket_rows, (off0, off1, off2, off3), shards)
    sc1 = Scatter(keep1, send1, pos, False)
    gb_in, = tie(send1, gb)
    gx = qkv_gx(x, gb_in, dq, dk, dv, gains, w_qkv)
    sc1.other, = tie(gx, sc1.other)
    sc1.fold()
    out4, out_chip, out_core = tie(sc1.own, out4, out_chip, out_core)
    layer_out = place(out4, out_chip, out_core, me)
    sc1.came_x, sc1.came_y = tie((layer_out, sc2.came), sc1.came_x, sc1.came_y)
    sc1.turn()
    sc2.came = list(tie(sc1.sent, *sc2.came))
    sc3.came = list(tie(sc1.sent, *sc3.came))
    r2, r_a = sc2.result(), sc3.result()
    sc1.came_x, sc1.came_y = tie(r2, sc1.came_x, sc1.came_y)
    sc1.column()
    gx, = tie(sc1.mine, gx)
    gx4 = gx.reshape(parts, rows, width)
    gx_chip = send_chip(gx4, me)
    gx_chip, = tie(sc1.came, gx_chip)
    gx_core = send_core(gx4, gx_chip, me)
    input_grad = place(gx4, gx_chip, gx_core, me)
    sc1.came = list(tie(input_grad, *sc1.came))
    r1 = sc1.result()
    join = lambda v: jnp.concatenate([v[i:i + own] for i in range(0, v.shape[0], own)], 1).reshape(own, shards, 1, half)
    g_in = jnp.concatenate([join(r_a[half:]), join(r2[half + own:])], 2).reshape(w_in.shape)
    g_back = jnp.concatenate([r_a[:half], r2[:half]], 0)
    prod = up(shard1[:3 * own]) * r1[:3 * own]
    g_gain1 = jnp.sum(prod[:own] + prod[own:2 * own] + prod[2 * own:], axis=1) / up(low(norm1_gain))
    g_gain2 = jnp.sum(up(low(w_in)) * g_in, axis=1) / up(low(norm2_gain))
    return (layer_out.reshape(tokens.shape), input_grad.reshape(tokens.shape), g_gain1, r1[:own], r1[own:2 * own], r1[2 * own:3 * own],
            r2[half:half + own], r1[3 * own, :HEADS], g_gain2, g_in, g_back)


def local_any(shape, tokens, *rest):
    fits = tuple(shape) == (8, 4) and tokens.shape[0] * tokens.shape[1] == 4 and tokens.shape[3] == HEADS * DH == 1024
    return (local_whole if fits else local)(tokens, *rest)


def solution(mesh):
    return jax.shard_map(
        functools.partial(local_any, mesh.devices.shape),
        mesh=mesh,
        in_specs=(
            P(None, "dp", "seq", None),
            P(None, "dp", "seq", None),
            P(None, "dp"),
            P(),
            P(("dp", "seq")),
            P(("dp", "seq"), None),
            P(("dp", "seq"), None),
            P(("dp", "seq"), None),
            P(("dp", "seq"), None),
            P(("dp", "seq")),
            P(("dp", "seq")),
            P(("dp", "seq"), None),
            P(("dp", "seq"), None),
        ),
        out_specs=(
            P(None, "dp", "seq", None),
            P(None, "dp", "seq", None),
            P(("dp", "seq")),
            P(("dp", "seq"), None),
            P(("dp", "seq"), None),
            P(("dp", "seq"), None),
            P(("dp", "seq"), None),
            P(("dp", "seq")),
            P(("dp", "seq")),
            P(("dp", "seq"), None),
            P(("dp", "seq"), None),
        ),
        check_vma=False,
    )
```

```python
import functools

import jax
import jax.numpy as jnp
from jax import lax
from jax.experimental import pallas as pl
from jax.experimental.pallas import tpu as pltpu
from jax.sharding import PartitionSpec as P

HEADS = 16
DH = 64
BUCKETS = 32


epsilon = 1e-06
floor_score = -1e30
highest = lax.Precision.HIGHEST
root_coef = 0.7978845608
cubic_coef = 0.044715


def gelu_tanh(values):
    return (
        0.5
        * values
        * (1.0 + jnp.tanh(root_coef * (values + cubic_coef * values * values * values)))
    )


def gelu_slope(values):
    inner = jnp.tanh(root_coef * (values + cubic_coef * values * values * values))
    return 0.5 * (1.0 + inner) + 0.5 * values * (1.0 - inner * inner) * root_coef * (
        1.0 + 3.0 * cubic_coef * values * values
    )


def project(acts, weight):
    return jnp.einsum("srd,de->sre", acts, weight, preferred_element_type=jnp.float32)


def project_back(grads_in, weight):
    return jnp.einsum("sre,de->srd", grads_in, weight, preferred_element_type=jnp.float32)


def contract(acts, grads_in):
    return jnp.einsum("srd,sre->de", acts, grads_in, preferred_element_type=jnp.float32)


def rms_forward(values, gain):
    inverse = lax.rsqrt(jnp.mean(values * values, axis=-1, keepdims=True) + epsilon)
    normed = values * inverse
    return (normed, inverse, (normed * gain.astype(jnp.float32)).astype(jnp.bfloat16))


def rms_backward(grad_hidden, normed, inverse, gain):
    scaled = grad_hidden * gain.astype(jnp.float32)
    grad_values = inverse * (scaled - normed * jnp.mean(scaled * normed, axis=-1, keepdims=True))
    return (grad_values, jnp.sum(grad_hidden * normed, axis=(0, 1)))


def score_block(per_head_queries, per_head_keys, rel_bias, key_valid):
    scores = (
        jnp.einsum(
            "ofck,owck->ocfw", per_head_queries, per_head_keys, preferred_element_type=jnp.float32
        )
        + rel_bias[None]
    )
    return jnp.where(key_valid, scores, floor_score)


def offset_sums(grid, first_row, seq_len):
    head_count, row_count, key_count = grid.shape
    flipped = grid[:, ::-1, :]
    padded = jnp.pad(flipped, ((0, 0), (0, 0), (0, row_count)))
    wide_len = key_count + row_count
    skewed = padded.reshape(head_count, row_count * wide_len)[:, : row_count * (wide_len - 1)]
    skewed = skewed.reshape(head_count, row_count, wide_len - 1)
    column_sums = jnp.sum(skewed, axis=1)
    placed = jnp.zeros((head_count, 2 * seq_len - 1), jnp.float32)
    begin = seq_len - row_count - first_row
    return lax.dynamic_update_slice(placed, column_sums, (jnp.int32(0), begin))


def run_micro(inputs, incoming, seq_lens, attn_set, mlp_set, context):
    onehot, offsets, row_pos, key_pos, first_row, seq_len = context
    gain_one, query_w, key_w, value_w, out_w, bias_table = attn_set
    gain_two, in_w, return_projection_weight = mlp_set
    seq_count, row_count, model_width = inputs.shape
    values = inputs.astype(jnp.float32)
    normed_one, inverse_one, hidden_one = rms_forward(values, gain_one)
    queries = project(hidden_one, query_w).astype(jnp.bfloat16)
    keys_own = project(hidden_one, key_w).astype(jnp.bfloat16)
    values_own = project(hidden_one, value_w).astype(jnp.bfloat16)
    keys_all, values_all = (
        lax.all_gather(keys_own, "seq", axis=1, tiled=True),
        lax.all_gather(values_own, "seq", axis=1, tiled=True),
    )
    per_offset = jnp.dot(
        onehot, bias_table.reshape(BUCKETS, HEADS), preferred_element_type=jnp.float32
    )
    rel_bias = jnp.transpose(per_offset[offsets], (2, 0, 1))
    key_valid = (key_pos[None, :] < seq_lens[:, None])[:, None, None, :]
    per_head_queries = queries.reshape(seq_count, row_count, HEADS, DH)
    per_head_keys = keys_all.reshape(seq_count, seq_len, HEADS, DH)
    per_head_values = values_all.reshape(seq_count, seq_len, HEADS, DH)
    scores = score_block(per_head_queries, per_head_keys, rel_bias, key_valid)
    row_max = jnp.max(scores, axis=-1, keepdims=True)
    exp_scores = jnp.exp(scores - row_max)
    row_total = jnp.sum(exp_scores, axis=-1, keepdims=True)
    attn_probs = exp_scores / row_total
    log_total = row_max + jnp.log(row_total)
    reduced_precision_probs = attn_probs.astype(jnp.bfloat16)
    attended = jnp.einsum(
        "jfpe,jefn->jpfn",
        reduced_precision_probs,
        per_head_values,
        preferred_element_type=jnp.float32,
    )
    attended = attended.reshape(seq_count, row_count, model_width).astype(jnp.bfloat16)
    residual_mid = values + project(attended, out_w)
    normed_two, inverse_two, hidden_two = rms_forward(residual_mid, gain_two)
    pre_act = project(hidden_two, in_w)
    active = gelu_tanh(pre_act).astype(jnp.bfloat16)
    result = (residual_mid + project(active, return_projection_weight)).astype(jnp.bfloat16)
    row_valid = (row_pos[None, :] < seq_lens[:, None]).astype(jnp.float32)[:, :, None]
    grad_out = incoming.astype(jnp.float32) * row_valid
    grad_low = grad_out.astype(jnp.bfloat16)
    grad_back = contract(active, grad_low)
    gradient_active_rows = project_back(grad_low, return_projection_weight)
    grad_pre = (gradient_active_rows * gelu_slope(pre_act)).astype(jnp.bfloat16)
    grad_in = contract(hidden_two, grad_pre)
    grad_hidden_two = project_back(grad_pre, in_w)
    grad_mixed, grad_gain_two = rms_backward(grad_hidden_two, normed_two, inverse_two, gain_two)
    grad_mixed = grad_mixed + grad_out
    grad_branch = grad_mixed.astype(jnp.bfloat16)
    grad_outw = contract(attended, grad_branch)
    gradient_attended_values = project_back(grad_branch, out_w).astype(jnp.bfloat16)
    gradient_attended_values = gradient_attended_values.reshape(seq_count, row_count, HEADS, DH)
    scores = score_block(per_head_queries, per_head_keys, rel_bias, key_valid)
    attn_probs = jnp.exp(scores - log_total)
    reduced_precision_probs = attn_probs.astype(jnp.bfloat16)
    grad_probs = jnp.einsum(
        "ofck,owck->ocfw",
        gradient_attended_values,
        per_head_values,
        preferred_element_type=jnp.float32,
    )
    inner_sum = jnp.sum(attn_probs * grad_probs, axis=-1, keepdims=True)
    gradient_score_matrix = (attn_probs * (grad_probs - inner_sum)).astype(jnp.bfloat16)
    grad_query = jnp.einsum(
        "jfpe,jefn->jpfn", gradient_score_matrix, per_head_keys, preferred_element_type=jnp.float32
    )
    grad_query = grad_query.astype(jnp.bfloat16).reshape(seq_count, row_count, model_width)
    key_part = jnp.einsum(
        "eciv,eicq->evcq",
        gradient_score_matrix,
        per_head_queries,
        preferred_element_type=jnp.float32,
    )
    value_part = jnp.einsum(
        "eciv,eicq->evcq",
        reduced_precision_probs,
        gradient_attended_values,
        preferred_element_type=jnp.float32,
    )
    key_part = key_part.reshape(seq_count, seq_len, model_width)
    value_part = value_part.reshape(seq_count, seq_len, model_width)
    grad_key, grad_value = (
        lax.psum_scatter(
            key_part.astype(jnp.bfloat16), "seq", scatter_dimension=1, tiled=True
        ).astype(jnp.float32),
        lax.psum_scatter(
            value_part.astype(jnp.bfloat16), "seq", scatter_dimension=1, tiled=True
        ).astype(jnp.float32),
    )
    grad_key = grad_key.astype(jnp.bfloat16)
    grad_value = grad_value.astype(jnp.bfloat16)
    offset_grad = offset_sums(
        jnp.sum(gradient_score_matrix.astype(jnp.float32), axis=0), first_row, seq_len
    )
    grad_table = jnp.dot(onehot.astype(jnp.float32).T, offset_grad.T, precision=highest).reshape(-1)
    grad_qw = contract(hidden_one, grad_query)
    grad_kw = contract(hidden_one, grad_key)
    grad_vw = contract(hidden_one, grad_value)
    grad_hidden_one = (
        project_back(grad_query, query_w)
        + project_back(grad_key, key_w)
        + project_back(grad_value, value_w)
    )
    grad_values, grad_gain_one = rms_backward(grad_hidden_one, normed_one, inverse_one, gain_one)
    grad_values = grad_values + grad_mixed
    gradients = (
        grad_gain_one,
        grad_qw,
        grad_kw,
        grad_vw,
        grad_outw,
        grad_table,
        grad_gain_two,
        grad_in,
        grad_back,
    )
    return (result, grad_values.astype(jnp.bfloat16), gradients)


def local(
    tokens,
    cotangent,
    lengths,
    buckets,
    norm1_gain,
    w_query,
    w_key,
    w_value,
    w_out,
    rel_table,
    norm2_gain,
    w_in,
    w_back,
):
    micro_count, seq_count, row_count, model_width = tokens.shape
    seq_parts = lax.axis_size("seq")
    seq_len = row_count * seq_parts
    first_row = lax.axis_index("seq") * row_count
    row_pos = first_row + jnp.arange(row_count, dtype=jnp.int32)
    key_pos = jnp.arange(seq_len, dtype=jnp.int32)
    onehot = (buckets[:, None] == jnp.arange(BUCKETS, dtype=jnp.int32)[None, :]).astype(
        jnp.bfloat16
    )
    offsets = key_pos[None, :] - row_pos[:, None] + (seq_len - 1)
    context = (onehot, offsets, row_pos, key_pos, first_row, seq_len)
    outputs = []
    input_grads = []
    pending = None
    shard_sums = None
    for micro_step in range(micro_count):
        attn_set = (
            lax.all_gather(norm1_gain.astype(jnp.bfloat16), ("dp", "seq"), axis=0, tiled=True),
            lax.all_gather(w_query.astype(jnp.bfloat16), ("dp", "seq"), axis=0, tiled=True),
            lax.all_gather(w_key.astype(jnp.bfloat16), ("dp", "seq"), axis=0, tiled=True),
            lax.all_gather(w_value.astype(jnp.bfloat16), ("dp", "seq"), axis=0, tiled=True),
            lax.all_gather(w_out.astype(jnp.bfloat16), ("dp", "seq"), axis=0, tiled=True),
            lax.all_gather(rel_table.astype(jnp.bfloat16), ("dp", "seq"), axis=0, tiled=True),
        )
        mlp_set = (
            lax.all_gather(norm2_gain.astype(jnp.bfloat16), ("dp", "seq"), axis=0, tiled=True),
            lax.all_gather(w_in.astype(jnp.bfloat16), ("dp", "seq"), axis=0, tiled=True),
            lax.all_gather(w_back.astype(jnp.bfloat16), ("dp", "seq"), axis=0, tiled=True),
        )
        layer_part, grad_part, gradients = run_micro(
            tokens[micro_step],
            cotangent[micro_step],
            lengths[micro_step],
            attn_set,
            mlp_set,
            context,
        )
        outputs.append(layer_part)
        input_grads.append(grad_part)
        pending = gradients if pending is None else jax.tree.map(jnp.add, pending, gradients)
    shard_sums = (
        lax.psum_scatter(pending[0], ("dp", "seq"), scatter_dimension=0, tiled=True),
        lax.psum_scatter(pending[1], ("dp", "seq"), scatter_dimension=0, tiled=True),
        lax.psum_scatter(pending[2], ("dp", "seq"), scatter_dimension=0, tiled=True),
        lax.psum_scatter(pending[3], ("dp", "seq"), scatter_dimension=0, tiled=True),
        lax.psum_scatter(pending[4], ("dp", "seq"), scatter_dimension=0, tiled=True),
        lax.psum_scatter(pending[5], ("dp", "seq"), scatter_dimension=0, tiled=True),
        lax.psum_scatter(pending[6], ("dp", "seq"), scatter_dimension=0, tiled=True),
        lax.psum_scatter(pending[7], ("dp", "seq"), scatter_dimension=0, tiled=True),
        lax.psum_scatter(pending[8], ("dp", "seq"), scatter_dimension=0, tiled=True),
    )
    return (
        jnp.stack(outputs),
        jnp.stack(input_grads),
        shard_sums[0],
        shard_sums[1],
        shard_sums[2],
        shard_sums[3],
        shard_sums[4],
        shard_sums[5],
        shard_sums[6],
        shard_sums[7],
        shard_sums[8],
    )


NT = (((1,), (1,)), ((), ()))
TN = (((0,), (0,)), ((), ()))
STRIP = 128
LOG2E = 1.4426950408889634
LN2 = 0.6931471805599453
LIMIT = 58 << 20
LIGHT = pl.CostEstimate(flops=1, bytes_accessed=1, transcendentals=0)

def _dot(a, b, dims=(((1,), (0,)), ((), ()))):
    return lax.dot_general(a, b, dims, preferred_element_type=jnp.float32)

def with_extras(x, which, extras, width=64):
    lane = lax.broadcasted_iota(jnp.int32, (1, x.shape[1]), 1)
    spare = lane - width if which == 0 else lane
    own = (lane < width) if which == 0 else (lane >= width)
    fill = jnp.zeros_like(x)
    for i, extra in enumerate(extras):
        fill = jnp.where(spare == i, extra, fill)
    return jnp.where(own, x, fill).astype(jnp.bfloat16)

def three_parts(x):
    low = lambda v: v.astype(jnp.bfloat16).astype(jnp.float32)
    high = low(x)
    middle = low(x - high)
    return [high, middle, low(x - high - middle)]

def slot_floor(size, length):
    return jnp.where(lax.broadcasted_iota(jnp.int32, (size, 1), 0) < length, 0.0, floor_score)

def skew(row, wide):
    return pltpu.roll(jnp.broadcast_to(row, (STRIP, wide)), wide - (STRIP - 1), 1, stride=1, stride_axis=0)

def fwd_kernel(len_ref, q_ref, k_ref, v_ref, t_ref, *refs, rows, seq_len, first):
    o_ref, lse_ref, strip, kx, vx = refs[-5:]
    wide = t_ref.shape[-1]
    pair = first + pl.program_id(0)
    per = rows // STRIP
    lane = lax.broadcasted_iota(jnp.int32, (1, 128), 1)
    k2 = k_ref[...].astype(jnp.float32)
    vx[:, 0:128] = v_ref[...]
    vx[:, 128:256] = jnp.ones_like(v_ref[...])
    for a in range(2):
        kx[a] = with_extras(k2, a, [slot_floor(seq_len, len_ref[0])])
        strip[a] = skew(t_ref[pl.ds(2 * pair + a, 1), :], wide)

    def step(b, carry):
        base = b * rows
        q2 = q_ref[pl.ds(base, rows), :].astype(jnp.float32)
        outs, stats = [], []
        for a in range(2):
            scores = _dot(with_extras(q2, a, [1.0]), kx[a], NT)
            parts = []
            for i in range(per):
                off = (seq_len - STRIP) - (b * per + i) * STRIP
                parts.append(strip[a, :, pl.ds(off, seq_len)])
            scores = scores + (jnp.concatenate(parts, 0) if per > 1 else parts[0])
            top = jnp.max(scores, axis=1, keepdims=True)
            probs = jnp.exp2(scores - top).astype(jnp.bfloat16)
            out = _dot(probs, vx[...])
            outs.append(out[:, 0:128] / out[:, 128:256])
            stats.append(top + jnp.log2(out[:, 128:256]))
        o_ref[pl.ds(base, rows), :] = jnp.where(lane < 64, outs[0], outs[1]).astype(jnp.bfloat16)
        lse_ref[0, pl.ds(base, rows), :] = jnp.where(lane < 64, stats[0], stats[1])
        return carry

    for b in range(seq_len // rows):
        step(b, 0)

def attn_fwd(length, q, k, v, t, first, count, prev=(), rows=256):
    seq_len, width = q.shape
    pairs = width // 128
    wide = t.shape[-1]
    blk = pl.BlockSpec((seq_len, 128), lambda p, n: (0, first + p))
    return pl.pallas_call(
        functools.partial(fwd_kernel, rows=rows, seq_len=seq_len, first=first),
        out_shape=(jax.ShapeDtypeStruct((seq_len, width), jnp.bfloat16),
                   jax.ShapeDtypeStruct((pairs, seq_len, 128), jnp.float32)),
        grid_spec=pltpu.PrefetchScalarGridSpec(
            num_scalar_prefetch=1, grid=(count,),
            in_specs=[blk, blk, blk, pl.BlockSpec(t.shape, lambda p, n: (0, 0))] + [pl.BlockSpec(memory_space=pl.ANY)] * len(prev),
            out_specs=[blk, pl.BlockSpec((1, seq_len, 128), lambda p, n: (first + p, 0, 0))],
            scratch_shapes=[pltpu.VMEM((2, STRIP, wide), jnp.float32), pltpu.VMEM((2, seq_len, 128), jnp.bfloat16),
                            pltpu.VMEM((seq_len, 256), jnp.bfloat16)]),
        input_output_aliases={5 + i: i for i in range(len(prev))},
        compiler_params=pltpu.CompilerParams(vmem_limit_bytes=LIMIT),
        cost_estimate=LIGHT,
        name="attn_fwd",
    )(length, q, k, v, t, *prev)

def bwd_kernel(len_ref, q_ref, k_ref, v_ref, do_ref, o_ref, lse_ref, t_ref, *refs, rows, seq_len, first):
    dq_ref, dk_ref, dv_ref, g_ref, strip, acc, dq_acc, qx, kx, vx, dox = refs[-11:]
    wide = t_ref.shape[-1]
    local_pair = pl.program_id(0)
    pair = first + local_pair
    per = rows // STRIP
    lane = lax.broadcasted_iota(jnp.int32, (1, 128), 1)
    up = lambda ref: ref[...].astype(jnp.float32)
    floor = slot_floor(seq_len, len_ref[0])
    prod = up(do_ref) * up(o_ref)
    for a in range(2):
        mine = (lane < 64) if a == 0 else (lane >= 64)
        delta = jnp.sum(jnp.where(mine, prod, 0.0), axis=1, keepdims=True)
        lse = lse_ref[0, :, 64 * a:64 * a + 1]
        qx[a] = with_extras(up(q_ref), a, [1.0] + three_parts(-lse))
        kx[a] = with_extras(up(k_ref), a, [floor, 1.0, 1.0, 1.0])
        vx[a] = with_extras(up(v_ref), a, [1.0, 1.0, 1.0])
        dox[a] = with_extras(up(do_ref), a, three_parts(-delta))
        strip[a] = skew(t_ref[pl.ds(2 * pair + a, 1), :], wide)
    acc[...] = jnp.zeros_like(acc)
    k2t = k_ref[...].T
    dq_acc[...] = jnp.zeros_like(dq_acc)

    def step(b, carry):
        at = pl.ds(b * rows, rows)
        dks, dvs = [], []
        for a in range(2):
            scores = _dot(kx[a, at, :], qx[a], NT)
            offs = [(seq_len - STRIP) - (b * per + i) * STRIP for i in range(per)]
            bias = [strip[a, :, pl.ds(off, seq_len)] for off in offs]
            probs = jnp.exp2(scores + (jnp.concatenate(bias, 0) if per > 1 else bias[0]))
            grad_scores = probs * _dot(vx[a, at, :], dox[a], NT)
            for i, off in enumerate(offs):
                acc[a, :, pl.ds(off, seq_len)] += grad_scores[i * STRIP:(i + 1) * STRIP]
            probs_b = probs.astype(jnp.bfloat16)
            gs_b = grad_scores.astype(jnp.bfloat16)
            dvs.append(_dot(probs_b, do_ref[...]))
            dks.append(_dot(gs_b, q_ref[...]))
            dq_acc[a] += _dot(k2t[:, b * rows:(b + 1) * rows], gs_b)
        dk_ref[at, :] = (jnp.where(lane < 64, dks[0], dks[1]) * LN2).astype(jnp.bfloat16)
        dv_ref[at, :] = jnp.where(lane < 64, dvs[0], dvs[1]).astype(jnp.bfloat16)
        return carry

    for b in range(seq_len // rows):
        step(b, 0)
    dq_ref[...] = jnp.concatenate([dq_acc[0, 0:64], dq_acc[1, 64:128]], 0).T.astype(jnp.bfloat16)
    for a in range(2):
        sums = acc[a]
        half = STRIP
        while half > 8:
            half //= 2
            sums = sums[:half] + pltpu.roll(sums[half:], wide - half, 1)
        while half > 1:
            half //= 2
            sums = sums + pltpu.roll(pltpu.roll(sums, 8 - half, 0), wide - half, 1)
        g_ref[pl.ds(2 * local_pair + a, 1), :] = pltpu.roll(sums, STRIP - 1, 1)[0:1]

def attn_bwd(length, q, k, v, do, o, lse, trev, first, count, prev=None, rows=512):
    seq_len, width = q.shape
    wide = trev.shape[-1]
    blk = pl.BlockSpec((seq_len, 128), lambda p, n: (0, first + p))
    mat = jax.ShapeDtypeStruct((seq_len, width), jnp.bfloat16)
    prev = tuple(prev) if prev is not None else ()
    return pl.pallas_call(
        functools.partial(bwd_kernel, rows=rows, seq_len=seq_len, first=first),
        out_shape=(mat, mat, mat, jax.ShapeDtypeStruct((2 * count, wide), jnp.float32)),
        grid_spec=pltpu.PrefetchScalarGridSpec(
            num_scalar_prefetch=1, grid=(count,),
            in_specs=[blk, blk, blk, blk, blk, pl.BlockSpec((1, seq_len, 128), lambda p, n: (first + p, 0, 0)),
                      pl.BlockSpec(trev.shape, lambda p, n: (0, 0))] + [pl.BlockSpec(memory_space=pl.ANY)] * len(prev),
            out_specs=[blk, blk, blk, pl.BlockSpec((2 * count, wide), lambda p, n: (0, 0))],
            scratch_shapes=[pltpu.VMEM((2, STRIP, wide), jnp.float32), pltpu.VMEM((2, STRIP, wide), jnp.float32),
                            pltpu.VMEM((2, 128, seq_len), jnp.float32)] + [pltpu.VMEM((2, seq_len, 128), jnp.bfloat16)] * 4),
        input_output_aliases={8 + i: i for i in range(len(prev))},
        compiler_params=pltpu.CompilerParams(vmem_limit_bytes=LIMIT),
        cost_estimate=LIGHT,
        name="attn_bwd",
    )(length, q, k, v, do, o, lse, trev, *prev)

ANY = pl.BlockSpec(memory_space=pl.ANY)
VM = pl.BlockSpec(memory_space=pltpu.VMEM)
SM = pl.BlockSpec(memory_space=pltpu.SMEM)

def rms_inverse(value):
    return lax.rsqrt(jnp.mean(value * value, axis=1, keepdims=True) + epsilon)

def pull_sequence(me, whole_ref, chip_ref, core_ref, dst, sem):
    rows = whole_ref.shape[1]
    for mask, src in enumerate((whole_ref.at[me], core_ref.at[0], chip_ref.at[me & 1], core_ref.at[1])):
        at = pl.multiple_of((me ^ mask) * rows, rows)
        pltpu.make_async_copy(src, dst.at[pl.ds(at, rows), :], sem).start()

def qkv_kernel(ids_ref, x4_ref, chip_ref, core_ref, *refs, masks):
    gathered = refs[:len(masks)]
    bucket_ref = refs[len(masks)]
    x_out, h_out, q_out, k_out, v_out, w_out, gain_ref, t_ref, trev_ref, xs, hs, ps, ws, es, sems = refs[len(masks) + 1:]
    me, flat = ids_ref[0], ids_ref[1]
    width = xs.shape[1]
    own = width // es.shape[0]
    pull_sequence(me, x4_ref, chip_ref, core_ref, xs, sems.at[0])
    for ref, ids in zip(gathered, masks):
        for j, mask in enumerate(ids):
            shard = flat ^ mask
            pltpu.make_async_copy(ref.at[j, 3 * own:3 * own + 16, :], es.at[shard], sems.at[1]).start()
    for ref, ids in zip(gathered, masks):
        for j, mask in enumerate(ids):
            at = pl.multiple_of((flat ^ mask) * own, own)
            for i in range(3):
                pltpu.make_async_copy(ref.at[j, i * own:(i + 1) * own, :], ws.at[pl.ds(at, own), i * width:(i + 1) * width], sems.at[2]).start()
    pltpu.make_async_copy(es, es, sems.at[1]).wait()
    extras = es[...].astype(jnp.float32)
    gains = jnp.sum(extras, axis=0)
    gain_ref[...] = gains[0:8]
    table = extras[:, 8, 0:128].astype(jnp.bfloat16)
    ids = lax.broadcasted_iota(jnp.int32, (es.shape[0], 1), 0)
    heads = t_ref.shape[0]
    for i, ref in enumerate((t_ref, trev_ref)):
        hot = jnp.where(bucket_ref[i:i + 1, :] == ids, 1.0, 0.0).astype(jnp.bfloat16)
        ref[...] = _dot(table, hot, TN)[0:heads] * LOG2E
    pltpu.make_async_copy(xs, xs, sems.at[0]).wait()
    part = 256
    def norm(i, carry):
        at = pl.ds(pl.multiple_of(i * part, part), part)
        x = xs[at, :].astype(jnp.float32)
        hs[at, :] = (x * rms_inverse(x) * gains[0:1]).astype(jnp.bfloat16)
        return carry
    lax.fori_loop(0, xs.shape[0] // part, norm, 0)
    copies = [pltpu.make_async_copy(xs, x_out, sems.at[0]), pltpu.make_async_copy(hs, h_out, sems.at[1])]
    for copy in copies:
        copy.start()
    pltpu.make_async_copy(ws, ws, sems.at[2]).wait()
    copies.append(pltpu.make_async_copy(ws, w_out, sems.at[2]))
    copies[-1].start()
    for i, ref in enumerate((q_out, k_out, v_out)):
        full = _dot(hs[...], ws[:, i * width:(i + 1) * width])
        ps[i] = (full * LOG2E if i == 0 else full).astype(jnp.bfloat16)
        copies.append(pltpu.make_async_copy(ps.at[i], ref, sems.at[3 + i]))
        copies[-1].start()
    for copy in copies:
        copy.wait()

def qkv_fwd(ids, x4, came, gathered, masks, bucket_rows, heads):
    parts, rows, width = x4.shape
    total = parts * rows
    shards = sum(len(m) for m in masks)
    mat = jax.ShapeDtypeStruct((total, width), jnp.bfloat16)
    wide = bucket_rows.shape[1]
    vm = lambda *s: pltpu.VMEM(s, jnp.bfloat16)
    return pl.pallas_call(
        functools.partial(qkv_kernel, masks=masks),
        out_shape=(mat,) * 5 + (jax.ShapeDtypeStruct((width, 3 * width), jnp.bfloat16), jax.ShapeDtypeStruct((8, width), jnp.float32),
                                jax.ShapeDtypeStruct((heads, wide), jnp.float32), jax.ShapeDtypeStruct((heads, wide), jnp.float32)),
        in_specs=[SM] + [ANY] * (3 + len(gathered)) + [VM],
        out_specs=[ANY] * 6 + [VM] * 3,
        scratch_shapes=[vm(total, width), vm(total, width), vm(3, total, width), vm(width, 3 * width), vm(shards, 16, width), pltpu.SemaphoreType.DMA((6,))],
        compiler_params=pltpu.CompilerParams(vmem_limit_bytes=LIMIT),
        cost_estimate=LIGHT,
        name="qkv_fwd",
    )(ids, x4, *came, *gathered, bucket_rows)

def gelu_both(v):
    t = jnp.tanh(root_coef * (v + cubic_coef * v * v * v))
    half = 0.5 * (1.0 + t)
    slope = half + 0.5 * v * (1.0 - t * t) * (root_coef * (1.0 + 3.0 * cubic_coef * v * v))
    return v * half, slope

def by_core(core, keep, send, src, dst_rows, sem, lead=slice(None), src_rows=slice(None), lanes=slice(None)):
    for parity in range(2):
        @pl.when(core == parity)
        def _():
            for dst, at in ((keep, parity), (send, 1 - parity)):
                pltpu.make_async_copy(src.at[lead, at, src_rows, lanes], dst.at[lead, dst_rows, lanes], sem).start()

def ff_chunks(h2, h2t, gm, acc, gh2, ws_in, ws_back, st_in, st_back, row_in, emit, before_add, cols=512):
    steps = ws_in.shape[1] // cols
    half, width = st_back.shape[2:]
    own = width // (2 * st_in.shape[0])
    wide = width // cols
    group = cols // (2 * half)

    def step(c, carry):
        at = pl.ds(pl.multiple_of(c * cols, cols), cols)
        win, wback = ws_in[:, at], ws_back[at, :]
        pre = _dot(h2[...], win)
        grad_active = _dot(gm[...], wback, NT)
        act, slope = gelu_both(pre)
        active = act.astype(jnp.bfloat16)
        gpre = (grad_active * slope).astype(jnp.bfloat16)
        @pl.when(c == 0)
        def _():
            before_add()
        acc[...] += _dot(active, wback)
        gh2[...] += _dot(gpre, win, NT)
        lead = pl.ds(c * group, group)
        st_back[lead] = _dot(active, gm[...], TN).astype(jnp.bfloat16).reshape(group, 2, half, width)
        emit(st_back, 0, lead=lead, dst_rows=slice(0, half))
        up = pl.multiple_of((c // wide) * own, own)
        lanes = pl.ds(pl.multiple_of((c % wide) * cols, cols), cols)
        st_in[:, :, pl.ds(up, own), lanes] = _dot(h2t[...], gpre).astype(jnp.bfloat16).reshape(-1, 2, own, cols)
        emit(st_in, 1, src_rows=pl.ds(up, own), dst_rows=pl.ds(row_in + up, own), lanes=lanes)
        return carry
    lax.fori_loop(0, steps, step, 0)

def finish_chunks(st_in, st_back, sems):
    pltpu.make_async_copy(st_back, st_back, sems.at[0]).wait()
    pltpu.make_async_copy(st_in, st_in, sems.at[1]).wait()

def aligned(at, size):
    return at if isinstance(at, int) else pl.multiple_of(at, size)

def pull_ff(flat, gathered, masks, ws_in, ws_back, row_in, sems):
    width = ws_in.shape[0]
    shards = sum(len(m) for m in masks)
    own, half = width // shards, ws_back.shape[0] // shards
    for ref, ids in zip(gathered, masks):
        for j, mask in enumerate(ids):
            shard = flat ^ mask
            pltpu.make_async_copy(ref.at[j, 0:half, :], ws_back.at[pl.ds(aligned(shard * half, half), half), :], sems.at[1]).start()
            at = pl.ds(aligned(shard * own, own), own)
            for i in range(ws_in.shape[1] // width):
                pltpu.make_async_copy(ref.at[j, row_in + i * own:row_in + (i + 1) * own, :], ws_in.at[at, i * width:(i + 1) * width], sems.at[0]).start()

def mid_a_kernel(ids_ref, x_hbm, o_hbm, g4_ref, chip_ref, core_ref, gain_ref, *refs, masks):
    gathered = refs[:len(masks)]
    (mixed_out, acc_out, gh2_out, h2_out, h2t_out, gm_out, wo_out, keep_out, send_out,
     xs, os, wo, ws_in, ws_back, mixed, h2, h2t, acc, gh2, gm, st_in, st_back, sems) = refs[len(masks):]
    flat = ids_ref[1]
    rows, width = xs.shape
    half, own = st_back.shape[2], width // (2 * st_in.shape[0])
    core = flat & 1
    def emit(src, which, **at):
        by_core(core, keep_out, send_out, src, sem=sems.at[which], **at)
    loads = [pltpu.make_async_copy(x_hbm, xs, sems.at[0]), pltpu.make_async_copy(o_hbm, os, sems.at[1])]
    for load in loads:
        load.start()
    for ref, ids in zip(gathered, masks):
        for j, mask in enumerate(ids):
            at = pl.ds(pl.multiple_of((flat ^ mask) * own, own), own)
            pltpu.make_async_copy(ref.at[j, half:half + own, :], wo.at[at, :], sems.at[2]).start()
    pull_ff(flat, gathered, masks, ws_in, ws_back, half + own, sems.at[3:5])
    pull_sequence(ids_ref[0], g4_ref, chip_ref, core_ref, gm, sems.at[5])
    for load in loads:
        load.wait()
    pltpu.make_async_copy(wo, wo, sems.at[2]).wait()
    stores = [pltpu.make_async_copy(wo, wo_out, sems.at[2])]
    stores[0].start()
    part = 256
    def load_rows(i, carry):
        at = pl.ds(pl.multiple_of(i * part, part), part)
        value = xs[at, :].astype(jnp.float32) + _dot(os[at, :], wo[...])
        mixed[at, :] = value
        acc[at, :] = value
        hidden = (value * rms_inverse(value) * gain_ref[1:2, :]).astype(jnp.bfloat16)
        h2[at, :] = hidden
        h2t[:, at] = hidden.T
        gh2[at, :] = jnp.zeros_like(value)
        return carry
    lax.fori_loop(0, rows // part, load_rows, 0)
    pltpu.make_async_copy(gm, gm, sems.at[5]).wait()
    row_ok = lax.broadcasted_iota(jnp.int32, (rows, 1), 0) < ids_ref[2]
    gm[...] = jnp.where(row_ok, gm[...], jnp.zeros_like(gm[...]))
    pltpu.make_async_copy(ws_in, ws_in, sems.at[3]).wait()
    pltpu.make_async_copy(ws_back, ws_back, sems.at[4]).wait()
    for i, (src, dst) in enumerate(((mixed, mixed_out), (h2, h2_out), (h2t, h2t_out), (gm, gm_out))):
        stores.append(pltpu.make_async_copy(src, dst, sems.at[6 + i]))
        stores[-1].start()
    ff_chunks(h2, h2t, gm, acc, gh2, ws_in, ws_back, st_in, st_back, half, emit, lambda: None)
    for i, (src, dst) in enumerate(((acc, acc_out), (gh2, gh2_out))):
        stores.append(pltpu.make_async_copy(src, dst, sems.at[3 + i]))
        stores[-1].start()
    finish_chunks(st_in, st_back, sems.at[0:2])
    for store in stores:
        store.wait()

def mid_a(ids, x, o, g4, came, gains, gathered, masks, ff):
    rows, width = x.shape
    shards = sum(len(m) for m in masks)
    half = ff // shards
    low = lambda *s: jax.ShapeDtypeStruct(s, jnp.bfloat16)
    full = lambda *s: jax.ShapeDtypeStruct(s, jnp.float32)
    vm = lambda *s: pltpu.VMEM(s, jnp.bfloat16)
    vf = lambda *s: pltpu.VMEM(s, jnp.float32)
    stack = half + ff // width * (width // shards)
    return pl.pallas_call(
        functools.partial(mid_a_kernel, masks=masks),
        out_shape=(full(rows, width), full(rows, width), full(rows, width), low(rows, width), low(width, rows), low(rows, width), low(width, width), low(shards // 2, stack, width), low(shards // 2, stack, width)),
        in_specs=[SM] + [ANY] * 5 + [VM] + [ANY] * len(gathered), out_specs=[ANY] * 9,
        scratch_shapes=[vm(rows, width), vm(rows, width), vm(width, width), vm(width, ff), vm(ff, width), vf(rows, width), vm(rows, width), vm(width, rows),
                        vf(rows, width), vf(rows, width), vm(rows, width), vm(shards // 2, 2, stack - half, width), vm(shards // 2, 2, half, width), pltpu.SemaphoreType.DMA((10,))],
        compiler_params=pltpu.CompilerParams(vmem_limit_bytes=LIMIT),
        cost_estimate=LIGHT,
        name="mid_a",
    )(ids, x, o, g4, *came, gains, *gathered)

def mid_b_kernel(ids_ref, gain_ref, mixed_hbm, acc_hbm, gh2_hbm, h2_hbm, h2t_hbm, gm_hbm, wo_hbm, o_hbm, full_ref, *refs):
    (out_ref, gb_out, do_ref, keep_out, send_out,
     os, wo, ws_in, ws_back, mixed, h2, h2t, acc, gh2, gm, gb, st_in, st_back, st_o, sems) = refs
    rows, width = os.shape
    shards, half, own = 2 * st_in.shape[0], st_back.shape[2], width // (2 * st_in.shape[0])
    core = ids_ref[1] & 1
    def emit(src, which, **at):
        by_core(core, keep_out, send_out, src, sem=sems.at[which], **at)
    early = [(h2_hbm, h2), (gm_hbm, gm), (h2t_hbm, h2t)]
    late = [(acc_hbm, acc), (gh2_hbm, gh2), (mixed_hbm, mixed), (wo_hbm, wo), (o_hbm, os)]
    early = [pltpu.make_async_copy(a, b, sems.at[4 + i]) for i, (a, b) in enumerate(early)]
    late = [pltpu.make_async_copy(a, b, sems.at[7 + i]) for i, (a, b) in enumerate(late)]
    for load in early:
        load.start()
    pull_ff(0, (full_ref,), (range(shards),), ws_in, ws_back, half, sems.at[2:4])
    for load in late:
        load.start()
    for load in early:
        load.wait()
    pltpu.make_async_copy(ws_in, ws_in, sems.at[2]).wait()
    pltpu.make_async_copy(ws_back, ws_back, sems.at[3]).wait()
    def before_add():
        late[0].wait()
        late[1].wait()
    ff_chunks(h2, h2t, gm, acc, gh2, ws_in, ws_back, st_in, st_back, half + own, emit, before_add)
    for load in late[2:]:
        load.wait()
    part = 256
    def finish(i, carry):
        at = pl.ds(pl.multiple_of(i * part, part), part)
        out_ref[at, :] = acc[at, :].astype(jnp.bfloat16)
        value = mixed[at, :]
        inverse = rms_inverse(value)
        normed = value * inverse
        scaled = gh2[at, :] * gain_ref[1:2, :]
        grad = inverse * (scaled - normed * jnp.mean(scaled * normed, axis=1, keepdims=True)) + gm[at, :].astype(jnp.float32)
        low = grad.astype(jnp.bfloat16)
        gb[at, :] = low
        do_ref[at, :] = _dot(low, wo[...], NT).astype(jnp.bfloat16)
        return carry
    lax.fori_loop(0, rows // part, finish, 0)
    st_o[...] = _dot(os[...], gb[...], TN).astype(jnp.bfloat16).reshape(st_o.shape)
    emit(st_o, 2, dst_rows=slice(half, half + own))
    store = pltpu.make_async_copy(gb, gb_out, sems.at[3])
    store.start()
    finish_chunks(st_in, st_back, sems.at[0:2])
    pltpu.make_async_copy(st_o, st_o, sems.at[2]).wait()
    store.wait()

def mid_b(ids, gains, state, o, full, ff):
    rows, width = o.shape
    shards = full.shape[0]
    half, own = ff // shards, width // shards
    low = lambda *s: jax.ShapeDtypeStruct(s, jnp.bfloat16)
    vm = lambda *s: pltpu.VMEM(s, jnp.bfloat16)
    vf = lambda *s: pltpu.VMEM(s, jnp.float32)
    rest = ff // width * own
    return pl.pallas_call(
        mid_b_kernel,
        out_shape=(low(rows, width), low(rows, width), low(rows, width), low(shards // 2, half + own + rest, width), low(shards // 2, half + own + rest, width)),
        in_specs=[SM, VM] + [ANY] * 9, out_specs=[VM, ANY, VM, ANY, ANY],
        scratch_shapes=[vm(rows, width), vm(width, width), vm(width, ff), vm(ff, width), vf(rows, width), vm(rows, width), vm(width, rows),
                        vf(rows, width), vf(rows, width), vm(rows, width), vm(rows, width), vm(shards // 2, 2, rest, width), vm(shards // 2, 2, half, width), vm(shards // 2, 2, own, width),
                        pltpu.SemaphoreType.DMA((12,))],
        compiler_params=pltpu.CompilerParams(vmem_limit_bytes=LIMIT),
        cost_estimate=LIGHT,
        name="mid_b",
    )(ids, gains, *state, o, full)

def gw_kernel(ids_ref, h_ref, dq_ref, dk_ref, dv_ref, bucket_ref, *refs):
    keep_out, send_out, st, sems = refs[-4:]
    pairs, _, stack, cols = st.shape
    own = h_ref.shape[1] // (2 * pairs)
    core = ids_ref[1] & 1
    if refs[:-4]:
        offs = jnp.concatenate([ref[...] for ref in refs[:-4]], 0)
        ids = lax.broadcasted_iota(jnp.int32, (2 * pairs, 1), 0)
        hot = jnp.where(bucket_ref[1:2, :] == ids, 1.0, 0.0)
        table = lax.dot_general(hot, offs, NT, precision=lax.Precision.HIGHEST, preferred_element_type=jnp.float32)
        heads = offs.shape[0]
        st[:, :, 3 * own:, :] = jnp.zeros((pairs, 2, stack - 3 * own, cols), jnp.bfloat16)
        st[:, :, 3 * own:3 * own + 1, 0:heads] = table.astype(jnp.bfloat16).reshape(pairs, 2, 1, heads)
    for i, ref in enumerate((dq_ref, dk_ref, dv_ref)):
        at = slice(i * own, (i + 1) * own) if i < 2 else slice(i * own, stack)
        st[:, :, i * own:(i + 1) * own, :] = _dot(h_ref[...], ref[...], TN).astype(jnp.bfloat16).reshape(pairs, 2, own, cols)
        by_core(core, keep_out, send_out, st, at, sems.at[0], src_rows=at)
    pltpu.make_async_copy(st, st, sems.at[0]).wait()

def qkv_gw(ids, h, dq, dk, dv, bucket_rows, offs, shards, first, cols):
    rows, width = h.shape
    stack = 3 * width // shards + (16 if offs else 0)
    half = jax.ShapeDtypeStruct((shards // 2, stack, cols), jnp.bfloat16)
    part = pl.BlockSpec((rows, cols), lambda i: (0, first // cols))
    whole = lambda a: pl.BlockSpec(a.shape, lambda i: (0, 0))
    return pl.pallas_call(
        gw_kernel, out_shape=(half, half), grid=(1,),
        in_specs=[SM, whole(h), part, part, part, whole(bucket_rows)] + [whole(o) for o in offs], out_specs=[ANY, ANY],
        scratch_shapes=[pltpu.VMEM((shards // 2, 2, stack, cols), jnp.bfloat16), pltpu.SemaphoreType.DMA((1,))],
        compiler_params=pltpu.CompilerParams(vmem_limit_bytes=LIMIT),
        cost_estimate=LIGHT,
        name="qkv_gw",
    )(ids, h, dq, dk, dv, bucket_rows, *offs)

def gx_kernel(x_ref, gb_ref, dq_ref, dk_ref, dv_ref, gain_ref, w_ref, out_ref):
    width = x_ref.shape[1]
    grad = _dot(dq_ref[...], w_ref[:, :width], NT)
    grad += _dot(dk_ref[...], w_ref[:, width:2 * width], NT)
    grad += _dot(dv_ref[...], w_ref[:, 2 * width:3 * width], NT)
    x = x_ref[...].astype(jnp.float32)
    inverse = rms_inverse(x)
    normed = x * inverse
    scaled = grad * gain_ref[0:1, :]
    out = inverse * (scaled - normed * jnp.mean(scaled * normed, axis=1, keepdims=True)) + gb_ref[...].astype(jnp.float32)
    out_ref[...] = out.astype(jnp.bfloat16)

def qkv_gx(x, gb, dq, dk, dv, gains, w, rows=512):
    total, width = x.shape
    blk = pl.BlockSpec((rows, width), lambda i: (i, 0))
    return pl.pallas_call(
        gx_kernel, out_shape=jax.ShapeDtypeStruct((total, width), jnp.bfloat16), grid=(total // rows,),
        in_specs=[blk] * 5 + [pl.BlockSpec(gains.shape, lambda i: (0, 0)),
                              pl.BlockSpec((width, 3 * width), lambda i: (0, 0), pipeline_mode=pl.Buffered(1))],
        out_specs=blk,
        compiler_params=pltpu.CompilerParams(vmem_limit_bytes=LIMIT),
        cost_estimate=LIGHT,
        name="qkv_gx",
    )(x, gb, dq, dk, dv, gains, w)

def swap(value, axis, mask):
    return lax.ppermute(value, axis, [(i, i ^ mask) for i in range(lax.axis_size(axis))])


def send_chip(blocks, me):
    return swap(lax.dynamic_slice_in_dim(blocks, 2 * (1 - me // 2), 2, 0), "seq", 2)


def send_core(blocks, from_chip, me):
    own = lax.dynamic_index_in_dim(blocks, me ^ 1, 0)
    passed = lax.dynamic_index_in_dim(from_chip, 1 - me % 2, 0)
    return swap(jnp.concatenate([own, passed], 0), "seq", 1)


class Gather:
    def __init__(self, shard):
        shard = shard[None]
        self.sent = [shard] + [swap(shard, "dp", 2 * z) for z in (1, 2, 3)]
        self.pieces, self.masks = [], []

    def take(self, piece, mask, rows=(0, 1, 2, 3)):
        ids = tuple(8 * z | mask for z in rows)
        self.pieces += [piece, swap(piece, "seq", 1)]
        self.masks += [ids, tuple(m | 1 for m in ids)]

    def fill(self):
        self.own = jnp.concatenate(self.sent, 0)

    def sides(self):
        self.x, self.y = swap(self.own, "seq", 2), swap(self.own, "dp", 1)

    def corner_halves(self):
        self.near, self.far = swap(self.y[:2], "seq", 2), swap(self.x[2:], "dp", 1)

    def corner_y(self):
        self.corner = swap(self.x, "dp", 1)

    def all_pieces(self):
        return tuple(self.pieces), tuple(self.masks)


class Scatter:
    def __init__(self, keep, send, pos, corner_y):
        self.z, self.y, self.x = pos
        cube = (4, 2, 2) + keep.shape[1:]
        self.mine, self.sent, self.corner_y = keep.reshape(cube), send.reshape(cube), corner_y
        self.other = swap(self.sent, "seq", 1)

    def fold(self):
        pick = lambda v, at, axis: lax.dynamic_index_in_dim(v, at, axis, keepdims=False)
        def quarter(dy, dx):
            cut = lambda v: pick(pick(v, self.y ^ dy, 1), self.x ^ dx, 1).astype(jnp.float32)
            return (cut(self.mine) + cut(self.other)).astype(jnp.bfloat16)
        far = quarter(1, 1)
        self.to_x, self.to_y, self.own = quarter(0, 1), quarter(1, 0), quarter(0, 0)
        if self.corner_y:
            self.came_x, self.came_y = None, swap(far, "dp", 1)
        else:
            self.came_x, self.came_y = swap(far[:2], "seq", 2), swap(far[2:], "dp", 1)

    def turn(self):
        add = lambda a, b: (a.astype(jnp.float32) + b.astype(jnp.float32)).astype(jnp.bfloat16)
        if self.corner_y:
            to_y, = tie(self.came_y, self.to_y)
            to_x = add(self.to_x, self.came_y)
        else:
            to_x = jnp.concatenate([self.to_x[:2], add(self.to_x[2:], self.came_y)], 0)
            to_y = jnp.concatenate([add(self.to_y[:2], self.came_x), self.to_y[2:]], 0)
        self.sent = (to_x, to_y)
        self.came_x, self.came_y = swap(to_x, "seq", 2), swap(to_y, "dp", 1)

    def column(self):
        total = self.own.astype(jnp.float32) + self.came_x.astype(jnp.float32) + self.came_y.astype(jnp.float32)
        total = total.astype(jnp.bfloat16)
        block = lambda k: lax.dynamic_index_in_dim(total, self.z ^ k, 0, keepdims=False)
        self.mine = block(0)
        self.came = [swap(block(k), "dp", 2 * k) for k in (1, 2, 3)]

    def result(self):
        return sum((c.astype(jnp.float32) for c in self.came), self.mine.astype(jnp.float32))


def place(blocks, from_chip, from_core, me):
    for mask, block in ((1, from_core[0:1]), (2, lax.dynamic_index_in_dim(from_chip, me % 2, 0)), (3, from_core[1:2])):
        blocks = lax.dynamic_update_slice_in_dim(blocks, block, me ^ mask, 0)
    return blocks


def tie(first, *later):
    return lax.optimization_barrier((first,) + later)[1:]


def local_whole(tokens, cotangent, lengths, buckets, norm1_gain, w_query, w_key, w_value, w_out, rel_table, norm2_gain, w_in, w_back):
    micro_count, seq_count, rows, width = tokens.shape
    parts = micro_count * seq_count
    both = ("dp", "seq")
    me, dp = lax.axis_index("seq"), lax.axis_index("dp")
    shards = lax.axis_size("seq") * lax.axis_size("dp")
    flat = dp * parts + me
    pos = (dp // 2, dp % 2, me // 2)
    low = lambda v: v.astype(jnp.bfloat16)
    up = lambda v: v.astype(jnp.float32)
    own, ff_own = w_query.shape[0], w_back.shape[0]
    ids = jnp.stack([me, flat, lax.dynamic_index_in_dim(lengths.reshape(parts), me, 0, keepdims=False)])
    length = ids[2:3]

    place_row = lambda v: lax.dynamic_update_slice(jnp.zeros((1, width), jnp.bfloat16), low(v)[None], (0, flat * own))
    small = jnp.concatenate([place_row(norm1_gain), place_row(norm2_gain), jnp.zeros((6, width), jnp.bfloat16),
                             jnp.pad(low(rel_table)[None], ((0, 7), (0, width - HEADS)))], 0)
    shard1 = jnp.concatenate([low(w_query), low(w_key), low(w_value), small], 0)
    ff = w_in.shape[1] // 2
    half = ff_own // 2
    halves = low(w_in).reshape(own, shards, 2, half)
    in_half = lambda i: [halves[:, :, i].reshape(own, ff)[:, j:j + width] for j in range(0, ff, width)]
    shard2 = jnp.concatenate([low(w_back[:half]), low(w_out)] + in_half(0), 0)
    shard3 = jnp.concatenate([low(w_back[half:])] + in_half(1), 0)
    x4, g4 = tokens.reshape(parts, rows, width), cotangent.reshape(parts, rows, width)
    bucket_rows = jnp.stack([jnp.pad(buckets, (0, 1), constant_values=-1), jnp.pad(buckets[::-1], (0, 1), constant_values=-1)])

    g1 = Gather(shard1)
    x_chip = send_chip(x4, me)
    g2 = Gather(shard2)
    g1.fill()
    g1.own, = tie((x_chip, g2.sent[1], shard3), g1.own)
    g1.sides()
    g1.x, g1.y = tie(g2.sent[2], g1.x, g1.y)
    g1.corner_halves()
    g2.fill()
    g1.take(g1.own, 0)
    g1.near, g1.far, g2.own = tie(g1.pieces[1], g1.near, g1.far, g2.own)
    g2.sides()
    g1.x, g1.y, x4_in = tie((g1.near, g1.far), g1.x, g1.y, x4)
    g1.take(g1.x, 2)
    g1.take(g1.y, 4)
    g1.take(g1.near, 6, (0, 1))
    g1.take(g1.far, 6, (2, 3))
    x_core = send_core(x4_in, x_chip, me)
    shard3, = tie((g1.near, g1.far), shard3)
    full3 = lax.all_gather(shard3, both, axis=0, tiled=False)
    x, hidden, q, k, v, w_qkv, gains, t, t_back = qkv_fwd(ids, x4, (x_chip, x_core), *g1.all_pieces(), bucket_rows, HEADS)
    pairs = HEADS // 2
    att = attn_fwd(length, q, k, v, t, 0, pairs // 2)
    g2.take(g2.own, 0)
    g2.x, g2.y = tie((att[0], g2.pieces[1]), g2.x, g2.y)
    g2.corner_y()
    g4_in, = tie(g2.x, g4)
    g_chip = send_chip(g4_in, me)
    g2.take(g2.x, 2)
    g2.take(g2.y, 4)
    q_in, = tie((g2.x, g2.y), q)
    attended, lse = attn_fwd(length, q_in, k, v, t, pairs // 2, pairs // 2, att)
    g2.corner, g_chip = tie((attended, g2.pieces[3], g2.pieces[5]), g2.corner, g_chip)
    g2.take(g2.corner, 6)
    g_core = send_core(g4, g_chip, me)
    *state, keep3, send3 = mid_a(ids, x, attended, g4, (g_chip, g_core), gains, *g2.all_pieces(), ff)
    sc3 = Scatter(keep3, send3, pos, True)
    out, gb, g_att, keep2, send2 = mid_b(ids, gains, state, attended, full3, ff)
    sc3.other, = tie(gb, sc3.other)
    sc3.fold()
    send2, = tie(sc3.own, send2)
    sc2 = Scatter(keep2, send2, pos, False)
    out4 = out.reshape(parts, rows, width)
    out4, = tie(sc3.own, out4)
    out_chip = send_chip(out4, me)
    count = pairs // 4
    back = lambda first, g, prev: attn_bwd(length, q, k, v, g, attended, lse, t_back, first, count, prev)
    g_att, = tie(sc3.own, g_att)
    dq, dk, dv, off0 = back(0, g_att, None)
    sc2.other, = tie(off0, sc2.other)
    sc2.fold()
    sc3.came_y, = tie(sc2.own, sc3.came_y)
    sc3.turn()
    g_att, = tie(sc3.sent, g_att)
    dq, dk, dv, off1 = back(count, g_att, (dq, dk, dv))
    sc2.came_x, sc2.came_y = tie((off1, out_chip), sc2.came_x, sc2.came_y)
    sc2.turn()
    out4_in, out_chip = tie(sc2.sent, out4, out_chip)
    out_core = send_core(out4_in, out_chip, me)
    g_att, = tie(sc2.sent, g_att)
    dq, dk, dv, off2 = back(2 * count, g_att, (dq, dk, dv))
    cols = 128 * count
    sc3.came_x, sc3.came_y = tie((off2, out_core), sc3.came_x, sc3.came_y)
    h_in, = tie((sc3.came_x, sc3.came_y), hidden)
    keep, send = qkv_gw(ids, h_in, dq, dk, dv, bucket_rows, (), shards, 0, 3 * cols)
    sc3.came_x, sc2.came_x, sc2.came_y = tie(keep, sc3.came_x, sc2.came_x, sc2.came_y)
    sc3.column()
    sc2.column()
    g_att, send = tie((sc3.mine, sc2.mine), g_att, send)
    sc1 = Scatter(keep, send, pos, False)
    dq, dk, dv, off3 = back(3 * count, g_att, (dq, dk, dv))
    sc1.other, = tie(off3, sc1.other)
    sc1.fold()
    h_in, = tie((sc1.own, sc3.came), hidden)
    keep, send = qkv_gw(ids, h_in, dq, dk, dv, bucket_rows, (off0, off1, off2, off3), shards, 3 * cols, cols)
    sc0 = Scatter(keep, send, pos, False)
    gb_in, = tie(keep, gb)
    gx = qkv_gx(x, gb_in, dq, dk, dv, gains, w_qkv)
    sc1.came_x, sc1.came_y = tie(gx, sc1.came_x, sc1.came_y)
    sc1.turn()
    gx, = tie(sc1.sent, gx)
    gx4 = gx.reshape(parts, rows, width)
    gx_chip = send_chip(gx4, me)
    sc0.other, = tie((sc1.sent, sc2.came), sc0.other)
    sc0.fold()
    out4, out_chip, out_core = tie(sc0.own, out4, out_chip, out_core)
    layer_out = place(out4, out_chip, out_core, me)
    sc1.came_x, sc1.came_y = tie(layer_out, sc1.came_x, sc1.came_y)
    sc1.column()
    sc0.came_x, sc0.came_y = tie(sc1.mine, sc0.came_x, sc0.came_y)
    sc0.turn()
    sc2.came = list(tie(sc0.sent, *sc2.came))
    sc3.came = list(tie(sc0.sent, *sc3.came))
    r2, r_a = sc2.result(), sc3.result()
    sc0.came_x, sc0.came_y = tie((r2, sc1.came[0]), sc0.came_x, sc0.came_y)
    sc0.column()
    gx4, gx_chip = tie((sc0.mine, sc1.came, sc0.came[0]), gx4, gx_chip)
    gx_core = send_core(gx4, gx_chip, me)
    input_grad = place(gx4, gx_chip, gx_core, me)
    sc0.came = list(tie(input_grad, *sc0.came))
    r1, r0 = sc1.result(), sc0.result()
    join = lambda v: jnp.concatenate([v[i:i + own] for i in range(0, v.shape[0], own)], 1).reshape(own, shards, 1, half)
    g_in = jnp.concatenate([join(r_a[half:]), join(r2[half + own:])], 2).reshape(w_in.shape)
    g_back = jnp.concatenate([r_a[:half], r2[:half]], 0)
    table_row = r0[3 * own, :HEADS]
    r1 = jnp.concatenate([r1, r0[:3 * own]], 1)
    prod = up(shard1[:3 * own]) * r1
    g_gain1 = jnp.sum(prod[:own] + prod[own:2 * own] + prod[2 * own:], axis=1) / up(low(norm1_gain))
    g_gain2 = jnp.sum(up(low(w_in)) * g_in, axis=1) / up(low(norm2_gain))
    return (layer_out.reshape(tokens.shape), input_grad.reshape(tokens.shape), g_gain1, r1[:own], r1[own:2 * own], r1[2 * own:3 * own],
            r2[half:half + own], table_row, g_gain2, g_in, g_back)


def local_any(shape, tokens, *rest):
    fits = tuple(shape) == (8, 4) and tokens.shape[0] * tokens.shape[1] == 4 and tokens.shape[3] == HEADS * DH == 1024
    return (local_whole if fits else local)(tokens, *rest)


def solution(mesh):
    return jax.shard_map(
        functools.partial(local_any, mesh.devices.shape),
        mesh=mesh,
        in_specs=(
            P(None, "dp", "seq", None),
            P(None, "dp", "seq", None),
            P(None, "dp"),
            P(),
            P(("dp", "seq")),
            P(("dp", "seq"), None),
            P(("dp", "seq"), None),
            P(("dp", "seq"), None),
            P(("dp", "seq"), None),
            P(("dp", "seq")),
            P(("dp", "seq")),
            P(("dp", "seq"), None),
            P(("dp", "seq"), None),
        ),
        out_specs=(
            P(None, "dp", "seq", None),
            P(None, "dp", "seq", None),
            P(("dp", "seq")),
            P(("dp", "seq"), None),
            P(("dp", "seq"), None),
            P(("dp", "seq"), None),
            P(("dp", "seq"), None),
            P(("dp", "seq")),
            P(("dp", "seq")),
            P(("dp", "seq"), None),
            P(("dp", "seq"), None),
        ),
        check_vma=False,
    )
```

```python
import functools

import jax
import jax.numpy as jnp
from jax import lax
from jax.experimental import pallas as pl
from jax.experimental.pallas import tpu as pltpu
from jax.sharding import PartitionSpec as P

HEADS = 16
DH = 64
BUCKETS = 32


epsilon = 1e-06
floor_score = -1e30
highest = lax.Precision.HIGHEST
root_coef = 0.7978845608
cubic_coef = 0.044715


def gelu_tanh(values):
    return (
        0.5
        * values
        * (1.0 + jnp.tanh(root_coef * (values + cubic_coef * values * values * values)))
    )


def gelu_slope(values):
    inner = jnp.tanh(root_coef * (values + cubic_coef * values * values * values))
    return 0.5 * (1.0 + inner) + 0.5 * values * (1.0 - inner * inner) * root_coef * (
        1.0 + 3.0 * cubic_coef * values * values
    )


def project(acts, weight):
    return jnp.einsum("srd,de->sre", acts, weight, preferred_element_type=jnp.float32)


def project_back(grads_in, weight):
    return jnp.einsum("sre,de->srd", grads_in, weight, preferred_element_type=jnp.float32)


def contract(acts, grads_in):
    return jnp.einsum("srd,sre->de", acts, grads_in, preferred_element_type=jnp.float32)


def rms_forward(values, gain):
    inverse = lax.rsqrt(jnp.mean(values * values, axis=-1, keepdims=True) + epsilon)
    normed = values * inverse
    return (normed, inverse, (normed * gain.astype(jnp.float32)).astype(jnp.bfloat16))


def rms_backward(grad_hidden, normed, inverse, gain):
    scaled = grad_hidden * gain.astype(jnp.float32)
    grad_values = inverse * (scaled - normed * jnp.mean(scaled * normed, axis=-1, keepdims=True))
    return (grad_values, jnp.sum(grad_hidden * normed, axis=(0, 1)))


def score_block(per_head_queries, per_head_keys, rel_bias, key_valid):
    scores = (
        jnp.einsum(
            "ofck,owck->ocfw", per_head_queries, per_head_keys, preferred_element_type=jnp.float32
        )
        + rel_bias[None]
    )
    return jnp.where(key_valid, scores, floor_score)


def offset_sums(grid, first_row, seq_len):
    head_count, row_count, key_count = grid.shape
    flipped = grid[:, ::-1, :]
    padded = jnp.pad(flipped, ((0, 0), (0, 0), (0, row_count)))
    wide_len = key_count + row_count
    skewed = padded.reshape(head_count, row_count * wide_len)[:, : row_count * (wide_len - 1)]
    skewed = skewed.reshape(head_count, row_count, wide_len - 1)
    column_sums = jnp.sum(skewed, axis=1)
    placed = jnp.zeros((head_count, 2 * seq_len - 1), jnp.float32)
    begin = seq_len - row_count - first_row
    return lax.dynamic_update_slice(placed, column_sums, (jnp.int32(0), begin))


def run_micro(inputs, incoming, seq_lens, attn_set, mlp_set, context):
    onehot, offsets, row_pos, key_pos, first_row, seq_len = context
    gain_one, query_w, key_w, value_w, out_w, bias_table = attn_set
    gain_two, in_w, return_projection_weight = mlp_set
    seq_count, row_count, model_width = inputs.shape
    values = inputs.astype(jnp.float32)
    normed_one, inverse_one, hidden_one = rms_forward(values, gain_one)
    queries = project(hidden_one, query_w).astype(jnp.bfloat16)
    keys_own = project(hidden_one, key_w).astype(jnp.bfloat16)
    values_own = project(hidden_one, value_w).astype(jnp.bfloat16)
    keys_all, values_all = (
        lax.all_gather(keys_own, "seq", axis=1, tiled=True),
        lax.all_gather(values_own, "seq", axis=1, tiled=True),
    )
    per_offset = jnp.dot(
        onehot, bias_table.reshape(BUCKETS, HEADS), preferred_element_type=jnp.float32
    )
    rel_bias = jnp.transpose(per_offset[offsets], (2, 0, 1))
    key_valid = (key_pos[None, :] < seq_lens[:, None])[:, None, None, :]
    per_head_queries = queries.reshape(seq_count, row_count, HEADS, DH)
    per_head_keys = keys_all.reshape(seq_count, seq_len, HEADS, DH)
    per_head_values = values_all.reshape(seq_count, seq_len, HEADS, DH)
    scores = score_block(per_head_queries, per_head_keys, rel_bias, key_valid)
    row_max = jnp.max(scores, axis=-1, keepdims=True)
    exp_scores = jnp.exp(scores - row_max)
    row_total = jnp.sum(exp_scores, axis=-1, keepdims=True)
    attn_probs = exp_scores / row_total
    log_total = row_max + jnp.log(row_total)
    reduced_precision_probs = attn_probs.astype(jnp.bfloat16)
    attended = jnp.einsum(
        "jfpe,jefn->jpfn",
        reduced_precision_probs,
        per_head_values,
        preferred_element_type=jnp.float32,
    )
    attended = attended.reshape(seq_count, row_count, model_width).astype(jnp.bfloat16)
    residual_mid = values + project(attended, out_w)
    normed_two, inverse_two, hidden_two = rms_forward(residual_mid, gain_two)
    pre_act = project(hidden_two, in_w)
    active = gelu_tanh(pre_act).astype(jnp.bfloat16)
    result = (residual_mid + project(active, return_projection_weight)).astype(jnp.bfloat16)
    row_valid = (row_pos[None, :] < seq_lens[:, None]).astype(jnp.float32)[:, :, None]
    grad_out = incoming.astype(jnp.float32) * row_valid
    grad_low = grad_out.astype(jnp.bfloat16)
    grad_back = contract(active, grad_low)
    gradient_active_rows = project_back(grad_low, return_projection_weight)
    grad_pre = (gradient_active_rows * gelu_slope(pre_act)).astype(jnp.bfloat16)
    grad_in = contract(hidden_two, grad_pre)
    grad_hidden_two = project_back(grad_pre, in_w)
    grad_mixed, grad_gain_two = rms_backward(grad_hidden_two, normed_two, inverse_two, gain_two)
    grad_mixed = grad_mixed + grad_out
    grad_branch = grad_mixed.astype(jnp.bfloat16)
    grad_outw = contract(attended, grad_branch)
    gradient_attended_values = project_back(grad_branch, out_w).astype(jnp.bfloat16)
    gradient_attended_values = gradient_attended_values.reshape(seq_count, row_count, HEADS, DH)
    scores = score_block(per_head_queries, per_head_keys, rel_bias, key_valid)
    attn_probs = jnp.exp(scores - log_total)
    reduced_precision_probs = attn_probs.astype(jnp.bfloat16)
    grad_probs = jnp.einsum(
        "ofck,owck->ocfw",
        gradient_attended_values,
        per_head_values,
        preferred_element_type=jnp.float32,
    )
    inner_sum = jnp.sum(attn_probs * grad_probs, axis=-1, keepdims=True)
    gradient_score_matrix = (attn_probs * (grad_probs - inner_sum)).astype(jnp.bfloat16)
    grad_query = jnp.einsum(
        "jfpe,jefn->jpfn", gradient_score_matrix, per_head_keys, preferred_element_type=jnp.float32
    )
    grad_query = grad_query.astype(jnp.bfloat16).reshape(seq_count, row_count, model_width)
    key_part = jnp.einsum(
        "eciv,eicq->evcq",
        gradient_score_matrix,
        per_head_queries,
        preferred_element_type=jnp.float32,
    )
    value_part = jnp.einsum(
        "eciv,eicq->evcq",
        reduced_precision_probs,
        gradient_attended_values,
        preferred_element_type=jnp.float32,
    )
    key_part = key_part.reshape(seq_count, seq_len, model_width)
    value_part = value_part.reshape(seq_count, seq_len, model_width)
    grad_key, grad_value = (
        lax.psum_scatter(
            key_part.astype(jnp.bfloat16), "seq", scatter_dimension=1, tiled=True
        ).astype(jnp.float32),
        lax.psum_scatter(
            value_part.astype(jnp.bfloat16), "seq", scatter_dimension=1, tiled=True
        ).astype(jnp.float32),
    )
    grad_key = grad_key.astype(jnp.bfloat16)
    grad_value = grad_value.astype(jnp.bfloat16)
    offset_grad = offset_sums(
        jnp.sum(gradient_score_matrix.astype(jnp.float32), axis=0), first_row, seq_len
    )
    grad_table = jnp.dot(onehot.astype(jnp.float32).T, offset_grad.T, precision=highest).reshape(-1)
    grad_qw = contract(hidden_one, grad_query)
    grad_kw = contract(hidden_one, grad_key)
    grad_vw = contract(hidden_one, grad_value)
    grad_hidden_one = (
        project_back(grad_query, query_w)
        + project_back(grad_key, key_w)
        + project_back(grad_value, value_w)
    )
    grad_values, grad_gain_one = rms_backward(grad_hidden_one, normed_one, inverse_one, gain_one)
    grad_values = grad_values + grad_mixed
    gradients = (
        grad_gain_one,
        grad_qw,
        grad_kw,
        grad_vw,
        grad_outw,
        grad_table,
        grad_gain_two,
        grad_in,
        grad_back,
    )
    return (result, grad_values.astype(jnp.bfloat16), gradients)


def local(
    tokens,
    cotangent,
    lengths,
    buckets,
    norm1_gain,
    w_query,
    w_key,
    w_value,
    w_out,
    rel_table,
    norm2_gain,
    w_in,
    w_back,
):
    micro_count, seq_count, row_count, model_width = tokens.shape
    seq_parts = lax.axis_size("seq")
    seq_len = row_count * seq_parts
    first_row = lax.axis_index("seq") * row_count
    row_pos = first_row + jnp.arange(row_count, dtype=jnp.int32)
    key_pos = jnp.arange(seq_len, dtype=jnp.int32)
    onehot = (buckets[:, None] == jnp.arange(BUCKETS, dtype=jnp.int32)[None, :]).astype(
        jnp.bfloat16
    )
    offsets = key_pos[None, :] - row_pos[:, None] + (seq_len - 1)
    context = (onehot, offsets, row_pos, key_pos, first_row, seq_len)
    outputs = []
    input_grads = []
    pending = None
    shard_sums = None
    for micro_step in range(micro_count):
        attn_set = (
            lax.all_gather(norm1_gain.astype(jnp.bfloat16), ("dp", "seq"), axis=0, tiled=True),
            lax.all_gather(w_query.astype(jnp.bfloat16), ("dp", "seq"), axis=0, tiled=True),
            lax.all_gather(w_key.astype(jnp.bfloat16), ("dp", "seq"), axis=0, tiled=True),
            lax.all_gather(w_value.astype(jnp.bfloat16), ("dp", "seq"), axis=0, tiled=True),
            lax.all_gather(w_out.astype(jnp.bfloat16), ("dp", "seq"), axis=0, tiled=True),
            lax.all_gather(rel_table.astype(jnp.bfloat16), ("dp", "seq"), axis=0, tiled=True),
        )
        mlp_set = (
            lax.all_gather(norm2_gain.astype(jnp.bfloat16), ("dp", "seq"), axis=0, tiled=True),
            lax.all_gather(w_in.astype(jnp.bfloat16), ("dp", "seq"), axis=0, tiled=True),
            lax.all_gather(w_back.astype(jnp.bfloat16), ("dp", "seq"), axis=0, tiled=True),
        )
        layer_part, grad_part, gradients = run_micro(
            tokens[micro_step],
            cotangent[micro_step],
            lengths[micro_step],
            attn_set,
            mlp_set,
            context,
        )
        outputs.append(layer_part)
        input_grads.append(grad_part)
        pending = gradients if pending is None else jax.tree.map(jnp.add, pending, gradients)
    shard_sums = (
        lax.psum_scatter(pending[0], ("dp", "seq"), scatter_dimension=0, tiled=True),
        lax.psum_scatter(pending[1], ("dp", "seq"), scatter_dimension=0, tiled=True),
        lax.psum_scatter(pending[2], ("dp", "seq"), scatter_dimension=0, tiled=True),
        lax.psum_scatter(pending[3], ("dp", "seq"), scatter_dimension=0, tiled=True),
        lax.psum_scatter(pending[4], ("dp", "seq"), scatter_dimension=0, tiled=True),
        lax.psum_scatter(pending[5], ("dp", "seq"), scatter_dimension=0, tiled=True),
        lax.psum_scatter(pending[6], ("dp", "seq"), scatter_dimension=0, tiled=True),
        lax.psum_scatter(pending[7], ("dp", "seq"), scatter_dimension=0, tiled=True),
        lax.psum_scatter(pending[8], ("dp", "seq"), scatter_dimension=0, tiled=True),
    )
    return (
        jnp.stack(outputs),
        jnp.stack(input_grads),
        shard_sums[0],
        shard_sums[1],
        shard_sums[2],
        shard_sums[3],
        shard_sums[4],
        shard_sums[5],
        shard_sums[6],
        shard_sums[7],
        shard_sums[8],
    )


NT = (((1,), (1,)), ((), ()))
TN = (((0,), (0,)), ((), ()))
STRIP = 128
LOG2E = 1.4426950408889634
LN2 = 0.6931471805599453
LIMIT = 58 << 20
LIGHT = pl.CostEstimate(flops=1 << 20, bytes_accessed=1 << 16, transcendentals=0)

def _dot(a, b, dims=(((1,), (0,)), ((), ()))):
    return lax.dot_general(a, b, dims, preferred_element_type=jnp.float32)

def with_extras(x, which, extras, width=64):
    lane = lax.broadcasted_iota(jnp.int32, (1, x.shape[1]), 1)
    spare = lane - width if which == 0 else lane
    own = (lane < width) if which == 0 else (lane >= width)
    fill = jnp.zeros_like(x)
    for i, extra in enumerate(extras):
        fill = jnp.where(spare == i, extra, fill)
    return jnp.where(own, x, fill).astype(jnp.bfloat16)

def three_parts(x):
    low = lambda v: v.astype(jnp.bfloat16).astype(jnp.float32)
    high = low(x)
    middle = low(x - high)
    return [high, middle, low(x - high - middle)]

def slot_floor(size, length):
    return jnp.where(lax.broadcasted_iota(jnp.int32, (size, 1), 0) < length, 0.0, floor_score)

def skew(row, wide):
    return pltpu.roll(jnp.broadcast_to(row, (STRIP, wide)), wide - (STRIP - 1), 1, stride=1, stride_axis=0)

def fwd_kernel(len_ref, q_ref, k_ref, v_ref, t_ref, *refs, rows, seq_len, first):
    o_ref, lse_ref, strip, kx, vx = refs[-5:]
    wide = t_ref.shape[-1]
    pair = first + pl.program_id(0)
    per = rows // STRIP
    lane = lax.broadcasted_iota(jnp.int32, (1, 128), 1)
    k2 = k_ref[...].astype(jnp.float32)
    vx[:, 0:128] = v_ref[...]
    vx[:, 128:256] = jnp.ones_like(v_ref[...])
    for a in range(2):
        kx[a] = with_extras(k2, a, [slot_floor(seq_len, len_ref[0])])
        strip[a] = skew(t_ref[pl.ds(2 * pair + a, 1), :], wide)

    def step(b, carry):
        base = b * rows
        q2 = q_ref[pl.ds(base, rows), :].astype(jnp.float32)
        outs, stats = [], []
        for a in range(2):
            scores = _dot(with_extras(q2, a, [1.0]), kx[a], NT)
            parts = []
            for i in range(per):
                off = (seq_len - STRIP) - (b * per + i) * STRIP
                parts.append(strip[a, :, pl.ds(off, seq_len)])
            scores = scores + (jnp.concatenate(parts, 0) if per > 1 else parts[0])
            top = jnp.max(scores, axis=1, keepdims=True)
            probs = jnp.exp2(scores - top).astype(jnp.bfloat16)
            out = _dot(probs, vx[...])
            outs.append(out[:, 0:128] / out[:, 128:256])
            stats.append(top + jnp.log2(out[:, 128:256]))
        o_ref[pl.ds(base, rows), :] = jnp.where(lane < 64, outs[0], outs[1]).astype(jnp.bfloat16)
        lse_ref[0, pl.ds(base, rows), :] = jnp.where(lane < 64, stats[0], stats[1])
        return carry

    for b in range(seq_len // rows):
        step(b, 0)

def attn_fwd(length, q, k, v, t, first, count, prev=(), rows=256):
    seq_len, width = q.shape
    pairs = width // 128
    wide = t.shape[-1]
    blk = pl.BlockSpec((seq_len, 128), lambda p, n: (0, first + p))
    return pl.pallas_call(
        functools.partial(fwd_kernel, rows=rows, seq_len=seq_len, first=first),
        out_shape=(jax.ShapeDtypeStruct((seq_len, width), jnp.bfloat16),
                   jax.ShapeDtypeStruct((pairs, seq_len, 128), jnp.float32)),
        grid_spec=pltpu.PrefetchScalarGridSpec(
            num_scalar_prefetch=1, grid=(count,),
            in_specs=[blk, blk, blk, pl.BlockSpec(t.shape, lambda p, n: (0, 0))] + [pl.BlockSpec(memory_space=pl.ANY)] * len(prev),
            out_specs=[blk, pl.BlockSpec((1, seq_len, 128), lambda p, n: (first + p, 0, 0))],
            scratch_shapes=[pltpu.VMEM((2, STRIP, wide), jnp.float32), pltpu.VMEM((2, seq_len, 128), jnp.bfloat16),
                            pltpu.VMEM((seq_len, 256), jnp.bfloat16)]),
        input_output_aliases={5 + i: i for i in range(len(prev))},
        compiler_params=pltpu.CompilerParams(vmem_limit_bytes=LIMIT),
        cost_estimate=LIGHT,
        name="attn_fwd",
    )(length, q, k, v, t, *prev)

def bwd_kernel(len_ref, q_ref, k_ref, v_ref, do_ref, o_ref, lse_ref, t_ref, *refs, rows, seq_len, first):
    dq_ref, dk_ref, dv_ref, g_ref, strip, acc, dq_acc, qx, kx, vx, dox = refs[-11:]
    wide = t_ref.shape[-1]
    local_pair = pl.program_id(0)
    pair = first + local_pair
    per = rows // STRIP
    lane = lax.broadcasted_iota(jnp.int32, (1, 128), 1)
    up = lambda ref: ref[...].astype(jnp.float32)
    floor = slot_floor(seq_len, len_ref[0])
    prod = up(do_ref) * up(o_ref)
    for a in range(2):
        mine = (lane < 64) if a == 0 else (lane >= 64)
        delta = jnp.sum(jnp.where(mine, prod, 0.0), axis=1, keepdims=True)
        lse = lse_ref[0, :, 64 * a:64 * a + 1]
        qx[a] = with_extras(up(q_ref), a, [1.0] + three_parts(-lse))
        kx[a] = with_extras(up(k_ref), a, [floor, 1.0, 1.0, 1.0])
        vx[a] = with_extras(up(v_ref), a, [1.0, 1.0, 1.0])
        dox[a] = with_extras(up(do_ref), a, three_parts(-delta))
        strip[a] = skew(t_ref[pl.ds(2 * pair + a, 1), :], wide)
    acc[...] = jnp.zeros_like(acc)
    k2t = k_ref[...].T
    dq_acc[...] = jnp.zeros_like(dq_acc)

    def step(b, carry):
        at = pl.ds(b * rows, rows)
        dks, dvs = [], []
        for a in range(2):
            scores = _dot(kx[a, at, :], qx[a], NT)
            offs = [(seq_len - STRIP) - (b * per + i) * STRIP for i in range(per)]
            bias = [strip[a, :, pl.ds(off, seq_len)] for off in offs]
            probs = jnp.exp2(scores + (jnp.concatenate(bias, 0) if per > 1 else bias[0]))
            grad_scores = probs * _dot(vx[a, at, :], dox[a], NT)
            for i, off in enumerate(offs):
                acc[a, :, pl.ds(off, seq_len)] += grad_scores[i * STRIP:(i + 1) * STRIP]
            probs_b = probs.astype(jnp.bfloat16)
            gs_b = grad_scores.astype(jnp.bfloat16)
            dvs.append(_dot(probs_b, do_ref[...]))
            dks.append(_dot(gs_b, q_ref[...]))
            dq_acc[a] += _dot(k2t[:, b * rows:(b + 1) * rows], gs_b)
        dk_ref[at, :] = (jnp.where(lane < 64, dks[0], dks[1]) * LN2).astype(jnp.bfloat16)
        dv_ref[at, :] = jnp.where(lane < 64, dvs[0], dvs[1]).astype(jnp.bfloat16)
        return carry

    for b in range(seq_len // rows):
        step(b, 0)
    dq_ref[...] = jnp.concatenate([dq_acc[0, 0:64], dq_acc[1, 64:128]], 0).T.astype(jnp.bfloat16)
    for a in range(2):
        sums = acc[a]
        half = STRIP
        while half > 8:
            half //= 2
            sums = sums[:half] + pltpu.roll(sums[half:], wide - half, 1)
        while half > 1:
            half //= 2
            sums = sums + pltpu.roll(pltpu.roll(sums, 8 - half, 0), wide - half, 1)
        g_ref[pl.ds(2 * local_pair + a, 1), :] = pltpu.roll(sums, STRIP - 1, 1)[0:1]

def attn_bwd(length, q, k, v, do, o, lse, trev, first, count, prev=None, rows=512):
    seq_len, width = q.shape
    wide = trev.shape[-1]
    blk = pl.BlockSpec((seq_len, 128), lambda p, n: (0, first + p))
    mat = jax.ShapeDtypeStruct((seq_len, width), jnp.bfloat16)
    prev = tuple(prev) if prev is not None else ()
    return pl.pallas_call(
        functools.partial(bwd_kernel, rows=rows, seq_len=seq_len, first=first),
        out_shape=(mat, mat, mat, jax.ShapeDtypeStruct((2 * count, wide), jnp.float32)),
        grid_spec=pltpu.PrefetchScalarGridSpec(
            num_scalar_prefetch=1, grid=(count,),
            in_specs=[blk, blk, blk, blk, blk, pl.BlockSpec((1, seq_len, 128), lambda p, n: (first + p, 0, 0)),
                      pl.BlockSpec(trev.shape, lambda p, n: (0, 0))] + [pl.BlockSpec(memory_space=pl.ANY)] * len(prev),
            out_specs=[blk, blk, blk, pl.BlockSpec((2 * count, wide), lambda p, n: (0, 0))],
            scratch_shapes=[pltpu.VMEM((2, STRIP, wide), jnp.float32), pltpu.VMEM((2, STRIP, wide), jnp.float32),
                            pltpu.VMEM((2, 128, seq_len), jnp.float32)] + [pltpu.VMEM((2, seq_len, 128), jnp.bfloat16)] * 4),
        input_output_aliases={8 + i: i for i in range(len(prev))},
        compiler_params=pltpu.CompilerParams(vmem_limit_bytes=LIMIT),
        cost_estimate=LIGHT,
        name="attn_bwd",
    )(length, q, k, v, do, o, lse, trev, *prev)

ANY = pl.BlockSpec(memory_space=pl.ANY)
VM = pl.BlockSpec(memory_space=pltpu.VMEM)
SM = pl.BlockSpec(memory_space=pltpu.SMEM)

def rms_inverse(value):
    return lax.rsqrt(jnp.mean(value * value, axis=1, keepdims=True) + epsilon)

def pull_sequence(me, whole_ref, chip_ref, core_ref, dst, sem):
    rows = whole_ref.shape[1]
    for mask, src in enumerate((whole_ref.at[me], core_ref.at[0], chip_ref.at[me & 1], core_ref.at[1])):
        at = pl.multiple_of((me ^ mask) * rows, rows)
        pltpu.make_async_copy(src, dst.at[pl.ds(at, rows), :], sem).start()

def qkv_kernel(ids_ref, x4_ref, chip_ref, core_ref, *refs, masks):
    gathered = refs[:len(masks)]
    bucket_ref = refs[len(masks)]
    x_out, h_out, q_out, k_out, v_out, w_out, gain_ref, t_ref, trev_ref, xs, hs, ps, ws, es, sems = refs[len(masks) + 1:]
    me, flat = ids_ref[0], ids_ref[1]
    width = xs.shape[1]
    own = width // es.shape[0]
    pull_sequence(me, x4_ref, chip_ref, core_ref, xs, sems.at[0])
    for ref, ids in zip(gathered, masks):
        for j, mask in enumerate(ids):
            shard = flat ^ mask
            pltpu.make_async_copy(ref.at[j, 3 * own:3 * own + 16, :], es.at[shard], sems.at[1]).start()
    for ref, ids in zip(gathered, masks):
        for j, mask in enumerate(ids):
            at = pl.multiple_of((flat ^ mask) * own, own)
            for i in range(3):
                pltpu.make_async_copy(ref.at[j, i * own:(i + 1) * own, :], ws.at[pl.ds(at, own), i * width:(i + 1) * width], sems.at[2]).start()
    pltpu.make_async_copy(es, es, sems.at[1]).wait()
    extras = es[...].astype(jnp.float32)
    gains = jnp.sum(extras, axis=0)
    gain_ref[...] = gains[0:8]
    table = extras[:, 8, 0:128].astype(jnp.bfloat16)
    ids = lax.broadcasted_iota(jnp.int32, (es.shape[0], 1), 0)
    heads = t_ref.shape[0]
    for i, ref in enumerate((t_ref, trev_ref)):
        hot = jnp.where(bucket_ref[i:i + 1, :] == ids, 1.0, 0.0).astype(jnp.bfloat16)
        ref[...] = _dot(table, hot, TN)[0:heads] * LOG2E
    pltpu.make_async_copy(xs, xs, sems.at[0]).wait()
    part = 256
    def norm(i, carry):
        at = pl.ds(pl.multiple_of(i * part, part), part)
        x = xs[at, :].astype(jnp.float32)
        hs[at, :] = (x * rms_inverse(x) * gains[0:1]).astype(jnp.bfloat16)
        return carry
    lax.fori_loop(0, xs.shape[0] // part, norm, 0)
    copies = [pltpu.make_async_copy(xs, x_out, sems.at[0]), pltpu.make_async_copy(hs, h_out, sems.at[1])]
    for copy in copies:
        copy.start()
    pltpu.make_async_copy(ws, ws, sems.at[2]).wait()
    copies.append(pltpu.make_async_copy(ws, w_out, sems.at[2]))
    copies[-1].start()
    for i, ref in enumerate((q_out, k_out, v_out)):
        full = _dot(hs[...], ws[:, i * width:(i + 1) * width])
        ps[i] = (full * LOG2E if i == 0 else full).astype(jnp.bfloat16)
        copies.append(pltpu.make_async_copy(ps.at[i], ref, sems.at[3 + i]))
        copies[-1].start()
    for copy in copies:
        copy.wait()

def qkv_fwd(ids, x4, came, gathered, masks, bucket_rows, heads):
    parts, rows, width = x4.shape
    total = parts * rows
    shards = sum(len(m) for m in masks)
    mat = jax.ShapeDtypeStruct((total, width), jnp.bfloat16)
    wide = bucket_rows.shape[1]
    vm = lambda *s: pltpu.VMEM(s, jnp.bfloat16)
    return pl.pallas_call(
        functools.partial(qkv_kernel, masks=masks),
        out_shape=(mat,) * 5 + (jax.ShapeDtypeStruct((width, 3 * width), jnp.bfloat16), jax.ShapeDtypeStruct((8, width), jnp.float32),
                                jax.ShapeDtypeStruct((heads, wide), jnp.float32), jax.ShapeDtypeStruct((heads, wide), jnp.float32)),
        in_specs=[SM] + [ANY] * (3 + len(gathered)) + [VM],
        out_specs=[ANY] * 6 + [VM] * 3,
        scratch_shapes=[vm(total, width), vm(total, width), vm(3, total, width), vm(width, 3 * width), vm(shards, 16, width), pltpu.SemaphoreType.DMA((6,))],
        compiler_params=pltpu.CompilerParams(vmem_limit_bytes=LIMIT),
        cost_estimate=LIGHT,
        name="qkv_fwd",
    )(ids, x4, *came, *gathered, bucket_rows)

def gelu_both(v):
    t = jnp.tanh(root_coef * (v + cubic_coef * v * v * v))
    half = 0.5 * (1.0 + t)
    slope = half + 0.5 * v * (1.0 - t * t) * (root_coef * (1.0 + 3.0 * cubic_coef * v * v))
    return v * half, slope

def by_core(core, keep, send, src, dst_rows, sem, lead=slice(None), src_rows=slice(None), lanes=slice(None)):
    for parity in range(2):
        @pl.when(core == parity)
        def _():
            for dst, at in ((keep, parity), (send, 1 - parity)):
                pltpu.make_async_copy(src.at[lead, at, src_rows, lanes], dst.at[lead, dst_rows, lanes], sem).start()

def ff_chunks(h2, h2t, gm, acc, gh2, ws_in, ws_back, st_in, st_back, row_in, emit, before_add, cols=512):
    steps = ws_in.shape[1] // cols
    half, width = st_back.shape[2:]
    own = width // (2 * st_in.shape[0])
    wide = width // cols
    group = cols // (2 * half)

    def step(c, carry):
        at = pl.ds(pl.multiple_of(c * cols, cols), cols)
        win, wback = ws_in[:, at], ws_back[at, :]
        pre = _dot(h2[...], win)
        grad_active = _dot(gm[...], wback, NT)
        act, slope = gelu_both(pre)
        active = act.astype(jnp.bfloat16)
        gpre = (grad_active * slope).astype(jnp.bfloat16)
        @pl.when(c == 0)
        def _():
            before_add()
        acc[...] += _dot(active, wback)
        gh2[...] += _dot(gpre, win, NT)
        lead = pl.ds(c * group, group)
        st_back[lead] = _dot(active, gm[...], TN).astype(jnp.bfloat16).reshape(group, 2, half, width)
        emit(st_back, 0, lead=lead, dst_rows=slice(0, half))
        up = pl.multiple_of((c // wide) * own, own)
        lanes = pl.ds(pl.multiple_of((c % wide) * cols, cols), cols)
        st_in[:, :, pl.ds(up, own), lanes] = _dot(h2t[...], gpre).astype(jnp.bfloat16).reshape(-1, 2, own, cols)
        emit(st_in, 1, src_rows=pl.ds(up, own), dst_rows=pl.ds(row_in + up, own), lanes=lanes)
        return carry
    lax.fori_loop(0, steps, step, 0)

def finish_chunks(st_in, st_back, sems):
    pltpu.make_async_copy(st_back, st_back, sems.at[0]).wait()
    pltpu.make_async_copy(st_in, st_in, sems.at[1]).wait()

def aligned(at, size):
    return at if isinstance(at, int) else pl.multiple_of(at, size)

def pull_ff(flat, gathered, masks, ws_in, ws_back, row_in, sems):
    width = ws_in.shape[0]
    shards = sum(len(m) for m in masks)
    own, half = width // shards, ws_back.shape[0] // shards
    for ref, ids in zip(gathered, masks):
        for j, mask in enumerate(ids):
            shard = flat ^ mask
            pltpu.make_async_copy(ref.at[j, 0:half, :], ws_back.at[pl.ds(aligned(shard * half, half), half), :], sems.at[1]).start()
            at = pl.ds(aligned(shard * own, own), own)
            for i in range(ws_in.shape[1] // width):
                pltpu.make_async_copy(ref.at[j, row_in + i * own:row_in + (i + 1) * own, :], ws_in.at[at, i * width:(i + 1) * width], sems.at[0]).start()

def mid_a_kernel(ids_ref, x_hbm, o_hbm, g4_ref, chip_ref, core_ref, gain_ref, *refs, masks):
    gathered = refs[:len(masks)]
    (mixed_out, acc_out, gh2_out, h2_out, h2t_out, gm_out, wo_out, keep_out, send_out,
     xs, os, wo, ws_in, ws_back, mixed, h2, h2t, acc, gh2, gm, st_in, st_back, sems) = refs[len(masks):]
    flat = ids_ref[1]
    rows, width = xs.shape
    half, own = st_back.shape[2], width // (2 * st_in.shape[0])
    core = flat & 1
    def emit(src, which, **at):
        by_core(core, keep_out, send_out, src, sem=sems.at[which], **at)
    loads = [pltpu.make_async_copy(x_hbm, xs, sems.at[0]), pltpu.make_async_copy(o_hbm, os, sems.at[1])]
    for load in loads:
        load.start()
    for ref, ids in zip(gathered, masks):
        for j, mask in enumerate(ids):
            at = pl.ds(pl.multiple_of((flat ^ mask) * own, own), own)
            pltpu.make_async_copy(ref.at[j, half:half + own, :], wo.at[at, :], sems.at[2]).start()
    pull_ff(flat, gathered, masks, ws_in, ws_back, half + own, sems.at[3:5])
    pull_sequence(ids_ref[0], g4_ref, chip_ref, core_ref, gm, sems.at[5])
    for load in loads:
        load.wait()
    pltpu.make_async_copy(wo, wo, sems.at[2]).wait()
    stores = [pltpu.make_async_copy(wo, wo_out, sems.at[2])]
    stores[0].start()
    part = 256
    def load_rows(i, carry):
        at = pl.ds(pl.multiple_of(i * part, part), part)
        value = xs[at, :].astype(jnp.float32) + _dot(os[at, :], wo[...])
        mixed[at, :] = value
        acc[at, :] = value
        hidden = (value * rms_inverse(value) * gain_ref[1:2, :]).astype(jnp.bfloat16)
        h2[at, :] = hidden
        h2t[:, at] = hidden.T
        gh2[at, :] = jnp.zeros_like(value)
        return carry
    lax.fori_loop(0, rows // part, load_rows, 0)
    pltpu.make_async_copy(gm, gm, sems.at[5]).wait()
    row_ok = lax.broadcasted_iota(jnp.int32, (rows, 1), 0) < ids_ref[2]
    gm[...] = jnp.where(row_ok, gm[...], jnp.zeros_like(gm[...]))
    pltpu.make_async_copy(ws_in, ws_in, sems.at[3]).wait()
    pltpu.make_async_copy(ws_back, ws_back, sems.at[4]).wait()
    for i, (src, dst) in enumerate(((mixed, mixed_out), (h2, h2_out), (h2t, h2t_out), (gm, gm_out))):
        stores.append(pltpu.make_async_copy(src, dst, sems.at[6 + i]))
        stores[-1].start()
    ff_chunks(h2, h2t, gm, acc, gh2, ws_in, ws_back, st_in, st_back, half, emit, lambda: None)
    for i, (src, dst) in enumerate(((acc, acc_out), (gh2, gh2_out))):
        stores.append(pltpu.make_async_copy(src, dst, sems.at[3 + i]))
        stores[-1].start()
    finish_chunks(st_in, st_back, sems.at[0:2])
    for store in stores:
        store.wait()

def mid_a(ids, x, o, g4, came, gains, gathered, masks, ff):
    rows, width = x.shape
    shards = sum(len(m) for m in masks)
    half = ff // shards
    low = lambda *s: jax.ShapeDtypeStruct(s, jnp.bfloat16)
    full = lambda *s: jax.ShapeDtypeStruct(s, jnp.float32)
    vm = lambda *s: pltpu.VMEM(s, jnp.bfloat16)
    vf = lambda *s: pltpu.VMEM(s, jnp.float32)
    stack = half + ff // width * (width // shards)
    return pl.pallas_call(
        functools.partial(mid_a_kernel, masks=masks),
        out_shape=(full(rows, width), full(rows, width), full(rows, width), low(rows, width), low(width, rows), low(rows, width), low(width, width), low(shards // 2, stack, width), low(shards // 2, stack, width)),
        in_specs=[SM] + [ANY] * 5 + [VM] + [ANY] * len(gathered), out_specs=[ANY] * 9,
        scratch_shapes=[vm(rows, width), vm(rows, width), vm(width, width), vm(width, ff), vm(ff, width), vf(rows, width), vm(rows, width), vm(width, rows),
                        vf(rows, width), vf(rows, width), vm(rows, width), vm(shards // 2, 2, stack - half, width), vm(shards // 2, 2, half, width), pltpu.SemaphoreType.DMA((10,))],
        compiler_params=pltpu.CompilerParams(vmem_limit_bytes=LIMIT),
        cost_estimate=LIGHT,
        name="mid_a",
    )(ids, x, o, g4, *came, gains, *gathered)

def mid_b_kernel(ids_ref, gain_ref, mixed_hbm, acc_hbm, gh2_hbm, h2_hbm, h2t_hbm, gm_hbm, wo_hbm, o_hbm, full_ref, *refs):
    (out_ref, gb_out, do_ref, keep_out, send_out,
     os, wo, ws_in, ws_back, mixed, h2, h2t, acc, gh2, gm, gb, st_in, st_back, st_o, sems) = refs
    rows, width = os.shape
    shards, half, own = 2 * st_in.shape[0], st_back.shape[2], width // (2 * st_in.shape[0])
    core = ids_ref[1] & 1
    def emit(src, which, **at):
        by_core(core, keep_out, send_out, src, sem=sems.at[which], **at)
    early = [(h2_hbm, h2), (gm_hbm, gm), (h2t_hbm, h2t)]
    late = [(acc_hbm, acc), (gh2_hbm, gh2), (mixed_hbm, mixed), (wo_hbm, wo), (o_hbm, os)]
    early = [pltpu.make_async_copy(a, b, sems.at[4 + i]) for i, (a, b) in enumerate(early)]
    late = [pltpu.make_async_copy(a, b, sems.at[7 + i]) for i, (a, b) in enumerate(late)]
    for load in early:
        load.start()
    pull_ff(0, (full_ref,), (range(shards),), ws_in, ws_back, half, sems.at[2:4])
    for load in late:
        load.start()
    for load in early:
        load.wait()
    pltpu.make_async_copy(ws_in, ws_in, sems.at[2]).wait()
    pltpu.make_async_copy(ws_back, ws_back, sems.at[3]).wait()
    def before_add():
        late[0].wait()
        late[1].wait()
    ff_chunks(h2, h2t, gm, acc, gh2, ws_in, ws_back, st_in, st_back, half + own, emit, before_add)
    for load in late[2:]:
        load.wait()
    part = 256
    def finish(i, carry):
        at = pl.ds(pl.multiple_of(i * part, part), part)
        out_ref[at, :] = acc[at, :].astype(jnp.bfloat16)
        value = mixed[at, :]
        inverse = rms_inverse(value)
        normed = value * inverse
        scaled = gh2[at, :] * gain_ref[1:2, :]
        grad = inverse * (scaled - normed * jnp.mean(scaled * normed, axis=1, keepdims=True)) + gm[at, :].astype(jnp.float32)
        low = grad.astype(jnp.bfloat16)
        gb[at, :] = low
        do_ref[at, :] = _dot(low, wo[...], NT).astype(jnp.bfloat16)
        return carry
    lax.fori_loop(0, rows // part, finish, 0)
    st_o[...] = _dot(os[...], gb[...], TN).astype(jnp.bfloat16).reshape(st_o.shape)
    emit(st_o, 2, dst_rows=slice(half, half + own))
    store = pltpu.make_async_copy(gb, gb_out, sems.at[3])
    store.start()
    finish_chunks(st_in, st_back, sems.at[0:2])
    pltpu.make_async_copy(st_o, st_o, sems.at[2]).wait()
    store.wait()

def mid_b(ids, gains, state, o, full, ff):
    rows, width = o.shape
    shards = full.shape[0]
    half, own = ff // shards, width // shards
    low = lambda *s: jax.ShapeDtypeStruct(s, jnp.bfloat16)
    vm = lambda *s: pltpu.VMEM(s, jnp.bfloat16)
    vf = lambda *s: pltpu.VMEM(s, jnp.float32)
    rest = ff // width * own
    return pl.pallas_call(
        mid_b_kernel,
        out_shape=(low(rows, width), low(rows, width), low(rows, width), low(shards // 2, half + own + rest, width), low(shards // 2, half + own + rest, width)),
        in_specs=[SM, VM] + [ANY] * 9, out_specs=[VM, ANY, VM, ANY, ANY],
        scratch_shapes=[vm(rows, width), vm(width, width), vm(width, ff), vm(ff, width), vf(rows, width), vm(rows, width), vm(width, rows),
                        vf(rows, width), vf(rows, width), vm(rows, width), vm(rows, width), vm(shards // 2, 2, rest, width), vm(shards // 2, 2, half, width), vm(shards // 2, 2, own, width),
                        pltpu.SemaphoreType.DMA((12,))],
        compiler_params=pltpu.CompilerParams(vmem_limit_bytes=LIMIT),
        cost_estimate=LIGHT,
        name="mid_b",
    )(ids, gains, *state, o, full)

def gw_kernel(ids_ref, h_ref, dq_ref, dk_ref, dv_ref, bucket_ref, *refs):
    keep_out, send_out, st, sems = refs[-4:]
    offs = jnp.concatenate([ref[...] for ref in refs[:-4]], 0)
    pairs, _, stack, width = st.shape
    own = width // (2 * pairs)
    core = ids_ref[1] & 1
    ids = lax.broadcasted_iota(jnp.int32, (2 * pairs, 1), 0)
    hot = jnp.where(bucket_ref[1:2, :] == ids, 1.0, 0.0)
    table = lax.dot_general(hot, offs, NT, precision=lax.Precision.HIGHEST, preferred_element_type=jnp.float32)
    heads = offs.shape[0]
    st[:, :, 3 * own:, :] = jnp.zeros((pairs, 2, stack - 3 * own, width), jnp.bfloat16)
    st[:, :, 3 * own:3 * own + 1, 0:heads] = table.astype(jnp.bfloat16).reshape(pairs, 2, 1, heads)
    for i, ref in enumerate((dq_ref, dk_ref, dv_ref)):
        at = slice(i * own, (i + 1) * own) if i < 2 else slice(i * own, stack)
        st[:, :, i * own:(i + 1) * own, :] = _dot(h_ref[...], ref[...], TN).astype(jnp.bfloat16).reshape(pairs, 2, own, width)
        by_core(core, keep_out, send_out, st, at, sems.at[0], src_rows=at)
    pltpu.make_async_copy(st, st, sems.at[0]).wait()

def qkv_gw(ids, h, dq, dk, dv, bucket_rows, offs, shards):
    rows, width = h.shape
    stack = 3 * width // shards + 16
    half = jax.ShapeDtypeStruct((shards // 2, stack, width), jnp.bfloat16)
    return pl.pallas_call(
        gw_kernel, out_shape=(half, half),
        in_specs=[SM] + [VM] * (5 + len(offs)), out_specs=[ANY, ANY],
        scratch_shapes=[pltpu.VMEM((shards // 2, 2, stack, width), jnp.bfloat16), pltpu.SemaphoreType.DMA((1,))],
        compiler_params=pltpu.CompilerParams(vmem_limit_bytes=LIMIT),
        cost_estimate=LIGHT,
        name="qkv_gw",
    )(ids, h, dq, dk, dv, bucket_rows, *offs)

def gx_kernel(x_ref, gb_ref, dq_ref, dk_ref, dv_ref, gain_ref, w_ref, out_ref):
    width = x_ref.shape[1]
    grad = _dot(dq_ref[...], w_ref[:, :width], NT)
    grad += _dot(dk_ref[...], w_ref[:, width:2 * width], NT)
    grad += _dot(dv_ref[...], w_ref[:, 2 * width:3 * width], NT)
    x = x_ref[...].astype(jnp.float32)
    inverse = rms_inverse(x)
    normed = x * inverse
    scaled = grad * gain_ref[0:1, :]
    out = inverse * (scaled - normed * jnp.mean(scaled * normed, axis=1, keepdims=True)) + gb_ref[...].astype(jnp.float32)
    out_ref[...] = out.astype(jnp.bfloat16)

def qkv_gx(x, gb, dq, dk, dv, gains, w, rows=512):
    total, width = x.shape
    blk = pl.BlockSpec((rows, width), lambda i: (i, 0))
    return pl.pallas_call(
        gx_kernel, out_shape=jax.ShapeDtypeStruct((total, width), jnp.bfloat16), grid=(total // rows,),
        in_specs=[blk] * 5 + [pl.BlockSpec(gains.shape, lambda i: (0, 0)),
                              pl.BlockSpec((width, 3 * width), lambda i: (0, 0), pipeline_mode=pl.Buffered(1))],
        out_specs=blk,
        compiler_params=pltpu.CompilerParams(vmem_limit_bytes=LIMIT),
        cost_estimate=LIGHT,
        name="qkv_gx",
    )(x, gb, dq, dk, dv, gains, w)

def swap(value, axis, mask):
    return lax.ppermute(value, axis, [(i, i ^ mask) for i in range(lax.axis_size(axis))])


def send_chip(blocks, me):
    return swap(lax.dynamic_slice_in_dim(blocks, 2 * (1 - me // 2), 2, 0), "seq", 2)


def send_core(blocks, from_chip, me):
    own = lax.dynamic_index_in_dim(blocks, me ^ 1, 0)
    passed = lax.dynamic_index_in_dim(from_chip, 1 - me % 2, 0)
    return swap(jnp.concatenate([own, passed], 0), "seq", 1)


class Gather:
    def __init__(self, shard):
        shard = shard[None]
        self.sent = [shard] + [swap(shard, "dp", 2 * z) for z in (1, 2, 3)]
        self.pieces, self.masks = [], []

    def take(self, piece, mask, rows=(0, 1, 2, 3)):
        ids = tuple(8 * z | mask for z in rows)
        self.pieces += [piece, swap(piece, "seq", 1)]
        self.masks += [ids, tuple(m | 1 for m in ids)]

    def fill(self):
        self.own = jnp.concatenate(self.sent, 0)

    def sides(self):
        self.x, self.y = swap(self.own, "seq", 2), swap(self.own, "dp", 1)

    def corner_halves(self):
        self.near, self.far = swap(self.y[:2], "seq", 2), swap(self.x[2:], "dp", 1)

    def corner_y(self):
        self.corner = swap(self.x, "dp", 1)

    def all_pieces(self):
        return tuple(self.pieces), tuple(self.masks)


class Scatter:
    def __init__(self, keep, send, pos, corner_y):
        self.z, self.y, self.x = pos
        cube = (4, 2, 2) + keep.shape[1:]
        self.mine, self.sent, self.corner_y = keep.reshape(cube), send.reshape(cube), corner_y
        self.other = swap(self.sent, "seq", 1)

    def fold(self):
        pick = lambda v, at, axis: lax.dynamic_index_in_dim(v, at, axis, keepdims=False)
        def quarter(dy, dx):
            cut = lambda v: pick(pick(v, self.y ^ dy, 1), self.x ^ dx, 1).astype(jnp.float32)
            return (cut(self.mine) + cut(self.other)).astype(jnp.bfloat16)
        far = quarter(1, 1)
        self.to_x, self.to_y, self.own = quarter(0, 1), quarter(1, 0), quarter(0, 0)
        if self.corner_y:
            self.came_x, self.came_y = None, swap(far, "dp", 1)
        else:
            self.came_x, self.came_y = swap(far[:2], "seq", 2), swap(far[2:], "dp", 1)

    def turn(self):
        add = lambda a, b: (a.astype(jnp.float32) + b.astype(jnp.float32)).astype(jnp.bfloat16)
        if self.corner_y:
            to_y, = tie(self.came_y, self.to_y)
            to_x = add(self.to_x, self.came_y)
        else:
            to_x = lax.dynamic_update_slice_in_dim(self.to_x, add(self.to_x[2:], self.came_y), 2, 0)
            to_y = lax.dynamic_update_slice_in_dim(self.to_y, add(self.to_y[:2], self.came_x), 0, 0)
        self.sent = (to_x, to_y)
        self.came_x, self.came_y = swap(to_x, "seq", 2), swap(to_y, "dp", 1)

    def column(self):
        total = self.own.astype(jnp.float32) + self.came_x.astype(jnp.float32) + self.came_y.astype(jnp.float32)
        total = total.astype(jnp.bfloat16)
        block = lambda k: lax.dynamic_index_in_dim(total, self.z ^ k, 0, keepdims=False)
        self.mine = block(0)
        self.came = [swap(block(k), "dp", 2 * k) for k in (1, 2, 3)]

    def result(self):
        return sum((c.astype(jnp.float32) for c in self.came), self.mine.astype(jnp.float32))


def place(blocks, from_chip, from_core, me):
    for mask, block in ((1, from_core[0:1]), (2, lax.dynamic_index_in_dim(from_chip, me % 2, 0)), (3, from_core[1:2])):
        blocks = lax.dynamic_update_slice_in_dim(blocks, block, me ^ mask, 0)
    return blocks


def tie(first, *later):
    return lax.optimization_barrier((first,) + later)[1:]


def local_whole(tokens, cotangent, lengths, buckets, norm1_gain, w_query, w_key, w_value, w_out, rel_table, norm2_gain, w_in, w_back):
    micro_count, seq_count, rows, width = tokens.shape
    parts = micro_count * seq_count
    both = ("dp", "seq")
    me, dp = lax.axis_index("seq"), lax.axis_index("dp")
    shards = lax.axis_size("seq") * lax.axis_size("dp")
    flat = dp * parts + me
    pos = (dp // 2, dp % 2, me // 2)
    low = lambda v: v.astype(jnp.bfloat16)
    up = lambda v: v.astype(jnp.float32)
    own, ff_own = w_query.shape[0], w_back.shape[0]
    ids = jnp.stack([me, flat, lax.dynamic_index_in_dim(lengths.reshape(parts), me, 0, keepdims=False)])
    length = ids[2:3]

    place_row = lambda v: lax.dynamic_update_slice(jnp.zeros((1, width), jnp.bfloat16), low(v)[None], (0, flat * own))
    small = jnp.concatenate([place_row(norm1_gain), place_row(norm2_gain), jnp.zeros((6, width), jnp.bfloat16),
                             jnp.pad(low(rel_table)[None], ((0, 7), (0, width - HEADS)))], 0)
    shard1 = jnp.concatenate([low(w_query), low(w_key), low(w_value), small], 0)
    ff = w_in.shape[1] // 2
    half = ff_own // 2
    halves = low(w_in).reshape(own, shards, 2, half)
    in_half = lambda i: [halves[:, :, i].reshape(own, ff)[:, j:j + width] for j in range(0, ff, width)]
    shard2 = jnp.concatenate([low(w_back[:half]), low(w_out)] + in_half(0), 0)
    shard3 = jnp.concatenate([low(w_back[half:])] + in_half(1), 0)
    x4, g4 = tokens.reshape(parts, rows, width), cotangent.reshape(parts, rows, width)
    bucket_rows = jnp.stack([jnp.pad(buckets, (0, 1), constant_values=-1), jnp.pad(buckets[::-1], (0, 1), constant_values=-1)])

    g1 = Gather(shard1)
    x_chip = send_chip(x4, me)
    g2 = Gather(shard2)
    g1.fill()
    g1.own, = tie((x_chip, g2.sent[1], shard3), g1.own)
    g1.sides()
    g1.x, g1.y = tie(g2.sent[2], g1.x, g1.y)
    g1.corner_halves()
    g2.fill()
    g1.take(g1.own, 0)
    g1.near, g1.far, g2.own = tie(g1.pieces[1], g1.near, g1.far, g2.own)
    g2.sides()
    g1.x, g1.y, x4_in = tie((g1.near, g1.far), g1.x, g1.y, x4)
    g1.take(g1.x, 2)
    g1.take(g1.y, 4)
    g1.take(g1.near, 6, (0, 1))
    g1.take(g1.far, 6, (2, 3))
    x_core = send_core(x4_in, x_chip, me)
    shard3, = tie((g1.near, g1.far), shard3)
    full3 = lax.all_gather(shard3, both, axis=0, tiled=False)
    x, hidden, q, k, v, w_qkv, gains, t, t_back = qkv_fwd(ids, x4, (x_chip, x_core), *g1.all_pieces(), bucket_rows, HEADS)
    pairs = HEADS // 2
    att = attn_fwd(length, q, k, v, t, 0, pairs // 2)
    g2.take(g2.own, 0)
    g2.x, g2.y = tie((att[0], g2.pieces[1]), g2.x, g2.y)
    g2.corner_y()
    g4_in, = tie(g2.x, g4)
    g_chip = send_chip(g4_in, me)
    g2.take(g2.x, 2)
    g2.take(g2.y, 4)
    q_in, = tie((g2.x, g2.y), q)
    attended, lse = attn_fwd(length, q_in, k, v, t, pairs // 2, pairs // 2, att)
    g2.corner, g_chip = tie((attended, g2.pieces[3], g2.pieces[5]), g2.corner, g_chip)
    g2.take(g2.corner, 6)
    g_core = send_core(g4, g_chip, me)
    *state, keep3, send3 = mid_a(ids, x, attended, g4, (g_chip, g_core), gains, *g2.all_pieces(), ff)
    sc3 = Scatter(keep3, send3, pos, True)
    out, gb, g_att, keep2, send2 = mid_b(ids, gains, state, attended, full3, ff)
    sc3.other, = tie(gb, sc3.other)
    sc3.fold()
    send2, = tie(sc3.own, send2)
    sc2 = Scatter(keep2, send2, pos, True)
    out4 = out.reshape(parts, rows, width)
    out4, = tie(sc3.own, out4)
    out_chip = send_chip(out4, me)
    count = pairs // 4
    back = lambda first, g, prev: attn_bwd(length, q, k, v, g, attended, lse, t_back, first, count, prev)
    g_att, = tie(sc3.own, g_att)
    dq, dk, dv, off0 = back(0, g_att, None)
    sc2.other, = tie(off0, sc2.other)
    sc2.fold()
    sc3.came_y, = tie(sc2.own, sc3.came_y)
    sc3.turn()
    g_att, = tie(sc3.sent, g_att)
    dq, dk, dv, off1 = back(count, g_att, (dq, dk, dv))
    sc2.came_x, sc2.came_y = tie((off1, out_chip), sc2.came_x, sc2.came_y)
    sc2.turn()
    out4_in, out_chip = tie(sc2.sent, out4, out_chip)
    out_core = send_core(out4_in, out_chip, me)
    g_att, = tie(sc2.sent, g_att)
    dq, dk, dv, off2 = back(2 * count, g_att, (dq, dk, dv))
    sc3.came_x, sc3.came_y = tie((off2, out_core), sc3.came_x, sc3.came_y)
    sc3.column()
    g_att, = tie(sc3.mine, g_att)
    dq, dk, dv, off3 = back(3 * count, g_att, (dq, dk, dv))
    sc2.came_x, sc2.came_y = tie(off3, sc2.came_x, sc2.came_y)
    sc2.column()
    h_in, = tie((sc2.mine, sc3.came), hidden)
    keep1, send1 = qkv_gw(ids, h_in, dq, dk, dv, bucket_rows, (off0, off1, off2, off3), shards)
    sc1 = Scatter(keep1, send1, pos, False)
    gb_in, = tie(send1, gb)
    gx = qkv_gx(x, gb_in, dq, dk, dv, gains, w_qkv)
    sc1.other, = tie(gx, sc1.other)
    sc1.fold()
    out4, out_chip, out_core = tie(sc1.own, out4, out_chip, out_core)
    layer_out = place(out4, out_chip, out_core, me)
    sc1.came_x, sc1.came_y = tie((layer_out, sc2.came), sc1.came_x, sc1.came_y)
    sc1.turn()
    sc2.came = list(tie(sc1.sent, *sc2.came))
    sc3.came = list(tie(sc1.sent, *sc3.came))
    r2, r_a = sc2.result(), sc3.result()
    join = lambda v: jnp.concatenate([v[i:i + own] for i in range(0, v.shape[0], own)], 1).reshape(own, shards, 1, half)
    g_in = jnp.concatenate([join(r_a[half:]), join(r2[half + own:])], 2).reshape(w_in.shape)
    g_back = jnp.concatenate([r_a[:half], r2[:half]], 0)
    g_out = r2[half:half + own]
    g_gain2 = jnp.sum(up(low(w_in)) * g_in, axis=1) / up(low(norm2_gain))
    sc1.came_x, sc1.came_y, g_in, g_back, g_out, g_gain2 = lax.optimization_barrier((sc1.came_x, sc1.came_y, g_in, g_back, g_out, g_gain2))
    sc1.column()
    gx, = tie(sc1.mine, gx)
    gx4 = gx.reshape(parts, rows, width)
    gx_chip = send_chip(gx4, me)
    gx_chip, = tie(sc1.came, gx_chip)
    gx_core = send_core(gx4, gx_chip, me)
    input_grad = place(gx4, gx_chip, gx_core, me)
    sc1.came = list(tie(input_grad, *sc1.came))
    r1 = sc1.result()
    prod = up(shard1[:3 * own]) * r1[:3 * own]
    g_gain1 = jnp.sum(prod[:own] + prod[own:2 * own] + prod[2 * own:], axis=1) / up(low(norm1_gain))
    return (layer_out.reshape(tokens.shape), input_grad.reshape(tokens.shape), g_gain1, r1[:own], r1[own:2 * own], r1[2 * own:3 * own],
            g_out, r1[3 * own, :HEADS], g_gain2, g_in, g_back)


def local_any(shape, tokens, *rest):
    fits = tuple(shape) == (8, 4) and tokens.shape[0] * tokens.shape[1] == 4 and tokens.shape[3] == HEADS * DH == 1024
    return (local_whole if fits else local)(tokens, *rest)


def solution(mesh):
    return jax.shard_map(
        functools.partial(local_any, mesh.devices.shape),
        mesh=mesh,
        in_specs=(
            P(None, "dp", "seq", None),
            P(None, "dp", "seq", None),
            P(None, "dp"),
            P(),
            P(("dp", "seq")),
            P(("dp", "seq"), None),
            P(("dp", "seq"), None),
            P(("dp", "seq"), None),
            P(("dp", "seq"), None),
            P(("dp", "seq")),
            P(("dp", "seq")),
            P(("dp", "seq"), None),
            P(("dp", "seq"), None),
        ),
        out_specs=(
            P(None, "dp", "seq", None),
            P(None, "dp", "seq", None),
            P(("dp", "seq")),
            P(("dp", "seq"), None),
            P(("dp", "seq"), None),
            P(("dp", "seq"), None),
            P(("dp", "seq"), None),
            P(("dp", "seq")),
            P(("dp", "seq")),
            P(("dp", "seq"), None),
            P(("dp", "seq"), None),
        ),
        check_vma=False,
    )
```

```python
import functools

import jax
import jax.numpy as jnp
from jax import lax
from jax.experimental import pallas as pl
from jax.experimental.pallas import tpu as pltpu
from jax.sharding import PartitionSpec as P

HEADS = 16
DH = 64
BUCKETS = 32


epsilon = 1e-06
floor_score = -1e30
highest = lax.Precision.HIGHEST
root_coef = 0.7978845608
cubic_coef = 0.044715


def gelu_tanh(values):
    return (
        0.5
        * values
        * (1.0 + jnp.tanh(root_coef * (values + cubic_coef * values * values * values)))
    )


def gelu_slope(values):
    inner = jnp.tanh(root_coef * (values + cubic_coef * values * values * values))
    return 0.5 * (1.0 + inner) + 0.5 * values * (1.0 - inner * inner) * root_coef * (
        1.0 + 3.0 * cubic_coef * values * values
    )


def project(acts, weight):
    return jnp.einsum("srd,de->sre", acts, weight, preferred_element_type=jnp.float32)


def project_back(grads_in, weight):
    return jnp.einsum("sre,de->srd", grads_in, weight, preferred_element_type=jnp.float32)


def contract(acts, grads_in):
    return jnp.einsum("srd,sre->de", acts, grads_in, preferred_element_type=jnp.float32)


def rms_forward(values, gain):
    inverse = lax.rsqrt(jnp.mean(values * values, axis=-1, keepdims=True) + epsilon)
    normed = values * inverse
    return (normed, inverse, (normed * gain.astype(jnp.float32)).astype(jnp.bfloat16))


def rms_backward(grad_hidden, normed, inverse, gain):
    scaled = grad_hidden * gain.astype(jnp.float32)
    grad_values = inverse * (scaled - normed * jnp.mean(scaled * normed, axis=-1, keepdims=True))
    return (grad_values, jnp.sum(grad_hidden * normed, axis=(0, 1)))


def score_block(per_head_queries, per_head_keys, rel_bias, key_valid):
    scores = (
        jnp.einsum(
            "ofck,owck->ocfw", per_head_queries, per_head_keys, preferred_element_type=jnp.float32
        )
        + rel_bias[None]
    )
    return jnp.where(key_valid, scores, floor_score)


def offset_sums(grid, first_row, seq_len):
    head_count, row_count, key_count = grid.shape
    flipped = grid[:, ::-1, :]
    padded = jnp.pad(flipped, ((0, 0), (0, 0), (0, row_count)))
    wide_len = key_count + row_count
    skewed = padded.reshape(head_count, row_count * wide_len)[:, : row_count * (wide_len - 1)]
    skewed = skewed.reshape(head_count, row_count, wide_len - 1)
    column_sums = jnp.sum(skewed, axis=1)
    placed = jnp.zeros((head_count, 2 * seq_len - 1), jnp.float32)
    begin = seq_len - row_count - first_row
    return lax.dynamic_update_slice(placed, column_sums, (jnp.int32(0), begin))


def run_micro(inputs, incoming, seq_lens, attn_set, mlp_set, context):
    onehot, offsets, row_pos, key_pos, first_row, seq_len = context
    gain_one, query_w, key_w, value_w, out_w, bias_table = attn_set
    gain_two, in_w, return_projection_weight = mlp_set
    seq_count, row_count, model_width = inputs.shape
    values = inputs.astype(jnp.float32)
    normed_one, inverse_one, hidden_one = rms_forward(values, gain_one)
    queries = project(hidden_one, query_w).astype(jnp.bfloat16)
    keys_own = project(hidden_one, key_w).astype(jnp.bfloat16)
    values_own = project(hidden_one, value_w).astype(jnp.bfloat16)
    keys_all, values_all = (
        lax.all_gather(keys_own, "seq", axis=1, tiled=True),
        lax.all_gather(values_own, "seq", axis=1, tiled=True),
    )
    per_offset = jnp.dot(
        onehot, bias_table.reshape(BUCKETS, HEADS), preferred_element_type=jnp.float32
    )
    rel_bias = jnp.transpose(per_offset[offsets], (2, 0, 1))
    key_valid = (key_pos[None, :] < seq_lens[:, None])[:, None, None, :]
    per_head_queries = queries.reshape(seq_count, row_count, HEADS, DH)
    per_head_keys = keys_all.reshape(seq_count, seq_len, HEADS, DH)
    per_head_values = values_all.reshape(seq_count, seq_len, HEADS, DH)
    scores = score_block(per_head_queries, per_head_keys, rel_bias, key_valid)
    row_max = jnp.max(scores, axis=-1, keepdims=True)
    exp_scores = jnp.exp(scores - row_max)
    row_total = jnp.sum(exp_scores, axis=-1, keepdims=True)
    attn_probs = exp_scores / row_total
    log_total = row_max + jnp.log(row_total)
    reduced_precision_probs = attn_probs.astype(jnp.bfloat16)
    attended = jnp.einsum(
        "jfpe,jefn->jpfn",
        reduced_precision_probs,
        per_head_values,
        preferred_element_type=jnp.float32,
    )
    attended = attended.reshape(seq_count, row_count, model_width).astype(jnp.bfloat16)
    residual_mid = values + project(attended, out_w)
    normed_two, inverse_two, hidden_two = rms_forward(residual_mid, gain_two)
    pre_act = project(hidden_two, in_w)
    active = gelu_tanh(pre_act).astype(jnp.bfloat16)
    result = (residual_mid + project(active, return_projection_weight)).astype(jnp.bfloat16)
    row_valid = (row_pos[None, :] < seq_lens[:, None]).astype(jnp.float32)[:, :, None]
    grad_out = incoming.astype(jnp.float32) * row_valid
    grad_low = grad_out.astype(jnp.bfloat16)
    grad_back = contract(active, grad_low)
    gradient_active_rows = project_back(grad_low, return_projection_weight)
    grad_pre = (gradient_active_rows * gelu_slope(pre_act)).astype(jnp.bfloat16)
    grad_in = contract(hidden_two, grad_pre)
    grad_hidden_two = project_back(grad_pre, in_w)
    grad_mixed, grad_gain_two = rms_backward(grad_hidden_two, normed_two, inverse_two, gain_two)
    grad_mixed = grad_mixed + grad_out
    grad_branch = grad_mixed.astype(jnp.bfloat16)
    grad_outw = contract(attended, grad_branch)
    gradient_attended_values = project_back(grad_branch, out_w).astype(jnp.bfloat16)
    gradient_attended_values = gradient_attended_values.reshape(seq_count, row_count, HEADS, DH)
    scores = score_block(per_head_queries, per_head_keys, rel_bias, key_valid)
    attn_probs = jnp.exp(scores - log_total)
    reduced_precision_probs = attn_probs.astype(jnp.bfloat16)
    grad_probs = jnp.einsum(
        "ofck,owck->ocfw",
        gradient_attended_values,
        per_head_values,
        preferred_element_type=jnp.float32,
    )
    inner_sum = jnp.sum(attn_probs * grad_probs, axis=-1, keepdims=True)
    gradient_score_matrix = (attn_probs * (grad_probs - inner_sum)).astype(jnp.bfloat16)
    grad_query = jnp.einsum(
        "jfpe,jefn->jpfn", gradient_score_matrix, per_head_keys, preferred_element_type=jnp.float32
    )
    grad_query = grad_query.astype(jnp.bfloat16).reshape(seq_count, row_count, model_width)
    key_part = jnp.einsum(
        "eciv,eicq->evcq",
        gradient_score_matrix,
        per_head_queries,
        preferred_element_type=jnp.float32,
    )
    value_part = jnp.einsum(
        "eciv,eicq->evcq",
        reduced_precision_probs,
        gradient_attended_values,
        preferred_element_type=jnp.float32,
    )
    key_part = key_part.reshape(seq_count, seq_len, model_width)
    value_part = value_part.reshape(seq_count, seq_len, model_width)
    grad_key, grad_value = (
        lax.psum_scatter(
            key_part.astype(jnp.bfloat16), "seq", scatter_dimension=1, tiled=True
        ).astype(jnp.float32),
        lax.psum_scatter(
            value_part.astype(jnp.bfloat16), "seq", scatter_dimension=1, tiled=True
        ).astype(jnp.float32),
    )
    grad_key = grad_key.astype(jnp.bfloat16)
    grad_value = grad_value.astype(jnp.bfloat16)
    offset_grad = offset_sums(
        jnp.sum(gradient_score_matrix.astype(jnp.float32), axis=0), first_row, seq_len
    )
    grad_table = jnp.dot(onehot.astype(jnp.float32).T, offset_grad.T, precision=highest).reshape(-1)
    grad_qw = contract(hidden_one, grad_query)
    grad_kw = contract(hidden_one, grad_key)
    grad_vw = contract(hidden_one, grad_value)
    grad_hidden_one = (
        project_back(grad_query, query_w)
        + project_back(grad_key, key_w)
        + project_back(grad_value, value_w)
    )
    grad_values, grad_gain_one = rms_backward(grad_hidden_one, normed_one, inverse_one, gain_one)
    grad_values = grad_values + grad_mixed
    gradients = (
        grad_gain_one,
        grad_qw,
        grad_kw,
        grad_vw,
        grad_outw,
        grad_table,
        grad_gain_two,
        grad_in,
        grad_back,
    )
    return (result, grad_values.astype(jnp.bfloat16), gradients)


def local(
    tokens,
    cotangent,
    lengths,
    buckets,
    norm1_gain,
    w_query,
    w_key,
    w_value,
    w_out,
    rel_table,
    norm2_gain,
    w_in,
    w_back,
):
    micro_count, seq_count, row_count, model_width = tokens.shape
    seq_parts = lax.axis_size("seq")
    seq_len = row_count * seq_parts
    first_row = lax.axis_index("seq") * row_count
    row_pos = first_row + jnp.arange(row_count, dtype=jnp.int32)
    key_pos = jnp.arange(seq_len, dtype=jnp.int32)
    onehot = (buckets[:, None] == jnp.arange(BUCKETS, dtype=jnp.int32)[None, :]).astype(
        jnp.bfloat16
    )
    offsets = key_pos[None, :] - row_pos[:, None] + (seq_len - 1)
    context = (onehot, offsets, row_pos, key_pos, first_row, seq_len)
    outputs = []
    input_grads = []
    pending = None
    shard_sums = None
    for micro_step in range(micro_count):
        attn_set = (
            lax.all_gather(norm1_gain.astype(jnp.bfloat16), ("dp", "seq"), axis=0, tiled=True),
            lax.all_gather(w_query.astype(jnp.bfloat16), ("dp", "seq"), axis=0, tiled=True),
            lax.all_gather(w_key.astype(jnp.bfloat16), ("dp", "seq"), axis=0, tiled=True),
            lax.all_gather(w_value.astype(jnp.bfloat16), ("dp", "seq"), axis=0, tiled=True),
            lax.all_gather(w_out.astype(jnp.bfloat16), ("dp", "seq"), axis=0, tiled=True),
            lax.all_gather(rel_table.astype(jnp.bfloat16), ("dp", "seq"), axis=0, tiled=True),
        )
        mlp_set = (
            lax.all_gather(norm2_gain.astype(jnp.bfloat16), ("dp", "seq"), axis=0, tiled=True),
            lax.all_gather(w_in.astype(jnp.bfloat16), ("dp", "seq"), axis=0, tiled=True),
            lax.all_gather(w_back.astype(jnp.bfloat16), ("dp", "seq"), axis=0, tiled=True),
        )
        layer_part, grad_part, gradients = run_micro(
            tokens[micro_step],
            cotangent[micro_step],
            lengths[micro_step],
            attn_set,
            mlp_set,
            context,
        )
        outputs.append(layer_part)
        input_grads.append(grad_part)
        pending = gradients if pending is None else jax.tree.map(jnp.add, pending, gradients)
    shard_sums = (
        lax.psum_scatter(pending[0], ("dp", "seq"), scatter_dimension=0, tiled=True),
        lax.psum_scatter(pending[1], ("dp", "seq"), scatter_dimension=0, tiled=True),
        lax.psum_scatter(pending[2], ("dp", "seq"), scatter_dimension=0, tiled=True),
        lax.psum_scatter(pending[3], ("dp", "seq"), scatter_dimension=0, tiled=True),
        lax.psum_scatter(pending[4], ("dp", "seq"), scatter_dimension=0, tiled=True),
        lax.psum_scatter(pending[5], ("dp", "seq"), scatter_dimension=0, tiled=True),
        lax.psum_scatter(pending[6], ("dp", "seq"), scatter_dimension=0, tiled=True),
        lax.psum_scatter(pending[7], ("dp", "seq"), scatter_dimension=0, tiled=True),
        lax.psum_scatter(pending[8], ("dp", "seq"), scatter_dimension=0, tiled=True),
    )
    return (
        jnp.stack(outputs),
        jnp.stack(input_grads),
        shard_sums[0],
        shard_sums[1],
        shard_sums[2],
        shard_sums[3],
        shard_sums[4],
        shard_sums[5],
        shard_sums[6],
        shard_sums[7],
        shard_sums[8],
    )


NT = (((1,), (1,)), ((), ()))
TN = (((0,), (0,)), ((), ()))
STRIP = 128
LOG2E = 1.4426950408889634
LN2 = 0.6931471805599453
LIMIT = 58 << 20
LIGHT = pl.CostEstimate(flops=1 << 20, bytes_accessed=1 << 16, transcendentals=0)

def _dot(a, b, dims=(((1,), (0,)), ((), ()))):
    return lax.dot_general(a, b, dims, preferred_element_type=jnp.float32)

def with_extras(x, which, extras, width=64):
    lane = lax.broadcasted_iota(jnp.int32, (1, x.shape[1]), 1)
    spare = lane - width if which == 0 else lane
    own = (lane < width) if which == 0 else (lane >= width)
    fill = jnp.zeros_like(x)
    for i, extra in enumerate(extras):
        fill = jnp.where(spare == i, extra, fill)
    return jnp.where(own, x, fill).astype(jnp.bfloat16)

def three_parts(x):
    low = lambda v: v.astype(jnp.bfloat16).astype(jnp.float32)
    high = low(x)
    middle = low(x - high)
    return [high, middle, low(x - high - middle)]

def slot_floor(size, length):
    return jnp.where(lax.broadcasted_iota(jnp.int32, (size, 1), 0) < length, 0.0, floor_score)

def skew(row, wide):
    return pltpu.roll(jnp.broadcast_to(row, (STRIP, wide)), wide - (STRIP - 1), 1, stride=1, stride_axis=0)

def fwd_kernel(len_ref, q_ref, k_ref, v_ref, t_ref, *refs, rows, seq_len, first):
    o_ref, lse_ref, strip, kx, vx = refs[-5:]
    wide = t_ref.shape[-1]
    pair = first + pl.program_id(0)
    per = rows // STRIP
    lane = lax.broadcasted_iota(jnp.int32, (1, 128), 1)
    k2 = k_ref[...].astype(jnp.float32)
    vx[:, 0:128] = v_ref[...]
    vx[:, 128:256] = jnp.ones_like(v_ref[...])
    for a in range(2):
        kx[a] = with_extras(k2, a, [slot_floor(seq_len, len_ref[0])])
        strip[a] = skew(t_ref[pl.ds(2 * pair + a, 1), :], wide)

    def step(b, carry):
        base = b * rows
        q2 = q_ref[pl.ds(base, rows), :].astype(jnp.float32)
        outs, stats = [], []
        for a in range(2):
            scores = _dot(with_extras(q2, a, [1.0]), kx[a], NT)
            parts = []
            for i in range(per):
                off = (seq_len - STRIP) - (b * per + i) * STRIP
                parts.append(strip[a, :, pl.ds(off, seq_len)])
            scores = scores + (jnp.concatenate(parts, 0) if per > 1 else parts[0])
            top = jnp.max(scores, axis=1, keepdims=True)
            probs = jnp.exp2(scores - top).astype(jnp.bfloat16)
            out = _dot(probs, vx[...])
            outs.append(out[:, 0:128] / out[:, 128:256])
            stats.append(top + jnp.log2(out[:, 128:256]))
        o_ref[pl.ds(base, rows), :] = jnp.where(lane < 64, outs[0], outs[1]).astype(jnp.bfloat16)
        lse_ref[0, pl.ds(base, rows), :] = jnp.where(lane < 64, stats[0], stats[1])
        return carry

    for b in range(seq_len // rows):
        step(b, 0)

def attn_fwd(length, q, k, v, t, first, count, prev=(), rows=256):
    seq_len, width = q.shape
    pairs = width // 128
    wide = t.shape[-1]
    blk = pl.BlockSpec((seq_len, 128), lambda p, n: (0, first + p))
    return pl.pallas_call(
        functools.partial(fwd_kernel, rows=rows, seq_len=seq_len, first=first),
        out_shape=(jax.ShapeDtypeStruct((seq_len, width), jnp.bfloat16),
                   jax.ShapeDtypeStruct((pairs, seq_len, 128), jnp.float32)),
        grid_spec=pltpu.PrefetchScalarGridSpec(
            num_scalar_prefetch=1, grid=(count,),
            in_specs=[blk, blk, blk, pl.BlockSpec(t.shape, lambda p, n: (0, 0))] + [pl.BlockSpec(memory_space=pl.ANY)] * len(prev),
            out_specs=[blk, pl.BlockSpec((1, seq_len, 128), lambda p, n: (first + p, 0, 0))],
            scratch_shapes=[pltpu.VMEM((2, STRIP, wide), jnp.float32), pltpu.VMEM((2, seq_len, 128), jnp.bfloat16),
                            pltpu.VMEM((seq_len, 256), jnp.bfloat16)]),
        input_output_aliases={5 + i: i for i in range(len(prev))},
        compiler_params=pltpu.CompilerParams(vmem_limit_bytes=LIMIT),
        cost_estimate=LIGHT,
        name="attn_fwd",
    )(length, q, k, v, t, *prev)

def bwd_kernel(len_ref, q_ref, k_ref, v_ref, do_ref, o_ref, lse_ref, t_ref, *refs, rows, seq_len, first):
    dq_ref, dk_ref, dv_ref, g_ref, strip, acc, dq_acc, qx, kx, vx, dox = refs[-11:]
    wide = t_ref.shape[-1]
    local_pair = pl.program_id(0)
    pair = first + local_pair
    per = rows // STRIP
    lane = lax.broadcasted_iota(jnp.int32, (1, 128), 1)
    up = lambda ref: ref[...].astype(jnp.float32)
    floor = slot_floor(seq_len, len_ref[0])
    prod = up(do_ref) * up(o_ref)
    for a in range(2):
        mine = (lane < 64) if a == 0 else (lane >= 64)
        delta = jnp.sum(jnp.where(mine, prod, 0.0), axis=1, keepdims=True)
        lse = lse_ref[0, :, 64 * a:64 * a + 1]
        qx[a] = with_extras(up(q_ref), a, [1.0] + three_parts(-lse))
        kx[a] = with_extras(up(k_ref), a, [floor, 1.0, 1.0, 1.0])
        vx[a] = with_extras(up(v_ref), a, [1.0, 1.0, 1.0])
        dox[a] = with_extras(up(do_ref), a, three_parts(-delta))
        strip[a] = skew(t_ref[pl.ds(2 * pair + a, 1), :], wide)
    acc[...] = jnp.zeros_like(acc)
    k2t = k_ref[...].T
    dq_acc[...] = jnp.zeros_like(dq_acc)

    def step(b, carry):
        at = pl.ds(b * rows, rows)
        dks, dvs = [], []
        for a in range(2):
            scores = _dot(kx[a, at, :], qx[a], NT)
            offs = [(seq_len - STRIP) - (b * per + i) * STRIP for i in range(per)]
            bias = [strip[a, :, pl.ds(off, seq_len)] for off in offs]
            probs = jnp.exp2(scores + (jnp.concatenate(bias, 0) if per > 1 else bias[0]))
            grad_scores = probs * _dot(vx[a, at, :], dox[a], NT)
            for i, off in enumerate(offs):
                acc[a, :, pl.ds(off, seq_len)] += grad_scores[i * STRIP:(i + 1) * STRIP]
            probs_b = probs.astype(jnp.bfloat16)
            gs_b = grad_scores.astype(jnp.bfloat16)
            dvs.append(_dot(probs_b, do_ref[...]))
            dks.append(_dot(gs_b, q_ref[...]))
            dq_acc[a] += _dot(k2t[:, b * rows:(b + 1) * rows], gs_b)
        dk_ref[at, :] = (jnp.where(lane < 64, dks[0], dks[1]) * LN2).astype(jnp.bfloat16)
        dv_ref[at, :] = jnp.where(lane < 64, dvs[0], dvs[1]).astype(jnp.bfloat16)
        return carry

    for b in range(seq_len // rows):
        step(b, 0)
    dq_ref[...] = jnp.concatenate([dq_acc[0, 0:64], dq_acc[1, 64:128]], 0).T.astype(jnp.bfloat16)
    for a in range(2):
        sums = acc[a]
        half = STRIP
        while half > 8:
            half //= 2
            sums = sums[:half] + pltpu.roll(sums[half:], wide - half, 1)
        while half > 1:
            half //= 2
            sums = sums + pltpu.roll(pltpu.roll(sums, 8 - half, 0), wide - half, 1)
        g_ref[pl.ds(2 * local_pair + a, 1), :] = pltpu.roll(sums, STRIP - 1, 1)[0:1]

def attn_bwd(length, q, k, v, do, o, lse, trev, first, count, prev=None, rows=512):
    seq_len, width = q.shape
    wide = trev.shape[-1]
    blk = pl.BlockSpec((seq_len, 128), lambda p, n: (0, first + p))
    mat = jax.ShapeDtypeStruct((seq_len, width), jnp.bfloat16)
    prev = tuple(prev) if prev is not None else ()
    return pl.pallas_call(
        functools.partial(bwd_kernel, rows=rows, seq_len=seq_len, first=first),
        out_shape=(mat, mat, mat, jax.ShapeDtypeStruct((2 * count, wide), jnp.float32)),
        grid_spec=pltpu.PrefetchScalarGridSpec(
            num_scalar_prefetch=1, grid=(count,),
            in_specs=[blk, blk, blk, blk, blk, pl.BlockSpec((1, seq_len, 128), lambda p, n: (first + p, 0, 0)),
                      pl.BlockSpec(trev.shape, lambda p, n: (0, 0))] + [pl.BlockSpec(memory_space=pl.ANY)] * len(prev),
            out_specs=[blk, blk, blk, pl.BlockSpec((2 * count, wide), lambda p, n: (0, 0))],
            scratch_shapes=[pltpu.VMEM((2, STRIP, wide), jnp.float32), pltpu.VMEM((2, STRIP, wide), jnp.float32),
                            pltpu.VMEM((2, 128, seq_len), jnp.float32)] + [pltpu.VMEM((2, seq_len, 128), jnp.bfloat16)] * 4),
        input_output_aliases={8 + i: i for i in range(len(prev))},
        compiler_params=pltpu.CompilerParams(vmem_limit_bytes=LIMIT),
        cost_estimate=LIGHT,
        name="attn_bwd",
    )(length, q, k, v, do, o, lse, trev, *prev)

ANY = pl.BlockSpec(memory_space=pl.ANY)
VM = pl.BlockSpec(memory_space=pltpu.VMEM)
SM = pl.BlockSpec(memory_space=pltpu.SMEM)

def rms_inverse(value):
    return lax.rsqrt(jnp.mean(value * value, axis=1, keepdims=True) + epsilon)

def pull_sequence(me, whole_ref, chip_ref, core_ref, dst, sem):
    rows = whole_ref.shape[1]
    for mask, src in enumerate((whole_ref.at[me], core_ref.at[0], chip_ref.at[me & 1], core_ref.at[1])):
        at = pl.multiple_of((me ^ mask) * rows, rows)
        pltpu.make_async_copy(src, dst.at[pl.ds(at, rows), :], sem).start()

def qkv_kernel(ids_ref, x4_ref, chip_ref, core_ref, *refs, masks):
    gathered = refs[:len(masks)]
    bucket_ref = refs[len(masks)]
    x_out, h_out, q_out, k_out, v_out, w_out, gain_ref, t_ref, trev_ref, xs, hs, ps, ws, es, sems = refs[len(masks) + 1:]
    me, flat = ids_ref[0], ids_ref[1]
    width = xs.shape[1]
    own = width // es.shape[0]
    pull_sequence(me, x4_ref, chip_ref, core_ref, xs, sems.at[0])
    for ref, ids in zip(gathered, masks):
        for j, mask in enumerate(ids):
            shard = flat ^ mask
            pltpu.make_async_copy(ref.at[j, 3 * own:3 * own + 16, :], es.at[shard], sems.at[1]).start()
    for ref, ids in zip(gathered, masks):
        for j, mask in enumerate(ids):
            at = pl.multiple_of((flat ^ mask) * own, own)
            for i in range(3):
                pltpu.make_async_copy(ref.at[j, i * own:(i + 1) * own, :], ws.at[pl.ds(at, own), i * width:(i + 1) * width], sems.at[2]).start()
    pltpu.make_async_copy(es, es, sems.at[1]).wait()
    extras = es[...].astype(jnp.float32)
    gains = jnp.sum(extras, axis=0)
    gain_ref[...] = gains[0:8]
    table = extras[:, 8, 0:128].astype(jnp.bfloat16)
    ids = lax.broadcasted_iota(jnp.int32, (es.shape[0], 1), 0)
    heads = t_ref.shape[0]
    for i, ref in enumerate((t_ref, trev_ref)):
        hot = jnp.where(bucket_ref[i:i + 1, :] == ids, 1.0, 0.0).astype(jnp.bfloat16)
        ref[...] = _dot(table, hot, TN)[0:heads] * LOG2E
    pltpu.make_async_copy(xs, xs, sems.at[0]).wait()
    part = 256
    def norm(i, carry):
        at = pl.ds(pl.multiple_of(i * part, part), part)
        x = xs[at, :].astype(jnp.float32)
        hs[at, :] = (x * rms_inverse(x) * gains[0:1]).astype(jnp.bfloat16)
        return carry
    lax.fori_loop(0, xs.shape[0] // part, norm, 0)
    copies = [pltpu.make_async_copy(xs, x_out, sems.at[0]), pltpu.make_async_copy(hs, h_out, sems.at[1])]
    for copy in copies:
        copy.start()
    pltpu.make_async_copy(ws, ws, sems.at[2]).wait()
    copies.append(pltpu.make_async_copy(ws, w_out, sems.at[2]))
    copies[-1].start()
    for i, ref in enumerate((q_out, k_out, v_out)):
        full = _dot(hs[...], ws[:, i * width:(i + 1) * width])
        ps[i] = (full * LOG2E if i == 0 else full).astype(jnp.bfloat16)
        copies.append(pltpu.make_async_copy(ps.at[i], ref, sems.at[3 + i]))
        copies[-1].start()
    for copy in copies:
        copy.wait()

def qkv_fwd(ids, x4, came, gathered, masks, bucket_rows, heads):
    parts, rows, width = x4.shape
    total = parts * rows
    shards = sum(len(m) for m in masks)
    mat = jax.ShapeDtypeStruct((total, width), jnp.bfloat16)
    wide = bucket_rows.shape[1]
    vm = lambda *s: pltpu.VMEM(s, jnp.bfloat16)
    return pl.pallas_call(
        functools.partial(qkv_kernel, masks=masks),
        out_shape=(mat,) * 5 + (jax.ShapeDtypeStruct((width, 3 * width), jnp.bfloat16), jax.ShapeDtypeStruct((8, width), jnp.float32),
                                jax.ShapeDtypeStruct((heads, wide), jnp.float32), jax.ShapeDtypeStruct((heads, wide), jnp.float32)),
        in_specs=[SM] + [ANY] * (3 + len(gathered)) + [VM],
        out_specs=[ANY] * 6 + [VM] * 3,
        scratch_shapes=[vm(total, width), vm(total, width), vm(3, total, width), vm(width, 3 * width), vm(shards, 16, width), pltpu.SemaphoreType.DMA((6,))],
        compiler_params=pltpu.CompilerParams(vmem_limit_bytes=LIMIT),
        cost_estimate=LIGHT,
        name="qkv_fwd",
    )(ids, x4, *came, *gathered, bucket_rows)

def gelu_both(v):
    t = jnp.tanh(root_coef * (v + cubic_coef * v * v * v))
    half = 0.5 * (1.0 + t)
    slope = half + 0.5 * v * (1.0 - t * t) * (root_coef * (1.0 + 3.0 * cubic_coef * v * v))
    return v * half, slope

def by_core(core, keep, send, src, dst_rows, sem, lead=slice(None), src_rows=slice(None), lanes=slice(None)):
    for parity in range(2):
        @pl.when(core == parity)
        def _():
            for dst, at in ((keep, parity), (send, 1 - parity)):
                pltpu.make_async_copy(src.at[lead, at, src_rows, lanes], dst.at[lead, dst_rows, lanes], sem).start()

def ff_chunks(h2, h2t, gm, acc, gh2, ws_in, ws_back, st_in, st_back, row_in, emit, before_add, cols=512):
    steps = ws_in.shape[1] // cols
    half, width = st_back.shape[2:]
    own = width // (2 * st_in.shape[0])
    wide = width // cols
    group = cols // (2 * half)

    def step(c, carry):
        at = pl.ds(pl.multiple_of(c * cols, cols), cols)
        win, wback = ws_in[:, at], ws_back[at, :]
        pre = _dot(h2[...], win)
        grad_active = _dot(gm[...], wback, NT)
        act, slope = gelu_both(pre)
        active = act.astype(jnp.bfloat16)
        gpre = (grad_active * slope).astype(jnp.bfloat16)
        @pl.when(c == 0)
        def _():
            before_add()
        acc[...] += _dot(active, wback)
        gh2[...] += _dot(gpre, win, NT)
        lead = pl.ds(c * group, group)
        st_back[lead] = _dot(active, gm[...], TN).astype(jnp.bfloat16).reshape(group, 2, half, width)
        emit(st_back, 0, lead=lead, dst_rows=slice(0, half))
        up = pl.multiple_of((c // wide) * own, own)
        lanes = pl.ds(pl.multiple_of((c % wide) * cols, cols), cols)
        st_in[:, :, pl.ds(up, own), lanes] = _dot(h2t[...], gpre).astype(jnp.bfloat16).reshape(-1, 2, own, cols)
        emit(st_in, 1, src_rows=pl.ds(up, own), dst_rows=pl.ds(row_in + up, own), lanes=lanes)
        return carry
    lax.fori_loop(0, steps, step, 0)

def finish_chunks(st_in, st_back, sems):
    pltpu.make_async_copy(st_back, st_back, sems.at[0]).wait()
    pltpu.make_async_copy(st_in, st_in, sems.at[1]).wait()

def aligned(at, size):
    return at if isinstance(at, int) else pl.multiple_of(at, size)

def pull_ff(flat, gathered, masks, ws_in, ws_back, row_in, sems):
    width = ws_in.shape[0]
    shards = sum(len(m) for m in masks)
    own, half = width // shards, ws_back.shape[0] // shards
    for ref, ids in zip(gathered, masks):
        for j, mask in enumerate(ids):
            shard = flat ^ mask
            pltpu.make_async_copy(ref.at[j, 0:half, :], ws_back.at[pl.ds(aligned(shard * half, half), half), :], sems.at[1]).start()
            at = pl.ds(aligned(shard * own, own), own)
            for i in range(ws_in.shape[1] // width):
                pltpu.make_async_copy(ref.at[j, row_in + i * own:row_in + (i + 1) * own, :], ws_in.at[at, i * width:(i + 1) * width], sems.at[0]).start()

def mid_a_kernel(ids_ref, x_hbm, o_hbm, g4_ref, chip_ref, core_ref, gain_ref, *refs, masks):
    gathered = refs[:len(masks)]
    (mixed_out, acc_out, gh2_out, h2_out, h2t_out, gm_out, wo_out, keep_out, send_out,
     xs, os, wo, ws_in, ws_back, mixed, h2, h2t, acc, gh2, gm, st_in, st_back, sems) = refs[len(masks):]
    flat = ids_ref[1]
    rows, width = xs.shape
    half, own = st_back.shape[2], width // (2 * st_in.shape[0])
    core = flat & 1
    def emit(src, which, **at):
        by_core(core, keep_out, send_out, src, sem=sems.at[which], **at)
    loads = [pltpu.make_async_copy(x_hbm, xs, sems.at[0]), pltpu.make_async_copy(o_hbm, os, sems.at[1])]
    for load in loads:
        load.start()
    for ref, ids in zip(gathered, masks):
        for j, mask in enumerate(ids):
            at = pl.ds(pl.multiple_of((flat ^ mask) * own, own), own)
            pltpu.make_async_copy(ref.at[j, half:half + own, :], wo.at[at, :], sems.at[2]).start()
    pull_ff(flat, gathered, masks, ws_in, ws_back, half + own, sems.at[3:5])
    pull_sequence(ids_ref[0], g4_ref, chip_ref, core_ref, gm, sems.at[5])
    for load in loads:
        load.wait()
    pltpu.make_async_copy(wo, wo, sems.at[2]).wait()
    stores = [pltpu.make_async_copy(wo, wo_out, sems.at[2])]
    stores[0].start()
    part = 256
    def load_rows(i, carry):
        at = pl.ds(pl.multiple_of(i * part, part), part)
        value = xs[at, :].astype(jnp.float32) + _dot(os[at, :], wo[...])
        mixed[at, :] = value
        acc[at, :] = value
        hidden = (value * rms_inverse(value) * gain_ref[1:2, :]).astype(jnp.bfloat16)
        h2[at, :] = hidden
        h2t[:, at] = hidden.T
        gh2[at, :] = jnp.zeros_like(value)
        return carry
    lax.fori_loop(0, rows // part, load_rows, 0)
    pltpu.make_async_copy(gm, gm, sems.at[5]).wait()
    row_ok = lax.broadcasted_iota(jnp.int32, (rows, 1), 0) < ids_ref[2]
    gm[...] = jnp.where(row_ok, gm[...], jnp.zeros_like(gm[...]))
    pltpu.make_async_copy(ws_in, ws_in, sems.at[3]).wait()
    pltpu.make_async_copy(ws_back, ws_back, sems.at[4]).wait()
    for i, (src, dst) in enumerate(((mixed, mixed_out), (h2, h2_out), (h2t, h2t_out), (gm, gm_out))):
        stores.append(pltpu.make_async_copy(src, dst, sems.at[6 + i]))
        stores[-1].start()
    ff_chunks(h2, h2t, gm, acc, gh2, ws_in, ws_back, st_in, st_back, half, emit, lambda: None)
    for i, (src, dst) in enumerate(((acc, acc_out), (gh2, gh2_out))):
        stores.append(pltpu.make_async_copy(src, dst, sems.at[3 + i]))
        stores[-1].start()
    finish_chunks(st_in, st_back, sems.at[0:2])
    for store in stores:
        store.wait()

def mid_a(ids, x, o, g4, came, gains, gathered, masks, ff):
    rows, width = x.shape
    shards = sum(len(m) for m in masks)
    half = ff // shards
    low = lambda *s: jax.ShapeDtypeStruct(s, jnp.bfloat16)
    full = lambda *s: jax.ShapeDtypeStruct(s, jnp.float32)
    vm = lambda *s: pltpu.VMEM(s, jnp.bfloat16)
    vf = lambda *s: pltpu.VMEM(s, jnp.float32)
    stack = half + ff // width * (width // shards)
    return pl.pallas_call(
        functools.partial(mid_a_kernel, masks=masks),
        out_shape=(full(rows, width), full(rows, width), full(rows, width), low(rows, width), low(width, rows), low(rows, width), low(width, width), low(shards // 2, stack, width), low(shards // 2, stack, width)),
        in_specs=[SM] + [ANY] * 5 + [VM] + [ANY] * len(gathered), out_specs=[ANY] * 9,
        scratch_shapes=[vm(rows, width), vm(rows, width), vm(width, width), vm(width, ff), vm(ff, width), vf(rows, width), vm(rows, width), vm(width, rows),
                        vf(rows, width), vf(rows, width), vm(rows, width), vm(shards // 2, 2, stack - half, width), vm(shards // 2, 2, half, width), pltpu.SemaphoreType.DMA((10,))],
        compiler_params=pltpu.CompilerParams(vmem_limit_bytes=LIMIT),
        cost_estimate=LIGHT,
        name="mid_a",
    )(ids, x, o, g4, *came, gains, *gathered)

def mid_b_kernel(ids_ref, gain_ref, mixed_hbm, acc_hbm, gh2_hbm, h2_hbm, h2t_hbm, gm_hbm, wo_hbm, o_hbm, full_ref, *refs):
    (out_ref, gb_out, do_ref, keep_out, send_out,
     os, wo, ws_in, ws_back, mixed, h2, h2t, acc, gh2, gm, gb, st_in, st_back, st_o, sems) = refs
    rows, width = os.shape
    shards, half, own = 2 * st_in.shape[0], st_back.shape[2], width // (2 * st_in.shape[0])
    core = ids_ref[1] & 1
    def emit(src, which, **at):
        by_core(core, keep_out, send_out, src, sem=sems.at[which], **at)
    early = [(h2_hbm, h2), (gm_hbm, gm), (h2t_hbm, h2t)]
    late = [(acc_hbm, acc), (gh2_hbm, gh2), (mixed_hbm, mixed), (wo_hbm, wo), (o_hbm, os)]
    early = [pltpu.make_async_copy(a, b, sems.at[4 + i]) for i, (a, b) in enumerate(early)]
    late = [pltpu.make_async_copy(a, b, sems.at[7 + i]) for i, (a, b) in enumerate(late)]
    for load in early:
        load.start()
    pull_ff(0, (full_ref,), (range(shards),), ws_in, ws_back, half, sems.at[2:4])
    for load in late:
        load.start()
    for load in early:
        load.wait()
    pltpu.make_async_copy(ws_in, ws_in, sems.at[2]).wait()
    pltpu.make_async_copy(ws_back, ws_back, sems.at[3]).wait()
    def before_add():
        late[0].wait()
        late[1].wait()
    ff_chunks(h2, h2t, gm, acc, gh2, ws_in, ws_back, st_in, st_back, half + own, emit, before_add)
    for load in late[2:]:
        load.wait()
    part = 256
    def finish(i, carry):
        at = pl.ds(pl.multiple_of(i * part, part), part)
        out_ref[at, :] = acc[at, :].astype(jnp.bfloat16)
        value = mixed[at, :]
        inverse = rms_inverse(value)
        normed = value * inverse
        scaled = gh2[at, :] * gain_ref[1:2, :]
        grad = inverse * (scaled - normed * jnp.mean(scaled * normed, axis=1, keepdims=True)) + gm[at, :].astype(jnp.float32)
        low = grad.astype(jnp.bfloat16)
        gb[at, :] = low
        do_ref[at, :] = _dot(low, wo[...], NT).astype(jnp.bfloat16)
        return carry
    lax.fori_loop(0, rows // part, finish, 0)
    st_o[...] = _dot(os[...], gb[...], TN).astype(jnp.bfloat16).reshape(st_o.shape)
    emit(st_o, 2, dst_rows=slice(half, half + own))
    store = pltpu.make_async_copy(gb, gb_out, sems.at[3])
    store.start()
    finish_chunks(st_in, st_back, sems.at[0:2])
    pltpu.make_async_copy(st_o, st_o, sems.at[2]).wait()
    store.wait()

def mid_b(ids, gains, state, o, full, ff):
    rows, width = o.shape
    shards = full.shape[0]
    half, own = ff // shards, width // shards
    low = lambda *s: jax.ShapeDtypeStruct(s, jnp.bfloat16)
    vm = lambda *s: pltpu.VMEM(s, jnp.bfloat16)
    vf = lambda *s: pltpu.VMEM(s, jnp.float32)
    rest = ff // width * own
    return pl.pallas_call(
        mid_b_kernel,
        out_shape=(low(rows, width), low(rows, width), low(rows, width), low(shards // 2, half + own + rest, width), low(shards // 2, half + own + rest, width)),
        in_specs=[SM, VM] + [ANY] * 9, out_specs=[VM, ANY, VM, ANY, ANY],
        scratch_shapes=[vm(rows, width), vm(width, width), vm(width, ff), vm(ff, width), vf(rows, width), vm(rows, width), vm(width, rows),
                        vf(rows, width), vf(rows, width), vm(rows, width), vm(rows, width), vm(shards // 2, 2, rest, width), vm(shards // 2, 2, half, width), vm(shards // 2, 2, own, width),
                        pltpu.SemaphoreType.DMA((12,))],
        compiler_params=pltpu.CompilerParams(vmem_limit_bytes=LIMIT),
        cost_estimate=LIGHT,
        name="mid_b",
    )(ids, gains, *state, o, full)

def gw_kernel(ids_ref, h_ref, dq_ref, dk_ref, dv_ref, bucket_ref, *refs):
    keep_out, send_out, st, sems = refs[-4:]
    offs = jnp.concatenate([ref[...] for ref in refs[:-4]], 0)
    pairs, _, stack, width = st.shape
    own = width // (2 * pairs)
    core = ids_ref[1] & 1
    ids = lax.broadcasted_iota(jnp.int32, (2 * pairs, 1), 0)
    hot = jnp.where(bucket_ref[1:2, :] == ids, 1.0, 0.0)
    table = lax.dot_general(hot, offs, NT, precision=lax.Precision.HIGHEST, preferred_element_type=jnp.float32)
    heads = offs.shape[0]
    st[:, :, 3 * own:, :] = jnp.zeros((pairs, 2, stack - 3 * own, width), jnp.bfloat16)
    st[:, :, 3 * own:3 * own + 1, 0:heads] = table.astype(jnp.bfloat16).reshape(pairs, 2, 1, heads)
    for i, ref in enumerate((dq_ref, dk_ref, dv_ref)):
        at = slice(i * own, (i + 1) * own) if i < 2 else slice(i * own, stack)
        st[:, :, i * own:(i + 1) * own, :] = _dot(h_ref[...], ref[...], TN).astype(jnp.bfloat16).reshape(pairs, 2, own, width)
        by_core(core, keep_out, send_out, st, at, sems.at[0], src_rows=at)
    pltpu.make_async_copy(st, st, sems.at[0]).wait()

def qkv_gw(ids, h, dq, dk, dv, bucket_rows, offs, shards):
    rows, width = h.shape
    stack = 3 * width // shards + 16
    half = jax.ShapeDtypeStruct((shards // 2, stack, width), jnp.bfloat16)
    return pl.pallas_call(
        gw_kernel, out_shape=(half, half),
        in_specs=[SM] + [VM] * (5 + len(offs)), out_specs=[ANY, ANY],
        scratch_shapes=[pltpu.VMEM((shards // 2, 2, stack, width), jnp.bfloat16), pltpu.SemaphoreType.DMA((1,))],
        compiler_params=pltpu.CompilerParams(vmem_limit_bytes=LIMIT),
        cost_estimate=LIGHT,
        name="qkv_gw",
    )(ids, h, dq, dk, dv, bucket_rows, *offs)

def gx_kernel(x_ref, gb_ref, dq_ref, dk_ref, dv_ref, gain_ref, w_ref, out_ref):
    width = x_ref.shape[1]
    grad = _dot(dq_ref[...], w_ref[:, :width], NT)
    grad += _dot(dk_ref[...], w_ref[:, width:2 * width], NT)
    grad += _dot(dv_ref[...], w_ref[:, 2 * width:3 * width], NT)
    x = x_ref[...].astype(jnp.float32)
    inverse = rms_inverse(x)
    normed = x * inverse
    scaled = grad * gain_ref[0:1, :]
    out = inverse * (scaled - normed * jnp.mean(scaled * normed, axis=1, keepdims=True)) + gb_ref[...].astype(jnp.float32)
    out_ref[...] = out.astype(jnp.bfloat16)

def qkv_gx(x, gb, dq, dk, dv, gains, w, rows=512):
    total, width = x.shape
    blk = pl.BlockSpec((rows, width), lambda i: (i, 0))
    return pl.pallas_call(
        gx_kernel, out_shape=jax.ShapeDtypeStruct((total, width), jnp.bfloat16), grid=(total // rows,),
        in_specs=[blk] * 5 + [pl.BlockSpec(gains.shape, lambda i: (0, 0)),
                              pl.BlockSpec((width, 3 * width), lambda i: (0, 0), pipeline_mode=pl.Buffered(1))],
        out_specs=blk,
        compiler_params=pltpu.CompilerParams(vmem_limit_bytes=LIMIT),
        cost_estimate=LIGHT,
        name="qkv_gx",
    )(x, gb, dq, dk, dv, gains, w)

def swap(value, axis, mask):
    return lax.ppermute(value, axis, [(i, i ^ mask) for i in range(lax.axis_size(axis))])


def send_chip(blocks, me):
    return swap(lax.dynamic_slice_in_dim(blocks, 2 * (1 - me // 2), 2, 0), "seq", 2)


def send_core(blocks, from_chip, me):
    own = lax.dynamic_index_in_dim(blocks, me ^ 1, 0)
    passed = lax.dynamic_index_in_dim(from_chip, 1 - me % 2, 0)
    return swap(jnp.concatenate([own, passed], 0), "seq", 1)


class Gather:
    def __init__(self, shard):
        shard = shard[None]
        self.sent = [shard] + [swap(shard, "dp", 2 * z) for z in (1, 2, 3)]
        self.pieces, self.masks = [], []

    def take(self, piece, mask, rows=(0, 1, 2, 3)):
        ids = tuple(8 * z | mask for z in rows)
        self.pieces += [piece, swap(piece, "seq", 1)]
        self.masks += [ids, tuple(m | 1 for m in ids)]

    def fill(self):
        self.own = jnp.concatenate(self.sent, 0)

    def sides(self):
        self.x, self.y = swap(self.own, "seq", 2), swap(self.own, "dp", 1)

    def corner_halves(self):
        self.near, self.far = swap(self.y[:2], "seq", 2), swap(self.x[2:], "dp", 1)

    def corner_y(self):
        self.corner = swap(self.x, "dp", 1)

    def all_pieces(self):
        return tuple(self.pieces), tuple(self.masks)


class Scatter:
    def __init__(self, keep, send, pos, corner_y):
        self.z, self.y, self.x = pos
        cube = (4, 2, 2) + keep.shape[1:]
        self.mine, self.sent, self.corner_y = keep.reshape(cube), send.reshape(cube), corner_y
        self.other = swap(self.sent, "seq", 1)

    def fold(self):
        pick = lambda v, at, axis: lax.dynamic_index_in_dim(v, at, axis, keepdims=False)
        def quarter(dy, dx):
            cut = lambda v: pick(pick(v, self.y ^ dy, 1), self.x ^ dx, 1).astype(jnp.float32)
            return (cut(self.mine) + cut(self.other)).astype(jnp.bfloat16)
        far = quarter(1, 1)
        self.to_x, self.to_y, self.own = quarter(0, 1), quarter(1, 0), quarter(0, 0)
        if self.corner_y:
            self.came_x, self.came_y = None, swap(far, "dp", 1)
        else:
            self.came_x, self.came_y = swap(far[:2], "seq", 2), swap(far[2:], "dp", 1)

    def turn(self):
        add = lambda a, b: (a.astype(jnp.float32) + b.astype(jnp.float32)).astype(jnp.bfloat16)
        if self.corner_y:
            to_y, = tie(self.came_y, self.to_y)
            to_x = add(self.to_x, self.came_y)
        else:
            to_x = lax.dynamic_update_slice_in_dim(self.to_x, add(self.to_x[2:], self.came_y), 2, 0)
            to_y = lax.dynamic_update_slice_in_dim(self.to_y, add(self.to_y[:2], self.came_x), 0, 0)
        self.sent = (to_x, to_y)
        self.came_x, self.came_y = swap(to_x, "seq", 2), swap(to_y, "dp", 1)

    def column(self):
        total = self.own.astype(jnp.float32) + self.came_x.astype(jnp.float32) + self.came_y.astype(jnp.float32)
        total = total.astype(jnp.bfloat16)
        block = lambda k: lax.dynamic_index_in_dim(total, self.z ^ k, 0, keepdims=False)
        self.mine = block(0)
        self.came = [swap(block(k), "dp", 2 * k) for k in (1, 2, 3)]

    def result(self):
        return sum((c.astype(jnp.float32) for c in self.came), self.mine.astype(jnp.float32))


def place(blocks, from_chip, from_core, me):
    for mask, block in ((1, from_core[0:1]), (2, lax.dynamic_index_in_dim(from_chip, me % 2, 0)), (3, from_core[1:2])):
        blocks = lax.dynamic_update_slice_in_dim(blocks, block, me ^ mask, 0)
    return blocks


def tie(first, *later):
    return lax.optimization_barrier((first,) + later)[1:]


def local_whole(tokens, cotangent, lengths, buckets, norm1_gain, w_query, w_key, w_value, w_out, rel_table, norm2_gain, w_in, w_back):
    micro_count, seq_count, rows, width = tokens.shape
    parts = micro_count * seq_count
    both = ("dp", "seq")
    me, dp = lax.axis_index("seq"), lax.axis_index("dp")
    shards = lax.axis_size("seq") * lax.axis_size("dp")
    flat = dp * parts + me
    pos = (dp // 2, dp % 2, me // 2)
    low = lambda v: v.astype(jnp.bfloat16)
    up = lambda v: v.astype(jnp.float32)
    own, ff_own = w_query.shape[0], w_back.shape[0]
    ids = jnp.stack([me, flat, lax.dynamic_index_in_dim(lengths.reshape(parts), me, 0, keepdims=False)])
    length = ids[2:3]

    place_row = lambda v: lax.dynamic_update_slice(jnp.zeros((1, width), jnp.bfloat16), low(v)[None], (0, flat * own))
    small = jnp.concatenate([place_row(norm1_gain), place_row(norm2_gain), jnp.zeros((6, width), jnp.bfloat16),
                             jnp.pad(low(rel_table)[None], ((0, 7), (0, width - HEADS)))], 0)
    shard1 = jnp.concatenate([low(w_query), low(w_key), low(w_value), small], 0)
    ff = w_in.shape[1] // 2
    half = ff_own // 2
    halves = low(w_in).reshape(own, shards, 2, half)
    in_half = lambda i: [halves[:, :, i].reshape(own, ff)[:, j:j + width] for j in range(0, ff, width)]
    shard2 = jnp.concatenate([low(w_back[:half]), low(w_out)] + in_half(0), 0)
    shard3 = jnp.concatenate([low(w_back[half:])] + in_half(1), 0)
    x4, g4 = tokens.reshape(parts, rows, width), cotangent.reshape(parts, rows, width)
    bucket_rows = jnp.stack([jnp.pad(buckets, (0, 1), constant_values=-1), jnp.pad(buckets[::-1], (0, 1), constant_values=-1)])

    g1 = Gather(shard1)
    x_chip = send_chip(x4, me)
    g2 = Gather(shard2)
    g1.fill()
    g1.own, = tie((x_chip, g2.sent[1], shard3), g1.own)
    g1.sides()
    g1.x, g1.y = tie(g2.sent[2], g1.x, g1.y)
    g1.corner_halves()
    g2.fill()
    g1.take(g1.own, 0)
    g1.near, g1.far, g2.own = tie(g1.pieces[1], g1.near, g1.far, g2.own)
    g2.sides()
    g1.x, g1.y, x4_in = tie((g1.near, g1.far), g1.x, g1.y, x4)
    g1.take(g1.x, 2)
    g1.take(g1.y, 4)
    g1.take(g1.near, 6, (0, 1))
    g1.take(g1.far, 6, (2, 3))
    x_core = send_core(x4_in, x_chip, me)
    shard3, = tie((g1.near, g1.far), shard3)
    full3 = lax.all_gather(shard3, both, axis=0, tiled=False)
    x, hidden, q, k, v, w_qkv, gains, t, t_back = qkv_fwd(ids, x4, (x_chip, x_core), *g1.all_pieces(), bucket_rows, HEADS)
    pairs = HEADS // 2
    att = attn_fwd(length, q, k, v, t, 0, 3)
    g2.take(g2.own, 0)
    g2.x, g2.y = tie((att[0], g2.pieces[1]), g2.x, g2.y)
    g2.corner_y()
    g4_in, = tie(g2.x, g4)
    g_chip = send_chip(g4_in, me)
    g2.take(g2.x, 2)
    g2.take(g2.y, 4)
    q_in, = tie((g2.x, g2.y), q)
    attended, lse = attn_fwd(length, q_in, k, v, t, 3, pairs - 3, att)
    g2.corner, g_chip = tie((attended, g2.pieces[3], g2.pieces[5]), g2.corner, g_chip)
    g2.take(g2.corner, 6)
    g_core = send_core(g4, g_chip, me)
    *state, keep3, send3 = mid_a(ids, x, attended, g4, (g_chip, g_core), gains, *g2.all_pieces(), ff)
    sc3 = Scatter(keep3, send3, pos, True)
    out, gb, g_att, keep2, send2 = mid_b(ids, gains, state, attended, full3, ff)
    sc3.other, = tie(gb, sc3.other)
    sc3.fold()
    send2, = tie(sc3.own, send2)
    sc2 = Scatter(keep2, send2, pos, True)
    out4 = out.reshape(parts, rows, width)
    out4, = tie(sc3.own, out4)
    out_chip = send_chip(out4, me)
    count = pairs // 4
    back = lambda first, g, prev: attn_bwd(length, q, k, v, g, attended, lse, t_back, first, count, prev)
    g_att, = tie(sc3.own, g_att)
    dq, dk, dv, off0 = back(0, g_att, None)
    sc2.other, = tie(off0, sc2.other)
    sc2.fold()
    sc3.came_y, = tie(sc2.own, sc3.came_y)
    sc3.turn()
    g_att, = tie(sc3.sent, g_att)
    dq, dk, dv, off1 = back(count, g_att, (dq, dk, dv))
    sc2.came_x, sc2.came_y = tie((off1, out_chip), sc2.came_x, sc2.came_y)
    sc2.turn()
    out4_in, out_chip = tie(sc2.sent, out4, out_chip)
    out_core = send_core(out4_in, out_chip, me)
    g_att, = tie(sc2.sent, g_att)
    dq, dk, dv, off2 = back(2 * count, g_att, (dq, dk, dv))
    sc3.came_x, sc3.came_y = tie((off2, out_core), sc3.came_x, sc3.came_y)
    sc3.column()
    g_att, = tie(sc3.mine, g_att)
    dq, dk, dv, off3 = back(3 * count, g_att, (dq, dk, dv))
    sc2.came_x, sc2.came_y = tie(off3, sc2.came_x, sc2.came_y)
    sc2.column()
    h_in, = tie((sc2.mine, sc3.came), hidden)
    keep1, send1 = qkv_gw(ids, h_in, dq, dk, dv, bucket_rows, (off0, off1, off2, off3), shards)
    sc1 = Scatter(keep1, send1, pos, False)
    gb_in, = tie(send1, gb)
    gx = qkv_gx(x, gb_in, dq, dk, dv, gains, w_qkv)
    sc1.other, = tie(gx, sc1.other)
    sc1.fold()
    out4, out_chip, out_core = tie(sc1.own, out4, out_chip, out_core)
    layer_out = place(out4, out_chip, out_core, me)
    sc1.came_x, sc1.came_y = tie((layer_out, sc2.came), sc1.came_x, sc1.came_y)
    sc1.turn()
    sc2.came = list(tie(sc1.sent, *sc2.came))
    sc3.came = list(tie(sc1.sent, *sc3.came))
    r2, r_a = sc2.result(), sc3.result()
    join = lambda v: jnp.concatenate([v[i:i + own] for i in range(0, v.shape[0], own)], 1).reshape(own, shards, 1, half)
    g_in = jnp.concatenate([join(r_a[half:]), join(r2[half + own:])], 2).reshape(w_in.shape)
    g_back = jnp.concatenate([r_a[:half], r2[:half]], 0)
    g_out = r2[half:half + own]
    g_gain2 = jnp.sum(up(low(w_in)) * g_in, axis=1) / up(low(norm2_gain))
    sc1.came_x, sc1.came_y, g_in, g_back, g_out, g_gain2 = lax.optimization_barrier((sc1.came_x, sc1.came_y, g_in, g_back, g_out, g_gain2))
    sc1.column()
    gx, = tie(sc1.mine, gx)
    gx4 = gx.reshape(parts, rows, width)
    gx_chip = send_chip(gx4, me)
    gx_chip, = tie(sc1.came, gx_chip)
    gx_core = send_core(gx4, gx_chip, me)
    input_grad = place(gx4, gx_chip, gx_core, me)
    sc1.came = list(tie(gx_chip, *sc1.came))
    r1 = sc1.result()
    prod = up(shard1[:3 * own]) * r1[:3 * own]
    g_gain1 = jnp.sum(prod[:own] + prod[own:2 * own] + prod[2 * own:], axis=1) / up(low(norm1_gain))
    return (layer_out.reshape(tokens.shape), input_grad.reshape(tokens.shape), g_gain1, r1[:own], r1[own:2 * own], r1[2 * own:3 * own],
            g_out, r1[3 * own, :HEADS], g_gain2, g_in, g_back)


def local_any(shape, tokens, *rest):
    fits = tuple(shape) == (8, 4) and tokens.shape[0] * tokens.shape[1] == 4 and tokens.shape[3] == HEADS * DH == 1024
    return (local_whole if fits else local)(tokens, *rest)


def solution(mesh):
    return jax.shard_map(
        functools.partial(local_any, mesh.devices.shape),
        mesh=mesh,
        in_specs=(
            P(None, "dp", "seq", None),
            P(None, "dp", "seq", None),
            P(None, "dp"),
            P(),
            P(("dp", "seq")),
            P(("dp", "seq"), None),
            P(("dp", "seq"), None),
            P(("dp", "seq"), None),
            P(("dp", "seq"), None),
            P(("dp", "seq")),
            P(("dp", "seq")),
            P(("dp", "seq"), None),
            P(("dp", "seq"), None),
        ),
        out_specs=(
            P(None, "dp", "seq", None),
            P(None, "dp", "seq", None),
            P(("dp", "seq")),
            P(("dp", "seq"), None),
            P(("dp", "seq"), None),
            P(("dp", "seq"), None),
            P(("dp", "seq"), None),
            P(("dp", "seq")),
            P(("dp", "seq")),
            P(("dp", "seq"), None),
            P(("dp", "seq"), None),
        ),
        check_vma=False,
    )
```

```python
import functools

import jax
import jax.numpy as jnp
from jax import lax
from jax.experimental import pallas as pl
from jax.experimental.pallas import tpu as pltpu
from jax.sharding import PartitionSpec as P

HEADS = 16
DH = 64
BUCKETS = 32


epsilon = 1e-06
floor_score = -1e30
highest = lax.Precision.HIGHEST
root_coef = 0.7978845608
cubic_coef = 0.044715


def gelu_tanh(values):
    return (
        0.5
        * values
        * (1.0 + jnp.tanh(root_coef * (values + cubic_coef * values * values * values)))
    )


def gelu_slope(values):
    inner = jnp.tanh(root_coef * (values + cubic_coef * values * values * values))
    return 0.5 * (1.0 + inner) + 0.5 * values * (1.0 - inner * inner) * root_coef * (
        1.0 + 3.0 * cubic_coef * values * values
    )


def project(acts, weight):
    return jnp.einsum("srd,de->sre", acts, weight, preferred_element_type=jnp.float32)


def project_back(grads_in, weight):
    return jnp.einsum("sre,de->srd", grads_in, weight, preferred_element_type=jnp.float32)


def contract(acts, grads_in):
    return jnp.einsum("srd,sre->de", acts, grads_in, preferred_element_type=jnp.float32)


def rms_forward(values, gain):
    inverse = lax.rsqrt(jnp.mean(values * values, axis=-1, keepdims=True) + epsilon)
    normed = values * inverse
    return (normed, inverse, (normed * gain.astype(jnp.float32)).astype(jnp.bfloat16))


def rms_backward(grad_hidden, normed, inverse, gain):
    scaled = grad_hidden * gain.astype(jnp.float32)
    grad_values = inverse * (scaled - normed * jnp.mean(scaled * normed, axis=-1, keepdims=True))
    return (grad_values, jnp.sum(grad_hidden * normed, axis=(0, 1)))


def score_block(per_head_queries, per_head_keys, rel_bias, key_valid):
    scores = (
        jnp.einsum(
            "ofck,owck->ocfw", per_head_queries, per_head_keys, preferred_element_type=jnp.float32
        )
        + rel_bias[None]
    )
    return jnp.where(key_valid, scores, floor_score)


def offset_sums(grid, first_row, seq_len):
    head_count, row_count, key_count = grid.shape
    flipped = grid[:, ::-1, :]
    padded = jnp.pad(flipped, ((0, 0), (0, 0), (0, row_count)))
    wide_len = key_count + row_count
    skewed = padded.reshape(head_count, row_count * wide_len)[:, : row_count * (wide_len - 1)]
    skewed = skewed.reshape(head_count, row_count, wide_len - 1)
    column_sums = jnp.sum(skewed, axis=1)
    placed = jnp.zeros((head_count, 2 * seq_len - 1), jnp.float32)
    begin = seq_len - row_count - first_row
    return lax.dynamic_update_slice(placed, column_sums, (jnp.int32(0), begin))


def run_micro(inputs, incoming, seq_lens, attn_set, mlp_set, context):
    onehot, offsets, row_pos, key_pos, first_row, seq_len = context
    gain_one, query_w, key_w, value_w, out_w, bias_table = attn_set
    gain_two, in_w, return_projection_weight = mlp_set
    seq_count, row_count, model_width = inputs.shape
    values = inputs.astype(jnp.float32)
    normed_one, inverse_one, hidden_one = rms_forward(values, gain_one)
    queries = project(hidden_one, query_w).astype(jnp.bfloat16)
    keys_own = project(hidden_one, key_w).astype(jnp.bfloat16)
    values_own = project(hidden_one, value_w).astype(jnp.bfloat16)
    keys_all, values_all = (
        lax.all_gather(keys_own, "seq", axis=1, tiled=True),
        lax.all_gather(values_own, "seq", axis=1, tiled=True),
    )
    per_offset = jnp.dot(
        onehot, bias_table.reshape(BUCKETS, HEADS), preferred_element_type=jnp.float32
    )
    rel_bias = jnp.transpose(per_offset[offsets], (2, 0, 1))
    key_valid = (key_pos[None, :] < seq_lens[:, None])[:, None, None, :]
    per_head_queries = queries.reshape(seq_count, row_count, HEADS, DH)
    per_head_keys = keys_all.reshape(seq_count, seq_len, HEADS, DH)
    per_head_values = values_all.reshape(seq_count, seq_len, HEADS, DH)
    scores = score_block(per_head_queries, per_head_keys, rel_bias, key_valid)
    row_max = jnp.max(scores, axis=-1, keepdims=True)
    exp_scores = jnp.exp(scores - row_max)
    row_total = jnp.sum(exp_scores, axis=-1, keepdims=True)
    attn_probs = exp_scores / row_total
    log_total = row_max + jnp.log(row_total)
    reduced_precision_probs = attn_probs.astype(jnp.bfloat16)
    attended = jnp.einsum(
        "jfpe,jefn->jpfn",
        reduced_precision_probs,
        per_head_values,
        preferred_element_type=jnp.float32,
    )
    attended = attended.reshape(seq_count, row_count, model_width).astype(jnp.bfloat16)
    residual_mid = values + project(attended, out_w)
    normed_two, inverse_two, hidden_two = rms_forward(residual_mid, gain_two)
    pre_act = project(hidden_two, in_w)
    active = gelu_tanh(pre_act).astype(jnp.bfloat16)
    result = (residual_mid + project(active, return_projection_weight)).astype(jnp.bfloat16)
    row_valid = (row_pos[None, :] < seq_lens[:, None]).astype(jnp.float32)[:, :, None]
    grad_out = incoming.astype(jnp.float32) * row_valid
    grad_low = grad_out.astype(jnp.bfloat16)
    grad_back = contract(active, grad_low)
    gradient_active_rows = project_back(grad_low, return_projection_weight)
    grad_pre = (gradient_active_rows * gelu_slope(pre_act)).astype(jnp.bfloat16)
    grad_in = contract(hidden_two, grad_pre)
    grad_hidden_two = project_back(grad_pre, in_w)
    grad_mixed, grad_gain_two = rms_backward(grad_hidden_two, normed_two, inverse_two, gain_two)
    grad_mixed = grad_mixed + grad_out
    grad_branch = grad_mixed.astype(jnp.bfloat16)
    grad_outw = contract(attended, grad_branch)
    gradient_attended_values = project_back(grad_branch, out_w).astype(jnp.bfloat16)
    gradient_attended_values = gradient_attended_values.reshape(seq_count, row_count, HEADS, DH)
    scores = score_block(per_head_queries, per_head_keys, rel_bias, key_valid)
    attn_probs = jnp.exp(scores - log_total)
    reduced_precision_probs = attn_probs.astype(jnp.bfloat16)
    grad_probs = jnp.einsum(
        "ofck,owck->ocfw",
        gradient_attended_values,
        per_head_values,
        preferred_element_type=jnp.float32,
    )
    inner_sum = jnp.sum(attn_probs * grad_probs, axis=-1, keepdims=True)
    gradient_score_matrix = (attn_probs * (grad_probs - inner_sum)).astype(jnp.bfloat16)
    grad_query = jnp.einsum(
        "jfpe,jefn->jpfn", gradient_score_matrix, per_head_keys, preferred_element_type=jnp.float32
    )
    grad_query = grad_query.astype(jnp.bfloat16).reshape(seq_count, row_count, model_width)
    key_part = jnp.einsum(
        "eciv,eicq->evcq",
        gradient_score_matrix,
        per_head_queries,
        preferred_element_type=jnp.float32,
    )
    value_part = jnp.einsum(
        "eciv,eicq->evcq",
        reduced_precision_probs,
        gradient_attended_values,
        preferred_element_type=jnp.float32,
    )
    key_part = key_part.reshape(seq_count, seq_len, model_width)
    value_part = value_part.reshape(seq_count, seq_len, model_width)
    grad_key, grad_value = (
        lax.psum_scatter(
            key_part.astype(jnp.bfloat16), "seq", scatter_dimension=1, tiled=True
        ).astype(jnp.float32),
        lax.psum_scatter(
            value_part.astype(jnp.bfloat16), "seq", scatter_dimension=1, tiled=True
        ).astype(jnp.float32),
    )
    grad_key = grad_key.astype(jnp.bfloat16)
    grad_value = grad_value.astype(jnp.bfloat16)
    offset_grad = offset_sums(
        jnp.sum(gradient_score_matrix.astype(jnp.float32), axis=0), first_row, seq_len
    )
    grad_table = jnp.dot(onehot.astype(jnp.float32).T, offset_grad.T, precision=highest).reshape(-1)
    grad_qw = contract(hidden_one, grad_query)
    grad_kw = contract(hidden_one, grad_key)
    grad_vw = contract(hidden_one, grad_value)
    grad_hidden_one = (
        project_back(grad_query, query_w)
        + project_back(grad_key, key_w)
        + project_back(grad_value, value_w)
    )
    grad_values, grad_gain_one = rms_backward(grad_hidden_one, normed_one, inverse_one, gain_one)
    grad_values = grad_values + grad_mixed
    gradients = (
        grad_gain_one,
        grad_qw,
        grad_kw,
        grad_vw,
        grad_outw,
        grad_table,
        grad_gain_two,
        grad_in,
        grad_back,
    )
    return (result, grad_values.astype(jnp.bfloat16), gradients)


def local(
    tokens,
    cotangent,
    lengths,
    buckets,
    norm1_gain,
    w_query,
    w_key,
    w_value,
    w_out,
    rel_table,
    norm2_gain,
    w_in,
    w_back,
):
    micro_count, seq_count, row_count, model_width = tokens.shape
    seq_parts = lax.axis_size("seq")
    seq_len = row_count * seq_parts
    first_row = lax.axis_index("seq") * row_count
    row_pos = first_row + jnp.arange(row_count, dtype=jnp.int32)
    key_pos = jnp.arange(seq_len, dtype=jnp.int32)
    onehot = (buckets[:, None] == jnp.arange(BUCKETS, dtype=jnp.int32)[None, :]).astype(
        jnp.bfloat16
    )
    offsets = key_pos[None, :] - row_pos[:, None] + (seq_len - 1)
    context = (onehot, offsets, row_pos, key_pos, first_row, seq_len)
    outputs = []
    input_grads = []
    pending = None
    shard_sums = None
    for micro_step in range(micro_count):
        attn_set = (
            lax.all_gather(norm1_gain.astype(jnp.bfloat16), ("dp", "seq"), axis=0, tiled=True),
            lax.all_gather(w_query.astype(jnp.bfloat16), ("dp", "seq"), axis=0, tiled=True),
            lax.all_gather(w_key.astype(jnp.bfloat16), ("dp", "seq"), axis=0, tiled=True),
            lax.all_gather(w_value.astype(jnp.bfloat16), ("dp", "seq"), axis=0, tiled=True),
            lax.all_gather(w_out.astype(jnp.bfloat16), ("dp", "seq"), axis=0, tiled=True),
            lax.all_gather(rel_table.astype(jnp.bfloat16), ("dp", "seq"), axis=0, tiled=True),
        )
        mlp_set = (
            lax.all_gather(norm2_gain.astype(jnp.bfloat16), ("dp", "seq"), axis=0, tiled=True),
            lax.all_gather(w_in.astype(jnp.bfloat16), ("dp", "seq"), axis=0, tiled=True),
            lax.all_gather(w_back.astype(jnp.bfloat16), ("dp", "seq"), axis=0, tiled=True),
        )
        layer_part, grad_part, gradients = run_micro(
            tokens[micro_step],
            cotangent[micro_step],
            lengths[micro_step],
            attn_set,
            mlp_set,
            context,
        )
        outputs.append(layer_part)
        input_grads.append(grad_part)
        pending = gradients if pending is None else jax.tree.map(jnp.add, pending, gradients)
    shard_sums = (
        lax.psum_scatter(pending[0], ("dp", "seq"), scatter_dimension=0, tiled=True),
        lax.psum_scatter(pending[1], ("dp", "seq"), scatter_dimension=0, tiled=True),
        lax.psum_scatter(pending[2], ("dp", "seq"), scatter_dimension=0, tiled=True),
        lax.psum_scatter(pending[3], ("dp", "seq"), scatter_dimension=0, tiled=True),
        lax.psum_scatter(pending[4], ("dp", "seq"), scatter_dimension=0, tiled=True),
        lax.psum_scatter(pending[5], ("dp", "seq"), scatter_dimension=0, tiled=True),
        lax.psum_scatter(pending[6], ("dp", "seq"), scatter_dimension=0, tiled=True),
        lax.psum_scatter(pending[7], ("dp", "seq"), scatter_dimension=0, tiled=True),
        lax.psum_scatter(pending[8], ("dp", "seq"), scatter_dimension=0, tiled=True),
    )
    return (
        jnp.stack(outputs),
        jnp.stack(input_grads),
        shard_sums[0],
        shard_sums[1],
        shard_sums[2],
        shard_sums[3],
        shard_sums[4],
        shard_sums[5],
        shard_sums[6],
        shard_sums[7],
        shard_sums[8],
    )


NT = (((1,), (1,)), ((), ()))
TN = (((0,), (0,)), ((), ()))
STRIP = 128
LOG2E = 1.4426950408889634
LN2 = 0.6931471805599453
LIMIT = 58 << 20
LIGHT = pl.CostEstimate(flops=1 << 20, bytes_accessed=1 << 16, transcendentals=0)

def _dot(a, b, dims=(((1,), (0,)), ((), ()))):
    return lax.dot_general(a, b, dims, preferred_element_type=jnp.float32)

def with_extras(x, which, extras, width=64):
    lane = lax.broadcasted_iota(jnp.int32, (1, x.shape[1]), 1)
    spare = lane - width if which == 0 else lane
    own = (lane < width) if which == 0 else (lane >= width)
    fill = jnp.zeros_like(x)
    for i, extra in enumerate(extras):
        fill = jnp.where(spare == i, extra, fill)
    return jnp.where(own, x, fill).astype(jnp.bfloat16)

def three_parts(x):
    low = lambda v: v.astype(jnp.bfloat16).astype(jnp.float32)
    high = low(x)
    middle = low(x - high)
    return [high, middle, low(x - high - middle)]

def slot_floor(size, length):
    return jnp.where(lax.broadcasted_iota(jnp.int32, (size, 1), 0) < length, 0.0, floor_score)

def skew(row, wide):
    return pltpu.roll(jnp.broadcast_to(row, (STRIP, wide)), wide - (STRIP - 1), 1, stride=1, stride_axis=0)

def fwd_kernel(len_ref, q_ref, k_ref, v_ref, t_ref, *refs, rows, seq_len, first):
    o_ref, lse_ref, strip, kx, vx = refs[-5:]
    wide = t_ref.shape[-1]
    pair = first + pl.program_id(0)
    per = rows // STRIP
    lane = lax.broadcasted_iota(jnp.int32, (1, 128), 1)
    k2 = k_ref[...].astype(jnp.float32)
    vx[:, 0:128] = v_ref[...]
    vx[:, 128:256] = jnp.ones_like(v_ref[...])
    for a in range(2):
        kx[a] = with_extras(k2, a, [slot_floor(seq_len, len_ref[0])])
        strip[a] = skew(t_ref[pl.ds(2 * pair + a, 1), :], wide)

    def step(b, carry):
        base = b * rows
        q2 = q_ref[pl.ds(base, rows), :].astype(jnp.float32)
        outs, stats = [], []
        for a in range(2):
            scores = _dot(with_extras(q2, a, [1.0]), kx[a], NT)
            parts = []
            for i in range(per):
                off = (seq_len - STRIP) - (b * per + i) * STRIP
                parts.append(strip[a, :, pl.ds(off, seq_len)])
            scores = scores + (jnp.concatenate(parts, 0) if per > 1 else parts[0])
            top = jnp.max(scores, axis=1, keepdims=True)
            probs = jnp.exp2(scores - top).astype(jnp.bfloat16)
            out = _dot(probs, vx[...])
            outs.append(out[:, 0:128] / out[:, 128:256])
            stats.append(top + jnp.log2(out[:, 128:256]))
        o_ref[pl.ds(base, rows), :] = jnp.where(lane < 64, outs[0], outs[1]).astype(jnp.bfloat16)
        lse_ref[0, pl.ds(base, rows), :] = jnp.where(lane < 64, stats[0], stats[1])
        return carry

    for b in range(seq_len // rows):
        step(b, 0)

def attn_fwd(length, q, k, v, t, first, count, prev=(), rows=256):
    seq_len, width = q.shape
    pairs = width // 128
    wide = t.shape[-1]
    blk = pl.BlockSpec((seq_len, 128), lambda p, n: (0, first + p))
    return pl.pallas_call(
        functools.partial(fwd_kernel, rows=rows, seq_len=seq_len, first=first),
        out_shape=(jax.ShapeDtypeStruct((seq_len, width), jnp.bfloat16),
                   jax.ShapeDtypeStruct((pairs, seq_len, 128), jnp.float32)),
        grid_spec=pltpu.PrefetchScalarGridSpec(
            num_scalar_prefetch=1, grid=(count,),
            in_specs=[blk, blk, blk, pl.BlockSpec(t.shape, lambda p, n: (0, 0))] + [pl.BlockSpec(memory_space=pl.ANY)] * len(prev),
            out_specs=[blk, pl.BlockSpec((1, seq_len, 128), lambda p, n: (first + p, 0, 0))],
            scratch_shapes=[pltpu.VMEM((2, STRIP, wide), jnp.float32), pltpu.VMEM((2, seq_len, 128), jnp.bfloat16),
                            pltpu.VMEM((seq_len, 256), jnp.bfloat16)]),
        input_output_aliases={5 + i: i for i in range(len(prev))},
        compiler_params=pltpu.CompilerParams(vmem_limit_bytes=LIMIT),
        cost_estimate=LIGHT,
        name="attn_fwd",
    )(length, q, k, v, t, *prev)

def bwd_kernel(len_ref, q_ref, k_ref, v_ref, do_ref, o_ref, lse_ref, t_ref, *refs, rows, seq_len, first):
    dq_ref, dk_ref, dv_ref, g_ref, strip, acc, dq_acc, qx, kx, vx, dox = refs[-11:]
    wide = t_ref.shape[-1]
    local_pair = pl.program_id(0)
    pair = first + local_pair
    per = rows // STRIP
    lane = lax.broadcasted_iota(jnp.int32, (1, 128), 1)
    up = lambda ref: ref[...].astype(jnp.float32)
    floor = slot_floor(seq_len, len_ref[0])
    prod = up(do_ref) * up(o_ref)
    for a in range(2):
        mine = (lane < 64) if a == 0 else (lane >= 64)
        delta = jnp.sum(jnp.where(mine, prod, 0.0), axis=1, keepdims=True)
        lse = lse_ref[0, :, 64 * a:64 * a + 1]
        qx[a] = with_extras(up(q_ref), a, [1.0] + three_parts(-lse))
        kx[a] = with_extras(up(k_ref), a, [floor, 1.0, 1.0, 1.0])
        vx[a] = with_extras(up(v_ref), a, [1.0, 1.0, 1.0])
        dox[a] = with_extras(up(do_ref), a, three_parts(-delta))
        strip[a] = skew(t_ref[pl.ds(2 * pair + a, 1), :], wide)
    acc[...] = jnp.zeros_like(acc)
    k2t = k_ref[...].T
    dq_acc[...] = jnp.zeros_like(dq_acc)

    def step(b, carry):
        at = pl.ds(b * rows, rows)
        dks, dvs = [], []
        for a in range(2):
            scores = _dot(kx[a, at, :], qx[a], NT)
            offs = [(seq_len - STRIP) - (b * per + i) * STRIP for i in range(per)]
            bias = [strip[a, :, pl.ds(off, seq_len)] for off in offs]
            probs = jnp.exp2(scores + (jnp.concatenate(bias, 0) if per > 1 else bias[0]))
            grad_scores = probs * _dot(vx[a, at, :], dox[a], NT)
            for i, off in enumerate(offs):
                acc[a, :, pl.ds(off, seq_len)] += grad_scores[i * STRIP:(i + 1) * STRIP]
            probs_b = probs.astype(jnp.bfloat16)
            gs_b = grad_scores.astype(jnp.bfloat16)
            dvs.append(_dot(probs_b, do_ref[...]))
            dks.append(_dot(gs_b, q_ref[...]))
            dq_acc[a] += _dot(k2t[:, b * rows:(b + 1) * rows], gs_b)
        dk_ref[at, :] = (jnp.where(lane < 64, dks[0], dks[1]) * LN2).astype(jnp.bfloat16)
        dv_ref[at, :] = jnp.where(lane < 64, dvs[0], dvs[1]).astype(jnp.bfloat16)
        return carry

    for b in range(seq_len // rows):
        step(b, 0)
    dq_ref[...] = jnp.concatenate([dq_acc[0, 0:64], dq_acc[1, 64:128]], 0).T.astype(jnp.bfloat16)
    for a in range(2):
        sums = acc[a]
        half = STRIP
        while half > 8:
            half //= 2
            sums = sums[:half] + pltpu.roll(sums[half:], wide - half, 1)
        while half > 1:
            half //= 2
            sums = sums + pltpu.roll(pltpu.roll(sums, 8 - half, 0), wide - half, 1)
        g_ref[pl.ds(2 * local_pair + a, 1), :] = pltpu.roll(sums, STRIP - 1, 1)[0:1]

def attn_bwd(length, q, k, v, do, o, lse, trev, first, count, prev=None, rows=512):
    seq_len, width = q.shape
    wide = trev.shape[-1]
    blk = pl.BlockSpec((seq_len, 128), lambda p, n: (0, first + p))
    mat = jax.ShapeDtypeStruct((seq_len, width), jnp.bfloat16)
    prev = tuple(prev) if prev is not None else ()
    return pl.pallas_call(
        functools.partial(bwd_kernel, rows=rows, seq_len=seq_len, first=first),
        out_shape=(mat, mat, mat, jax.ShapeDtypeStruct((2 * count, wide), jnp.float32)),
        grid_spec=pltpu.PrefetchScalarGridSpec(
            num_scalar_prefetch=1, grid=(count,),
            in_specs=[blk, blk, blk, blk, blk, pl.BlockSpec((1, seq_len, 128), lambda p, n: (first + p, 0, 0)),
                      pl.BlockSpec(trev.shape, lambda p, n: (0, 0))] + [pl.BlockSpec(memory_space=pl.ANY)] * len(prev),
            out_specs=[blk, blk, blk, pl.BlockSpec((2 * count, wide), lambda p, n: (0, 0))],
            scratch_shapes=[pltpu.VMEM((2, STRIP, wide), jnp.float32), pltpu.VMEM((2, STRIP, wide), jnp.float32),
                            pltpu.VMEM((2, 128, seq_len), jnp.float32)] + [pltpu.VMEM((2, seq_len, 128), jnp.bfloat16)] * 4),
        input_output_aliases={8 + i: i for i in range(len(prev))},
        compiler_params=pltpu.CompilerParams(vmem_limit_bytes=LIMIT),
        cost_estimate=LIGHT,
        name="attn_bwd",
    )(length, q, k, v, do, o, lse, trev, *prev)

ANY = pl.BlockSpec(memory_space=pl.ANY)
VM = pl.BlockSpec(memory_space=pltpu.VMEM)
SM = pl.BlockSpec(memory_space=pltpu.SMEM)

def rms_inverse(value):
    return lax.rsqrt(jnp.mean(value * value, axis=1, keepdims=True) + epsilon)

def pull_sequence(me, whole_ref, chip_ref, core_ref, dst, sem):
    rows = whole_ref.shape[1]
    for mask, src in enumerate((whole_ref.at[me], core_ref.at[0], chip_ref.at[me & 1], core_ref.at[1])):
        at = pl.multiple_of((me ^ mask) * rows, rows)
        pltpu.make_async_copy(src, dst.at[pl.ds(at, rows), :], sem).start()

def qkv_kernel(ids_ref, x4_ref, chip_ref, core_ref, *refs, masks):
    gathered = refs[:len(masks)]
    bucket_ref = refs[len(masks)]
    x_out, h_out, q_out, k_out, v_out, w_out, gain_ref, t_ref, trev_ref, xs, hs, ps, ws, es, sems = refs[len(masks) + 1:]
    me, flat = ids_ref[0], ids_ref[1]
    width = xs.shape[1]
    own = width // es.shape[0]
    pull_sequence(me, x4_ref, chip_ref, core_ref, xs, sems.at[0])
    for ref, ids in zip(gathered, masks):
        for j, mask in enumerate(ids):
            shard = flat ^ mask
            pltpu.make_async_copy(ref.at[j, 3 * own:3 * own + 16, :], es.at[shard], sems.at[1]).start()
    for ref, ids in zip(gathered, masks):
        for j, mask in enumerate(ids):
            at = pl.multiple_of((flat ^ mask) * own, own)
            for i in range(3):
                pltpu.make_async_copy(ref.at[j, i * own:(i + 1) * own, :], ws.at[pl.ds(at, own), i * width:(i + 1) * width], sems.at[2]).start()
    pltpu.make_async_copy(es, es, sems.at[1]).wait()
    extras = es[...].astype(jnp.float32)
    gains = jnp.sum(extras, axis=0)
    gain_ref[...] = gains[0:8]
    table = extras[:, 8, 0:128].astype(jnp.bfloat16)
    ids = lax.broadcasted_iota(jnp.int32, (es.shape[0], 1), 0)
    heads = t_ref.shape[0]
    for i, ref in enumerate((t_ref, trev_ref)):
        hot = jnp.where(bucket_ref[i:i + 1, :] == ids, 1.0, 0.0).astype(jnp.bfloat16)
        ref[...] = _dot(table, hot, TN)[0:heads] * LOG2E
    pltpu.make_async_copy(xs, xs, sems.at[0]).wait()
    part = 256
    def norm(i, carry):
        at = pl.ds(pl.multiple_of(i * part, part), part)
        x = xs[at, :].astype(jnp.float32)
        hs[at, :] = (x * rms_inverse(x) * gains[0:1]).astype(jnp.bfloat16)
        return carry
    lax.fori_loop(0, xs.shape[0] // part, norm, 0)
    copies = [pltpu.make_async_copy(xs, x_out, sems.at[0]), pltpu.make_async_copy(hs, h_out, sems.at[1])]
    for copy in copies:
        copy.start()
    pltpu.make_async_copy(ws, ws, sems.at[2]).wait()
    copies.append(pltpu.make_async_copy(ws, w_out, sems.at[2]))
    copies[-1].start()
    for i, ref in enumerate((q_out, k_out, v_out)):
        full = _dot(hs[...], ws[:, i * width:(i + 1) * width])
        ps[i] = (full * LOG2E if i == 0 else full).astype(jnp.bfloat16)
        copies.append(pltpu.make_async_copy(ps.at[i], ref, sems.at[3 + i]))
        copies[-1].start()
    for copy in copies:
        copy.wait()

def qkv_fwd(ids, x4, came, gathered, masks, bucket_rows, heads):
    parts, rows, width = x4.shape
    total = parts * rows
    shards = sum(len(m) for m in masks)
    mat = jax.ShapeDtypeStruct((total, width), jnp.bfloat16)
    wide = bucket_rows.shape[1]
    vm = lambda *s: pltpu.VMEM(s, jnp.bfloat16)
    return pl.pallas_call(
        functools.partial(qkv_kernel, masks=masks),
        out_shape=(mat,) * 5 + (jax.ShapeDtypeStruct((width, 3 * width), jnp.bfloat16), jax.ShapeDtypeStruct((8, width), jnp.float32),
                                jax.ShapeDtypeStruct((heads, wide), jnp.float32), jax.ShapeDtypeStruct((heads, wide), jnp.float32)),
        in_specs=[SM] + [ANY] * (3 + len(gathered)) + [VM],
        out_specs=[ANY] * 6 + [VM] * 3,
        scratch_shapes=[vm(total, width), vm(total, width), vm(3, total, width), vm(width, 3 * width), vm(shards, 16, width), pltpu.SemaphoreType.DMA((6,))],
        compiler_params=pltpu.CompilerParams(vmem_limit_bytes=LIMIT),
        cost_estimate=LIGHT,
        name="qkv_fwd",
    )(ids, x4, *came, *gathered, bucket_rows)

def gelu_both(v):
    t = jnp.tanh(root_coef * (v + cubic_coef * v * v * v))
    half = 0.5 * (1.0 + t)
    slope = half + 0.5 * v * (1.0 - t * t) * (root_coef * (1.0 + 3.0 * cubic_coef * v * v))
    return v * half, slope

def by_core(core, keep, send, src, dst_rows, sem, lead=slice(None), src_rows=slice(None), lanes=slice(None)):
    for parity in range(2):
        @pl.when(core == parity)
        def _():
            for dst, at in ((keep, parity), (send, 1 - parity)):
                pltpu.make_async_copy(src.at[lead, at, src_rows, lanes], dst.at[lead, dst_rows, lanes], sem).start()

def ff_chunks(h2, h2t, gm, acc, gh2, ws_in, ws_back, st_in, st_back, row_in, emit, before_add, cols=512):
    steps = ws_in.shape[1] // cols
    half, width = st_back.shape[2:]
    own = width // (2 * st_in.shape[0])
    wide = width // cols
    group = cols // (2 * half)

    def step(c, carry):
        at = pl.ds(pl.multiple_of(c * cols, cols), cols)
        win, wback = ws_in[:, at], ws_back[at, :]
        pre = _dot(h2[...], win)
        grad_active = _dot(gm[...], wback, NT)
        act, slope = gelu_both(pre)
        active = act.astype(jnp.bfloat16)
        gpre = (grad_active * slope).astype(jnp.bfloat16)
        @pl.when(c == 0)
        def _():
            before_add()
        acc[...] += _dot(active, wback)
        gh2[...] += _dot(gpre, win, NT)
        lead = pl.ds(c * group, group)
        st_back[lead] = _dot(active, gm[...], TN).astype(jnp.bfloat16).reshape(group, 2, half, width)
        emit(st_back, 0, lead=lead, dst_rows=slice(0, half))
        up = pl.multiple_of((c // wide) * own, own)
        lanes = pl.ds(pl.multiple_of((c % wide) * cols, cols), cols)
        st_in[:, :, pl.ds(up, own), lanes] = _dot(h2t[...], gpre).astype(jnp.bfloat16).reshape(-1, 2, own, cols)
        emit(st_in, 1, src_rows=pl.ds(up, own), dst_rows=pl.ds(row_in + up, own), lanes=lanes)
        return carry
    lax.fori_loop(0, steps, step, 0)

def finish_chunks(st_in, st_back, sems):
    pltpu.make_async_copy(st_back, st_back, sems.at[0]).wait()
    pltpu.make_async_copy(st_in, st_in, sems.at[1]).wait()

def aligned(at, size):
    return at if isinstance(at, int) else pl.multiple_of(at, size)

def pull_ff(flat, gathered, masks, ws_in, ws_back, row_in, sems):
    width = ws_in.shape[0]
    shards = sum(len(m) for m in masks)
    own, half = width // shards, ws_back.shape[0] // shards
    for ref, ids in zip(gathered, masks):
        for j, mask in enumerate(ids):
            shard = flat ^ mask
            pltpu.make_async_copy(ref.at[j, 0:half, :], ws_back.at[pl.ds(aligned(shard * half, half), half), :], sems.at[1]).start()
            at = pl.ds(aligned(shard * own, own), own)
            for i in range(ws_in.shape[1] // width):
                pltpu.make_async_copy(ref.at[j, row_in + i * own:row_in + (i + 1) * own, :], ws_in.at[at, i * width:(i + 1) * width], sems.at[0]).start()

def mid_a_kernel(ids_ref, x_hbm, o_hbm, g4_ref, chip_ref, core_ref, gain_ref, *refs, masks):
    gathered = refs[:len(masks)]
    (mixed_out, acc_out, gh2_out, h2_out, h2t_out, gm_out, wo_out, keep_out, send_out,
     xs, os, wo, ws_in, ws_back, mixed, h2, h2t, acc, gh2, gm, st_in, st_back, sems) = refs[len(masks):]
    flat = ids_ref[1]
    rows, width = xs.shape
    half, own = st_back.shape[2], width // (2 * st_in.shape[0])
    core = flat & 1
    def emit(src, which, **at):
        by_core(core, keep_out, send_out, src, sem=sems.at[which], **at)
    loads = [pltpu.make_async_copy(x_hbm, xs, sems.at[0]), pltpu.make_async_copy(o_hbm, os, sems.at[1])]
    for load in loads:
        load.start()
    for ref, ids in zip(gathered, masks):
        for j, mask in enumerate(ids):
            at = pl.ds(pl.multiple_of((flat ^ mask) * own, own), own)
            pltpu.make_async_copy(ref.at[j, half:half + own, :], wo.at[at, :], sems.at[2]).start()
    pull_ff(flat, gathered, masks, ws_in, ws_back, half + own, sems.at[3:5])
    pull_sequence(ids_ref[0], g4_ref, chip_ref, core_ref, gm, sems.at[5])
    for load in loads:
        load.wait()
    pltpu.make_async_copy(wo, wo, sems.at[2]).wait()
    stores = [pltpu.make_async_copy(wo, wo_out, sems.at[2])]
    stores[0].start()
    part = 256
    def load_rows(i, carry):
        at = pl.ds(pl.multiple_of(i * part, part), part)
        value = xs[at, :].astype(jnp.float32) + _dot(os[at, :], wo[...])
        mixed[at, :] = value
        acc[at, :] = value
        hidden = (value * rms_inverse(value) * gain_ref[1:2, :]).astype(jnp.bfloat16)
        h2[at, :] = hidden
        h2t[:, at] = hidden.T
        gh2[at, :] = jnp.zeros_like(value)
        return carry
    lax.fori_loop(0, rows // part, load_rows, 0)
    pltpu.make_async_copy(gm, gm, sems.at[5]).wait()
    row_ok = lax.broadcasted_iota(jnp.int32, (rows, 1), 0) < ids_ref[2]
    gm[...] = jnp.where(row_ok, gm[...], jnp.zeros_like(gm[...]))
    pltpu.make_async_copy(ws_in, ws_in, sems.at[3]).wait()
    pltpu.make_async_copy(ws_back, ws_back, sems.at[4]).wait()
    for i, (src, dst) in enumerate(((mixed, mixed_out), (h2, h2_out), (h2t, h2t_out), (gm, gm_out))):
        stores.append(pltpu.make_async_copy(src, dst, sems.at[6 + i]))
        stores[-1].start()
    ff_chunks(h2, h2t, gm, acc, gh2, ws_in, ws_back, st_in, st_back, half, emit, lambda: None)
    for i, (src, dst) in enumerate(((acc, acc_out), (gh2, gh2_out))):
        stores.append(pltpu.make_async_copy(src, dst, sems.at[3 + i]))
        stores[-1].start()
    finish_chunks(st_in, st_back, sems.at[0:2])
    for store in stores:
        store.wait()

def mid_a(ids, x, o, g4, came, gains, gathered, masks, ff):
    rows, width = x.shape
    shards = sum(len(m) for m in masks)
    half = ff // shards
    low = lambda *s: jax.ShapeDtypeStruct(s, jnp.bfloat16)
    full = lambda *s: jax.ShapeDtypeStruct(s, jnp.float32)
    vm = lambda *s: pltpu.VMEM(s, jnp.bfloat16)
    vf = lambda *s: pltpu.VMEM(s, jnp.float32)
    stack = half + ff // width * (width // shards)
    return pl.pallas_call(
        functools.partial(mid_a_kernel, masks=masks),
        out_shape=(full(rows, width), full(rows, width), full(rows, width), low(rows, width), low(width, rows), low(rows, width), low(width, width), low(shards // 2, stack, width), low(shards // 2, stack, width)),
        in_specs=[SM] + [ANY] * 5 + [VM] + [ANY] * len(gathered), out_specs=[ANY] * 9,
        scratch_shapes=[vm(rows, width), vm(rows, width), vm(width, width), vm(width, ff), vm(ff, width), vf(rows, width), vm(rows, width), vm(width, rows),
                        vf(rows, width), vf(rows, width), vm(rows, width), vm(shards // 2, 2, stack - half, width), vm(shards // 2, 2, half, width), pltpu.SemaphoreType.DMA((10,))],
        compiler_params=pltpu.CompilerParams(vmem_limit_bytes=LIMIT),
        cost_estimate=LIGHT,
        name="mid_a",
    )(ids, x, o, g4, *came, gains, *gathered)

def mid_b_kernel(ids_ref, gain_ref, mixed_hbm, acc_hbm, gh2_hbm, h2_hbm, h2t_hbm, gm_hbm, wo_hbm, o_hbm, full_ref, *refs):
    (out_ref, gb_out, do_ref, keep_out, send_out,
     os, wo, ws_in, ws_back, mixed, h2, h2t, acc, gh2, gm, gb, st_in, st_back, st_o, sems) = refs
    rows, width = os.shape
    shards, half, own = 2 * st_in.shape[0], st_back.shape[2], width // (2 * st_in.shape[0])
    core = ids_ref[1] & 1
    def emit(src, which, **at):
        by_core(core, keep_out, send_out, src, sem=sems.at[which], **at)
    early = [(h2_hbm, h2), (gm_hbm, gm), (h2t_hbm, h2t)]
    late = [(acc_hbm, acc), (gh2_hbm, gh2), (mixed_hbm, mixed), (wo_hbm, wo), (o_hbm, os)]
    early = [pltpu.make_async_copy(a, b, sems.at[4 + i]) for i, (a, b) in enumerate(early)]
    late = [pltpu.make_async_copy(a, b, sems.at[7 + i]) for i, (a, b) in enumerate(late)]
    for load in early:
        load.start()
    pull_ff(0, (full_ref,), (range(shards),), ws_in, ws_back, half, sems.at[2:4])
    for load in late:
        load.start()
    for load in early:
        load.wait()
    pltpu.make_async_copy(ws_in, ws_in, sems.at[2]).wait()
    pltpu.make_async_copy(ws_back, ws_back, sems.at[3]).wait()
    def before_add():
        late[0].wait()
        late[1].wait()
    ff_chunks(h2, h2t, gm, acc, gh2, ws_in, ws_back, st_in, st_back, half + own, emit, before_add)
    for load in late[2:]:
        load.wait()
    part = 256
    def finish(i, carry):
        at = pl.ds(pl.multiple_of(i * part, part), part)
        out_ref[at, :] = acc[at, :].astype(jnp.bfloat16)
        value = mixed[at, :]
        inverse = rms_inverse(value)
        normed = value * inverse
        scaled = gh2[at, :] * gain_ref[1:2, :]
        grad = inverse * (scaled - normed * jnp.mean(scaled * normed, axis=1, keepdims=True)) + gm[at, :].astype(jnp.float32)
        low = grad.astype(jnp.bfloat16)
        gb[at, :] = low
        do_ref[at, :] = _dot(low, wo[...], NT).astype(jnp.bfloat16)
        return carry
    lax.fori_loop(0, rows // part, finish, 0)
    st_o[...] = _dot(os[...], gb[...], TN).astype(jnp.bfloat16).reshape(st_o.shape)
    emit(st_o, 2, dst_rows=slice(half, half + own))
    store = pltpu.make_async_copy(gb, gb_out, sems.at[3])
    store.start()
    finish_chunks(st_in, st_back, sems.at[0:2])
    pltpu.make_async_copy(st_o, st_o, sems.at[2]).wait()
    store.wait()

def mid_b(ids, gains, state, o, full, ff):
    rows, width = o.shape
    shards = full.shape[0]
    half, own = ff // shards, width // shards
    low = lambda *s: jax.ShapeDtypeStruct(s, jnp.bfloat16)
    vm = lambda *s: pltpu.VMEM(s, jnp.bfloat16)
    vf = lambda *s: pltpu.VMEM(s, jnp.float32)
    rest = ff // width * own
    return pl.pallas_call(
        mid_b_kernel,
        out_shape=(low(rows, width), low(rows, width), low(rows, width), low(shards // 2, half + own + rest, width), low(shards // 2, half + own + rest, width)),
        in_specs=[SM, VM] + [ANY] * 9, out_specs=[VM, ANY, VM, ANY, ANY],
        scratch_shapes=[vm(rows, width), vm(width, width), vm(width, ff), vm(ff, width), vf(rows, width), vm(rows, width), vm(width, rows),
                        vf(rows, width), vf(rows, width), vm(rows, width), vm(rows, width), vm(shards // 2, 2, rest, width), vm(shards // 2, 2, half, width), vm(shards // 2, 2, own, width),
                        pltpu.SemaphoreType.DMA((12,))],
        compiler_params=pltpu.CompilerParams(vmem_limit_bytes=LIMIT),
        cost_estimate=LIGHT,
        name="mid_b",
    )(ids, gains, *state, o, full)

def gw_kernel(ids_ref, h_ref, dq_ref, dk_ref, dv_ref, bucket_ref, *refs):
    keep_out, send_out, st, sems = refs[-4:]
    offs = jnp.concatenate([ref[...] for ref in refs[:-4]], 0)
    pairs, _, stack, width = st.shape
    own = width // (2 * pairs)
    core = ids_ref[1] & 1
    ids = lax.broadcasted_iota(jnp.int32, (2 * pairs, 1), 0)
    hot = jnp.where(bucket_ref[1:2, :] == ids, 1.0, 0.0)
    table = lax.dot_general(hot, offs, NT, precision=lax.Precision.HIGHEST, preferred_element_type=jnp.float32)
    heads = offs.shape[0]
    st[:, :, 3 * own:, :] = jnp.zeros((pairs, 2, stack - 3 * own, width), jnp.bfloat16)
    st[:, :, 3 * own:3 * own + 1, 0:heads] = table.astype(jnp.bfloat16).reshape(pairs, 2, 1, heads)
    for i, ref in enumerate((dq_ref, dk_ref, dv_ref)):
        at = slice(i * own, (i + 1) * own) if i < 2 else slice(i * own, stack)
        st[:, :, i * own:(i + 1) * own, :] = _dot(h_ref[...], ref[...], TN).astype(jnp.bfloat16).reshape(pairs, 2, own, width)
        by_core(core, keep_out, send_out, st, at, sems.at[0], src_rows=at)
    pltpu.make_async_copy(st, st, sems.at[0]).wait()

def qkv_gw(ids, h, dq, dk, dv, bucket_rows, offs, shards):
    rows, width = h.shape
    stack = 3 * width // shards + 16
    half = jax.ShapeDtypeStruct((shards // 2, stack, width), jnp.bfloat16)
    return pl.pallas_call(
        gw_kernel, out_shape=(half, half),
        in_specs=[SM] + [VM] * (5 + len(offs)), out_specs=[ANY, ANY],
        scratch_shapes=[pltpu.VMEM((shards // 2, 2, stack, width), jnp.bfloat16), pltpu.SemaphoreType.DMA((1,))],
        compiler_params=pltpu.CompilerParams(vmem_limit_bytes=LIMIT),
        cost_estimate=LIGHT,
        name="qkv_gw",
    )(ids, h, dq, dk, dv, bucket_rows, *offs)

def gx_kernel(x_ref, gb_ref, dq_ref, dk_ref, dv_ref, gain_ref, w_ref, out_ref):
    width = x_ref.shape[1]
    grad = _dot(dq_ref[...], w_ref[:, :width], NT)
    grad += _dot(dk_ref[...], w_ref[:, width:2 * width], NT)
    grad += _dot(dv_ref[...], w_ref[:, 2 * width:3 * width], NT)
    x = x_ref[...].astype(jnp.float32)
    inverse = rms_inverse(x)
    normed = x * inverse
    scaled = grad * gain_ref[0:1, :]
    out = inverse * (scaled - normed * jnp.mean(scaled * normed, axis=1, keepdims=True)) + gb_ref[...].astype(jnp.float32)
    out_ref[...] = out.astype(jnp.bfloat16)

def qkv_gx(x, gb, dq, dk, dv, gains, w, rows=512):
    total, width = x.shape
    blk = pl.BlockSpec((rows, width), lambda i: (i, 0))
    return pl.pallas_call(
        gx_kernel, out_shape=jax.ShapeDtypeStruct((total, width), jnp.bfloat16), grid=(total // rows,),
        in_specs=[blk] * 5 + [pl.BlockSpec(gains.shape, lambda i: (0, 0)),
                              pl.BlockSpec((width, 3 * width), lambda i: (0, 0), pipeline_mode=pl.Buffered(1))],
        out_specs=blk,
        compiler_params=pltpu.CompilerParams(vmem_limit_bytes=LIMIT),
        cost_estimate=LIGHT,
        name="qkv_gx",
    )(x, gb, dq, dk, dv, gains, w)

def swap(value, axis, mask):
    return lax.ppermute(value, axis, [(i, i ^ mask) for i in range(lax.axis_size(axis))])


def send_chip(blocks, me):
    return swap(lax.dynamic_slice_in_dim(blocks, 2 * (1 - me // 2), 2, 0), "seq", 2)


def send_core(blocks, from_chip, me):
    own = lax.dynamic_index_in_dim(blocks, me ^ 1, 0)
    passed = lax.dynamic_index_in_dim(from_chip, 1 - me % 2, 0)
    return swap(jnp.concatenate([own, passed], 0), "seq", 1)


class Gather:
    def __init__(self, shard):
        shard = shard[None]
        self.sent = [shard] + [swap(shard, "dp", 2 * z) for z in (1, 2, 3)]
        self.pieces, self.masks = [], []

    def take(self, piece, mask, rows=(0, 1, 2, 3)):
        ids = tuple(8 * z | mask for z in rows)
        self.pieces += [piece, swap(piece, "seq", 1)]
        self.masks += [ids, tuple(m | 1 for m in ids)]

    def fill(self):
        self.own = jnp.concatenate(self.sent, 0)

    def sides(self):
        self.x, self.y = swap(self.own, "seq", 2), swap(self.own, "dp", 1)

    def corner_halves(self):
        self.near, self.far = swap(self.y[:2], "seq", 2), swap(self.x[2:], "dp", 1)

    def corner_y(self):
        self.corner = swap(self.x, "dp", 1)

    def all_pieces(self):
        return tuple(self.pieces), tuple(self.masks)


class Scatter:
    def __init__(self, keep, send, pos, corner_y):
        self.z, self.y, self.x = pos
        cube = (4, 2, 2) + keep.shape[1:]
        self.mine, self.sent, self.corner_y = keep.reshape(cube), send.reshape(cube), corner_y
        self.other = swap(self.sent, "seq", 1)

    def fold(self):
        pick = lambda v, at, axis: lax.dynamic_index_in_dim(v, at, axis, keepdims=False)
        def quarter(dy, dx):
            cut = lambda v: pick(pick(v, self.y ^ dy, 1), self.x ^ dx, 1).astype(jnp.float32)
            return (cut(self.mine) + cut(self.other)).astype(jnp.bfloat16)
        far = quarter(1, 1)
        self.to_x, self.to_y, self.own = quarter(0, 1), quarter(1, 0), quarter(0, 0)
        if self.corner_y:
            self.came_x, self.came_y = None, swap(far, "dp", 1)
        else:
            self.came_x, self.came_y = swap(far[:2], "seq", 2), swap(far[2:], "dp", 1)

    def turn(self):
        add = lambda a, b: (a.astype(jnp.float32) + b.astype(jnp.float32)).astype(jnp.bfloat16)
        if self.corner_y:
            to_y, = tie(self.came_y, self.to_y)
            to_x = add(self.to_x, self.came_y)
        else:
            to_x = lax.dynamic_update_slice_in_dim(self.to_x, add(self.to_x[2:], self.came_y), 2, 0)
            to_y = lax.dynamic_update_slice_in_dim(self.to_y, add(self.to_y[:2], self.came_x), 0, 0)
        self.sent = (to_x, to_y)
        self.came_x, self.came_y = swap(to_x, "seq", 2), swap(to_y, "dp", 1)

    def column(self):
        total = self.own.astype(jnp.float32) + self.came_x.astype(jnp.float32) + self.came_y.astype(jnp.float32)
        total = total.astype(jnp.bfloat16)
        block = lambda k: lax.dynamic_index_in_dim(total, self.z ^ k, 0, keepdims=False)
        self.mine = block(0)
        self.came = [swap(block(k), "dp", 2 * k) for k in (1, 2, 3)]

    def result(self):
        return sum((c.astype(jnp.float32) for c in self.came), self.mine.astype(jnp.float32))


def place(blocks, from_chip, from_core, me):
    for mask, block in ((1, from_core[0:1]), (2, lax.dynamic_index_in_dim(from_chip, me % 2, 0)), (3, from_core[1:2])):
        blocks = lax.dynamic_update_slice_in_dim(blocks, block, me ^ mask, 0)
    return blocks


def tie(first, *later):
    return lax.optimization_barrier((first,) + later)[1:]


def local_whole(tokens, cotangent, lengths, buckets, norm1_gain, w_query, w_key, w_value, w_out, rel_table, norm2_gain, w_in, w_back):
    micro_count, seq_count, rows, width = tokens.shape
    parts = micro_count * seq_count
    both = ("dp", "seq")
    me, dp = lax.axis_index("seq"), lax.axis_index("dp")
    shards = lax.axis_size("seq") * lax.axis_size("dp")
    flat = dp * parts + me
    pos = (dp // 2, dp % 2, me // 2)
    low = lambda v: v.astype(jnp.bfloat16)
    up = lambda v: v.astype(jnp.float32)
    own, ff_own = w_query.shape[0], w_back.shape[0]
    ids = jnp.stack([me, flat, lax.dynamic_index_in_dim(lengths.reshape(parts), me, 0, keepdims=False)])
    length = ids[2:3]

    place_row = lambda v: lax.dynamic_update_slice(jnp.zeros((1, width), jnp.bfloat16), low(v)[None], (0, flat * own))
    small = jnp.concatenate([place_row(norm1_gain), place_row(norm2_gain), jnp.zeros((6, width), jnp.bfloat16),
                             jnp.pad(low(rel_table)[None], ((0, 7), (0, width - HEADS)))], 0)
    shard1 = jnp.concatenate([low(w_query), low(w_key), low(w_value), small], 0)
    ff = w_in.shape[1] // 2
    half = ff_own // 2
    halves = low(w_in).reshape(own, shards, 2, half)
    in_half = lambda i: [halves[:, :, i].reshape(own, ff)[:, j:j + width] for j in range(0, ff, width)]
    shard2 = jnp.concatenate([low(w_back[:half]), low(w_out)] + in_half(0), 0)
    shard3 = jnp.concatenate([low(w_back[half:])] + in_half(1), 0)
    x4, g4 = tokens.reshape(parts, rows, width), cotangent.reshape(parts, rows, width)
    bucket_rows = jnp.stack([jnp.pad(buckets, (0, 1), constant_values=-1), jnp.pad(buckets[::-1], (0, 1), constant_values=-1)])

    x_far = lax.dynamic_slice_in_dim(x4, 2 * (1 - me // 2), 2, 0)
    shard1_in, = tie(x_far, shard1)
    x_chip = swap(x_far, "seq", 2)
    g1 = Gather(shard1_in)
    g2 = Gather(shard2)
    g1.fill()
    g1.own, = tie((x_chip, g2.sent[1], shard3), g1.own)
    g1.sides()
    g1.x, g1.y = tie(g2.sent[2], g1.x, g1.y)
    g1.corner_halves()
    g2.fill()
    g1.take(g1.own, 0)
    g1.near, g1.far, g2.own = tie(g1.pieces[1], g1.near, g1.far, g2.own)
    g2.sides()
    g1.x, g1.y, x4_in = tie((g1.near, g1.far), g1.x, g1.y, x4)
    g1.take(g1.x, 2)
    g1.take(g1.y, 4)
    g1.take(g1.near, 6, (0, 1))
    g1.take(g1.far, 6, (2, 3))
    x_core = send_core(x4_in, x_chip, me)
    shard3, = tie((g1.near, g1.far), shard3)
    full3 = lax.all_gather(shard3, both, axis=0, tiled=False)
    x, hidden, q, k, v, w_qkv, gains, t, t_back = qkv_fwd(ids, x4, (x_chip, x_core), *g1.all_pieces(), bucket_rows, HEADS)
    pairs = HEADS // 2
    att = attn_fwd(length, q, k, v, t, 0, 3)
    g2.take(g2.own, 0)
    g2.x, g2.y = tie((att[0], g2.pieces[1]), g2.x, g2.y)
    g2.corner_y()
    g4_in, = tie(g2.x, g4)
    g_chip = send_chip(g4_in, me)
    g2.take(g2.x, 2)
    g2.take(g2.y, 4)
    q_in, = tie((g2.x, g2.y), q)
    attended, lse = attn_fwd(length, q_in, k, v, t, 3, pairs - 3, att)
    g2.corner, g_chip = tie((attended, g2.pieces[3], g2.pieces[5]), g2.corner, g_chip)
    g2.take(g2.corner, 6)
    g_core = send_core(g4, g_chip, me)
    *state, keep3, send3 = mid_a(ids, x, attended, g4, (g_chip, g_core), gains, *g2.all_pieces(), ff)
    sc3 = Scatter(keep3, send3, pos, True)
    out, gb, g_att, keep2, send2 = mid_b(ids, gains, state, attended, full3, ff)
    sc3.other, = tie(gb, sc3.other)
    sc3.fold()
    send2, = tie(sc3.own, send2)
    sc2 = Scatter(keep2, send2, pos, True)
    out4 = out.reshape(parts, rows, width)
    out4, = tie(sc3.own, out4)
    out_chip = send_chip(out4, me)
    count = pairs // 4
    back = lambda first, g, prev: attn_bwd(length, q, k, v, g, attended, lse, t_back, first, count, prev)
    g_att, = tie(sc3.own, g_att)
    dq, dk, dv, off0 = back(0, g_att, None)
    sc2.other, = tie(off0, sc2.other)
    sc2.fold()
    sc3.came_y, = tie(sc2.own, sc3.came_y)
    sc3.turn()
    g_att, = tie(sc3.sent, g_att)
    dq, dk, dv, off1 = back(count, g_att, (dq, dk, dv))
    sc2.came_x, sc2.came_y = tie((off1, out_chip), sc2.came_x, sc2.came_y)
    sc2.turn()
    out4_in, out_chip = tie(sc2.sent, out4, out_chip)
    out_core = send_core(out4_in, out_chip, me)
    g_att, = tie(sc2.sent, g_att)
    dq, dk, dv, off2 = back(2 * count, g_att, (dq, dk, dv))
    sc3.came_x, sc3.came_y = tie((off2, out_core), sc3.came_x, sc3.came_y)
    sc3.column()
    g_att, = tie(sc3.mine, g_att)
    dq, dk, dv, off3 = back(3 * count, g_att, (dq, dk, dv))
    sc2.came_x, sc2.came_y = tie(off3, sc2.came_x, sc2.came_y)
    sc2.column()
    h_in, = tie((sc2.mine, sc3.came), hidden)
    keep1, send1 = qkv_gw(ids, h_in, dq, dk, dv, bucket_rows, (off0, off1, off2, off3), shards)
    sc1 = Scatter(keep1, send1, pos, False)
    gb_in, = tie(send1, gb)
    gx = qkv_gx(x, gb_in, dq, dk, dv, gains, w_qkv)
    sc1.other, = tie(gx, sc1.other)
    sc1.fold()
    out4, out_chip, out_core = tie(sc1.own, out4, out_chip, out_core)
    layer_out = place(out4, out_chip, out_core, me)
    sc1.came_x, sc1.came_y = tie((layer_out, sc2.came), sc1.came_x, sc1.came_y)
    sc1.turn()
    sc2.came = list(tie(sc1.sent, *sc2.came))
    sc3.came = list(tie(sc1.sent, *sc3.came))
    r2, r_a = sc2.result(), sc3.result()
    join = lambda v: jnp.concatenate([v[i:i + own] for i in range(0, v.shape[0], own)], 1).reshape(own, shards, 1, half)
    g_in = jnp.concatenate([join(r_a[half:]), join(r2[half + own:])], 2).reshape(w_in.shape)
    g_back = jnp.concatenate([r_a[:half], r2[:half]], 0)
    g_out = r2[half:half + own]
    g_gain2 = jnp.sum(up(low(w_in)) * g_in, axis=1) / up(low(norm2_gain))
    sc1.came_x, sc1.came_y, g_in, g_back, g_out, g_gain2 = lax.optimization_barrier((sc1.came_x, sc1.came_y, g_in, g_back, g_out, g_gain2))
    sc1.column()
    gx, = tie(sc1.mine, gx)
    gx4 = gx.reshape(parts, rows, width)
    gx_chip = send_chip(gx4, me)
    gx_chip, = tie(sc1.came, gx_chip)
    gx_core = send_core(gx4, gx_chip, me)
    input_grad = place(gx4, gx_chip, gx_core, me)
    sc1.came = list(tie(gx_chip, *sc1.came))
    r1 = sc1.result()
    prod = up(shard1[:3 * own]) * r1[:3 * own]
    g_gain1 = jnp.sum(prod[:own] + prod[own:2 * own] + prod[2 * own:], axis=1) / up(low(norm1_gain))
    return (layer_out.reshape(tokens.shape), input_grad.reshape(tokens.shape), g_gain1, r1[:own], r1[own:2 * own], r1[2 * own:3 * own],
            g_out, r1[3 * own, :HEADS], g_gain2, g_in, g_back)


def local_any(shape, tokens, *rest):
    fits = tuple(shape) == (8, 4) and tokens.shape[0] * tokens.shape[1] == 4 and tokens.shape[3] == HEADS * DH == 1024
    return (local_whole if fits else local)(tokens, *rest)


def solution(mesh):
    return jax.shard_map(
        functools.partial(local_any, mesh.devices.shape),
        mesh=mesh,
        in_specs=(
            P(None, "dp", "seq", None),
            P(None, "dp", "seq", None),
            P(None, "dp"),
            P(),
            P(("dp", "seq")),
            P(("dp", "seq"), None),
            P(("dp", "seq"), None),
            P(("dp", "seq"), None),
            P(("dp", "seq"), None),
            P(("dp", "seq")),
            P(("dp", "seq")),
            P(("dp", "seq"), None),
            P(("dp", "seq"), None),
        ),
        out_specs=(
            P(None, "dp", "seq", None),
            P(None, "dp", "seq", None),
            P(("dp", "seq")),
            P(("dp", "seq"), None),
            P(("dp", "seq"), None),
            P(("dp", "seq"), None),
            P(("dp", "seq"), None),
            P(("dp", "seq")),
            P(("dp", "seq")),
            P(("dp", "seq"), None),
            P(("dp", "seq"), None),
        ),
        check_vma=False,
    )
```
